32 devices in a mesh: gx: 4 (over x, core), gy: 2 (over y), gz: 4 (over z).
Axes of the slice: x: 2, y: 2, z: 4, core: 2. Of those that a mesh axis runs over, the one named last changes fastest.
Arguments:
- features: bfloat16 [32, 64, 32, 512], P(None, 'gx', 'gy', 'gz'), may hold values from -6 to 6
- weight: bfloat16 [27, 32], replicated, may hold values from -0.21875 to 0.21875
- bias: float32 [1], replicated, may hold values from -2 to 2
- label: int32 [64, 32, 512], P('gx', 'gy', 'gz'), may hold values from 0 to 1, as said below
Outputs:
- loss: float32 [1], replicated
- grad_features: bfloat16 [32, 64, 32, 512], P(None, 'gx', 'gy', 'gz')
- grad_weight: float32 [27, 32], replicated
- grad_bias: float32 [1], replicated
The draws below stay inside these ranges and needn't reach their ends.
Inputs may be any that keep to these rules, and one draw needn't show every extreme that they name: label is 1 at vessel voxels and 0 elsewhere.
All inputs are finite; a program needn't handle non-finite values.
Results may differ from the reference program's by a relative error of at most 0.005.
Values may be sent and summed in bfloat16 or wider, within the bound.
No kernel may reach another device: no remote copies, remote signals or barrier semaphores. Data moves between devices by JAX's collectives and lax.ppermute only.
A program may use at most 128 MiB of HBM per device.

```python
import jax
import jax.numpy as jnp
from jax import lax

CH = 32
ITERS = 10
NX = 64
NY = 32
NZ = 512


def disk_mask(key, size_a, size_b, rising):
    count = max(size_a * size_b // 1024, 4)
    key_a = jax.random.fold_in(key, 1)
    key_b = jax.random.fold_in(key, 2)
    key_r = jax.random.fold_in(key, 3)
    key_c = jax.random.fold_in(key, 4)
    first = jax.random.randint(key_a, (count,), 0, size_a, dtype=jnp.int32)
    if rising:
        first = jnp.maximum(first, jax.random.randint(key_c, (count,), 0, size_a, dtype=jnp.int32))
    second = jax.random.randint(key_b, (count,), 0, size_b, dtype=jnp.int32)
    radius = jax.random.randint(key_r, (count,), 1, 4, dtype=jnp.int32)
    pos_a = jnp.arange(size_a, dtype=jnp.int32)[:, None, None]
    pos_b = jnp.arange(size_b, dtype=jnp.int32)[None, :, None]
    delta_a = pos_a - first[None, None, :]
    delta_b = pos_b - second[None, None, :]
    dist = delta_a * delta_a + delta_b * delta_b
    return jnp.any(dist <= radius * radius + radius, axis=2)


def draw_label(key, part):
    along_z = disk_mask(jax.random.fold_in(key, 11), NX, NY, True)
    along_y = disk_mask(jax.random.fold_in(key, 12), NX, NZ, True)
    along_x = disk_mask(jax.random.fold_in(key, 13), NY, NZ, False)
    vessels = along_z[:, :, None] | along_y[:, None, :] | along_x[None, :, :]
    return vessels.astype(jnp.int32)


def block_scale(own_key, extent, shards, low, largest):
    level = 1.0
    for position, blocks in shards:
        heights = jax.random.uniform(jax.random.fold_in(jax.random.fold_in(own_key, 6), position), (blocks,), jnp.float32, low / len(shards), largest / len(shards))
        level = level * jnp.repeat(jnp.exp(heights), extent[position] // blocks).reshape((-1,) + (1,) * (len(extent) - 1 - position))
    return level


def gaussian(rng, dims, spread, reach, cuts=(), kind=jnp.bfloat16):
    gain = block_scale(rng, dims, cuts, -0.22, 0.18) if cuts else 1.0
    result = jax.random.normal(rng, dims, jnp.float32) * spread * gain
    return jnp.minimum(jnp.maximum(result, -reach), reach).astype(kind)


def setup_inputs(seed: int = 0) -> dict:
    keys = jax.random.split(jax.random.key(seed), 5)
    features = gaussian(keys[0], (CH, NX, NY, NZ), 1.0, 6.0, ((1, 4), (2, 2), (3, 4)))
    weight = gaussian(keys[1], (27, CH), (27 * CH) ** -0.5, 0.21875)
    bias = gaussian(keys[2], (1,), 0.5, 2.0, (), jnp.float32)
    label = draw_label(jax.random.fold_in(keys[4], 71), 0)
    return {"features": features, "weight": weight, "bias": bias, "label": label}


temper = 20.0
sharpness = 40.0

def tap_offsets():
    return [(i - 1, j - 1, k - 1) for i in range(3) for j in range(3) for k in range(3)]

def shifted(field, off_x, off_y, off_z):
    padded = jnp.pad(field, 1)
    size_x, size_y, size_z = field.shape
    return padded[1 + off_x:1 + off_x + size_x, 1 + off_y:1 + off_y + size_y, 1 + off_z:1 + off_z + size_z]

def box_total(field):
    padded = jnp.pad(field, 1)
    part = padded[2:] + padded[1:-1] + padded[:-2]
    part = part[:, 2:] + part[:, 1:-1] + part[:, :-2]
    return part[:, :, 2:] + part[:, :, 1:-1] + part[:, :, :-2]

def cross_total(field):
    padded = jnp.pad(field, 1)
    total = padded[1:-1, 1:-1, 1:-1] + padded[2:, 1:-1, 1:-1] + padded[:-2, 1:-1, 1:-1]
    total = total + padded[1:-1, 2:, 1:-1] + padded[1:-1, :-2, 1:-1]
    return total + padded[1:-1, 1:-1, 2:] + padded[1:-1, 1:-1, :-2]

def smooth_relu(value):
    return jax.nn.softplus(sharpness * value) / sharpness

def soft_skeleton(field, box_count, cross_count):

    def erode(value):
        return -jnp.log(cross_total(jnp.exp(-temper * value)) / cross_count) / temper

    def dilate(value):
        return jnp.log(box_total(jnp.exp(temper * value)) / box_count) / temper
    eroded = erode(field)
    skeleton = smooth_relu(field - dilate(eroded))
    for repeat in range(ITERS):
        current = eroded
        eroded = erode(current)
        thinned = smooth_relu(current - dilate(eroded))
        skeleton = skeleton + smooth_relu(thinned - skeleton * thinned)
    return skeleton

def loss_from(totals):
    precision_term = (totals[0] + 1.0) / (totals[1] + 1.0)
    sensitivity = (totals[2] + 1.0) / (totals[3] + 1.0)
    cl_loss = 1.0 - 2.0 * precision_term * sensitivity / (precision_term + sensitivity)
    dice_loss = 1.0 - (2.0 * totals[4] + 1.0) / (totals[5] + totals[6] + 1.0)
    return 0.5 * dice_loss + 0.5 * cl_loss

def reference(features, weight, bias, label):
    channels = features.shape[0]
    shape = features.shape[1:]
    flat = features.reshape(channels, -1)
    tap_maps = jnp.dot(weight, flat, preferred_element_type=jnp.float32).reshape((27,) + shape)
    logits = jnp.zeros(shape, jnp.float32) + bias[0]
    for index, offset in enumerate(tap_offsets()):
        logits = logits + shifted(tap_maps[index], offset[0], offset[1], offset[2])
    ones_field = jnp.ones(shape, jnp.float32)
    box_count = box_total(ones_field)
    cross_count = cross_total(ones_field)
    target = label.astype(jnp.float32)
    target_skel = soft_skeleton(target, box_count, cross_count)

    def loss_of(values):
        predict = jax.nn.sigmoid(values)
        pred_skel = soft_skeleton(predict, box_count, cross_count)
        totals = jnp.stack([jnp.sum(pred_skel * target), jnp.sum(pred_skel), jnp.sum(target_skel * predict), jnp.sum(target_skel), jnp.sum(predict * target), jnp.sum(predict), jnp.sum(target)])
        return loss_from(totals)
    loss, pull_back = jax.vjp(loss_of, logits)
    grad_logits = pull_back(jnp.ones((), jnp.float32))[0]
    moved = jnp.stack([shifted(grad_logits, -offset[0], -offset[1], -offset[2]) for offset in tap_offsets()])
    moved = moved.reshape(27, -1)
    grad_weight = jnp.dot(moved, flat.astype(jnp.float32).T, precision=lax.Precision.HIGHEST, preferred_element_type=jnp.float32)
    grad_bias = jnp.sum(grad_logits).reshape(1)
    grad_features = jnp.dot(weight.T.astype(jnp.float32), moved, precision=lax.Precision.HIGHEST, preferred_element_type=jnp.float32)
    grad_features = grad_features.reshape(features.shape).astype(jnp.bfloat16)
    return (loss.reshape(1), grad_features, grad_weight, grad_bias)
```

```python
import functools

import jax
import jax.numpy as jnp
from jax import lax
from jax.experimental import pallas as pl
from jax.experimental.pallas import tpu as pltpu
from jax.sharding import PartitionSpec as P

ITERS = 10
SECTIONS = ITERS + 1
LANES = 128
REACH = SECTIONS + 2
HALO = 2 * SECTIONS + 3

temper = 20.0
sharpness = 40.0

GROUP = ("gx", "gy")
ALL_AXES = ("gx", "gy", "gz")
f32 = jnp.float32
bf16 = jnp.bfloat16


def up8(value):
    return -(-value // 8) * 8


class Plan:
    def __init__(self, mesh_shape, block):
        self.ch, self.nx, self.ny, self.nz = block
        self.gx, self.gy, self.gz = (mesh_shape[a] for a in ALL_AXES)
        self.members = self.gx * self.gy
        self.ranks = self.members * self.gz
        self.X = self.nx * self.gx
        self.Y = self.ny * self.gy
        self.Z = self.nz * self.gz
        assert LANES % self.Y == 0 and self.nz == LANES
        assert self.nz % self.members == 0
        self.zc = self.nz // self.members
        self.per = LANES // self.Y
        assert self.nx % self.per == 0
        self.tiles = self.X // self.per
        self.own = self.nx // self.per
        self.shared = self.per > 1
        self.sent = self.own + (1 if self.shared else 2)
        self.R = up8(self.zc + 2)
        self.base = 8 + up8(HALO)
        self.top = self.base + up8(self.zc + HALO)
        self.rows = self.top + 8
        self.lo = self.base - up8(REACH)
        self.hi = self.base + up8(self.zc + REACH)
        self.win = self.hi - self.lo
        self.at = self.base - self.lo
        self.tlo = self.base - 8
        self.thi = self.base + up8(self.zc + 1)
        self.hops = -(-HALO // self.zc)
        self.label_hops = -(-REACH // self.zc)

    def slot(self, x):
        if 0 <= x < self.nx:
            return x // self.per, (x % self.per) * self.Y
        if x == self.nx:
            return self.own, 0
        return self.sent - 1, LANES - self.Y


def lane_iota(shape):
    return lax.broadcasted_iota(jnp.int32, shape, len(shape) - 1)


def row_iota(shape):
    return lax.broadcasted_iota(jnp.int32, shape, len(shape) - 2)


def x_shift(plan, prev, cur, nxt):
    if plan.Y == LANES:
        return prev, nxt
    lane = lane_iota(cur.shape)
    lower = pltpu.roll(jnp.where(lane >= LANES - plan.Y, prev, cur), plan.Y, 1)
    upper = pltpu.roll(jnp.where(lane < plan.Y, nxt, cur), LANES - plan.Y, 1)
    return lower, upper


def y_shift(plan, cur):
    spot = lane_iota(cur.shape) % plan.Y
    lower = jnp.where(spot == 0, 0.0, pltpu.roll(cur, 1, 1))
    upper = jnp.where(spot == plan.Y - 1, 0.0, pltpu.roll(cur, LANES - 1, 1))
    return lower, upper


def cross_at(plan, load, tile, lo, hi):
    cur = load(tile, lo, hi)
    x_lower, x_upper = x_shift(plan, load(tile - 1, lo, hi), cur, load(tile + 1, lo, hi))
    y_lower, y_upper = y_shift(plan, cur)
    total = cur + load(tile, lo - 1, hi - 1) + load(tile, lo + 1, hi + 1)
    return total + x_lower + x_upper + y_lower + y_upper


def plane_sum(plan, ref, lo, hi):
    part = ref[lo - 1 : hi - 1] + ref[lo:hi] + ref[lo + 1 : hi + 1]
    lower, upper = y_shift(plan, part)
    return part + lower + upper


def x_sum(plan, ref, tile):
    cur = ref[tile]
    lower, upper = x_shift(plan, ref[tile - 1], cur, ref[tile + 1])
    return cur + lower + upper


def counts(plan, rank, tile, lo, hi):
    shape = (hi - lo, LANES)
    z = rank * plan.zc + row_iota(shape) + (lo - plan.base)
    flat = tile * LANES + lane_iota(shape)
    y = flat % plan.Y
    x = flat // plan.Y

    def along(spot, size):
        return 3.0 - (spot == 0).astype(f32) - (spot == size - 1).astype(f32)

    inside = ((z >= 0) & (z < plan.Z)).astype(f32)
    return along(x, plan.X), along(y, plan.Y), along(z, plan.Z), inside


def cross_inverse(plan, rank, tile, lo, hi):
    cx, cy, cz, inside = counts(plan, rank, tile, lo, hi)
    return inside / (cx + cy + cz - 2.0)


def box_inverse(plan, rank, tile, lo, hi):
    cx, cy, cz, inside = counts(plan, rank, tile, lo, hi)
    return inside / (cx * cy * cz)


def tap_condition(plan, member_y, shape, y_dim, in_dim):
    y = lax.broadcasted_iota(jnp.int32, shape, y_dim) % plan.Y
    own = lax.broadcasted_iota(jnp.int32, shape, in_dim) % plan.ny
    return own + member_y * plan.ny - y + 1


def conv_kernel(plan, pos_ref, w_ref, f_ref, out_ref, wide_ref, acc_ref):
    rows, inner = plan.Y, plan.ch * plan.ny
    spread = (
        lax.broadcasted_iota(jnp.int32, (plan.ch, inner), 0)
        == lax.broadcasted_iota(jnp.int32, (plan.ch, inner), 1) // plan.ny
    ).astype(f32)
    taps = jnp.dot(w_ref[...].astype(f32), spread, preferred_element_type=f32)
    tap_y = tap_condition(plan, pos_ref[1], (rows, inner), 0, 1)
    for i in range(3):
        for k in range(3):
            band = jnp.zeros((rows, inner), f32)
            for j in range(3):
                t = 9 * i + 3 * j + k
                band = jnp.where(tap_y == j, taps[t : t + 1], band)
            at = (3 * i + k) * rows
            wide_ref[at : at + rows] = band.astype(bf16)
    acc_ref[...] = jnp.zeros_like(acc_ref)

    def at_x(x, carry):
        block = f_ref[:, x].reshape(inner, plan.nz)
        out = jnp.dot(wide_ref[...], block, preferred_element_type=f32)
        for i in range(3):
            acc_ref[x + 2 - i] += out[3 * i * rows : 3 * (i + 1) * rows]
        return carry

    lax.fori_loop(0, plan.nx, at_x, 0)

    out_ref[...] = jnp.zeros_like(out_ref)
    places = {}
    for x in range(-1, plan.nx + 1):
        tile, lane = plan.slot(x)
        places.setdefault(tile, {})[lane] = x
    lane = lane_iota((rows, plan.nz))
    for tile in range(plan.sent):
        parts, spills = [], []
        for first in range(0, LANES, rows):
            x = places[tile].get(first)
            if x is None:
                parts.append(jnp.zeros((rows, plan.nz), f32))
                spills.append(jnp.zeros((rows, plan.nz), f32))
                continue
            low = acc_ref[x + 1, 0:rows]
            mid = acc_ref[x + 1, rows : 2 * rows]
            high = acc_ref[x + 1, 2 * rows : 3 * rows]
            total = mid + jnp.where(lane == 0, 0.0, pltpu.roll(low, 1, 1))
            total = total + jnp.where(lane == plan.nz - 1, 0.0, pltpu.roll(high, plan.nz - 1, 1))
            parts.append(total)
            spill = jnp.where(lane == 1, pltpu.roll(low, 2, 1), 0.0)
            spills.append(jnp.where(lane == 0, high, spill))
        turned = jnp.concatenate(parts, axis=0).T
        spill = jnp.concatenate(spills, axis=0).T
        for p in range(plan.members):
            out_ref[p, tile, 0 : plan.zc] = turned[p * plan.zc : (p + 1) * plan.zc]
        out_ref[0, tile, plan.zc : plan.zc + 1] = spill[0:1]
        out_ref[plan.members - 1, tile, plan.zc + 1 : plan.zc + 2] = spill[1:2]


def label_kernel(plan, pos_ref, l_ref, out_ref):
    rows = plan.Y
    sub = lax.broadcasted_iota(jnp.int32, (plan.gy, plan.ny, plan.nz), 0)
    for tile in range(plan.own):
        parts = []
        for n in range(plan.per):
            block = l_ref[tile * plan.per + n].astype(f32)[None]
            wide = jnp.where(sub == pos_ref[1], block, 0.0)
            parts.append(wide.reshape(rows, plan.nz))
        turned = jnp.concatenate(parts, axis=0).T
        for p in range(plan.members):
            out_ref[p, tile] = turned[p * plan.zc : (p + 1) * plan.zc].astype(bf16)


def gather_kernel(plan, got_ref, out_ref):
    lane = lane_iota((plan.R, LANES))
    out_ref[...] = jnp.zeros_like(out_ref)
    for a in range(plan.gx):
        for b in range(plan.gy):
            p = a * plan.gy + b
            for q in range(plan.own):
                out_ref[a * plan.own + q] += got_ref[p, q]
            if a > 0:
                out_ref[a * plan.own - 1] += jnp.where(
                    lane >= LANES - plan.Y, got_ref[p, plan.sent - 1], 0.0
                )
            if a < plan.gx - 1:
                out_ref[(a + 1) * plan.own] += jnp.where(lane < plan.Y, got_ref[p, plan.own], 0.0)


def label_gather_kernel(plan, got_ref, out_ref):
    for a in range(plan.gx):
        for q in range(plan.own):
            total = got_ref[a * plan.gy, q].astype(f32)
            for b in range(1, plan.gy):
                total = total + got_ref[a * plan.gy + b, q].astype(f32)
            out_ref[a * plan.own + q] = total.astype(bf16)


def erode(plan, load, store, g_ref, zy_ref, tile, inverse, first, last, wlo, whi):
    nxt = cross_at(plan, load, tile + 1, first, last) * inverse
    store(nxt)
    g_ref[first:last] = jnp.where(nxt > 0.0, 1.0 / nxt, 0.0)
    zy_ref[tile + 1] = plane_sum(plan, g_ref, wlo, whi)


def thin(e, box, inverse, s):
    ok = (e > 0.0) & (box > 0.0) & (inverse > 0.0)
    ratio = jnp.where(ok, e * box * inverse, 1.0)
    square = ratio * ratio
    slope = 1.0 / (1.0 + square)
    scaled = -jnp.log(square * slope)
    lift = scaled * (1.0 - s)
    small = jnp.exp(-jnp.abs(lift))
    part = 1.0 / (1.0 + small)
    rate = jnp.where(lift >= 0.0, part, small * part)
    grown = s + (jnp.maximum(lift, 0.0) - jnp.log(part)) * (1.0 / sharpness)
    thinned = scaled * (1.0 / sharpness)
    return ok, slope, rate, thinned, grown


def target_kernel(plan, *refs):
    hops = plan.label_hops
    pos_ref, own_ref = refs[:2]
    below, above = refs[2 : 2 + hops], refs[2 + hops : 2 + 2 * hops]
    target_ref, ts_ref = refs[2 + 2 * hops : 4 + 2 * hops]
    e_ref, inv7_ref, g_ref, zy_ref = refs[4 + 2 * hops :]
    lo, hi, win = plan.lo, plan.hi, plan.win
    wlo, whi = plan.tlo - lo + 8, plan.thi - lo + 8
    rank = pos_ref[0]
    e_ref[...] = jnp.zeros_like(e_ref)
    zy_ref[...] = jnp.zeros_like(zy_ref)
    g_ref[...] = jnp.zeros_like(g_ref)
    ts_ref[...] = jnp.zeros_like(ts_ref)
    target_ref[...] = jnp.zeros_like(target_ref)

    def fill(tile, carry):
        chunks = {0: own_ref}
        for h in range(1, hops + 1):
            chunks[-h] = below[h - 1]
            chunks[h] = above[h - 1]
        for h, ref in chunks.items():
            at = plan.at + h * plan.zc
            first, last = max(at, 0), min(at + plan.zc, win)
            if first < last:
                piece = ref[tile].astype(f32)
                target_ref[tile, first:last] = piece[first - at : last - at]
        cx, cy, cz, inside = counts(plan, rank, tile, lo, hi)
        e_ref[0, tile + 1, 8 : 8 + win] = jnp.exp(-temper * target_ref[tile]) * inside
        inv7_ref[tile] = inside / (cx + cy + cz - 2.0)
        return carry

    lax.fori_loop(0, plan.tiles, fill, 0)

    def section(step, carry):
        now = step % 2

        def first_pass(tile, carry):
            def load(n, a, b):
                return e_ref[now, n, a:b]

            def store(value):
                e_ref[1 - now, tile + 1, 8 : 8 + win] = value

            erode(plan, load, store, g_ref, zy_ref, tile, inv7_ref[tile], 8, 8 + win, wlo, whi)
            return carry

        lax.fori_loop(0, plan.tiles, first_pass, 0)

        def second_pass(tile, carry):
            box = x_sum(plan, zy_ref, tile + 1)
            inverse = box_inverse(plan, rank, tile, plan.tlo, plan.thi)
            s = ts_ref[tile]
            _, _, _, thinned, grown = thin(e_ref[now, tile + 1, wlo:whi], box, inverse, s)
            ts_ref[tile] = jnp.where(step == 0, thinned, grown)
            return carry

        lax.fori_loop(0, plan.tiles, second_pass, 0)
        return carry

    lax.fori_loop(0, SECTIONS, section, 0)


def forward_kernel(plan, *refs):
    hops = plan.hops
    pos_ref, bias_ref, target_ref, ts_ref, own_ref = refs[:5]
    refs = refs[5:]
    below, above = refs[:hops], refs[hops : 2 * hops]
    refs = refs[2 * hops :]
    m_ref, q_ref, t_ref, g2_ref, p_ref, sums_ref = refs[:6]
    e_ref, inv7_ref, inv27_ref, g_ref, zy_ref, s_ref = refs[6:]
    base, top, lo, hi, zc = plan.base, plan.top, plan.lo, plan.hi, plan.zc
    rank = pos_ref[0]
    step = pl.program_id(0)
    tiles = plan.tiles

    @pl.when(step == 0)
    def _():
        e_ref[...] = jnp.zeros_like(e_ref)
        zy_ref[...] = jnp.zeros_like(zy_ref)
        g_ref[...] = jnp.zeros_like(g_ref)
        s_ref[...] = jnp.zeros_like(s_ref)

        def fill(tile, carry):
            chunks = {0: own_ref}
            for h in range(1, hops + 1):
                chunks[-h] = below[h - 1]
                chunks[h] = above[h - 1]
            u = e_ref.at[0, tile + 1]
            for h, ref in chunks.items():
                at = base + h * zc
                first, last = max(at, 8), min(at + zc, top)
                if first < last:
                    u[first:last] = ref[tile, first - at : last - at]
            for h, ref in chunks.items():
                at = base + h * zc
                if 8 <= at - 1 < top:
                    u[at - 1 : at] += ref[tile, zc : zc + 1]
                if 8 <= at + zc < top:
                    u[at + zc : at + zc + 1] += ref[tile, zc + 1 : zc + 2]
            logits = u[8:top] + bias_ref[0]
            small = jnp.exp(-jnp.abs(logits))
            part = 1.0 / (1.0 + small)
            predict = jnp.where(logits >= 0, part, small * part)
            cx, cy, cz, inside = counts(plan, rank, tile, 8, top)
            u[8:top] = jnp.exp(-temper * predict) * inside
            inv7_ref[tile] = inside / (cx + cy + cz - 2.0)
            inv27_ref[tile] = (inside / (cx * cy * cz))[lo - 8 : hi - 8]
            p_ref[tile] = predict[plan.tlo - 8 : plan.thi - 8]
            return carry

        lax.fori_loop(0, tiles, fill, 0)

    now = step % 2

    def first_pass(tile, carry):
        def load(n, a, b):
            return e_ref[now, n, a:b]

        def store(value):
            e_ref[1 - now, tile + 1, 8:top] = value

        erode(plan, load, store, g_ref, zy_ref, tile, inv7_ref[tile], 8, top, lo, hi)
        grown = g_ref[lo:hi]
        g2_ref[0, tile] = grown * grown
        return carry

    lax.fori_loop(0, tiles, first_pass, 0)
    opening = step == 0

    def second_pass(tile, carry):
        e = e_ref[now, tile + 1, lo:hi]
        box = x_sum(plan, zy_ref, tile + 1)
        s = s_ref[tile]
        ok, slope, rate, thinned, grown = thin(e, box, inv27_ref[tile], s)
        s_ref[tile] = jnp.where(opening, thinned, grown)
        a = jnp.where(opening, slope, rate * (1.0 - s) * slope)
        m_ref[0, tile] = 1.0 - rate * thinned
        q_ref[0, tile] = jnp.where(ok, a / box, 0.0)
        t_ref[0, tile] = jnp.where(ok, a / e, 0.0)
        return carry

    lax.fori_loop(0, tiles, second_pass, 0)

    @pl.when(step == SECTIONS - 1)
    def _():
        at = plan.at
        span = up8(zc)
        mine = row_iota((span, LANES)) < zc

        def add(tile, totals):
            def own(value):
                return jnp.where(mine, value, 0.0)

            ps = own(s_ref[tile, at : at + span])
            ts = own(ts_ref[tile, 8 : 8 + span])
            predict = own(p_ref[tile, 8 : 8 + span])
            target = own(target_ref[tile, at : at + span])
            terms = (ps * target, ps, ts * predict, ts, predict * target, predict, target)
            return tuple(
                total + jnp.sum(term.reshape(-1, 8, LANES), axis=0)
                for total, term in zip(totals, terms)
            )

        totals = lax.fori_loop(0, tiles, add, (jnp.zeros((8, LANES), f32),) * 7)
        lines = [jnp.sum(total, axis=0, keepdims=True) for total in totals]
        lines.append(jnp.zeros((1, LANES), f32))
        sums_ref[...] = jnp.broadcast_to(
            jnp.concatenate(lines, axis=0)[None], (plan.ranks, 8, LANES)
        )


def backward_kernel(plan, *refs):
    (
        pos_ref, sums_ref, m_ref, q_ref, t_ref, g2_ref, p_ref, target_ref, ts_ref,
        out_ref, loss_ref,
        w_ref, h_ref, push_ref, zy_ref, pull_ref, inv7_ref, grad_ref,
    ) = refs
    step = pl.program_id(0)
    rank = pos_ref[0]
    win, lo, hi, zc, at = plan.win, plan.lo, plan.hi, plan.zc, plan.at
    tiles = plan.tiles

    lines = jnp.sum(jnp.sum(sums_ref[...], axis=0), axis=1, keepdims=True)
    s1, s2, s3, s4, s5, s6, s7 = (lines[n : n + 1] for n in range(7))
    prec = (s1 + 1.0) / (s2 + 1.0)
    sens = (s3 + 1.0) / (s4 + 1.0)

    @pl.when(step == 0)
    def _():
        zy_ref[...] = jnp.zeros_like(zy_ref)
        pull_ref[...] = jnp.zeros_like(pull_ref)
        push_ref[...] = jnp.zeros_like(push_ref)
        h_ref[...] = jnp.zeros_like(h_ref)

        def fill(tile, carry):
            w_ref[tile] = target_ref[tile] - prec
            inv7_ref[tile] = cross_inverse(plan, rank, tile, lo, hi)
            return carry

        lax.fori_loop(0, tiles, fill, 0)

    def first_pass(tile, carry):
        push_ref[8 : 8 + win] = w_ref[tile] * q_ref[0, tile]
        zy_ref[tile + 1] = plane_sum(plan, push_ref, 8, 8 + win)
        return carry

    lax.fori_loop(0, tiles, first_pass, 0)

    def second_pass(tile, carry):
        box = x_sum(plan, zy_ref, tile + 1)
        pull_ref[tile + 1, 8 : 8 + win] = (h_ref[tile] - g2_ref[0, tile] * box) * inv7_ref[tile]
        return carry

    lax.fori_loop(0, tiles, second_pass, 0)

    def third_pass(tile, carry):
        def load(n, a, b):
            return pull_ref[n, a:b]

        w = w_ref[tile]
        h_ref[tile] = w * t_ref[0, tile] + cross_at(plan, load, tile + 1, 8, 8 + win)
        w_ref[tile] = w * m_ref[0, tile]
        return carry

    lax.fori_loop(0, tiles, third_pass, 0)

    @pl.when(step == SECTIONS - 1)
    def _():
        both = prec + sens
        volume = s6 + s7 + 1.0
        cl_loss = 1.0 - 2.0 * prec * sens / both
        dice_loss = 1.0 - (2.0 * s5 + 1.0) / volume
        loss_ref[...] = jnp.broadcast_to(0.5 * dice_loss + 0.5 * cl_loss, (8, LANES))
        l0 = -(sens / both) * (sens / both) / (s2 + 1.0)
        l2 = -(prec / both) * (prec / both) / (s4 + 1.0)
        l4 = -1.0 / volume
        l5 = 0.5 * (2.0 * s5 + 1.0) / (volume * volume)
        grad_ref[...] = jnp.zeros_like(grad_ref)
        span = plan.thi - plan.tlo
        first = plan.tlo - lo

        def finish(tile, carry):
            z = rank * zc + row_iota((span, LANES)) + (plan.tlo - plan.base)
            inside = (z >= 0) & (z < plan.Z)
            rows = slice(first, first + span)
            predict = p_ref[tile]
            skel = l0 * jnp.exp(-temper * predict) * h_ref[tile, rows]
            whole = skel + l2 * ts_ref[tile] + l4 * target_ref[tile, rows] + l5
            grad = jnp.where(inside, whole * predict * (1.0 - predict), 0.0)
            grad_ref[tile + 1, 0:zc] = grad[8 : 8 + zc]
            grad_ref[tile + 1, zc : zc + 1] = grad[7:8]
            grad_ref[tile + 1, zc + 1 : zc + 2] = grad[8 + zc : 9 + zc]
            return carry

        lax.fori_loop(0, tiles, finish, 0)
        lane = lane_iota((plan.R, LANES))
        for a in range(plan.gx):
            pieces = [grad_ref[a * plan.own + q + 1] for q in range(plan.own)]
            after = grad_ref[(a + 1) * plan.own + 1]
            before = grad_ref[a * plan.own]
            if plan.shared:
                edge = jnp.where(lane < plan.Y, after, 0.0)
                pieces.append(jnp.where(lane >= LANES - plan.Y, before, edge))
            else:
                pieces += [after, before]
            for q, piece in enumerate(pieces):
                for b in range(plan.gy):
                    out_ref[a * plan.gy + b, q] = piece


def grad_kernel(plan, pos_ref, wt_ref, f_ref, got_ref, gf_ref, gw_ref, wide_ref, g_ref, dw_ref):
    rows, inner, bands = plan.Y, plan.ch * plan.ny, 9 * plan.Y
    spread = (
        lax.broadcasted_iota(jnp.int32, (inner, plan.ch), 0) // plan.ny
        == lax.broadcasted_iota(jnp.int32, (inner, plan.ch), 1)
    ).astype(f32)
    tap_y = tap_condition(plan, pos_ref[1], (inner, bands), 1, 0)
    wide = jnp.zeros((inner, bands), f32)
    tap = lax.broadcasted_iota(jnp.int32, (27, bands), 0)
    band = lax.broadcasted_iota(jnp.int32, (27, bands), 1) // rows
    for j in range(3):
        pick = (tap == 9 * (band // 3) + 3 * j + band % 3).astype(f32)
        chosen = jnp.dot(wt_ref[...].astype(f32), pick, preferred_element_type=f32)
        full = jnp.dot(spread, chosen, preferred_element_type=f32)
        wide = jnp.where(tap_y == j, full, wide)
    wide_ref[...] = wide.astype(bf16)

    zc = plan.zc
    lane = lane_iota((rows, plan.nz))
    bias = jnp.zeros((rows, plan.nz), f32)
    places = {}
    for x in range(-1, plan.nx + 1):
        tile, first = plan.slot(x)
        places.setdefault(tile, {})[first] = x
    for tile in range(plan.sent):
        stack = [got_ref[p, tile, 0:zc] for p in range(plan.members)]
        turned = jnp.concatenate(stack, axis=0).T
        low = got_ref[0, tile, zc : zc + 1]
        high = got_ref[plan.members - 1, tile, zc + 1 : zc + 2]
        ends = jnp.concatenate([low, high, jnp.zeros((LANES - 2, LANES), f32)], axis=0).T
        for first, x in places[tile].items():
            g = turned[first : first + rows]
            end = ends[first : first + rows]
            down = jnp.where(lane == plan.nz - 1, pltpu.roll(end, plan.nz - 2, 1), pltpu.roll(g, plan.nz - 1, 1))
            up = jnp.where(lane == 0, end, pltpu.roll(g, 1, 1))
            g_ref[x + 1] = jnp.concatenate([down, g, up], axis=0).astype(bf16)
            if 0 <= x < plan.nx:
                bias = bias + g
    y_own = lax.broadcasted_iota(jnp.int32, (rows, plan.nz), 0) // plan.ny == pos_ref[1]
    bias = jnp.sum(jnp.where(y_own, bias, 0.0))

    dw_ref[...] = jnp.zeros_like(dw_ref)

    def at_x(x, carry):
        block = f_ref[:, x].reshape(inner, plan.nz)
        moved = jnp.concatenate([g_ref[x + 2], g_ref[x + 1], g_ref[x]], axis=0)
        out = jnp.dot(wide_ref[...], moved, preferred_element_type=f32)
        gf_ref[:, x] = out.astype(bf16).reshape(plan.ch, plan.ny, plan.nz)
        dw_ref[...] += lax.dot_general(
            moved, block, (((1,), (1,)), ((), ())), preferred_element_type=f32
        )
        return carry

    lax.fori_loop(0, plan.nx, at_x, 0)

    tap_y = tap_condition(plan, pos_ref[1], (rows, inner), 0, 1)
    taps = []
    for t in range(27):
        i, j, k = t // 9, t // 3 % 3, t % 3
        at = (3 * i + k) * rows
        taps.append(jnp.sum(jnp.where(tap_y == j, dw_ref[at : at + rows], 0.0), axis=0, keepdims=True))
    taps += [jnp.zeros((1, inner), f32)] * 5
    total = jnp.zeros((8, LANES), f32)
    for n in range(4):
        place = (
            lax.broadcasted_iota(jnp.int32, (inner, LANES), 0) // plan.ny + 32 * n
            == lax.broadcasted_iota(jnp.int32, (inner, LANES), 1)
        ).astype(f32)
        total = total + jnp.dot(
            jnp.concatenate(taps[8 * n : 8 * n + 8], axis=0),
            place,
            precision=lax.Precision.HIGHEST,
            preferred_element_type=f32,
        )
    spot = (row_iota((8, LANES)) == 3) & (lane_iota((8, LANES)) == 96)
    total = jnp.where(spot, bias, total)
    gw_ref[...] = jnp.broadcast_to(total[None], (plan.ranks, 8, LANES))


def final_kernel(plan, got_ref, gw_ref, gb_ref):
    total = jnp.sum(got_ref[...], axis=0)
    for n in range(4):
        count = min(8, 27 - 8 * n)
        gw_ref[8 * n : 8 * n + count] = total[:count, 32 * n : 32 * n + plan.ch]
    gb_ref[...] = total[3:4, 96:97]


VMEM = pl.BlockSpec(memory_space=pltpu.VMEM)
SMEM = pl.BlockSpec(memory_space=pltpu.SMEM)
BIG = pltpu.CompilerParams(vmem_limit_bytes=63 * 1024 * 1024)


def shape(dims, dtype=f32):
    return jax.ShapeDtypeStruct(dims, dtype)


def per_device(mesh_shape, features, weight, bias, label):
    plan = Plan(mesh_shape, features.shape)
    members, sent, own, R, tiles = plan.members, plan.sent, plan.own, plan.R, plan.tiles
    inner, bands = plan.ch * plan.ny, 9 * plan.Y
    place = (lax.axis_index("gz") * members + lax.axis_index(GROUP)).astype(jnp.int32)
    pos = jnp.stack([place, lax.axis_index("gy").astype(jnp.int32)])

    def call(kernel, out_shape, in_specs, scratch=(), params=BIG):
        return pl.pallas_call(
            functools.partial(kernel, plan),
            out_shape=out_shape,
            in_specs=in_specs,
            out_specs=jax.tree.map(lambda s: VMEM, out_shape),
            scratch_shapes=list(scratch),
            compiler_params=params,
        )

    def exchange(array):
        return lax.all_to_all(array, GROUP, 0, 0, tiled=True)

    def everywhere(array):
        return lax.all_to_all(array, ALL_AXES, 0, 0, tiled=True)

    def hop(array, distance):
        def device(r):
            return (r % members) * plan.gz + r // members

        pairs = [
            (device(r), device(r + distance))
            for r in range(plan.ranks)
            if 0 <= r + distance < plan.ranks
        ]
        return lax.ppermute(array, ALL_AXES, pairs)

    label_sent = call(label_kernel, shape((members, own, plan.zc, LANES), bf16), [SMEM, VMEM])(
        pos, label
    )
    sent_logits = call(
        conv_kernel,
        shape((members, sent, R, LANES)),
        [SMEM, VMEM, VMEM],
        [
            pltpu.VMEM((bands, inner), bf16),
            pltpu.VMEM((plan.nx + 2, 3 * plan.Y, plan.nz), f32),
        ],
    )(pos, weight, features)
    label_chunk = call(label_gather_kernel, shape((tiles, plan.zc, LANES), bf16), [VMEM])(
        exchange(label_sent)
    )
    chunk = call(gather_kernel, shape((tiles, R, LANES)), [VMEM])(exchange(sent_logits))
    below = [hop(chunk, h) for h in range(1, plan.hops + 1)]
    above = [hop(chunk, -h) for h in range(1, plan.hops + 1)]
    label_below = [hop(label_chunk, h) for h in range(1, plan.label_hops + 1)]
    label_above = [hop(label_chunk, -h) for h in range(1, plan.label_hops + 1)]

    window = (tiles, plan.win, LANES)
    tspan = plan.thi - plan.tlo
    target, ts = call(
        target_kernel,
        [shape(window), shape((tiles, tspan, LANES))],
        [SMEM] + [VMEM] * (1 + 2 * plan.label_hops),
        [
            pltpu.VMEM((2, tiles + 2, plan.win + 16, LANES), f32),
            pltpu.VMEM(window, f32),
            pltpu.VMEM((plan.win + 16, LANES), f32),
            pltpu.VMEM((tiles + 2, tspan, LANES), f32),
        ],
    )(pos, label_chunk, *label_below, *label_above)
    record = pl.BlockSpec((1,) + window, lambda n: (n, 0, 0, 0))
    outs = pl.pallas_call(
        functools.partial(forward_kernel, plan),
        grid=(SECTIONS,),
        out_shape=[shape((SECTIONS,) + window)] * 4
        + [shape((tiles, tspan, LANES)), shape((plan.ranks, 8, LANES))],
        in_specs=[SMEM, SMEM] + [VMEM] * (3 + 2 * plan.hops),
        out_specs=[record] * 4 + [VMEM] * 2,
        scratch_shapes=[
            pltpu.VMEM((2, tiles + 2, plan.rows, LANES), f32),
            pltpu.VMEM((tiles, plan.top - 8, LANES), f32),
            pltpu.VMEM(window, f32),
            pltpu.VMEM((plan.rows, LANES), f32),
            pltpu.VMEM((tiles + 2, plan.win, LANES), f32),
            pltpu.VMEM(window, f32),
        ],
        compiler_params=BIG,
    )(pos, bias, target, ts, chunk, *below, *above)
    m, q, t, g2, predict, sums = outs
    sums = everywhere(sums)

    back = pl.BlockSpec((1,) + window, lambda n: (SECTIONS - 1 - n, 0, 0, 0))
    grad_sent, loss = pl.pallas_call(
        functools.partial(backward_kernel, plan),
        grid=(SECTIONS,),
        out_shape=[shape((members, sent, R, LANES)), shape((8, LANES))],
        in_specs=[SMEM, VMEM] + [back] * 4 + [VMEM] * 3,
        out_specs=[VMEM, VMEM],
        scratch_shapes=[
            pltpu.VMEM(window, f32),
            pltpu.VMEM(window, f32),
            pltpu.VMEM((plan.win + 16, LANES), f32),
            pltpu.VMEM((tiles + 2, plan.win, LANES), f32),
            pltpu.VMEM((tiles + 2, plan.win + 16, LANES), f32),
            pltpu.VMEM(window, f32),
            pltpu.VMEM((tiles + 2, R, LANES), f32),
        ],
        compiler_params=BIG,
    )(pos, sums, m, q, t, g2, predict, target, ts)

    grad_features, partial = call(
        grad_kernel,
        [shape(features.shape, bf16), shape((plan.ranks, 8, LANES))],
        [SMEM, VMEM, VMEM, VMEM],
        [
            pltpu.VMEM((inner, bands), bf16),
            pltpu.VMEM((plan.nx + 2, 3 * plan.Y, plan.nz), bf16),
            pltpu.VMEM((bands, inner), f32),
        ],
    )(pos, weight.T, features, exchange(grad_sent))
    grad_weight, grad_bias = call(
        final_kernel, [shape((27, plan.ch)), shape((1, 1))], [VMEM]
    )(everywhere(partial))
    return (loss[0, :1], grad_features, grad_weight, grad_bias.reshape(1))


def solution(mesh):
    in_specs = (P(None, "gx", "gy", "gz"), P(), P(), P("gx", "gy", "gz"))
    out_specs = (P(), P(None, "gx", "gy", "gz"), P(), P())
    return jax.shard_map(
        functools.partial(per_device, dict(mesh.shape)),
        mesh=mesh,
        in_specs=in_specs,
        out_specs=out_specs,
        check_vma=False,
    )
```

```python
import functools

import jax
import jax.numpy as jnp
from jax import lax
from jax.experimental import pallas as pl
from jax.experimental.pallas import tpu as pltpu
from jax.sharding import PartitionSpec as P

ITERS = 10
SECTIONS = ITERS + 1
LANES = 128
REACH = SECTIONS + 2
HALO = 2 * SECTIONS + 3

temper = 20.0
sharpness = 40.0

GROUP = ("gx", "gy")
ALL_AXES = ("gx", "gy", "gz")
f32 = jnp.float32
bf16 = jnp.bfloat16


def up8(value):
    return -(-value // 8) * 8


class Plan:
    def __init__(self, mesh_shape, block):
        self.ch, self.nx, self.ny, self.nz = block
        self.gx, self.gy, self.gz = (mesh_shape[a] for a in ALL_AXES)
        self.members = self.gx * self.gy
        self.ranks = self.members * self.gz
        self.X = self.nx * self.gx
        self.Y = self.ny * self.gy
        self.Z = self.nz * self.gz
        assert LANES % self.Y == 0 and self.nz == LANES
        assert self.nz % self.members == 0
        self.zc = self.nz // self.members
        self.per = LANES // self.Y
        assert self.nx % self.per == 0
        self.tiles = self.X // self.per
        self.own = self.nx // self.per
        self.shared = self.per > 1
        self.sent = self.own + (1 if self.shared else 2)
        self.R = up8(self.zc + 2)
        self.pad = self.tiles + 16
        self.win = self.zc + 2 * REACH
        self.span = self.zc + 2
        self.block = self.blocks_of(self.win)
        self.span_block = self.blocks_of(self.span)
        self.base = HALO + 1
        self.planes = self.zc + 2 * HALO + 2 + self.block
        self.hops = -(-HALO // self.zc)
        self.rest = HALO - (self.hops - 1) * self.zc
        self.label_hops = -(-REACH // self.zc)
        self.label_rest = REACH - (self.label_hops - 1) * self.zc

    def blocks_of(self, count):
        fits = [n for n in range(1, count + 1) if count % n == 0 and n * self.tiles <= 128]
        return fits[-1] if fits else 1

    def slot(self, x):
        if 0 <= x < self.nx:
            return x // self.per, (x % self.per) * self.Y
        if x == self.nx:
            return self.own, 0
        return self.sent - 1, LANES - self.Y


def lane_iota(shape):
    return lax.broadcasted_iota(jnp.int32, shape, len(shape) - 1)


def row_iota(shape):
    return lax.broadcasted_iota(jnp.int32, shape, len(shape) - 2)


def masks(plan):
    lane = lane_iota((plan.tiles, LANES))
    return lane, lane % plan.Y == 0, lane % plan.Y == plan.Y - 1


def x_neighbours(plan, mask, load, cur):
    lower, upper = load(-1), load(1)
    if plan.Y == LANES:
        return lower + upper
    lower = pltpu.roll(jnp.where(mask[0] >= LANES - plan.Y, lower, cur), plan.Y, 1)
    upper = pltpu.roll(jnp.where(mask[0] < plan.Y, upper, cur), LANES - plan.Y, 1)
    return lower + upper


def y_neighbours(plan, mask, cur):
    lower = jnp.where(mask[1], 0.0, pltpu.roll(cur, 1, 1))
    upper = jnp.where(mask[2], 0.0, pltpu.roll(cur, LANES - 1, 1))
    return lower + upper


def count_tables(plan, cross_ref, box_ref):
    flat = row_iota((plan.tiles, LANES)) * LANES + lane_iota((plan.tiles, LANES))
    y, x = flat % plan.Y, flat // plan.Y

    def along(spot, size):
        return 3.0 - (spot == 0).astype(f32) - (spot == size - 1).astype(f32)

    cx, cy = along(x, plan.X), along(y, plan.Y)
    for kind, cz in ((1, 2.0), (2, 3.0)):
        if cross_ref is not None:
            cross_ref[kind] = 1.0 / (cx + cy + cz - 2.0)
        if box_ref is not None:
            box_ref[kind] = 1.0 / (cx * cy * cz)
    for ref in (cross_ref, box_ref):
        if ref is not None:
            ref[0] = jnp.zeros((plan.tiles, LANES), f32)


def kind_of(plan, rank, plane):
    z = rank * plan.zc + plane
    inside = (z >= 0) & (z < plan.Z)
    edge = (z == 0) | (z == plan.Z - 1)
    return jnp.where(inside, jnp.where(edge, 1, 2), 0)


def store_all(pairs):
    for ref, at, value in pairs:
        ref[at] = value


def over(first, count, size, body):
    def at(n, carry):
        body(first + n * size)
        return carry

    lax.fori_loop(0, (count + size - 1) // size, at, 0)


def tap_condition(plan, member_y, shape, y_dim, in_dim):
    y = lax.broadcasted_iota(jnp.int32, shape, y_dim) % plan.Y
    own = lax.broadcasted_iota(jnp.int32, shape, in_dim) % plan.ny
    return own + member_y * plan.ny - y + 1


def conv_kernel(plan, pos_ref, w_ref, f_ref, out_ref, wide_ref, acc_ref):
    rows, inner = plan.Y, plan.ch * plan.ny
    spread = (
        lax.broadcasted_iota(jnp.int32, (plan.ch, inner), 0)
        == lax.broadcasted_iota(jnp.int32, (plan.ch, inner), 1) // plan.ny
    ).astype(f32)
    taps = jnp.dot(w_ref[...].astype(f32), spread, preferred_element_type=f32)
    tap_y = tap_condition(plan, pos_ref[1], (rows, inner), 0, 1)
    for i in range(3):
        for k in range(3):
            band = jnp.zeros((rows, inner), f32)
            for j in range(3):
                t = 9 * i + 3 * j + k
                band = jnp.where(tap_y == j, taps[t : t + 1], band)
            at = (3 * i + k) * rows
            wide_ref[at : at + rows] = band.astype(bf16)
    acc_ref[...] = jnp.zeros_like(acc_ref)

    def at_x(x, carry):
        block = f_ref[:, x].reshape(inner, plan.nz)
        out = jnp.dot(wide_ref[...], block, preferred_element_type=f32)
        for i in range(3):
            acc_ref[x + 2 - i] += out[3 * i * rows : 3 * (i + 1) * rows]
        return carry

    lax.fori_loop(0, plan.nx, at_x, 0)

    out_ref[...] = jnp.zeros_like(out_ref)
    places = {}
    for x in range(-1, plan.nx + 1):
        tile, lane = plan.slot(x)
        places.setdefault(tile, {})[lane] = x
    lane = lane_iota((rows, plan.nz))
    for tile in range(plan.sent):
        parts, spills = [], []
        for first in range(0, LANES, rows):
            x = places[tile].get(first)
            if x is None:
                parts.append(jnp.zeros((rows, plan.nz), f32))
                spills.append(jnp.zeros((rows, plan.nz), f32))
                continue
            low = acc_ref[x + 1, 0:rows]
            mid = acc_ref[x + 1, rows : 2 * rows]
            high = acc_ref[x + 1, 2 * rows : 3 * rows]
            total = mid + jnp.where(lane == 0, 0.0, pltpu.roll(low, 1, 1))
            total = total + jnp.where(lane == plan.nz - 1, 0.0, pltpu.roll(high, plan.nz - 1, 1))
            parts.append(total)
            spill = jnp.where(lane == 1, pltpu.roll(low, 2, 1), 0.0)
            spills.append(jnp.where(lane == 0, high, spill))
        turned = jnp.concatenate(parts, axis=0).T
        spill = jnp.concatenate(spills, axis=0).T
        for p in range(plan.members):
            out_ref[p, tile, 0 : plan.zc] = turned[p * plan.zc : (p + 1) * plan.zc]
        out_ref[0, tile, plan.zc : plan.zc + 1] = spill[0:1]
        out_ref[plan.members - 1, tile, plan.zc + 1 : plan.zc + 2] = spill[1:2]


def label_kernel(plan, pos_ref, l_ref, out_ref):
    rows = plan.Y
    sub = lax.broadcasted_iota(jnp.int32, (plan.gy, plan.ny, plan.nz), 0)
    for tile in range(plan.own):
        parts = []
        for n in range(plan.per):
            block = l_ref[tile * plan.per + n].astype(f32)[None]
            wide = jnp.where(sub == pos_ref[1], block, 0.0)
            parts.append(wide.reshape(rows, plan.nz))
        turned = jnp.concatenate(parts, axis=0).T
        for p in range(plan.members):
            out_ref[p, tile] = turned[p * plan.zc : (p + 1) * plan.zc].astype(bf16)


def gather_kernel(plan, got_ref, out_ref, head_ref, tail_ref):
    lane = lane_iota((plan.R, LANES))
    tiles, zc, rest = plan.tiles, plan.zc, plan.rest
    for a in range(plan.gx):
        for q in range(plan.own):
            total = jnp.zeros((plan.R, LANES), f32)
            for b in range(plan.gy):
                total = total + got_ref[a * plan.gy + b, q]
                if q == plan.own - 1 and a < plan.gx - 1:
                    edge = got_ref[(a + 1) * plan.gy + b, plan.sent - 1]
                    total = total + jnp.where(lane >= LANES - plan.Y, edge, 0.0)
                if q == 0 and a > 0:
                    edge = got_ref[(a - 1) * plan.gy + b, plan.own]
                    total = total + jnp.where(lane < plan.Y, edge, 0.0)
            tile = a * plan.own + q
            out_ref[pl.ds(tile, zc + 2, stride=tiles)] = total[: zc + 2]
    head_ref[: rest * tiles] = out_ref[: rest * tiles]
    head_ref[rest * tiles :] = out_ref[zc * tiles : (zc + 1) * tiles]
    tail_ref[: rest * tiles] = out_ref[(zc - rest) * tiles : zc * tiles]
    tail_ref[rest * tiles :] = out_ref[(zc + 1) * tiles :]


def label_gather_kernel(plan, got_ref, out_ref, head_ref, tail_ref, all_ref):
    tiles, zc, rest = plan.tiles, plan.zc, plan.label_rest
    for a in range(plan.gx):
        for q in range(plan.own):
            total = got_ref[a * plan.gy, q].astype(f32)
            for b in range(1, plan.gy):
                total = total + got_ref[a * plan.gy + b, q].astype(f32)
            all_ref[pl.ds(a * plan.own + q, zc, stride=tiles)] = total
    out_ref[...] = all_ref[...].astype(bf16)
    head_ref[...] = all_ref[: rest * tiles].astype(bf16)
    tail_ref[...] = all_ref[(zc - rest) * tiles :].astype(bf16)


def thin(e, box, inverse, s):
    ok = (e > 0.0) & (box > 0.0) & (inverse > 0.0)
    box = jnp.where(ok, box, 1.0)
    ratio = jnp.where(ok, e * box * inverse, 1.0)
    square = ratio * ratio
    more = 1.0 + square
    joint = 1.0 / (box * more)
    slope = joint * box
    scaled = -jnp.log(square * slope)
    lift = scaled * (1.0 - s)
    small = jnp.exp(-jnp.abs(lift))
    part = 1.0 / (1.0 + small)
    rate = jnp.where(lift >= 0.0, part, small * part)
    grown = s + (jnp.maximum(lift, 0.0) - jnp.log(part)) * (1.0 / sharpness)
    thinned = scaled * (1.0 / sharpness)
    return ok, slope, joint * more, rate, thinned, grown


def erode(plan, rank, mask, e_ref, g_ref, table_ref, now, base, first, count, size):
    tiles = slice(8, 8 + plan.tiles)

    def body(plane):
        out = []
        for n in range(size):
            at = plane + n + base
            cur = e_ref[now, at, tiles]

            def load(offset, at=at):
                return e_ref[now, at, 8 + offset : 8 + offset + plan.tiles]

            total = cur + e_ref[now, at - 1, tiles] + e_ref[now, at + 1, tiles]
            total = total + x_neighbours(plan, mask, load, cur) + y_neighbours(plan, mask, cur)
            total = total * table_ref[kind_of(plan, rank, plane + n)]
            out.append((e_ref, (1 - now, at, tiles), total))
            out.append((g_ref, (1 - now, at), jnp.where(total > 0.0, 1.0 / total, 0.0)))
        store_all(out)

    over(first, count, size, body)


def spread(plan, mask, g_ref, now, zy_ref, base, first, count, size):
    tiles = slice(8, 8 + plan.tiles)

    def body(plane):
        out = []
        values = [g_ref[now, plane + n + base] for n in range(-1, size + 1)]
        for n in range(size):
            part = values[n] + values[n + 1] + values[n + 2]
            part = part + y_neighbours(plan, mask, part)
            out.append((zy_ref, (plane + n - first, tiles), part))
        store_all(out)

    over(first, count, size, body)


def x_box(plan, mask, zy_ref, at):
    cur = zy_ref[at, 8 : 8 + plan.tiles]

    def load(offset):
        return zy_ref[at, 8 + offset : 8 + offset + plan.tiles]

    return cur + x_neighbours(plan, mask, load, cur)


def target_kernel(plan, *refs):
    hops = plan.label_hops
    pos_ref, own_ref = refs[:2]
    below, above = refs[2 : 2 + hops], refs[2 + hops : 2 + 2 * hops]
    target_ref, ts_ref = refs[2 + 2 * hops : 4 + 2 * hops]
    e_ref, g_ref, zy_ref, cross_ref, box_ref = refs[4 + 2 * hops :]
    zc, win, span = plan.zc, plan.win, plan.span
    size = plan.span_block
    base = REACH + 1
    tiles = slice(8, 8 + plan.tiles)
    rank = pos_ref[0]
    mask = masks(plan)
    count_tables(plan, cross_ref, box_ref)
    e_ref[...] = jnp.zeros_like(e_ref)
    zy_ref[...] = jnp.zeros_like(zy_ref)
    g_ref[...] = jnp.zeros_like(g_ref)
    target_ref[REACH : REACH + zc] = own_ref[...].astype(f32)
    for h in range(1, hops + 1):
        n = zc if h < hops else plan.label_rest
        first = REACH - (h - 1) * zc - n
        target_ref[first : first + n] = below[h - 1][...].astype(f32)
        first = REACH + h * zc
        target_ref[first : first + n] = above[h - 1][...].astype(f32)

    def fill(plane):
        out = []
        for n in range(plan.block):
            at = plane + n
            z = rank * zc + at - REACH
            inside = ((z >= 0) & (z < plan.Z)).astype(f32)
            out.append((e_ref, (0, at + 1, tiles), jnp.exp(-temper * target_ref[at]) * inside))
        store_all(out)

    over(0, win, plan.block, fill)

    def section(step, carry):
        now = step % 2
        reach = 2 + ITERS - step
        erode(
            plan, rank, mask, e_ref, g_ref, cross_ref, now, base, -reach, zc + 2 * reach, size
        )
        spread(plan, mask, g_ref, 1 - now, zy_ref, base, -1, span, size)

        def point(plane):
            out = []
            for n in range(size):
                at = plane + n
                box = x_box(plan, mask, zy_ref, at)
                s = jnp.where(step == 0, 0.0, ts_ref[at])
                inverse = box_ref[kind_of(plan, rank, at - 1)]
                result = thin(e_ref[now, at - 1 + base, tiles], box, inverse, s)
                out.append((ts_ref, at, jnp.where(step == 0, result[4], result[5])))
            store_all(out)

        over(0, span, size, point)
        return carry

    lax.fori_loop(0, SECTIONS, section, 0)


def forward_kernel(plan, *refs):
    hops = plan.hops
    pos_ref, bias_ref, target_ref, ts_ref, own_ref = refs[:5]
    refs = refs[5:]
    below, above = refs[:hops], refs[hops : 2 * hops]
    refs = refs[2 * hops :]
    m_ref, q_ref, t_ref, g2_ref, p_ref, sums_ref = refs[:6]
    e_ref, g_ref, zy_ref, s_ref, cross_ref, box_ref = refs[6:]
    base, zc, size = plan.base, plan.zc, plan.block
    tiles = slice(8, 8 + plan.tiles)
    rank = pos_ref[0]
    step = pl.program_id(0)
    mask = masks(plan)

    @pl.when(step == 0)
    def _():
        e_ref[...] = jnp.zeros_like(e_ref)
        g_ref[...] = jnp.zeros_like(g_ref)
        zy_ref[...] = jnp.zeros_like(zy_ref)
        s_ref[...] = jnp.zeros_like(s_ref)
        count_tables(plan, cross_ref, box_ref)
        e_ref[0, base : base + zc, tiles] = own_ref[:zc]
        for h in range(1, hops + 1):
            n = zc if h < hops else plan.rest
            first = base - (h - 1) * zc - n
            e_ref[0, first : first + n, tiles] = below[h - 1][:n]
            first = base + h * zc
            e_ref[0, first : first + n, tiles] = above[h - 1][:n]
        e_ref[0, base - 1, tiles] += own_ref[zc]
        e_ref[0, base + zc, tiles] += own_ref[zc + 1]
        for h in range(1, hops + 1):
            if h < hops:
                e_ref[0, base - h * zc - 1, tiles] += below[h - 1][zc]
                e_ref[0, base + (h + 1) * zc, tiles] += above[h - 1][zc + 1]
                e_ref[0, base - (h - 1) * zc, tiles] += below[h - 1][zc + 1]
                e_ref[0, base + h * zc - 1, tiles] += above[h - 1][zc]
            else:
                e_ref[0, base - (h - 1) * zc, tiles] += below[h - 1][plan.rest]
                e_ref[0, base + h * zc - 1, tiles] += above[h - 1][plan.rest]

        def sigmoid(logits):
            small = jnp.exp(-jnp.abs(logits))
            part = 1.0 / (1.0 + small)
            return jnp.where(logits >= 0, part, small * part)

        for n in range(plan.span):
            p_ref[n] = sigmoid(e_ref[0, base - 1 + n, tiles] + bias_ref[0])

        def fill(plane):
            out = []
            for n in range(size):
                at = plane + n
                z = rank * zc + at - base
                inside = ((z >= 0) & (z < plan.Z)).astype(f32)
                predict = sigmoid(e_ref[0, at, tiles] + bias_ref[0])
                out.append((e_ref, (0, at, tiles), jnp.exp(-temper * predict) * inside))
            store_all(out)

        over(1, zc + 2 * HALO, size, fill)

    now = step % 2
    reach = REACH + 1 + ITERS - step
    erode(plan, rank, mask, e_ref, g_ref, cross_ref, now, base, -reach, zc + 2 * reach, size)
    spread(plan, mask, g_ref, 1 - now, zy_ref, base, -REACH, plan.win, size)
    opening = step == 0

    def point(at):
        out = []
        for n in range(size):
            spot = at + n
            plane = spot - REACH
            e = e_ref[now, plane + base, tiles]
            s = s_ref[spot]
            box = x_box(plan, mask, zy_ref, spot)
            inverse = box_ref[kind_of(plan, rank, plane)]
            ok, slope, over_box, rate, thinned, grown = thin(e, box, inverse, s)
            a = jnp.where(opening, slope, rate * (1.0 - s) * slope)
            a = jnp.where(ok, a, 0.0)
            before = jnp.where(opening, jnp.where(e > 0.0, 1.0 / e, 0.0), g_ref[now, plane + base])
            after = g_ref[1 - now, plane + base]
            out.append((s_ref, spot, jnp.where(opening, thinned, grown)))
            out.append((m_ref, (0, spot), 1.0 - rate * thinned))
            out.append((q_ref, (0, spot), a * over_box))
            out.append((t_ref, (0, spot), a * before))
            out.append((g2_ref, (0, spot), after * after))
        store_all(out)

    over(0, plan.win, size, point)

    @pl.when(step == SECTIONS - 1)
    def _():
        def add(n, totals):
            ps, ts = s_ref[REACH + n], ts_ref[1 + n]
            predict, target = p_ref[1 + n], target_ref[REACH + n]
            terms = (ps * target, ps, ts * predict, ts, predict * target, predict, target)
            return tuple(total + term for total, term in zip(totals, terms))

        start = (jnp.zeros((plan.tiles, LANES), f32),) * 7
        totals = lax.fori_loop(0, zc, add, start)
        lines = [jnp.sum(total, axis=0, keepdims=True) for total in totals]
        lines.append(jnp.zeros((1, LANES), f32))
        sums_ref[...] = jnp.broadcast_to(
            jnp.concatenate(lines, axis=0)[None], (plan.ranks, 8, LANES)
        )


def backward_kernel(plan, *refs):
    (
        pos_ref, sums_ref, m_ref, q_ref, t_ref, g2_ref, p_ref, target_ref, ts_ref,
        out_ref, loss_ref,
        w_ref, h_ref, zy_ref, pull_ref, cross_ref, grad_ref,
    ) = refs
    step = pl.program_id(0)
    rank = pos_ref[0]
    win, zc, size = plan.win, plan.zc, plan.block
    tiles = slice(8, 8 + plan.tiles)
    mask = masks(plan)

    lines = jnp.sum(jnp.sum(sums_ref[...], axis=0), axis=1, keepdims=True)
    s1, s2, s3, s4, s5, s6, s7 = (lines[n : n + 1] for n in range(7))
    prec = (s1 + 1.0) / (s2 + 1.0)
    sens = (s3 + 1.0) / (s4 + 1.0)

    @pl.when(step == 0)
    def _():
        zy_ref[...] = jnp.zeros_like(zy_ref)
        pull_ref[...] = jnp.zeros_like(pull_ref)
        h_ref[...] = jnp.zeros_like(h_ref)
        count_tables(plan, cross_ref, None)
        w_ref[...] = target_ref[...] - prec[None]

    def within(reach, body):
        count = (zc + 2 * reach + size - 1) // size
        first = jnp.minimum(REACH - reach, win - count * size)
        over(first, count * size, size, body)

    left = SECTIONS - 1 - step

    def push(at):
        values = []
        for n in range(-1, size + 1):
            spot = jnp.clip(at + n, 0, win - 1)
            values.append(w_ref[spot] * q_ref[0, spot])
        out = []
        for n in range(size):
            part = values[n] + values[n + 1] + values[n + 2]
            part = part + y_neighbours(plan, mask, part)
            out.append((zy_ref, (at + n, tiles), part))
        store_all(out)

    within(left + 2, push)

    def pull(at):
        out = []
        for n in range(size):
            spot = at + n
            box = x_box(plan, mask, zy_ref, spot)
            inverse = cross_ref[kind_of(plan, rank, spot - REACH)]
            value = (h_ref[spot] - g2_ref[0, spot] * box) * inverse
            out.append((pull_ref, (spot + 1, tiles), value))
        store_all(out)

    within(left + 2, pull)

    def join(at):
        out = []
        for n in range(size):
            spot = at + n
            cur = pull_ref[spot + 1, tiles]

            def load(offset, spot=spot):
                return pull_ref[spot + 1, 8 + offset : 8 + offset + plan.tiles]

            total = cur + pull_ref[spot, tiles] + pull_ref[spot + 2, tiles]
            total = total + x_neighbours(plan, mask, load, cur) + y_neighbours(plan, mask, cur)
            w = w_ref[spot]
            out.append((h_ref, spot, w * t_ref[0, spot] + total))
            out.append((w_ref, spot, w * m_ref[0, spot]))
        store_all(out)

    within(left + 2, join)

    @pl.when(step == SECTIONS - 1)
    def _():
        both = prec + sens
        volume = s6 + s7 + 1.0
        cl_loss = 1.0 - 2.0 * prec * sens / both
        dice_loss = 1.0 - (2.0 * s5 + 1.0) / volume
        loss_ref[...] = jnp.broadcast_to(0.5 * dice_loss + 0.5 * cl_loss, (8, LANES))
        l0 = -(sens / both) * (sens / both) / (s2 + 1.0)
        l2 = -(prec / both) * (prec / both) / (s4 + 1.0)
        l4 = -1.0 / volume
        l5 = 0.5 * (2.0 * s5 + 1.0) / (volume * volume)

        def finish(n, carry):
            z = rank * zc + n - 1
            inside = ((z >= 0) & (z < plan.Z)).astype(f32)
            at = n + REACH - 1
            predict = p_ref[n]
            skel = l0 * jnp.exp(-temper * predict) * h_ref[at]
            whole = skel + l2 * ts_ref[n] + l4 * target_ref[at] + l5
            grad = whole * predict * (1.0 - predict) * inside
            grad_ref[pl.ds(pl.multiple_of(n * plan.tiles, 8), plan.tiles)] = grad
            return carry

        lax.fori_loop(0, plan.span, finish, 0)
        lane = lane_iota((zc, LANES))
        fill = plan.R - zc - 2

        def column(tile):
            return [
                grad_ref[pl.ds(plan.tiles + tile, zc, stride=plan.tiles)],
                grad_ref[tile : tile + 1],
                grad_ref[(zc + 1) * plan.tiles + tile : (zc + 1) * plan.tiles + tile + 1],
            ]

        def place(a, q, pieces):
            for b in range(plan.gy):
                p = a * plan.gy + b
                out_ref[p, q, 0:zc] = pieces[0]
                out_ref[p, q, zc : zc + 1] = pieces[1]
                out_ref[p, q, zc + 1 : zc + 2] = pieces[2]
                if fill:
                    out_ref[p, q, zc + 2 :] = jnp.zeros((fill, LANES), f32)

        for a in range(plan.gx):
            for q in range(plan.own):
                place(a, q, column(a * plan.own + q))
            zero = [jnp.zeros((zc, LANES), f32)] + [jnp.zeros((1, LANES), f32)] * 2
            after = column((a + 1) * plan.own) if a < plan.gx - 1 else zero
            before = column(a * plan.own - 1) if a > 0 else zero
            if plan.shared:
                edge = [
                    jnp.where(lane[: x.shape[0]] < plan.Y, x, 0.0)
                    + jnp.where(lane[: y.shape[0]] >= LANES - plan.Y, y, 0.0)
                    for x, y in zip(after, before)
                ]
                place(a, plan.own, edge)
            else:
                place(a, plan.own, after)
                place(a, plan.own + 1, before)


def grad_kernel(plan, pos_ref, wt_ref, f_ref, got_ref, gf_ref, gw_ref, wide_ref, g_ref, dw_ref):
    rows, inner, bands = plan.Y, plan.ch * plan.ny, 9 * plan.Y
    spread = (
        lax.broadcasted_iota(jnp.int32, (inner, plan.ch), 0) // plan.ny
        == lax.broadcasted_iota(jnp.int32, (inner, plan.ch), 1)
    ).astype(f32)
    tap_y = tap_condition(plan, pos_ref[1], (inner, bands), 1, 0)
    wide = jnp.zeros((inner, bands), f32)
    tap = lax.broadcasted_iota(jnp.int32, (27, bands), 0)
    band = lax.broadcasted_iota(jnp.int32, (27, bands), 1) // rows
    for j in range(3):
        pick = (tap == 9 * (band // 3) + 3 * j + band % 3).astype(f32)
        chosen = jnp.dot(wt_ref[...].astype(f32), pick, preferred_element_type=f32)
        full = jnp.dot(spread, chosen, preferred_element_type=f32)
        wide = jnp.where(tap_y == j, full, wide)
    wide_ref[...] = wide.astype(bf16)

    zc = plan.zc
    lane = lane_iota((rows, plan.nz))
    bias = jnp.zeros((rows, plan.nz), f32)
    places = {}
    for x in range(-1, plan.nx + 1):
        tile, first = plan.slot(x)
        places.setdefault(tile, {})[first] = x
    for tile in range(plan.sent):
        stack = [got_ref[p, tile, 0:zc] for p in range(plan.members)]
        turned = jnp.concatenate(stack, axis=0).T
        low = got_ref[0, tile, zc : zc + 1]
        high = got_ref[plan.members - 1, tile, zc + 1 : zc + 2]
        ends = jnp.concatenate([low, high, jnp.zeros((LANES - 2, LANES), f32)], axis=0).T
        for first, x in places[tile].items():
            g = turned[first : first + rows]
            end = ends[first : first + rows]
            down = jnp.where(lane == plan.nz - 1, pltpu.roll(end, plan.nz - 2, 1), pltpu.roll(g, plan.nz - 1, 1))
            up = jnp.where(lane == 0, end, pltpu.roll(g, 1, 1))
            g_ref[x + 1] = jnp.concatenate([down, g, up], axis=0).astype(bf16)
            if 0 <= x < plan.nx:
                bias = bias + g
    y_own = lax.broadcasted_iota(jnp.int32, (rows, plan.nz), 0) // plan.ny == pos_ref[1]
    bias = jnp.sum(jnp.where(y_own, bias, 0.0))

    dw_ref[...] = jnp.zeros_like(dw_ref)

    def at_x(x, carry):
        block = f_ref[:, x].reshape(inner, plan.nz)
        moved = jnp.concatenate([g_ref[x + 2], g_ref[x + 1], g_ref[x]], axis=0)
        out = jnp.dot(wide_ref[...], moved, preferred_element_type=f32)
        gf_ref[:, x] = out.astype(bf16).reshape(plan.ch, plan.ny, plan.nz)
        dw_ref[...] += lax.dot_general(
            moved, block, (((1,), (1,)), ((), ())), preferred_element_type=f32
        )
        return carry

    lax.fori_loop(0, plan.nx, at_x, 0)

    tap_y = tap_condition(plan, pos_ref[1], (rows, inner), 0, 1)
    taps = []
    for t in range(27):
        i, j, k = t // 9, t // 3 % 3, t % 3
        at = (3 * i + k) * rows
        taps.append(jnp.sum(jnp.where(tap_y == j, dw_ref[at : at + rows], 0.0), axis=0, keepdims=True))
    taps += [jnp.zeros((1, inner), f32)] * 5
    total = jnp.zeros((8, LANES), f32)
    for n in range(4):
        place = (
            lax.broadcasted_iota(jnp.int32, (inner, LANES), 0) // plan.ny + 32 * n
            == lax.broadcasted_iota(jnp.int32, (inner, LANES), 1)
        ).astype(f32)
        total = total + jnp.dot(
            jnp.concatenate(taps[8 * n : 8 * n + 8], axis=0),
            place,
            precision=lax.Precision.HIGHEST,
            preferred_element_type=f32,
        )
    spot = (row_iota((8, LANES)) == 3) & (lane_iota((8, LANES)) == 96)
    total = jnp.where(spot, bias, total)
    gw_ref[...] = jnp.broadcast_to(total[None], (plan.ranks, 8, LANES))


def final_kernel(plan, got_ref, gw_ref, gb_ref):
    total = jnp.sum(got_ref[...], axis=0)
    for n in range(4):
        count = min(8, 27 - 8 * n)
        gw_ref[8 * n : 8 * n + count] = total[:count, 32 * n : 32 * n + plan.ch]
    gb_ref[...] = total[3:4, 96:97]


VMEM = pl.BlockSpec(memory_space=pltpu.VMEM)
SMEM = pl.BlockSpec(memory_space=pltpu.SMEM)
BIG = pltpu.CompilerParams(vmem_limit_bytes=63 * 1024 * 1024)


def shape(dims, dtype=f32):
    return jax.ShapeDtypeStruct(dims, dtype)


def per_device(mesh_shape, features, weight, bias, label):
    plan = Plan(mesh_shape, features.shape)
    members, sent, own, R, tiles = plan.members, plan.sent, plan.own, plan.R, plan.tiles
    inner, bands = plan.ch * plan.ny, 9 * plan.Y
    place = (lax.axis_index("gz") * members + lax.axis_index(GROUP)).astype(jnp.int32)
    pos = jnp.stack([place, lax.axis_index("gy").astype(jnp.int32)])

    def call(kernel, out_shape, in_specs, scratch=(), params=BIG):
        return pl.pallas_call(
            functools.partial(kernel, plan),
            out_shape=out_shape,
            in_specs=in_specs,
            out_specs=jax.tree.map(lambda s: VMEM, out_shape),
            scratch_shapes=list(scratch),
            compiler_params=params,
        )

    def exchange(array):
        return lax.all_to_all(array, GROUP, 0, 0, tiled=True)

    def everywhere(array):
        return lax.all_to_all(array, ALL_AXES, 0, 0, tiled=True)

    def hop(array, distance):
        def device(r):
            return (r % members) * plan.gz + r // members

        pairs = [
            (device(r), device(r + distance))
            for r in range(plan.ranks)
            if 0 <= r + distance < plan.ranks
        ]
        return lax.ppermute(array, ALL_AXES, pairs)

    label_sent = call(label_kernel, shape((members, own, plan.zc, LANES), bf16), [SMEM, VMEM])(
        pos, label
    )
    sent_logits = call(
        conv_kernel,
        shape((members, sent, R, LANES)),
        [SMEM, VMEM, VMEM],
        [
            pltpu.VMEM((bands, inner), bf16),
            pltpu.VMEM((plan.nx + 2, 3 * plan.Y, plan.nz), f32),
        ],
    )(pos, weight, features)
    def planes(array):
        return array.reshape(-1, tiles, LANES)

    def hops_of(parts, count):
        whole, head, tail = parts
        below = [hop(whole if h < count else tail, h) for h in range(1, count + 1)]
        above = [hop(whole if h < count else head, -h) for h in range(1, count + 1)]
        return below + above

    zc = plan.zc
    short = plan.label_rest * tiles
    label_parts = call(
        label_gather_kernel,
        [shape((zc * tiles, LANES), bf16)] + [shape((short, LANES), bf16)] * 2,
        [VMEM],
        [pltpu.VMEM((zc * tiles, LANES), f32)],
    )(exchange(label_sent))
    label_parts = [planes(part) for part in label_parts]
    short = (plan.rest + 1) * tiles
    parts = call(
        gather_kernel,
        [shape(((zc + 2) * tiles, LANES))] + [shape((short, LANES))] * 2,
        [VMEM],
    )(exchange(sent_logits))
    parts = [planes(part) for part in parts]
    around = hops_of(parts, plan.hops)
    label_around = hops_of(label_parts, plan.label_hops)

    window = (plan.win, tiles, LANES)
    span = (plan.span, tiles, LANES)
    table = pltpu.VMEM((3, tiles, LANES), f32)
    room = plan.win + 2 + plan.span_block
    target, ts = call(
        target_kernel,
        [shape(window), shape(span)],
        [SMEM] + [VMEM] * (1 + 2 * plan.label_hops),
        [
            pltpu.VMEM((2, room, plan.pad, LANES), f32),
            pltpu.VMEM((2, room, tiles, LANES), f32),
            pltpu.VMEM((plan.span, plan.pad, LANES), f32),
            table,
            table,
        ],
    )(pos, label_parts[0], *label_around)
    record = pl.BlockSpec((1,) + window, lambda n: (n, 0, 0, 0))
    outs = pl.pallas_call(
        functools.partial(forward_kernel, plan),
        grid=(SECTIONS,),
        out_shape=[shape((SECTIONS,) + window)] * 4
        + [shape(span), shape((plan.ranks, 8, LANES))],
        in_specs=[SMEM, SMEM] + [VMEM] * (3 + 2 * plan.hops),
        out_specs=[record] * 4 + [VMEM] * 2,
        scratch_shapes=[
            pltpu.VMEM((2, plan.planes, plan.pad, LANES), f32),
            pltpu.VMEM((2, plan.planes, tiles, LANES), f32),
            pltpu.VMEM((plan.win, plan.pad, LANES), f32),
            pltpu.VMEM(window, f32),
            table,
            table,
        ],
        compiler_params=BIG,
    )(pos, bias, target, ts, parts[0], *around)
    m, q, t, g2, predict, sums = outs
    sums = everywhere(sums)

    back = pl.BlockSpec((1,) + window, lambda n: (SECTIONS - 1 - n, 0, 0, 0))
    grad_sent, loss = pl.pallas_call(
        functools.partial(backward_kernel, plan),
        grid=(SECTIONS,),
        out_shape=[shape((members, sent, R, LANES)), shape((8, LANES))],
        in_specs=[SMEM, VMEM] + [back] * 4 + [VMEM] * 3,
        out_specs=[VMEM, VMEM],
        scratch_shapes=[
            pltpu.VMEM(window, f32),
            pltpu.VMEM(window, f32),
            pltpu.VMEM((plan.win, plan.pad, LANES), f32),
            pltpu.VMEM((plan.win + 2, plan.pad, LANES), f32),
            table,
            pltpu.VMEM((plan.span * tiles, LANES), f32),
        ],
        compiler_params=BIG,
    )(pos, sums, m, q, t, g2, predict, target, ts)

    grad_features, partial = call(
        grad_kernel,
        [shape(features.shape, bf16), shape((plan.ranks, 8, LANES))],
        [SMEM, VMEM, VMEM, VMEM],
        [
            pltpu.VMEM((inner, bands), bf16),
            pltpu.VMEM((plan.nx + 2, 3 * plan.Y, plan.nz), bf16),
            pltpu.VMEM((bands, inner), f32),
        ],
    )(pos, weight.T, features, exchange(grad_sent))
    grad_weight, grad_bias = call(
        final_kernel, [shape((27, plan.ch)), shape((1, 1))], [VMEM]
    )(everywhere(partial))
    return (loss[0, :1], grad_features, grad_weight, grad_bias.reshape(1))


def solution(mesh):
    in_specs = (P(None, "gx", "gy", "gz"), P(), P(), P("gx", "gy", "gz"))
    out_specs = (P(), P(None, "gx", "gy", "gz"), P(), P())
    return jax.shard_map(
        functools.partial(per_device, dict(mesh.shape)),
        mesh=mesh,
        in_specs=in_specs,
        out_specs=out_specs,
        check_vma=False,
    )
```

```python
import functools

import jax
import jax.numpy as jnp
from jax import lax
from jax.experimental import pallas as pl
from jax.experimental.pallas import tpu as pltpu
from jax.sharding import PartitionSpec as P

ITERS = 10
SECTIONS = ITERS + 1
LANES = 128
REACH = SECTIONS + 2
HALO = 2 * SECTIONS + 3

temper = 20.0
sharpness = 40.0

GROUP = ("gx", "gy")
ALL_AXES = ("gx", "gy", "gz")
f32 = jnp.float32
bf16 = jnp.bfloat16


def up8(value):
    return -(-value // 8) * 8


class Plan:
    def __init__(self, mesh_shape, block):
        self.ch, self.nx, self.ny, self.nz = block
        self.gx, self.gy, self.gz = (mesh_shape[a] for a in ALL_AXES)
        self.members = self.gx * self.gy
        self.ranks = self.members * self.gz
        self.X = self.nx * self.gx
        self.Y = self.ny * self.gy
        self.Z = self.nz * self.gz
        assert LANES % self.Y == 0 and self.nz == LANES
        assert self.nz % self.members == 0
        self.zc = self.nz // self.members
        self.per = LANES // self.Y
        assert self.nx % self.per == 0
        self.tiles = self.X // self.per
        self.own = self.nx // self.per
        self.shared = self.per > 1
        self.sent = self.own + (1 if self.shared else 2)
        self.R = up8(self.zc)
        self.extra = -(-2 * self.sent // self.R)
        self.R16 = -(-self.zc // 16) * 16
        self.extra16 = -(-2 * self.sent // self.R16)
        self.pad = self.tiles + 16
        self.win = self.zc + 2 * REACH
        self.span = self.zc + 2
        self.block = self.blocks_of(self.win)
        self.span_block = self.blocks_of(self.span)
        self.base = HALO + 1
        self.planes = self.zc + 2 * HALO + 2 + self.block
        self.hops = -(-HALO // self.zc)
        self.rest = HALO - (self.hops - 1) * self.zc
        self.label_hops = -(-REACH // self.zc)
        self.label_rest = REACH - (self.label_hops - 1) * self.zc

    def blocks_of(self, count):
        fits = [n for n in range(1, count + 1) if count % n == 0 and n * self.tiles <= 256]
        return fits[-1] if fits else 1

    def slot(self, x):
        if 0 <= x < self.nx:
            return x // self.per, (x % self.per) * self.Y
        if x == self.nx:
            return self.own, 0
        return self.sent - 1, LANES - self.Y


def lane_iota(shape):
    return lax.broadcasted_iota(jnp.int32, shape, len(shape) - 1)


def row_iota(shape):
    return lax.broadcasted_iota(jnp.int32, shape, len(shape) - 2)


def masks(plan):
    lane = lane_iota((plan.tiles, LANES))
    return lane, lane % plan.Y == 0, lane % plan.Y == plan.Y - 1


def x_neighbours(plan, mask, load, cur):
    lower, upper = load(-1), load(1)
    if plan.Y == LANES:
        return lower + upper
    lower = pltpu.roll(jnp.where(mask[0] >= LANES - plan.Y, lower, cur), plan.Y, 1)
    upper = pltpu.roll(jnp.where(mask[0] < plan.Y, upper, cur), LANES - plan.Y, 1)
    return lower + upper


def y_neighbours(plan, mask, cur):
    lower = jnp.where(mask[1], 0.0, pltpu.roll(cur, 1, 1))
    upper = jnp.where(mask[2], 0.0, pltpu.roll(cur, LANES - 1, 1))
    return lower + upper


def count_tables(plan, cross_ref, box_ref):
    flat = row_iota((plan.tiles, LANES)) * LANES + lane_iota((plan.tiles, LANES))
    y, x = flat % plan.Y, flat // plan.Y

    def along(spot, size):
        return 3.0 - (spot == 0).astype(f32) - (spot == size - 1).astype(f32)

    cx, cy = along(x, plan.X), along(y, plan.Y)
    for kind, cz in ((1, 2.0), (2, 3.0)):
        if cross_ref is not None:
            cross_ref[kind] = 1.0 / (cx + cy + cz - 2.0)
        if box_ref is not None:
            box_ref[kind] = 1.0 / (cx * cy * cz)
    for ref in (cross_ref, box_ref):
        if ref is not None:
            ref[0] = jnp.zeros((plan.tiles, LANES), f32)


def kind_of(plan, rank, plane):
    z = rank * plan.zc + plane
    inside = (z >= 0) & (z < plan.Z)
    edge = (z == 0) | (z == plan.Z - 1)
    return jnp.where(inside, jnp.where(edge, 1, 2), 0), jnp.where(inside, 0.0, 1.0)


def store_all(pairs):
    for ref, at, value in pairs:
        ref[at] = value


def over(first, count, size, body):
    def at(n, carry):
        body(first + n * size)
        return carry

    lax.fori_loop(0, (count + size - 1) // size, at, 0)


def tap_condition(plan, member_y, shape, y_dim, in_dim):
    y = lax.broadcasted_iota(jnp.int32, shape, y_dim) % plan.Y
    own = lax.broadcasted_iota(jnp.int32, shape, in_dim) % plan.ny
    return own + member_y * plan.ny - y + 1


def conv_kernel(plan, pos_ref, w_ref, f_ref, label_ref, out_ref, wide_ref, acc_ref):
    del label_ref
    rows, inner = plan.Y, plan.ch * plan.ny
    spread = (
        lax.broadcasted_iota(jnp.int32, (plan.ch, inner), 0)
        == lax.broadcasted_iota(jnp.int32, (plan.ch, inner), 1) // plan.ny
    ).astype(f32)
    taps = jnp.dot(w_ref[...].astype(f32), spread, preferred_element_type=f32)
    tap_y = tap_condition(plan, pos_ref[1], (rows, inner), 0, 1)
    for i in range(3):
        for k in range(3):
            band = jnp.zeros((rows, inner), f32)
            for j in range(3):
                t = 9 * i + 3 * j + k
                band = jnp.where(tap_y == j, taps[t : t + 1], band)
            at = (3 * i + k) * rows
            wide_ref[at : at + rows] = band.astype(bf16)
    acc_ref[...] = jnp.zeros_like(acc_ref)

    def at_x(x, carry):
        block = f_ref[:, x].reshape(inner, plan.nz)
        out = jnp.dot(wide_ref[...], block, preferred_element_type=f32)
        for i in range(3):
            acc_ref[x + 2 - i] += out[3 * i * rows : 3 * (i + 1) * rows]
        return carry

    lax.fori_loop(0, plan.nx, at_x, 0)

    out_ref[...] = jnp.zeros_like(out_ref)
    places = {}
    for x in range(-1, plan.nx + 1):
        tile, lane = plan.slot(x)
        places.setdefault(tile, {})[lane] = x
    lane = lane_iota((rows, plan.nz))
    for tile in range(plan.sent):
        parts, spills = [], []
        for first in range(0, LANES, rows):
            x = places[tile].get(first)
            if x is None:
                parts.append(jnp.zeros((rows, plan.nz), f32))
                spills.append(jnp.zeros((rows, plan.nz), f32))
                continue
            low = acc_ref[x + 1, 0:rows]
            mid = acc_ref[x + 1, rows : 2 * rows]
            high = acc_ref[x + 1, 2 * rows : 3 * rows]
            total = mid + jnp.where(lane == 0, 0.0, pltpu.roll(low, 1, 1))
            total = total + jnp.where(lane == plan.nz - 1, 0.0, pltpu.roll(high, plan.nz - 1, 1))
            parts.append(total)
            spill = jnp.where(lane == 1, pltpu.roll(low, 2, 1), 0.0)
            spills.append(jnp.where(lane == 0, high, spill))
        turned = jnp.concatenate(parts, axis=0).T
        spill = jnp.concatenate(spills, axis=0).T
        for p in range(plan.members):
            out_ref[p, tile, 0 : plan.zc] = turned[p * plan.zc : (p + 1) * plan.zc]
        for end, p in ((0, 0), (1, plan.members - 1)):
            n = 2 * tile + end
            at = plan.sent + n // plan.R
            out_ref[p, at, n % plan.R : n % plan.R + 1] = spill[end : end + 1]


def label_kernel(plan, pos_ref, l_ref, out_ref):
    rows = plan.Y
    sub = lax.broadcasted_iota(jnp.int32, (plan.gy, plan.ny, plan.nz), 0)
    for tile in range(plan.own):
        parts = []
        for n in range(plan.per):
            block = l_ref[tile * plan.per + n].astype(f32)[None]
            wide = jnp.where(sub == pos_ref[1], block, 0.0)
            parts.append(wide.reshape(rows, plan.nz))
        turned = jnp.concatenate(parts, axis=0).T
        for p in range(plan.members):
            out_ref[p, tile] = turned[p * plan.zc : (p + 1) * plan.zc].astype(bf16)


def gather_kernel(plan, got_ref, out_ref, head_ref, tail_ref):
    tiles, zc, rest = plan.tiles, plan.zc, plan.rest
    lane = lane_iota((1, LANES))

    def part(p, q):
        values = [got_ref[p, q, 0:zc]]
        for end in range(2):
            n = 2 * q + end
            at = plan.sent + n // plan.R
            values.append(got_ref[p, at, n % plan.R : n % plan.R + 1])
        return values

    for a in range(plan.gx):
        for q in range(plan.own):
            parts = []
            for b in range(plan.gy):
                parts.append(part(a * plan.gy + b, q))
                if q == plan.own - 1 and a < plan.gx - 1:
                    edge = part((a + 1) * plan.gy + b, plan.sent - 1)
                    parts.append([jnp.where(lane >= LANES - plan.Y, v, 0.0) for v in edge])
                if q == 0 and a > 0:
                    edge = part((a - 1) * plan.gy + b, plan.own)
                    parts.append([jnp.where(lane < plan.Y, v, 0.0) for v in edge])
            whole, low, high = (functools.reduce(jnp.add, vs) for vs in zip(*parts))
            tile = a * plan.own + q
            out_ref[pl.ds(tile, zc, stride=tiles)] = whole
            out_ref[zc * tiles + tile : zc * tiles + tile + 1] = low
            out_ref[(zc + 1) * tiles + tile : (zc + 1) * tiles + tile + 1] = high
    head_ref[: rest * tiles] = out_ref[: rest * tiles]
    head_ref[rest * tiles :] = out_ref[zc * tiles : (zc + 1) * tiles]
    tail_ref[: rest * tiles] = out_ref[(zc - rest) * tiles : zc * tiles]
    tail_ref[rest * tiles :] = out_ref[(zc + 1) * tiles :]


def label_gather_kernel(plan, got_ref, out_ref, head_ref, tail_ref, all_ref):
    tiles, zc, rest = plan.tiles, plan.zc, plan.label_rest
    for a in range(plan.gx):
        for q in range(plan.own):
            total = got_ref[a * plan.gy, q].astype(f32)
            for b in range(1, plan.gy):
                total = total + got_ref[a * plan.gy + b, q].astype(f32)
            all_ref[pl.ds(a * plan.own + q, zc, stride=tiles)] = total
    out_ref[...] = all_ref[...].astype(bf16)
    head_ref[...] = all_ref[: rest * tiles].astype(bf16)
    tail_ref[...] = all_ref[(zc - rest) * tiles :].astype(bf16)


LOG = 1.0 / sharpness


def thin(e, box, inverse, outside):
    box = box + outside
    ratio = e * box * inverse + outside
    square = ratio * ratio
    more = 1.0 + square
    joint = 1.0 / (box * more)
    slope = joint * box
    return joint * more, slope, jnp.log(square * slope)


def lift(scaled, s):
    small = jnp.exp(scaled * (s - 1.0))
    more = 1.0 + small
    return s + jnp.log(more) * LOG, small * (1.0 / more)


def erode(plan, rank, mask, e_ref, g_ref, table_ref, now, base, first, count, size):
    tiles = slice(8, 8 + plan.tiles)

    def body(plane):
        out = []
        for n in range(size):
            at = plane + n + base
            cur = e_ref[now, at, tiles]

            def load(offset, at=at):
                return e_ref[now, at, 8 + offset : 8 + offset + plan.tiles]

            total = cur + e_ref[now, at - 1, tiles] + e_ref[now, at + 1, tiles]
            total = total + x_neighbours(plan, mask, load, cur) + y_neighbours(plan, mask, cur)
            kind, outside = kind_of(plan, rank, plane + n)
            total = total * table_ref[kind]
            out.append((e_ref, (1 - now, at, tiles), total))
            out.append((g_ref, (1 - now, at), 1.0 / (total + outside) - outside))
        store_all(out)

    over(first, count, size, body)


def spread(plan, mask, g_ref, now, zy_ref, base, first, count, size):
    tiles = slice(8, 8 + plan.tiles)

    def body(plane):
        out = []
        values = [g_ref[now, plane + n + base] for n in range(-1, size + 1)]
        for n in range(size):
            part = values[n] + values[n + 1] + values[n + 2]
            part = part + y_neighbours(plan, mask, part)
            out.append((zy_ref, (plane + n - first, tiles), part))
        store_all(out)

    over(first, count, size, body)


def x_box(plan, mask, zy_ref, at):
    cur = zy_ref[at, 8 : 8 + plan.tiles]

    def load(offset):
        return zy_ref[at, 8 + offset : 8 + offset + plan.tiles]

    return cur + x_neighbours(plan, mask, load, cur)


def target_kernel(plan, *refs):
    hops = plan.label_hops
    pos_ref, own_ref = refs[:2]
    below, above = refs[2 : 2 + hops], refs[2 + hops : 2 + 2 * hops]
    target_ref, ts_ref = refs[2 + 2 * hops : 4 + 2 * hops]
    e_ref, g_ref, zy_ref, cross_ref, box_ref = refs[4 + 2 * hops :]
    zc, win, span = plan.zc, plan.win, plan.span
    size = plan.span_block
    base = REACH + 1
    tiles = slice(8, 8 + plan.tiles)
    rank = pos_ref[0]
    mask = masks(plan)
    count_tables(plan, cross_ref, box_ref)
    e_ref[...] = jnp.zeros_like(e_ref)
    zy_ref[...] = jnp.zeros_like(zy_ref)
    g_ref[...] = jnp.zeros_like(g_ref)
    target_ref[REACH : REACH + zc] = own_ref[...].astype(f32)
    for h in range(1, hops + 1):
        n = zc if h < hops else plan.label_rest
        first = REACH - (h - 1) * zc - n
        target_ref[first : first + n] = below[h - 1][...].astype(f32)
        first = REACH + h * zc
        target_ref[first : first + n] = above[h - 1][...].astype(f32)

    def fill(plane):
        out = []
        for n in range(plan.block):
            at = plane + n
            z = rank * zc + at - REACH
            inside = ((z >= 0) & (z < plan.Z)).astype(f32)
            out.append((e_ref, (0, at + 1, tiles), jnp.exp(-temper * target_ref[at]) * inside))
        store_all(out)

    over(0, win, plan.block, fill)

    def section(step, carry):
        now = step % 2
        reach = 2 + ITERS - step
        erode(
            plan, rank, mask, e_ref, g_ref, cross_ref, now, base, -reach, zc + 2 * reach, size
        )
        spread(plan, mask, g_ref, 1 - now, zy_ref, base, -1, span, size)

        def point(plane, opening):
            out = []
            for n in range(size):
                at = plane + n
                box = x_box(plan, mask, zy_ref, at)
                kind, outside = kind_of(plan, rank, at - 1)
                e = e_ref[now, at - 1 + base, tiles]
                _, _, scaled = thin(e, box, box_ref[kind], outside)
                value = scaled * -LOG if opening else lift(scaled, ts_ref[at])[0]
                out.append((ts_ref, at, value))
            store_all(out)

        @pl.when(step == 0)
        def _():
            over(0, span, size, lambda plane: point(plane, True))

        @pl.when(step > 0)
        def _():
            over(0, span, size, lambda plane: point(plane, False))

        return carry

    lax.fori_loop(0, SECTIONS, section, 0)


def forward_kernel(plan, *refs):
    hops = plan.hops
    pos_ref, bias_ref, target_ref, ts_ref, own_ref = refs[:5]
    refs = refs[5:]
    below, above = refs[:hops], refs[hops : 2 * hops]
    refs = refs[2 * hops :]
    m_ref, q_ref, t_ref, g2_ref, p_ref, sums_ref = refs[:6]
    e_ref, g_ref, zy_ref, s_ref, cross_ref, box_ref = refs[6:]
    base, zc, size = plan.base, plan.zc, plan.block
    tiles = slice(8, 8 + plan.tiles)
    rank = pos_ref[0]
    step = pl.program_id(0)
    mask = masks(plan)

    @pl.when(step == 0)
    def _():
        e_ref[...] = jnp.zeros_like(e_ref)
        g_ref[...] = jnp.zeros_like(g_ref)
        zy_ref[...] = jnp.zeros_like(zy_ref)
        s_ref[...] = jnp.zeros_like(s_ref)
        count_tables(plan, cross_ref, box_ref)
        e_ref[0, base : base + zc, tiles] = own_ref[:zc]
        for h in range(1, hops + 1):
            n = zc if h < hops else plan.rest
            first = base - (h - 1) * zc - n
            e_ref[0, first : first + n, tiles] = below[h - 1][:n]
            first = base + h * zc
            e_ref[0, first : first + n, tiles] = above[h - 1][:n]
        e_ref[0, base - 1, tiles] += own_ref[zc]
        e_ref[0, base + zc, tiles] += own_ref[zc + 1]
        for h in range(1, hops + 1):
            if h < hops:
                e_ref[0, base - h * zc - 1, tiles] += below[h - 1][zc]
                e_ref[0, base + (h + 1) * zc, tiles] += above[h - 1][zc + 1]
                e_ref[0, base - (h - 1) * zc, tiles] += below[h - 1][zc + 1]
                e_ref[0, base + h * zc - 1, tiles] += above[h - 1][zc]
            else:
                e_ref[0, base - (h - 1) * zc, tiles] += below[h - 1][plan.rest]
                e_ref[0, base + h * zc - 1, tiles] += above[h - 1][plan.rest]

        def sigmoid(logits):
            small = jnp.exp(-jnp.abs(logits))
            part = 1.0 / (1.0 + small)
            return jnp.where(logits >= 0, part, small * part)

        for n in range(plan.span):
            p_ref[n] = sigmoid(e_ref[0, base - 1 + n, tiles] + bias_ref[0])

        def fill(plane):
            out = []
            for n in range(size):
                at = plane + n
                z = rank * zc + at - base
                inside = ((z >= 0) & (z < plan.Z)).astype(f32)
                predict = sigmoid(e_ref[0, at, tiles] + bias_ref[0])
                out.append((e_ref, (0, at, tiles), jnp.exp(-temper * predict) * inside))
                out.append((g_ref, (0, at), jnp.exp(temper * predict) * inside))
            store_all(out)

        over(1, zc + 2 * HALO, size, fill)

    now = step % 2
    reach = REACH + 1 + ITERS - step
    erode(plan, rank, mask, e_ref, g_ref, cross_ref, now, base, -reach, zc + 2 * reach, size)
    spread(plan, mask, g_ref, 1 - now, zy_ref, base, -REACH, plan.win, size)
    def point(at, opening):
        out = []
        for n in range(size):
            spot = at + n
            plane = spot - REACH
            box = x_box(plan, mask, zy_ref, spot)
            kind, outside = kind_of(plan, rank, plane)
            e = e_ref[now, plane + base, tiles]
            over_box, slope, scaled = thin(e, box, box_ref[kind], outside)
            if opening:
                grown, a = scaled * -LOG, slope
            else:
                s = s_ref[spot]
                grown, rate = lift(scaled, s)
                a = rate * (1.0 - s) * slope
                out.append((m_ref, (0, spot), 1.0 + rate * scaled * LOG))
            after = g_ref[1 - now, plane + base]
            out.append((s_ref, spot, grown))
            out.append((q_ref, (0, spot), a * over_box))
            out.append((t_ref, (0, spot), a * g_ref[now, plane + base]))
            out.append((g2_ref, (0, spot), after * after))
        store_all(out)

    @pl.when(step == 0)
    def _():
        over(0, plan.win, size, lambda at: point(at, True))
        m_ref[...] = jnp.ones_like(m_ref)

    @pl.when(step > 0)
    def _():
        over(0, plan.win, size, lambda at: point(at, False))

    @pl.when(step == SECTIONS - 1)
    def _():
        def add(n, totals):
            ps, ts = s_ref[REACH + n], ts_ref[1 + n]
            predict, target = p_ref[1 + n], target_ref[REACH + n]
            terms = (ps * target, ps, ts * predict, ts, predict * target, predict, target)
            return tuple(total + term for total, term in zip(totals, terms))

        start = (jnp.zeros((plan.tiles, LANES), f32),) * 7
        totals = lax.fori_loop(0, zc, add, start)
        lines = [jnp.sum(total, axis=0, keepdims=True) for total in totals]
        lines.append(jnp.zeros((1, LANES), f32))
        sums_ref[...] = jnp.broadcast_to(
            jnp.concatenate(lines, axis=0)[None], (plan.ranks, 8, LANES)
        )


def backward_kernel(plan, *refs):
    (
        pos_ref, sums_ref, m_ref, q_ref, t_ref, g2_ref, p_ref, target_ref, ts_ref,
        out_ref, loss_ref, bias_ref,
        w_ref, h_ref, zy_ref, pull_ref, cross_ref, grad_ref,
    ) = refs
    step = pl.program_id(0)
    rank = pos_ref[0]
    win, zc, size = plan.win, plan.zc, plan.block
    tiles = slice(8, 8 + plan.tiles)
    mask = masks(plan)

    lines = jnp.sum(jnp.sum(sums_ref[...], axis=0), axis=1, keepdims=True)
    s1, s2, s3, s4, s5, s6, s7 = (lines[n : n + 1] for n in range(7))
    prec = (s1 + 1.0) / (s2 + 1.0)
    sens = (s3 + 1.0) / (s4 + 1.0)

    @pl.when(step == 0)
    def _():
        zy_ref[...] = jnp.zeros_like(zy_ref)
        pull_ref[...] = jnp.zeros_like(pull_ref)
        h_ref[...] = jnp.zeros_like(h_ref)
        count_tables(plan, cross_ref, None)
        for n in range(win):
            z = rank * zc + n - REACH
            inside = ((z >= 0) & (z < plan.Z)).astype(f32)
            w_ref[n] = (target_ref[n] - prec) * inside

    def within(reach, body):
        count = (zc + 2 * reach + size - 1) // size
        first = jnp.minimum(REACH - reach, win - count * size)
        over(first, count * size, size, body)

    left = SECTIONS - 1 - step

    def push(at):
        values = []
        for n in range(-1, size + 1):
            spot = jnp.clip(at + n, 0, win - 1)
            values.append(w_ref[spot] * q_ref[0, spot])
        out = []
        for n in range(size):
            part = values[n] + values[n + 1] + values[n + 2]
            part = part + y_neighbours(plan, mask, part)
            out.append((zy_ref, (at + n, tiles), part))
        store_all(out)

    within(left + 2, push)

    def pull(at):
        out = []
        for n in range(size):
            spot = at + n
            box = x_box(plan, mask, zy_ref, spot)
            inverse = cross_ref[kind_of(plan, rank, spot - REACH)[0]]
            value = (h_ref[spot] - g2_ref[0, spot] * box) * inverse
            out.append((pull_ref, (spot + 1, tiles), value))
        store_all(out)

    within(left + 2, pull)

    def join(at):
        out = []
        for n in range(size):
            spot = at + n
            cur = pull_ref[spot + 1, tiles]

            def load(offset, spot=spot):
                return pull_ref[spot + 1, 8 + offset : 8 + offset + plan.tiles]

            total = cur + pull_ref[spot, tiles] + pull_ref[spot + 2, tiles]
            total = total + x_neighbours(plan, mask, load, cur) + y_neighbours(plan, mask, cur)
            w = w_ref[spot]
            out.append((h_ref, spot, w * t_ref[0, spot] + total))
            out.append((w_ref, spot, w * m_ref[0, spot]))
        store_all(out)

    within(left + 2, join)

    @pl.when(step == SECTIONS - 1)
    def _():
        both = prec + sens
        volume = s6 + s7 + 1.0
        cl_loss = 1.0 - 2.0 * prec * sens / both
        dice_loss = 1.0 - (2.0 * s5 + 1.0) / volume
        loss_ref[...] = jnp.broadcast_to(0.5 * dice_loss + 0.5 * cl_loss, (8, LANES))
        l0 = -(sens / both) * (sens / both) / (s2 + 1.0)
        l2 = -(prec / both) * (prec / both) / (s4 + 1.0)
        l4 = -1.0 / volume
        l5 = 0.5 * (2.0 * s5 + 1.0) / (volume * volume)

        def finish(n, total):
            z = rank * zc + n - 1
            inside = ((z >= 0) & (z < plan.Z)).astype(f32)
            at = n + REACH - 1
            predict = p_ref[n]
            skel = l0 * jnp.exp(-temper * predict) * h_ref[at]
            whole = skel + l2 * ts_ref[n] + l4 * target_ref[at] + l5
            grad = whole * predict * (1.0 - predict) * inside
            grad_ref[pl.ds(pl.multiple_of(n * plan.tiles, 8), plan.tiles)] = grad
            mine = ((n >= 1) & (n <= zc)).astype(f32)
            return total + grad * mine

        total = lax.fori_loop(0, plan.span, finish, jnp.zeros((plan.tiles, LANES), f32))
        bias_ref[...] = jnp.sum(total.reshape(-1, 8, LANES), axis=0)
        lane = lane_iota((1, LANES))

        def column(tile):
            return [
                grad_ref[pl.ds(plan.tiles + tile, zc, stride=plan.tiles)],
                grad_ref[tile : tile + 1],
                grad_ref[(zc + 1) * plan.tiles + tile : (zc + 1) * plan.tiles + tile + 1],
            ]

        for a in range(plan.gx):
            pieces = [column(a * plan.own + q) for q in range(plan.own)]
            zero = [jnp.zeros((zc, LANES), f32)] + [jnp.zeros((1, LANES), f32)] * 2
            after = column((a + 1) * plan.own) if a < plan.gx - 1 else zero
            before = column(a * plan.own - 1) if a > 0 else zero
            if plan.shared:
                pieces.append(
                    [
                        jnp.where(lane < plan.Y, x, 0.0)
                        + jnp.where(lane >= LANES - plan.Y, y, 0.0)
                        for x, y in zip(after, before)
                    ]
                )
            else:
                pieces += [after, before]
            edges = [edge for piece in pieces for edge in piece[1:]]
            rows = plan.R16
            edges += [jnp.zeros((1, LANES), f32)] * (plan.extra16 * rows - len(edges))
            whole = [piece[0] for piece in pieces]
            if rows > zc:
                fill = jnp.zeros((rows - zc, LANES), f32)
                whole = [jnp.concatenate([piece, fill], axis=0) for piece in whole]
            whole += [
                jnp.concatenate(edges[n * rows : (n + 1) * rows], axis=0)
                for n in range(plan.extra16)
            ]
            for q, piece in enumerate(whole):
                piece = piece.astype(bf16)
                for b in range(plan.gy):
                    out_ref[a * plan.gy + b, q] = piece


def weight_kernel(plan, pos_ref, f_ref, bias_ref, got_ref, gw_ref, g_ref, dw_ref):
    rows, inner = plan.Y, plan.ch * plan.ny
    zc, nz = plan.zc, plan.nz
    lane = lane_iota((rows, nz))
    places = {}
    for x in range(-1, plan.nx + 1):
        tile, first = plan.slot(x)
        places.setdefault(tile, {})[first] = x
    for tile in range(plan.sent):
        stack = [got_ref[p, tile].astype(f32)[:zc] for p in range(plan.members)]
        turned = jnp.concatenate(stack, axis=0).T
        ends = []
        for end, p in ((0, 0), (1, plan.members - 1)):
            n = 2 * tile + end
            row = got_ref[p, plan.sent + n // plan.R16].astype(f32)
            ends.append(row[n % plan.R16 : n % plan.R16 + 1])
        ends = jnp.concatenate(ends + [jnp.zeros((LANES - 2, LANES), f32)], axis=0).T
        for first, x in places[tile].items():
            g = turned[first : first + rows]
            end = ends[first : first + rows]
            down = jnp.where(lane == nz - 1, pltpu.roll(end, nz - 2, 1), pltpu.roll(g, nz - 1, 1))
            up = jnp.where(lane == 0, end, pltpu.roll(g, 1, 1))
            g_ref[x + 1] = jnp.concatenate([down, g, up], axis=0).astype(bf16)

    dw_ref[...] = jnp.zeros_like(dw_ref)

    def at_x(x, carry):
        block = f_ref[:, x].reshape(inner, nz)
        moved = jnp.concatenate([g_ref[x + 2], g_ref[x + 1], g_ref[x]], axis=0)
        dw_ref[...] += lax.dot_general(
            moved, block, (((1,), (1,)), ((), ())), preferred_element_type=f32
        )
        return carry

    lax.fori_loop(0, plan.nx, at_x, 0)

    tap_y = tap_condition(plan, pos_ref[1], (rows, inner), 0, 1)
    taps = []
    for t in range(27):
        i, j, k = t // 9, t // 3 % 3, t % 3
        at = (3 * i + k) * rows
        taps.append(jnp.sum(jnp.where(tap_y == j, dw_ref[at : at + rows], 0.0), axis=0, keepdims=True))
    taps += [jnp.zeros((1, inner), f32)] * 5
    total = jnp.zeros((8, LANES), f32)
    for n in range(4):
        place = (
            lax.broadcasted_iota(jnp.int32, (inner, LANES), 0) // plan.ny + 32 * n
            == lax.broadcasted_iota(jnp.int32, (inner, LANES), 1)
        ).astype(f32)
        total = total + jnp.dot(
            jnp.concatenate(taps[8 * n : 8 * n + 8], axis=0),
            place,
            precision=lax.Precision.HIGHEST,
            preferred_element_type=f32,
        )
    spot = (row_iota((8, LANES)) == 3) & (lane_iota((8, LANES)) == 96)
    total = jnp.where(spot, jnp.sum(bias_ref[...]), total)
    gw_ref[...] = jnp.broadcast_to(total[None], (plan.ranks, 8, LANES))


def feature_kernel(plan, pos_ref, wt_ref, g_ref, after_ref, gf_ref, wide_ref):
    del after_ref
    rows, inner, bands = plan.Y, plan.ch * plan.ny, 9 * plan.Y
    spread = (
        lax.broadcasted_iota(jnp.int32, (inner, plan.ch), 0) // plan.ny
        == lax.broadcasted_iota(jnp.int32, (inner, plan.ch), 1)
    ).astype(f32)
    tap_y = tap_condition(plan, pos_ref[1], (inner, bands), 1, 0)
    wide = jnp.zeros((inner, bands), f32)
    tap = lax.broadcasted_iota(jnp.int32, (27, bands), 0)
    band = lax.broadcasted_iota(jnp.int32, (27, bands), 1) // rows
    for j in range(3):
        pick = (tap == 9 * (band // 3) + 3 * j + band % 3).astype(f32)
        chosen = jnp.dot(wt_ref[...].astype(f32), pick, preferred_element_type=f32)
        full = jnp.dot(spread, chosen, preferred_element_type=f32)
        wide = jnp.where(tap_y == j, full, wide)
    wide_ref[...] = wide.astype(bf16)

    def at_x(x, carry):
        moved = jnp.concatenate([g_ref[x + 2], g_ref[x + 1], g_ref[x]], axis=0)
        out = jnp.dot(wide_ref[...], moved, preferred_element_type=f32)
        gf_ref[:, x] = out.astype(bf16).reshape(plan.ch, plan.ny, plan.nz)
        return carry

    lax.fori_loop(0, plan.nx, at_x, 0)


def final_kernel(plan, got_ref, gw_ref, gb_ref):
    total = jnp.sum(got_ref[...], axis=0)
    for n in range(4):
        count = min(8, 27 - 8 * n)
        gw_ref[8 * n : 8 * n + count] = total[:count, 32 * n : 32 * n + plan.ch]
    gb_ref[...] = total[3:4, 96:97]


VMEM = pl.BlockSpec(memory_space=pltpu.VMEM)
SMEM = pl.BlockSpec(memory_space=pltpu.SMEM)
ANY = pl.BlockSpec(memory_space=pl.ANY)
MIB = 1024 * 1024


def shape(dims, dtype=f32):
    return jax.ShapeDtypeStruct(dims, dtype)


def held(dims, dtype):
    if len(dims) < 2:
        return 4096
    size = jnp.dtype(dtype).itemsize
    rows = 8 * 4 // size
    total = -(-dims[-2] // rows) * rows * -(-dims[-1] // LANES) * LANES * size
    for n in dims[:-2]:
        total *= n
    return total


def limits(arrays, scratch, micros):
    total = sum(held(a.shape, a.dtype) for a in arrays)
    total += sum(held(a.shape, a.dtype) for a in scratch)
    limit = min(63 * MIB, total + total // 8 + 4 * MIB)
    return dict(
        compiler_params=pltpu.CompilerParams(vmem_limit_bytes=limit),
        cost_estimate=pl.CostEstimate(
            flops=0, transcendentals=0, bytes_accessed=int(micros * 2.5e6)
        ),
    )


def per_device(mesh_shape, features, weight, bias, label):
    plan = Plan(mesh_shape, features.shape)
    members, sent, own, tiles = plan.members, plan.sent, plan.own, plan.tiles
    inner, bands = plan.ch * plan.ny, 9 * plan.Y
    place = (lax.axis_index("gz") * members + lax.axis_index(GROUP)).astype(jnp.int32)
    pos = jnp.stack([place, lax.axis_index("gy").astype(jnp.int32)])

    def call(kernel, out_shape, in_specs, operands, micros, scratch=()):
        outs = jax.tree.leaves(out_shape)
        ins = [a for spec, a in zip(in_specs, operands) if spec is VMEM]
        return pl.pallas_call(
            functools.partial(kernel, plan),
            out_shape=out_shape,
            in_specs=in_specs,
            out_specs=jax.tree.map(lambda s: VMEM, out_shape),
            scratch_shapes=list(scratch),
            **limits(ins + outs, scratch, micros),
        )(*operands)

    def exchange(array):
        return lax.all_to_all(array, GROUP, 0, 0, tiled=True)

    def everywhere(array):
        return lax.all_to_all(array, ALL_AXES, 0, 0, tiled=True)

    def hop(array, distance):
        def device(r):
            return (r % members) * plan.gz + r // members

        pairs = [
            (device(r), device(r + distance))
            for r in range(plan.ranks)
            if 0 <= r + distance < plan.ranks
        ]
        return lax.ppermute(array, ALL_AXES, pairs)

    label_sent = call(
        label_kernel, shape((members, own, plan.zc, LANES), bf16), [SMEM, VMEM], (pos, label), 1.5
    )
    sent_logits = call(
        conv_kernel,
        shape((members, sent + plan.extra, plan.R, LANES)),
        [SMEM, VMEM, VMEM, ANY],
        (pos, weight, features, label_sent),
        7,
        [
            pltpu.VMEM((bands, inner), bf16),
            pltpu.VMEM((plan.nx + 2, 3 * plan.Y, plan.nz), f32),
        ],
    )

    def planes(array):
        return array.reshape(-1, tiles, LANES)

    def hops_of(parts, count):
        whole, head, tail = parts
        below = [hop(whole if h < count else tail, h) for h in range(1, count + 1)]
        above = [hop(whole if h < count else head, -h) for h in range(1, count + 1)]
        return below + above

    zc = plan.zc
    short = plan.label_rest * tiles
    label_parts = call(
        label_gather_kernel,
        [shape((zc * tiles, LANES), bf16)] + [shape((short, LANES), bf16)] * 2,
        [VMEM],
        (exchange(label_sent),),
        1.5,
        [pltpu.VMEM((zc * tiles, LANES), f32)],
    )
    label_parts = [planes(part) for part in label_parts]
    short = (plan.rest + 1) * tiles
    parts = call(
        gather_kernel,
        [shape(((zc + 2) * tiles, LANES))] + [shape((short, LANES))] * 2,
        [VMEM],
        (exchange(sent_logits),),
        1.5,
    )
    parts = [planes(part) for part in parts]
    around = hops_of(parts, plan.hops)
    label_around = hops_of(label_parts, plan.label_hops)

    window = (plan.win, tiles, LANES)
    span = (plan.span, tiles, LANES)
    table = pltpu.VMEM((3, tiles, LANES), f32)
    room = plan.win + 2 + plan.span_block
    target, ts = call(
        target_kernel,
        [shape(window), shape(span)],
        [SMEM] + [VMEM] * (1 + 2 * plan.label_hops),
        (pos, label_parts[0], *label_around),
        14,
        [
            pltpu.VMEM((2, room, plan.pad, LANES), f32),
            pltpu.VMEM((2, room, tiles, LANES), f32),
            pltpu.VMEM((plan.span, plan.pad, LANES), f32),
            table,
            table,
        ],
    )
    record = pl.BlockSpec((1,) + window, lambda n: (n, 0, 0, 0))
    operands = (pos, bias, target, ts, parts[0], *around)
    scratch = [
        pltpu.VMEM((2, plan.planes, plan.pad, LANES), f32),
        pltpu.VMEM((2, plan.planes, tiles, LANES), f32),
        pltpu.VMEM((plan.win, plan.pad, LANES), f32),
        pltpu.VMEM(window, f32),
        table,
        table,
    ]
    small = [shape(span), shape((plan.ranks, 8, LANES))]
    outs = pl.pallas_call(
        functools.partial(forward_kernel, plan),
        grid=(SECTIONS,),
        out_shape=[shape((SECTIONS,) + window)] * 4 + small,
        in_specs=[SMEM, SMEM] + [VMEM] * (len(operands) - 2),
        out_specs=[record] * 4 + [VMEM] * 2,
        scratch_shapes=scratch,
        **limits([shape(window)] * 8 + small + list(operands[2:]), scratch, 25),
    )(*operands)
    m, q, t, g2, predict, sums = outs
    sums = everywhere(sums)

    back = pl.BlockSpec((1,) + window, lambda n: (SECTIONS - 1 - n, 0, 0, 0))
    operands = (pos, sums, m, q, t, g2, predict, target, ts)
    scratch = [
        pltpu.VMEM(window, f32),
        pltpu.VMEM(window, f32),
        pltpu.VMEM((plan.win, plan.pad, LANES), f32),
        pltpu.VMEM((plan.win + 2, plan.pad, LANES), f32),
        table,
        pltpu.VMEM((plan.span * tiles, LANES), f32),
    ]
    outs = [
        shape((members, sent + plan.extra16, plan.R16, LANES), bf16),
        shape((8, LANES)),
        shape((8, LANES)),
    ]
    arrays = [shape(window)] * 8 + outs + [sums, predict, target, ts]
    grad_sent, loss, bias_part = pl.pallas_call(
        functools.partial(backward_kernel, plan),
        grid=(SECTIONS,),
        out_shape=outs,
        in_specs=[SMEM, VMEM] + [back] * 4 + [VMEM] * 3,
        out_specs=[VMEM] * 3,
        scratch_shapes=scratch,
        **limits(arrays, scratch, 20),
    )(*operands)

    moved = shape((plan.nx + 2, 3 * plan.Y, plan.nz), bf16)
    partial, g = call(
        weight_kernel,
        [shape((plan.ranks, 8, LANES)), moved],
        [SMEM, VMEM, VMEM, VMEM],
        (pos, features, bias_part, exchange(grad_sent)),
        5,
        [pltpu.VMEM((bands, inner), f32)],
    )
    grad_features = call(
        feature_kernel,
        shape(features.shape, bf16),
        [SMEM, VMEM, VMEM, ANY],
        (pos, weight.T, g, partial),
        5,
        [pltpu.VMEM((inner, bands), bf16)],
    )
    grad_weight, grad_bias = call(
        final_kernel,
        [shape((27, plan.ch)), shape((1, 1))],
        [VMEM],
        (everywhere(partial),),
        1.5,
    )
    return (loss[0, :1], grad_features, grad_weight, grad_bias.reshape(1))


def solution(mesh):
    in_specs = (P(None, "gx", "gy", "gz"), P(), P(), P("gx", "gy", "gz"))
    out_specs = (P(), P(None, "gx", "gy", "gz"), P(), P())
    return jax.shard_map(
        functools.partial(per_device, dict(mesh.shape)),
        mesh=mesh,
        in_specs=in_specs,
        out_specs=out_specs,
        check_vma=False,
    )
```

```python
import functools

import jax
import jax.numpy as jnp
from jax import lax
from jax.experimental import pallas as pl
from jax.experimental.pallas import tpu as pltpu
from jax.sharding import PartitionSpec as P

ITERS = 10
SECTIONS = ITERS + 1
LANES = 128
REACH = SECTIONS + 2
HALO = 2 * SECTIONS + 3

temper = 20.0
sharpness = 40.0

GROUP = ("gx", "gy")
ALL_AXES = ("gx", "gy", "gz")
f32 = jnp.float32
bf16 = jnp.bfloat16


def up8(value):
    return -(-value // 8) * 8


class Plan:
    def __init__(self, mesh_shape, block):
        self.ch, self.nx, self.ny, self.nz = block
        self.gx, self.gy, self.gz = (mesh_shape[a] for a in ALL_AXES)
        self.members = self.gx * self.gy
        self.ranks = self.members * self.gz
        self.X = self.nx * self.gx
        self.Y = self.ny * self.gy
        self.Z = self.nz * self.gz
        assert LANES % self.Y == 0 and self.nz == LANES
        assert self.nz % self.members == 0
        self.zc = self.nz // self.members
        self.per = LANES // self.Y
        assert self.nx % self.per == 0
        self.tiles = self.X // self.per
        self.own = self.nx // self.per
        self.shared = self.per > 1
        self.sent = self.own + (1 if self.shared else 2)
        self.R = up8(self.zc)
        self.extra = -(-2 * self.sent // self.R)
        self.R16 = -(-self.zc // 16) * 16
        self.extra16 = -(-2 * self.sent // self.R16)
        self.pad = self.tiles + 16
        self.win = self.zc + 2 * REACH
        self.span = self.zc + 2
        self.block = self.blocks_of(self.win)
        self.span_block = self.blocks_of(self.span)
        self.base = HALO + 1
        self.planes = self.zc + 2 * HALO + 2 + self.block
        self.hops = -(-HALO // self.zc)
        self.rest = HALO - (self.hops - 1) * self.zc
        self.label_hops = -(-REACH // self.zc)
        self.label_rest = REACH - (self.label_hops - 1) * self.zc

    def blocks_of(self, count):
        fits = [n for n in range(1, count + 1) if count % n == 0 and n * self.tiles <= 256]
        return fits[-1] if fits else 1

    def slot(self, x):
        if 0 <= x < self.nx:
            return x // self.per, (x % self.per) * self.Y
        if x == self.nx:
            return self.own, 0
        return self.sent - 1, LANES - self.Y


def lane_iota(shape):
    return lax.broadcasted_iota(jnp.int32, shape, len(shape) - 1)


def row_iota(shape):
    return lax.broadcasted_iota(jnp.int32, shape, len(shape) - 2)


def masks(plan):
    lane = lane_iota((plan.tiles, LANES))
    return lane, lane % plan.Y == 0, lane % plan.Y == plan.Y - 1


def x_neighbours(plan, mask, load, cur):
    lower, upper = load(-1), load(1)
    if plan.Y == LANES:
        return lower + upper
    lower = pltpu.roll(jnp.where(mask[0] >= LANES - plan.Y, lower, cur), plan.Y, 1)
    upper = pltpu.roll(jnp.where(mask[0] < plan.Y, upper, cur), LANES - plan.Y, 1)
    return lower + upper


def y_neighbours(mask, cur):
    lower = jnp.where(mask[1], 0.0, pltpu.roll(cur, 1, 1))
    upper = jnp.where(mask[2], 0.0, pltpu.roll(cur, LANES - 1, 1))
    return lower + upper


def count_tables(plan, cross_ref, box_ref):
    flat = row_iota((plan.tiles, LANES)) * LANES + lane_iota((plan.tiles, LANES))
    y, x = flat % plan.Y, flat // plan.Y

    def along(spot, size):
        return 3.0 - (spot == 0).astype(f32) - (spot == size - 1).astype(f32)

    cx, cy = along(x, plan.X), along(y, plan.Y)
    for kind, cz in ((1, 2.0), (2, 3.0)):
        if cross_ref is not None:
            cross_ref[kind] = 1.0 / (cx + cy + cz - 2.0)
        if box_ref is not None:
            box_ref[kind] = 1.0 / (cx * cy * cz)
    for ref in (cross_ref, box_ref):
        if ref is not None:
            ref[0] = jnp.zeros((plan.tiles, LANES), f32)


def kind_of(plan, rank, plane):
    z = rank * plan.zc + plane
    inside = (z >= 0) & (z < plan.Z)
    edge = (z == 0) | (z == plan.Z - 1)
    return jnp.where(inside, jnp.where(edge, 1, 2), 0), jnp.where(inside, 0.0, 1.0)


def store_all(pairs):
    for ref, at, value in pairs:
        ref[at] = value


def over(first, count, size, body):
    def at(n, carry):
        body(first + n * size)
        return carry

    lax.fori_loop(0, (count + size - 1) // size, at, 0)


def tap_condition(plan, member_y, shape, y_dim, in_dim):
    y = lax.broadcasted_iota(jnp.int32, shape, y_dim) % plan.Y
    own = lax.broadcasted_iota(jnp.int32, shape, in_dim) % plan.ny
    return own + member_y * plan.ny - y + 1


def conv_kernel(
    plan, pos_ref, w_ref, far_ref, label_ref, out_ref, wide_ref, acc_ref, f_ref, sem_ref
):
    del label_ref
    parts = 4
    width = plan.nx // parts
    copies = []
    for n in range(parts):
        span = pl.ds(n * width, width)
        copies.append(
            pltpu.make_async_copy(far_ref.at[:, span], f_ref.at[:, span], sem_ref.at[n])
        )
        copies[-1].start()
    rows, inner = plan.Y, plan.ch * plan.ny
    spread = (
        lax.broadcasted_iota(jnp.int32, (plan.ch, inner), 0)
        == lax.broadcasted_iota(jnp.int32, (plan.ch, inner), 1) // plan.ny
    ).astype(f32)
    taps = jnp.dot(w_ref[...].astype(f32), spread, preferred_element_type=f32)
    tap_y = tap_condition(plan, pos_ref[1], (rows, inner), 0, 1)
    for i in range(3):
        for k in range(3):
            band = jnp.zeros((rows, inner), f32)
            for j in range(3):
                t = 9 * i + 3 * j + k
                band = jnp.where(tap_y == j, taps[t : t + 1], band)
            at = (3 * i + k) * rows
            wide_ref[at : at + rows] = band.astype(bf16)
    acc_ref[...] = jnp.zeros_like(acc_ref)

    def at_x(x, carry):
        block = f_ref[:, x].reshape(inner, plan.nz)
        out = jnp.dot(wide_ref[...], block, preferred_element_type=f32)
        for i in range(3):
            acc_ref[x + 2 - i] += out[3 * i * rows : 3 * (i + 1) * rows]
        return carry

    for n in range(parts):
        copies[n].wait()
        lax.fori_loop(n * width, (n + 1) * width, at_x, 0)

    out_ref[...] = jnp.zeros_like(out_ref)
    places = {}
    for x in range(-1, plan.nx + 1):
        tile, lane = plan.slot(x)
        places.setdefault(tile, {})[lane] = x
    lane = lane_iota((rows, plan.nz))
    for tile in range(plan.sent):
        parts, spills = [], []
        for first in range(0, LANES, rows):
            x = places[tile].get(first)
            if x is None:
                parts.append(jnp.zeros((rows, plan.nz), f32))
                spills.append(jnp.zeros((rows, plan.nz), f32))
                continue
            low = acc_ref[x + 1, 0:rows]
            mid = acc_ref[x + 1, rows : 2 * rows]
            high = acc_ref[x + 1, 2 * rows : 3 * rows]
            total = mid + jnp.where(lane == 0, 0.0, pltpu.roll(low, 1, 1))
            total = total + jnp.where(lane == plan.nz - 1, 0.0, pltpu.roll(high, plan.nz - 1, 1))
            parts.append(total)
            spill = jnp.where(lane == 1, pltpu.roll(low, 2, 1), 0.0)
            spills.append(jnp.where(lane == 0, high, spill))
        turned = jnp.concatenate(parts, axis=0).T
        spill = jnp.concatenate(spills, axis=0).T
        for p in range(plan.members):
            out_ref[p, tile, 0 : plan.zc] = turned[p * plan.zc : (p + 1) * plan.zc]
        for end, p in ((0, 0), (1, plan.members - 1)):
            n = 2 * tile + end
            at = plan.sent + n // plan.R
            out_ref[p, at, n % plan.R : n % plan.R + 1] = spill[end : end + 1]


def label_kernel(plan, pos_ref, l_ref, out_ref):
    rows = plan.Y
    sub = lax.broadcasted_iota(jnp.int32, (plan.gy, plan.ny, plan.nz), 0)
    for tile in range(plan.own):
        parts = []
        for n in range(plan.per):
            block = l_ref[tile * plan.per + n].astype(f32)[None]
            wide = jnp.where(sub == pos_ref[1], block, 0.0)
            parts.append(wide.reshape(rows, plan.nz))
        turned = jnp.concatenate(parts, axis=0).T
        for p in range(plan.members):
            out_ref[p, tile] = turned[p * plan.zc : (p + 1) * plan.zc].astype(bf16)


def gather_kernel(plan, got_ref, out_ref, head_ref, tail_ref):
    tiles, zc, rest = plan.tiles, plan.zc, plan.rest
    lane = lane_iota((1, LANES))

    def part(p, q):
        values = [got_ref[p, q, 0:zc]]
        for end in range(2):
            n = 2 * q + end
            at = plan.sent + n // plan.R
            values.append(got_ref[p, at, n % plan.R : n % plan.R + 1])
        return values

    for a in range(plan.gx):
        for q in range(plan.own):
            parts = []
            for b in range(plan.gy):
                parts.append(part(a * plan.gy + b, q))
                if q == plan.own - 1 and a < plan.gx - 1:
                    edge = part((a + 1) * plan.gy + b, plan.sent - 1)
                    parts.append([jnp.where(lane >= LANES - plan.Y, v, 0.0) for v in edge])
                if q == 0 and a > 0:
                    edge = part((a - 1) * plan.gy + b, plan.own)
                    parts.append([jnp.where(lane < plan.Y, v, 0.0) for v in edge])
            whole, low, high = (functools.reduce(jnp.add, vs) for vs in zip(*parts))
            tile = a * plan.own + q
            out_ref[pl.ds(tile, zc, stride=tiles)] = whole
            out_ref[zc * tiles + tile : zc * tiles + tile + 1] = low
            out_ref[(zc + 1) * tiles + tile : (zc + 1) * tiles + tile + 1] = high
    head_ref[: rest * tiles] = out_ref[: rest * tiles]
    head_ref[rest * tiles :] = out_ref[zc * tiles : (zc + 1) * tiles]
    tail_ref[: rest * tiles] = out_ref[(zc - rest) * tiles : zc * tiles]
    tail_ref[rest * tiles :] = out_ref[(zc + 1) * tiles :]


def label_gather_kernel(plan, got_ref, out_ref, head_ref, tail_ref, all_ref):
    tiles, zc, rest = plan.tiles, plan.zc, plan.label_rest
    for a in range(plan.gx):
        for q in range(plan.own):
            total = got_ref[a * plan.gy, q].astype(f32)
            for b in range(1, plan.gy):
                total = total + got_ref[a * plan.gy + b, q].astype(f32)
            all_ref[pl.ds(a * plan.own + q, zc, stride=tiles)] = total
    out_ref[...] = all_ref[...].astype(bf16)
    head_ref[...] = all_ref[: rest * tiles].astype(bf16)
    tail_ref[...] = all_ref[(zc - rest) * tiles :].astype(bf16)


LOG = 1.0 / sharpness


def thin(e, box, inverse, outside):
    box = box + outside
    ratio = e * box * inverse + outside
    square = ratio * ratio
    more = 1.0 + square
    joint = 1.0 / (box * more)
    slope = joint * box
    return joint * more, slope, jnp.log(square * slope)


def lift(scaled, s):
    small = jnp.exp(scaled * (s - 1.0))
    more = 1.0 + small
    return s + jnp.log(more) * LOG, small * (1.0 / more)


def erode(plan, rank, mask, e_ref, g_ref, table_ref, now, base, first, count, size):
    tiles = slice(8, 8 + plan.tiles)

    def body(plane):
        out = []
        for n in range(size):
            at = plane + n + base
            cur = e_ref[now, at, tiles]

            def load(offset, at=at):
                return e_ref[now, at, 8 + offset : 8 + offset + plan.tiles]

            total = cur + e_ref[now, at - 1, tiles] + e_ref[now, at + 1, tiles]
            total = total + x_neighbours(plan, mask, load, cur) + y_neighbours(mask, cur)
            kind, outside = kind_of(plan, rank, plane + n)
            total = total * table_ref[kind]
            out.append((e_ref, (1 - now, at, tiles), total))
            out.append((g_ref, (1 - now, at), 1.0 / (total + outside) - outside))
        store_all(out)

    over(first, count, size, body)


def spread(plan, mask, g_ref, now, zy_ref, base, first, count, size):
    tiles = slice(8, 8 + plan.tiles)

    def body(plane):
        out = []
        values = [g_ref[now, plane + n + base] for n in range(-1, size + 1)]
        for n in range(size):
            part = values[n] + values[n + 1] + values[n + 2]
            part = part + y_neighbours(mask, part)
            out.append((zy_ref, (plane + n - first, tiles), part))
        store_all(out)

    over(first, count, size, body)


def x_box(plan, mask, zy_ref, at):
    cur = zy_ref[at, 8 : 8 + plan.tiles]

    def load(offset):
        return zy_ref[at, 8 + offset : 8 + offset + plan.tiles]

    return cur + x_neighbours(plan, mask, load, cur)


def target_kernel(plan, *refs):
    hops = plan.label_hops
    pos_ref, own_ref = refs[:2]
    below, above = refs[2 : 2 + hops], refs[2 + hops : 2 + 2 * hops]
    target_ref, ts_ref = refs[2 + 2 * hops : 4 + 2 * hops]
    e_ref, g_ref, zy_ref, cross_ref, box_ref = refs[4 + 2 * hops :]
    zc, win, span = plan.zc, plan.win, plan.span
    size = plan.span_block
    base = REACH + 1
    tiles = slice(8, 8 + plan.tiles)
    rank = pos_ref[0]
    mask = masks(plan)
    count_tables(plan, cross_ref, box_ref)
    e_ref[...] = jnp.zeros_like(e_ref)
    zy_ref[...] = jnp.zeros_like(zy_ref)
    g_ref[...] = jnp.zeros_like(g_ref)
    target_ref[REACH : REACH + zc] = own_ref[...].astype(f32)
    for h in range(1, hops + 1):
        n = zc if h < hops else plan.label_rest
        first = REACH - (h - 1) * zc - n
        target_ref[first : first + n] = below[h - 1][...].astype(f32)
        first = REACH + h * zc
        target_ref[first : first + n] = above[h - 1][...].astype(f32)

    def fill(plane):
        out = []
        for n in range(plan.block):
            at = plane + n
            z = rank * zc + at - REACH
            inside = ((z >= 0) & (z < plan.Z)).astype(f32)
            out.append((e_ref, (0, at + 1, tiles), jnp.exp(-temper * target_ref[at]) * inside))
        store_all(out)

    over(0, win, plan.block, fill)

    def section(step, carry):
        now = step % 2
        reach = 2 + ITERS - step
        erode(
            plan, rank, mask, e_ref, g_ref, cross_ref, now, base, -reach, zc + 2 * reach, size
        )
        spread(plan, mask, g_ref, 1 - now, zy_ref, base, -1, span, size)

        def point(plane, opening):
            out = []
            for n in range(size):
                at = plane + n
                box = x_box(plan, mask, zy_ref, at)
                kind, outside = kind_of(plan, rank, at - 1)
                e = e_ref[now, at - 1 + base, tiles]
                _, _, scaled = thin(e, box, box_ref[kind], outside)
                value = scaled * -LOG if opening else lift(scaled, ts_ref[at])[0]
                out.append((ts_ref, at, value))
            store_all(out)

        @pl.when(step == 0)
        def _():
            over(0, span, size, lambda plane: point(plane, True))

        @pl.when(step > 0)
        def _():
            over(0, span, size, lambda plane: point(plane, False))

        return carry

    lax.fori_loop(0, SECTIONS, section, 0)


def forward_kernel(plan, *refs):
    hops = plan.hops
    pos_ref, bias_ref, target_ref, ts_ref, own_ref = refs[:5]
    refs = refs[5:]
    below, above = refs[:hops], refs[hops : 2 * hops]
    refs = refs[2 * hops :]
    m_ref, q_ref, t_ref, g2_ref, p_ref, sums_ref = refs[:6]
    e_ref, g_ref, zy_ref, s_ref, cross_ref, box_ref = refs[6:]
    base, zc, size = plan.base, plan.zc, plan.block
    tiles = slice(8, 8 + plan.tiles)
    rank = pos_ref[0]
    step = pl.program_id(0)
    mask = masks(plan)

    @pl.when(step == 0)
    def _():
        e_ref[...] = jnp.zeros_like(e_ref)
        g_ref[...] = jnp.zeros_like(g_ref)
        zy_ref[...] = jnp.zeros_like(zy_ref)
        s_ref[...] = jnp.zeros_like(s_ref)
        count_tables(plan, cross_ref, box_ref)
        e_ref[0, base : base + zc, tiles] = own_ref[:zc]
        for h in range(1, hops + 1):
            n = zc if h < hops else plan.rest
            first = base - (h - 1) * zc - n
            e_ref[0, first : first + n, tiles] = below[h - 1][:n]
            first = base + h * zc
            e_ref[0, first : first + n, tiles] = above[h - 1][:n]
        e_ref[0, base - 1, tiles] += own_ref[zc]
        e_ref[0, base + zc, tiles] += own_ref[zc + 1]
        for h in range(1, hops + 1):
            if h < hops:
                e_ref[0, base - h * zc - 1, tiles] += below[h - 1][zc]
                e_ref[0, base + (h + 1) * zc, tiles] += above[h - 1][zc + 1]
                e_ref[0, base - (h - 1) * zc, tiles] += below[h - 1][zc + 1]
                e_ref[0, base + h * zc - 1, tiles] += above[h - 1][zc]
            else:
                e_ref[0, base - (h - 1) * zc, tiles] += below[h - 1][plan.rest]
                e_ref[0, base + h * zc - 1, tiles] += above[h - 1][plan.rest]

        def sigmoid(logits):
            small = jnp.exp(-jnp.abs(logits))
            part = 1.0 / (1.0 + small)
            return jnp.where(logits >= 0, part, small * part)

        for n in range(plan.span):
            p_ref[n] = sigmoid(e_ref[0, base - 1 + n, tiles] + bias_ref[0])

        def fill(plane):
            out = []
            for n in range(size):
                at = plane + n
                z = rank * zc + at - base
                inside = ((z >= 0) & (z < plan.Z)).astype(f32)
                predict = sigmoid(e_ref[0, at, tiles] + bias_ref[0])
                out.append((e_ref, (0, at, tiles), jnp.exp(-temper * predict) * inside))
                out.append((g_ref, (0, at), jnp.exp(temper * predict) * inside))
            store_all(out)

        over(1, zc + 2 * HALO, size, fill)

    now = step % 2
    reach = REACH + 1 + ITERS - step
    erode(plan, rank, mask, e_ref, g_ref, cross_ref, now, base, -reach, zc + 2 * reach, size)
    spread(plan, mask, g_ref, 1 - now, zy_ref, base, -REACH, plan.win, size)

    def point(at, opening):
        out = []
        for n in range(size):
            spot = at + n
            plane = spot - REACH
            box = x_box(plan, mask, zy_ref, spot)
            kind, outside = kind_of(plan, rank, plane)
            e = e_ref[now, plane + base, tiles]
            over_box, slope, scaled = thin(e, box, box_ref[kind], outside)
            if opening:
                grown, a = scaled * -LOG, slope
            else:
                s = s_ref[spot]
                grown, rate = lift(scaled, s)
                a = rate * (1.0 - s) * slope
                out.append((m_ref, (0, spot), 1.0 + rate * scaled * LOG))
            after = g_ref[1 - now, plane + base]
            out.append((s_ref, spot, grown))
            out.append((q_ref, (0, spot), a * over_box))
            out.append((t_ref, (0, spot), a * g_ref[now, plane + base]))
            out.append((g2_ref, (0, spot), after * after))
        store_all(out)

    @pl.when(step == 0)
    def _():
        over(0, plan.win, size, lambda at: point(at, True))
        m_ref[...] = jnp.ones_like(m_ref)

    @pl.when(step > 0)
    def _():
        over(0, plan.win, size, lambda at: point(at, False))

    @pl.when(step == SECTIONS - 1)
    def _():
        def add(n, totals):
            ps, ts = s_ref[REACH + n], ts_ref[1 + n]
            predict, target = p_ref[1 + n], target_ref[REACH + n]
            terms = (ps * target, ps, ts * predict, ts, predict * target, predict, target)
            return tuple(total + term for total, term in zip(totals, terms))

        start = (jnp.zeros((plan.tiles, LANES), f32),) * 7
        totals = lax.fori_loop(0, zc, add, start)
        lines = [jnp.sum(total, axis=0, keepdims=True) for total in totals]
        lines.append(jnp.zeros((1, LANES), f32))
        sums_ref[...] = jnp.broadcast_to(
            jnp.concatenate(lines, axis=0)[None], (plan.ranks, 8, LANES)
        )


def backward_kernel(plan, *refs):
    (
        pos_ref, sums_ref, m_ref, q_ref, t_ref, g2_ref, p_ref, target_ref, ts_ref,
        out_ref, loss_ref, bias_ref,
        w_ref, h_ref, zy_ref, pull_ref, cross_ref, grad_ref,
    ) = refs
    step = pl.program_id(0)
    rank = pos_ref[0]
    win, zc, size = plan.win, plan.zc, plan.block
    tiles = slice(8, 8 + plan.tiles)
    mask = masks(plan)

    lines = jnp.sum(jnp.sum(sums_ref[...], axis=0), axis=1, keepdims=True)
    s1, s2, s3, s4, s5, s6, s7 = (lines[n : n + 1] for n in range(7))
    prec = (s1 + 1.0) / (s2 + 1.0)
    sens = (s3 + 1.0) / (s4 + 1.0)

    @pl.when(step == 0)
    def _():
        zy_ref[...] = jnp.zeros_like(zy_ref)
        pull_ref[...] = jnp.zeros_like(pull_ref)
        h_ref[...] = jnp.zeros_like(h_ref)
        count_tables(plan, cross_ref, None)
        for n in range(win):
            z = rank * zc + n - REACH
            inside = ((z >= 0) & (z < plan.Z)).astype(f32)
            w_ref[n] = (target_ref[n] - prec) * inside

    def within(reach, body):
        count = (zc + 2 * reach + size - 1) // size
        first = jnp.minimum(REACH - reach, win - count * size)
        over(first, count * size, size, body)

    left = SECTIONS - 1 - step

    def push(at):
        values = []
        for n in range(-1, size + 1):
            spot = jnp.clip(at + n, 0, win - 1)
            values.append(w_ref[spot] * q_ref[0, spot])
        out = []
        for n in range(size):
            part = values[n] + values[n + 1] + values[n + 2]
            part = part + y_neighbours(mask, part)
            out.append((zy_ref, (at + n, tiles), part))
        store_all(out)

    within(left + 2, push)

    def pull(at):
        out = []
        for n in range(size):
            spot = at + n
            box = x_box(plan, mask, zy_ref, spot)
            inverse = cross_ref[kind_of(plan, rank, spot - REACH)[0]]
            value = (h_ref[spot] - g2_ref[0, spot] * box) * inverse
            out.append((pull_ref, (spot + 1, tiles), value))
        store_all(out)

    within(left + 2, pull)

    def join(at):
        out = []
        for n in range(size):
            spot = at + n
            cur = pull_ref[spot + 1, tiles]

            def load(offset, spot=spot):
                return pull_ref[spot + 1, 8 + offset : 8 + offset + plan.tiles]

            total = cur + pull_ref[spot, tiles] + pull_ref[spot + 2, tiles]
            total = total + x_neighbours(plan, mask, load, cur) + y_neighbours(mask, cur)
            w = w_ref[spot]
            out.append((h_ref, spot, w * t_ref[0, spot] + total))
            out.append((w_ref, spot, w * m_ref[0, spot]))
        store_all(out)

    within(left + 2, join)

    @pl.when(step == SECTIONS - 1)
    def _():
        both = prec + sens
        volume = s6 + s7 + 1.0
        cl_loss = 1.0 - 2.0 * prec * sens / both
        dice_loss = 1.0 - (2.0 * s5 + 1.0) / volume
        loss_ref[...] = jnp.broadcast_to(0.5 * dice_loss + 0.5 * cl_loss, (8, LANES))
        l0 = -(sens / both) * (sens / both) / (s2 + 1.0)
        l2 = -(prec / both) * (prec / both) / (s4 + 1.0)
        l4 = -1.0 / volume
        l5 = 0.5 * (2.0 * s5 + 1.0) / (volume * volume)

        def finish(n, total):
            z = rank * zc + n - 1
            inside = ((z >= 0) & (z < plan.Z)).astype(f32)
            at = n + REACH - 1
            predict = p_ref[n]
            skel = l0 * jnp.exp(-temper * predict) * h_ref[at]
            whole = skel + l2 * ts_ref[n] + l4 * target_ref[at] + l5
            grad = whole * predict * (1.0 - predict) * inside
            grad_ref[pl.ds(pl.multiple_of(n * plan.tiles, 8), plan.tiles)] = grad
            mine = ((n >= 1) & (n <= zc)).astype(f32)
            return total + grad * mine

        total = lax.fori_loop(0, plan.span, finish, jnp.zeros((plan.tiles, LANES), f32))
        bias_ref[...] = jnp.sum(total.reshape(-1, 8, LANES), axis=0)
        lane = lane_iota((1, LANES))

        def column(tile):
            return [
                grad_ref[pl.ds(plan.tiles + tile, zc, stride=plan.tiles)],
                grad_ref[tile : tile + 1],
                grad_ref[(zc + 1) * plan.tiles + tile : (zc + 1) * plan.tiles + tile + 1],
            ]

        for a in range(plan.gx):
            pieces = [column(a * plan.own + q) for q in range(plan.own)]
            zero = [jnp.zeros((zc, LANES), f32)] + [jnp.zeros((1, LANES), f32)] * 2
            after = column((a + 1) * plan.own) if a < plan.gx - 1 else zero
            before = column(a * plan.own - 1) if a > 0 else zero
            if plan.shared:
                pieces.append(
                    [
                        jnp.where(lane < plan.Y, x, 0.0)
                        + jnp.where(lane >= LANES - plan.Y, y, 0.0)
                        for x, y in zip(after, before)
                    ]
                )
            else:
                pieces += [after, before]
            edges = [edge for piece in pieces for edge in piece[1:]]
            rows = plan.R16
            edges += [jnp.zeros((1, LANES), f32)] * (plan.extra16 * rows - len(edges))
            whole = [piece[0] for piece in pieces]
            if rows > zc:
                fill = jnp.zeros((rows - zc, LANES), f32)
                whole = [jnp.concatenate([piece, fill], axis=0) for piece in whole]
            whole += [
                jnp.concatenate(edges[n * rows : (n + 1) * rows], axis=0)
                for n in range(plan.extra16)
            ]
            for q, piece in enumerate(whole):
                piece = piece.astype(bf16)
                for b in range(plan.gy):
                    out_ref[a * plan.gy + b, q] = piece


def weight_kernel(plan, pos_ref, f_ref, bias_ref, got_ref, gw_ref, g_ref, dw_ref):
    rows, inner = plan.Y, plan.ch * plan.ny
    zc, nz = plan.zc, plan.nz
    lane = lane_iota((rows, nz))
    places = {}
    for x in range(-1, plan.nx + 1):
        tile, first = plan.slot(x)
        places.setdefault(tile, {})[first] = x
    for tile in range(plan.sent):
        stack = [got_ref[p, tile].astype(f32)[:zc] for p in range(plan.members)]
        turned = jnp.concatenate(stack, axis=0).T
        ends = []
        for end, p in ((0, 0), (1, plan.members - 1)):
            n = 2 * tile + end
            row = got_ref[p, plan.sent + n // plan.R16].astype(f32)
            ends.append(row[n % plan.R16 : n % plan.R16 + 1])
        ends = jnp.concatenate(ends + [jnp.zeros((LANES - 2, LANES), f32)], axis=0).T
        for first, x in places[tile].items():
            g = turned[first : first + rows]
            end = ends[first : first + rows]
            down = jnp.where(lane == nz - 1, pltpu.roll(end, nz - 2, 1), pltpu.roll(g, nz - 1, 1))
            up = jnp.where(lane == 0, end, pltpu.roll(g, 1, 1))
            g_ref[x + 1] = jnp.concatenate([down, g, up], axis=0).astype(bf16)

    dw_ref[...] = jnp.zeros_like(dw_ref)

    def at_x(x, carry):
        block = f_ref[:, x].reshape(inner, nz)
        moved = jnp.concatenate([g_ref[x + 2], g_ref[x + 1], g_ref[x]], axis=0)
        dw_ref[...] += lax.dot_general(
            moved, block, (((1,), (1,)), ((), ())), preferred_element_type=f32
        )
        return carry

    lax.fori_loop(0, plan.nx, at_x, 0)

    tap_y = tap_condition(plan, pos_ref[1], (rows, inner), 0, 1)
    taps = []
    for t in range(27):
        i, j, k = t // 9, t // 3 % 3, t % 3
        at = (3 * i + k) * rows
        taps.append(jnp.sum(jnp.where(tap_y == j, dw_ref[at : at + rows], 0.0), axis=0, keepdims=True))
    taps += [jnp.zeros((1, inner), f32)] * 5
    total = jnp.zeros((8, LANES), f32)
    for n in range(4):
        place = (
            lax.broadcasted_iota(jnp.int32, (inner, LANES), 0) // plan.ny + 32 * n
            == lax.broadcasted_iota(jnp.int32, (inner, LANES), 1)
        ).astype(f32)
        total = total + jnp.dot(
            jnp.concatenate(taps[8 * n : 8 * n + 8], axis=0),
            place,
            precision=lax.Precision.HIGHEST,
            preferred_element_type=f32,
        )
    spot = (row_iota((8, LANES)) == 3) & (lane_iota((8, LANES)) == 96)
    total = jnp.where(spot, jnp.sum(bias_ref[...]), total)
    gw_ref[...] = jnp.broadcast_to(total[None], (plan.ranks, 8, LANES))


def feature_kernel(plan, pos_ref, wt_ref, g_ref, after_ref, gf_ref, wide_ref):
    del after_ref
    rows, inner, bands = plan.Y, plan.ch * plan.ny, 9 * plan.Y
    spread = (
        lax.broadcasted_iota(jnp.int32, (inner, plan.ch), 0) // plan.ny
        == lax.broadcasted_iota(jnp.int32, (inner, plan.ch), 1)
    ).astype(f32)
    tap_y = tap_condition(plan, pos_ref[1], (inner, bands), 1, 0)
    wide = jnp.zeros((inner, bands), f32)
    tap = lax.broadcasted_iota(jnp.int32, (27, bands), 0)
    band = lax.broadcasted_iota(jnp.int32, (27, bands), 1) // rows
    for j in range(3):
        pick = (tap == 9 * (band // 3) + 3 * j + band % 3).astype(f32)
        chosen = jnp.dot(wt_ref[...].astype(f32), pick, preferred_element_type=f32)
        full = jnp.dot(spread, chosen, preferred_element_type=f32)
        wide = jnp.where(tap_y == j, full, wide)
    wide_ref[...] = wide.astype(bf16)

    def at_x(x, carry):
        moved = jnp.concatenate([g_ref[x + 2], g_ref[x + 1], g_ref[x]], axis=0)
        out = jnp.dot(wide_ref[...], moved, preferred_element_type=f32)
        gf_ref[:, x] = out.astype(bf16).reshape(plan.ch, plan.ny, plan.nz)
        return carry

    lax.fori_loop(0, plan.nx, at_x, 0)


def final_kernel(plan, got_ref, gw_ref, gb_ref):
    total = jnp.sum(got_ref[...], axis=0)
    for n in range(4):
        count = min(8, 27 - 8 * n)
        gw_ref[8 * n : 8 * n + count] = total[:count, 32 * n : 32 * n + plan.ch]
    gb_ref[...] = total[3:4, 96:97]


VMEM = pl.BlockSpec(memory_space=pltpu.VMEM)
SMEM = pl.BlockSpec(memory_space=pltpu.SMEM)
ANY = pl.BlockSpec(memory_space=pl.ANY)
FAR = pl.BlockSpec(memory_space=pltpu.HBM)
MIB = 1024 * 1024


def shape(dims, dtype=f32):
    return jax.ShapeDtypeStruct(dims, dtype)


def held(dims, dtype):
    if len(dims) < 2:
        return 4096
    size = jnp.dtype(dtype).itemsize
    rows = 8 * 4 // size
    total = -(-dims[-2] // rows) * rows * -(-dims[-1] // LANES) * LANES * size
    for n in dims[:-2]:
        total *= n
    return total


def limits(arrays, scratch, micros, least=0):
    total = sum(held(a.shape, a.dtype) for a in arrays)
    total += sum(held(a.shape, a.dtype) for a in scratch if len(a.shape) > 1)
    limit = max(least, min(63 * MIB, total + total // 8 + 4 * MIB))
    return dict(
        compiler_params=pltpu.CompilerParams(vmem_limit_bytes=limit),
        cost_estimate=pl.CostEstimate(
            flops=0, transcendentals=0, bytes_accessed=int(micros * 2.5e6)
        ),
    )


def per_device(mesh_shape, features, weight, bias, label):
    plan = Plan(mesh_shape, features.shape)
    members, sent, own, tiles = plan.members, plan.sent, plan.own, plan.tiles
    inner, bands = plan.ch * plan.ny, 9 * plan.Y
    place = (lax.axis_index("gz") * members + lax.axis_index(GROUP)).astype(jnp.int32)
    pos = jnp.stack([place, lax.axis_index("gy").astype(jnp.int32)])

    def call(kernel, out_shape, in_specs, operands, micros, scratch=(), least=0):
        outs = jax.tree.leaves(out_shape)
        ins = [a for spec, a in zip(in_specs, operands) if spec is VMEM]
        return pl.pallas_call(
            functools.partial(kernel, plan),
            out_shape=out_shape,
            in_specs=in_specs,
            out_specs=jax.tree.map(lambda s: VMEM, out_shape),
            scratch_shapes=list(scratch),
            **limits(ins + outs, scratch, micros, least),
        )(*operands)

    def exchange(array):
        return lax.all_to_all(array, GROUP, 0, 0, tiled=True)

    def everywhere(array):
        return lax.all_to_all(array, ALL_AXES, 0, 0, tiled=True)

    def hop(array, distance):
        def device(r):
            return (r % members) * plan.gz + r // members

        pairs = [
            (device(r), device(r + distance))
            for r in range(plan.ranks)
            if 0 <= r + distance < plan.ranks
        ]
        return lax.ppermute(array, ALL_AXES, pairs)

    label_sent = call(
        label_kernel, shape((members, own, plan.zc, LANES), bf16), [SMEM, VMEM], (pos, label), 1.5
    )
    sent_logits = call(
        conv_kernel,
        shape((members, sent + plan.extra, plan.R, LANES)),
        [SMEM, VMEM, FAR, ANY],
        (pos, weight, features, label_sent),
        7,
        [
            pltpu.VMEM((bands, inner), bf16),
            pltpu.VMEM((plan.nx + 2, 3 * plan.Y, plan.nz), f32),
            pltpu.VMEM(features.shape, bf16),
            pltpu.SemaphoreType.DMA((4,)),
        ],
        62 * MIB,
    )

    def planes(array):
        return array.reshape(-1, tiles, LANES)

    def hops_of(parts, count):
        whole, head, tail = parts
        below = [hop(whole if h < count else tail, h) for h in range(1, count + 1)]
        above = [hop(whole if h < count else head, -h) for h in range(1, count + 1)]
        return below + above

    zc = plan.zc
    short = plan.label_rest * tiles
    label_parts = call(
        label_gather_kernel,
        [shape((zc * tiles, LANES), bf16)] + [shape((short, LANES), bf16)] * 2,
        [VMEM],
        (exchange(label_sent),),
        1.5,
        [pltpu.VMEM((zc * tiles, LANES), f32)],
    )
    label_parts = [planes(part) for part in label_parts]
    short = (plan.rest + 1) * tiles
    parts = call(
        gather_kernel,
        [shape(((zc + 2) * tiles, LANES))] + [shape((short, LANES))] * 2,
        [VMEM],
        (exchange(sent_logits),),
        1.5,
    )
    parts = [planes(part) for part in parts]
    around = hops_of(parts, plan.hops)
    label_around = hops_of(label_parts, plan.label_hops)

    window = (plan.win, tiles, LANES)
    span = (plan.span, tiles, LANES)
    table = pltpu.VMEM((3, tiles, LANES), f32)
    room = plan.win + 2 + plan.span_block
    target, ts = call(
        target_kernel,
        [shape(window), shape(span)],
        [SMEM] + [VMEM] * (1 + 2 * plan.label_hops),
        (pos, label_parts[0], *label_around),
        14,
        [
            pltpu.VMEM((2, room, plan.pad, LANES), f32),
            pltpu.VMEM((2, room, tiles, LANES), f32),
            pltpu.VMEM((plan.span, plan.pad, LANES), f32),
            table,
            table,
        ],
    )
    record = pl.BlockSpec((1,) + window, lambda n: (n, 0, 0, 0))
    operands = (pos, bias, target, ts, parts[0], *around)
    scratch = [
        pltpu.VMEM((2, plan.planes, plan.pad, LANES), f32),
        pltpu.VMEM((2, plan.planes, tiles, LANES), f32),
        pltpu.VMEM((plan.win, plan.pad, LANES), f32),
        pltpu.VMEM(window, f32),
        table,
        table,
    ]
    small = [shape(span), shape((plan.ranks, 8, LANES))]
    outs = pl.pallas_call(
        functools.partial(forward_kernel, plan),
        grid=(SECTIONS,),
        out_shape=[shape((SECTIONS,) + window)] * 4 + small,
        in_specs=[SMEM, SMEM] + [VMEM] * (len(operands) - 2),
        out_specs=[record] * 4 + [VMEM] * 2,
        scratch_shapes=scratch,
        **limits([shape(window)] * 8 + small + list(operands[2:]), scratch, 25),
    )(*operands)
    m, q, t, g2, predict, sums = outs
    sums = everywhere(sums)

    back = pl.BlockSpec((1,) + window, lambda n: (SECTIONS - 1 - n, 0, 0, 0))
    operands = (pos, sums, m, q, t, g2, predict, target, ts)
    scratch = [
        pltpu.VMEM(window, f32),
        pltpu.VMEM(window, f32),
        pltpu.VMEM((plan.win, plan.pad, LANES), f32),
        pltpu.VMEM((plan.win + 2, plan.pad, LANES), f32),
        table,
        pltpu.VMEM((plan.span * tiles, LANES), f32),
    ]
    outs = [
        shape((members, sent + plan.extra16, plan.R16, LANES), bf16),
        shape((8, LANES)),
        shape((8, LANES)),
    ]
    arrays = [shape(window)] * 8 + outs + [sums, predict, target, ts]
    grad_sent, loss, bias_part = pl.pallas_call(
        functools.partial(backward_kernel, plan),
        grid=(SECTIONS,),
        out_shape=outs,
        in_specs=[SMEM, VMEM] + [back] * 4 + [VMEM] * 3,
        out_specs=[VMEM] * 3,
        scratch_shapes=scratch,
        **limits(arrays, scratch, 20),
    )(*operands)

    moved = shape((plan.nx + 2, 3 * plan.Y, plan.nz), bf16)
    partial, g = call(
        weight_kernel,
        [shape((plan.ranks, 8, LANES)), moved],
        [SMEM, VMEM, VMEM, VMEM],
        (pos, features, bias_part, exchange(grad_sent)),
        5,
        [pltpu.VMEM((bands, inner), f32)],
    )
    grad_features = call(
        feature_kernel,
        shape(features.shape, bf16),
        [SMEM, VMEM, VMEM, ANY],
        (pos, weight.T, g, partial),
        5,
        [pltpu.VMEM((inner, bands), bf16)],
    )
    grad_weight, grad_bias = call(
        final_kernel,
        [shape((27, plan.ch)), shape((1, 1))],
        [VMEM],
        (everywhere(partial),),
        1.5,
    )
    return (loss[0, :1], grad_features, grad_weight, grad_bias.reshape(1))


def solution(mesh):
    in_specs = (P(None, "gx", "gy", "gz"), P(), P(), P("gx", "gy", "gz"))
    out_specs = (P(), P(None, "gx", "gy", "gz"), P(), P())

    def body(*args):
        return per_device(dict(mesh.shape), *args)

    return jax.shard_map(
        body, mesh=mesh, in_specs=in_specs, out_specs=out_specs, check_vma=False
    )
```

```python
import functools

import jax
import jax.numpy as jnp
from jax import lax
from jax.experimental import pallas as pl
from jax.experimental.pallas import tpu as pltpu
from jax.sharding import PartitionSpec as P

ITERS = 10
SECTIONS = ITERS + 1
LANES = 128
HALO = SECTIONS + 1
BACK = SECTIONS + 1
REACH = SECTIONS + 2

temper = 20.0
sharpness = 40.0

GROUP = ("gx", "gy")
ALL_AXES = ("gx", "gy", "gz")
f32 = jnp.float32
bf16 = jnp.bfloat16


def up8(value):
    return -(-value // 8) * 8


class Plan:
    def __init__(self, mesh_shape, block):
        self.ch, self.nx, self.ny, self.nz = block
        self.gx, self.gy, self.gz = (mesh_shape[a] for a in ALL_AXES)
        self.members = self.gx * self.gy
        self.ranks = self.members * self.gz
        self.X = self.nx * self.gx
        self.Y = self.ny * self.gy
        self.Z = self.nz * self.gz
        assert LANES % self.Y == 0 and self.nz == LANES
        assert self.nz % self.members == 0
        self.zc = self.nz // self.members
        self.per = LANES // self.Y
        assert self.nx % self.per == 0
        self.tiles = self.X // self.per
        self.own = self.nx // self.per
        self.shared = self.per > 1
        self.sent = self.own + (1 if self.shared else 2)
        self.R = up8(self.zc)
        self.extra = -(-2 * self.sent // self.R)
        self.R16 = -(-self.zc // 16) * 16
        self.extra16 = -(-2 * self.sent // self.R16)
        self.pad = self.tiles + 16
        self.win = self.zc + 2 * REACH
        self.span = self.zc + 2
        self.block = self.blocks_of(self.zc, 16)
        self.span_block = self.blocks_of(self.span, 32)
        self.win_block = self.blocks_of(self.win, 32)
        self.erode_block = max(1, 160 // self.tiles)
        self.base = HALO + 1
        self.planes = self.zc + 2 * HALO + 2 + self.erode_block
        self.pull_base = BACK + 2
        self.pull_planes = self.zc + 2 * BACK + 4 + self.erode_block
        self.hops = -(-HALO // self.zc)
        self.rest = HALO - (self.hops - 1) * self.zc
        self.label_hops = -(-REACH // self.zc)
        self.label_rest = REACH - (self.label_hops - 1) * self.zc
        self.back_hops = -(-(BACK + 1) // self.zc)

    def back_count(self, h):
        return min(self.zc + BACK + 1 - h * self.zc, self.span)

    def blocks_of(self, count, most):
        fits = [n for n in range(1, count + 1) if count % n == 0 and n * self.tiles <= 8 * most]
        return fits[-1] if fits else 1

    def slot(self, x):
        if 0 <= x < self.nx:
            return x // self.per, (x % self.per) * self.Y
        if x == self.nx:
            return self.own, 0
        return self.sent - 1, LANES - self.Y


def lane_iota(shape):
    return lax.broadcasted_iota(jnp.int32, shape, len(shape) - 1)


def row_iota(shape):
    return lax.broadcasted_iota(jnp.int32, shape, len(shape) - 2)


def masks(plan):
    lane = lane_iota((plan.tiles, LANES))
    return lane, lane % plan.Y == 0, lane % plan.Y == plan.Y - 1


def x_neighbours(plan, mask, load, cur):
    lower, upper = load(-1), load(1)
    if plan.Y == LANES:
        return lower + upper
    lower = pltpu.roll(jnp.where(mask[0] >= LANES - plan.Y, lower, cur), plan.Y, 1)
    upper = pltpu.roll(jnp.where(mask[0] < plan.Y, upper, cur), LANES - plan.Y, 1)
    return lower + upper


def y_neighbours(mask, cur):
    lower = jnp.where(mask[1], 0.0, pltpu.roll(cur, 1, 1))
    upper = jnp.where(mask[2], 0.0, pltpu.roll(cur, LANES - 1, 1))
    return lower + upper


def count_tables(plan, cross_ref, box_ref):
    flat = row_iota((plan.tiles, LANES)) * LANES + lane_iota((plan.tiles, LANES))
    y, x = flat % plan.Y, flat // plan.Y

    def along(spot, size):
        return 3.0 - (spot == 0).astype(f32) - (spot == size - 1).astype(f32)

    cx, cy = along(x, plan.X), along(y, plan.Y)
    for kind, cz in ((1, 2.0), (2, 3.0)):
        if cross_ref is not None:
            cross_ref[kind] = 1.0 / (cx + cy + cz - 2.0)
        if box_ref is not None:
            box_ref[kind] = 1.0 / (cx * cy * cz)
    for ref in (cross_ref, box_ref):
        if ref is not None:
            ref[0] = jnp.zeros((plan.tiles, LANES), f32)


def kind_of(plan, rank, plane):
    z = rank * plan.zc + plane
    inside = (z >= 0) & (z < plan.Z)
    edge = (z == 0) | (z == plan.Z - 1)
    return jnp.where(inside, jnp.where(edge, 1, 2), 0), jnp.where(inside, 0.0, 1.0)


def store_all(pairs):
    for ref, at, value in pairs:
        ref[at] = value


def over(first, count, size, body):
    def at(n, carry):
        body(first + n * size)
        return carry

    lax.fori_loop(0, (count + size - 1) // size, at, 0)


def tap_condition(plan, member_y, shape, y_dim, in_dim):
    y = lax.broadcasted_iota(jnp.int32, shape, y_dim) % plan.Y
    own = lax.broadcasted_iota(jnp.int32, shape, in_dim) % plan.ny
    return own + member_y * plan.ny - y + 1


def conv_kernel(
    plan, pos_ref, w_ref, far_ref, label_ref, out_ref, wide_ref, acc_ref, f_ref, sem_ref
):
    del label_ref
    parts = 4
    width = plan.nx // parts
    copies = []
    for n in range(parts):
        span = pl.ds(n * width, width)
        copies.append(
            pltpu.make_async_copy(far_ref.at[:, span], f_ref.at[:, span], sem_ref.at[n])
        )
        copies[-1].start()
    rows, inner = plan.Y, plan.ch * plan.ny
    spread = (
        lax.broadcasted_iota(jnp.int32, (plan.ch, inner), 0)
        == lax.broadcasted_iota(jnp.int32, (plan.ch, inner), 1) // plan.ny
    ).astype(f32)
    taps = jnp.dot(w_ref[...].astype(f32), spread, preferred_element_type=f32)
    tap_y = tap_condition(plan, pos_ref[1], (rows, inner), 0, 1)
    for i in range(3):
        for k in range(3):
            band = jnp.zeros((rows, inner), f32)
            for j in range(3):
                t = 9 * i + 3 * j + k
                band = jnp.where(tap_y == j, taps[t : t + 1], band)
            at = (3 * i + k) * rows
            wide_ref[at : at + rows] = band.astype(bf16)
    acc_ref[...] = jnp.zeros_like(acc_ref)

    def at_x(x, carry):
        block = f_ref[:, x].reshape(inner, plan.nz)
        out = jnp.dot(wide_ref[...], block, preferred_element_type=f32)
        for i in range(3):
            acc_ref[x + 2 - i] += out[3 * i * rows : 3 * (i + 1) * rows]
        return carry

    for n in range(parts):
        copies[n].wait()
        lax.fori_loop(n * width, (n + 1) * width, at_x, 0)

    out_ref[...] = jnp.zeros_like(out_ref)
    places = {}
    for x in range(-1, plan.nx + 1):
        tile, lane = plan.slot(x)
        places.setdefault(tile, {})[lane] = x
    lane = lane_iota((rows, plan.nz))
    for tile in range(plan.sent):
        parts, spills = [], []
        for first in range(0, LANES, rows):
            x = places[tile].get(first)
            if x is None:
                parts.append(jnp.zeros((rows, plan.nz), f32))
                spills.append(jnp.zeros((rows, plan.nz), f32))
                continue
            low = acc_ref[x + 1, 0:rows]
            mid = acc_ref[x + 1, rows : 2 * rows]
            high = acc_ref[x + 1, 2 * rows : 3 * rows]
            total = mid + jnp.where(lane == 0, 0.0, pltpu.roll(low, 1, 1))
            total = total + jnp.where(lane == plan.nz - 1, 0.0, pltpu.roll(high, plan.nz - 1, 1))
            parts.append(total)
            spill = jnp.where(lane == 1, pltpu.roll(low, 2, 1), 0.0)
            spills.append(jnp.where(lane == 0, high, spill))
        turned = jnp.concatenate(parts, axis=0).T
        spill = jnp.concatenate(spills, axis=0).T
        for p in range(plan.members):
            out_ref[p, tile, 0 : plan.zc] = turned[p * plan.zc : (p + 1) * plan.zc]
        for end, p in ((0, 0), (1, plan.members - 1)):
            n = 2 * tile + end
            at = plan.sent + n // plan.R
            out_ref[p, at, n % plan.R : n % plan.R + 1] = spill[end : end + 1]


def label_kernel(plan, pos_ref, l_ref, out_ref):
    rows = plan.Y
    sub = lax.broadcasted_iota(jnp.int32, (plan.gy, plan.ny, plan.nz), 0)
    for tile in range(plan.own):
        parts = []
        for n in range(plan.per):
            block = l_ref[tile * plan.per + n].astype(f32)[None]
            wide = jnp.where(sub == pos_ref[1], block, 0.0)
            parts.append(wide.reshape(rows, plan.nz))
        turned = jnp.concatenate(parts, axis=0).T
        for p in range(plan.members):
            out_ref[p, tile] = turned[p * plan.zc : (p + 1) * plan.zc].astype(bf16)


def gather_kernel(plan, got_ref, out_ref, head_ref, tail_ref):
    tiles, zc, rest = plan.tiles, plan.zc, plan.rest
    lane = lane_iota((1, LANES))

    def part(p, q):
        values = [got_ref[p, q, 0:zc]]
        for end in range(2):
            n = 2 * q + end
            at = plan.sent + n // plan.R
            values.append(got_ref[p, at, n % plan.R : n % plan.R + 1])
        return values

    for a in range(plan.gx):
        for q in range(plan.own):
            parts = []
            for b in range(plan.gy):
                parts.append(part(a * plan.gy + b, q))
                if q == plan.own - 1 and a < plan.gx - 1:
                    edge = part((a + 1) * plan.gy + b, plan.sent - 1)
                    parts.append([jnp.where(lane >= LANES - plan.Y, v, 0.0) for v in edge])
                if q == 0 and a > 0:
                    edge = part((a - 1) * plan.gy + b, plan.own)
                    parts.append([jnp.where(lane < plan.Y, v, 0.0) for v in edge])
            whole, low, high = (functools.reduce(jnp.add, vs) for vs in zip(*parts))
            tile = a * plan.own + q
            out_ref[pl.ds(tile, zc, stride=tiles)] = whole
            out_ref[zc * tiles + tile : zc * tiles + tile + 1] = low
            out_ref[(zc + 1) * tiles + tile : (zc + 1) * tiles + tile + 1] = high
    head_ref[: rest * tiles] = out_ref[: rest * tiles]
    head_ref[rest * tiles :] = out_ref[zc * tiles : (zc + 1) * tiles]
    tail_ref[: rest * tiles] = out_ref[(zc - rest) * tiles : zc * tiles]
    tail_ref[rest * tiles :] = out_ref[(zc + 1) * tiles :]


def label_gather_kernel(plan, got_ref, out_ref, head_ref, tail_ref, all_ref):
    tiles, zc, rest = plan.tiles, plan.zc, plan.label_rest
    for a in range(plan.gx):
        for q in range(plan.own):
            total = got_ref[a * plan.gy, q].astype(f32)
            for b in range(1, plan.gy):
                total = total + got_ref[a * plan.gy + b, q].astype(f32)
            all_ref[pl.ds(a * plan.own + q, zc, stride=tiles)] = total
    out_ref[...] = all_ref[...].astype(bf16)
    head_ref[...] = all_ref[: rest * tiles].astype(bf16)
    tail_ref[...] = all_ref[(zc - rest) * tiles :].astype(bf16)


LOG = 1.0 / sharpness


def thin(e, box, inverse, outside):
    box = box + outside
    ratio = e * box * inverse + outside
    square = ratio * ratio
    more = 1.0 + square
    joint = 1.0 / (box * more)
    slope = joint * box
    return joint * more, slope, jnp.log(square * slope)


def lift(scaled, s):
    small = jnp.exp(scaled * (s - 1.0))
    more = 1.0 + small
    return s + jnp.log(more) * LOG, small * (1.0 / more)


def erode(plan, rank, mask, e_ref, g_ref, table_ref, now, base, first, count, size):
    tiles = slice(8, 8 + plan.tiles)

    def body(plane):
        out = []
        for n in range(size):
            at = plane + n + base
            cur = e_ref[now, at, tiles]

            def load(offset, at=at):
                return e_ref[now, at, 8 + offset : 8 + offset + plan.tiles]

            total = cur + e_ref[now, at - 1, tiles] + e_ref[now, at + 1, tiles]
            total = total + x_neighbours(plan, mask, load, cur) + y_neighbours(mask, cur)
            kind, outside = kind_of(plan, rank, plane + n)
            total = total * table_ref[kind]
            out.append((e_ref, (1 - now, at, tiles), total))
            out.append((g_ref, (1 - now, at), 1.0 / (total + outside) - outside))
        store_all(out)

    over(first, count, size, body)


def spread(plan, mask, g_ref, now, zy_ref, base, first, count, size):
    tiles = slice(8, 8 + plan.tiles)

    def body(plane):
        out = []
        values = [g_ref[now, plane + n + base] for n in range(-1, size + 1)]
        for n in range(size):
            part = values[n] + values[n + 1] + values[n + 2]
            part = part + y_neighbours(mask, part)
            out.append((zy_ref, (plane + n - first, tiles), part))
        store_all(out)

    over(first, count, size, body)


def x_box(plan, mask, zy_ref, at):
    cur = zy_ref[at, 8 : 8 + plan.tiles]

    def load(offset):
        return zy_ref[at, 8 + offset : 8 + offset + plan.tiles]

    return cur + x_neighbours(plan, mask, load, cur)


def target_kernel(plan, *refs):
    hops = plan.label_hops
    pos_ref, p_ref, own_ref = refs[:3]
    below, above = refs[3 : 3 + hops], refs[3 + hops : 3 + 2 * hops]
    target_ref, ts_ref, sums_ref = refs[3 + 2 * hops : 6 + 2 * hops]
    all_ref, e_ref, g_ref, zy_ref, cross_ref, box_ref = refs[6 + 2 * hops :]
    zc, win, span = plan.zc, plan.win, plan.span
    size = plan.span_block
    base = REACH + 1
    tiles = slice(8, 8 + plan.tiles)
    rank = pos_ref[0]
    mask = masks(plan)
    count_tables(plan, cross_ref, box_ref)
    e_ref[...] = jnp.zeros_like(e_ref)
    zy_ref[...] = jnp.zeros_like(zy_ref)
    g_ref[...] = jnp.zeros_like(g_ref)
    all_ref[REACH : REACH + zc] = own_ref[...].astype(f32)
    for h in range(1, hops + 1):
        n = zc if h < hops else plan.label_rest
        first = REACH - (h - 1) * zc - n
        all_ref[first : first + n] = below[h - 1][...].astype(f32)
        first = REACH + h * zc
        all_ref[first : first + n] = above[h - 1][...].astype(f32)
    target_ref[...] = all_ref[REACH - 1 : REACH + zc + 1]

    def fill(plane):
        out = []
        for n in range(plan.win_block):
            at = plane + n
            inside = 1.0 - kind_of(plan, rank, at - REACH)[1]
            out.append((e_ref, (0, at + 1, tiles), jnp.exp(-temper * all_ref[at]) * inside))
        store_all(out)

    over(0, win, plan.win_block, fill)

    def section(step, carry):
        now = step % 2
        reach = 2 + ITERS - step
        count = zc + 2 * reach
        erode(
            plan, rank, mask, e_ref, g_ref, cross_ref, now, base, -reach, count, plan.erode_block
        )
        spread(plan, mask, g_ref, 1 - now, zy_ref, base, -1, span, size)

        def point(plane, opening):
            out = []
            for n in range(size):
                at = plane + n
                box = x_box(plan, mask, zy_ref, at)
                kind, outside = kind_of(plan, rank, at - 1)
                e = e_ref[now, at - 1 + base, tiles]
                _, _, scaled = thin(e, box, box_ref[kind], outside)
                value = scaled * -LOG if opening else lift(scaled, ts_ref[at])[0]
                out.append((ts_ref, at, value))
            store_all(out)

        @pl.when(step == 0)
        def _():
            over(0, span, size, lambda plane: point(plane, True))

        @pl.when(step > 0)
        def _():
            over(0, span, size, lambda plane: point(plane, False))

        return carry

    lax.fori_loop(0, SECTIONS, section, 0)

    def add(n, totals):
        ts = ts_ref[1 + n]
        return totals[0] + ts * p_ref[1 + n], totals[1] + ts

    zero = jnp.zeros((plan.tiles, LANES), f32)
    put_sums(plan, sums_ref, lax.fori_loop(0, zc, add, (zero,) * 2))


def put_sums(plan, ref, totals):
    lines = [jnp.sum(total, axis=0, keepdims=True) for total in totals]
    lines += [jnp.zeros((1, LANES), f32)] * (8 - len(lines))
    ref[...] = jnp.broadcast_to(jnp.concatenate(lines, axis=0)[None], (plan.ranks, 8, LANES))


def get_sums(ref, count):
    lines = jnp.sum(jnp.sum(ref[...], axis=0), axis=1, keepdims=True)
    return [lines[n : n + 1] for n in range(count)]


def forward_kernel(plan, *refs):
    hops = plan.hops
    pos_ref, bias_ref, label_ref, own_ref = refs[:4]
    refs = refs[4:]
    below, above = refs[:hops], refs[hops : 2 * hops]
    refs = refs[2 * hops :]
    m_ref, q_ref, t_ref, grown_ref, p_ref, sums_ref = refs[:6]
    e_ref, g_ref, zy_ref, s_ref, cross_ref, box_ref = refs[6:]
    base, zc, size = plan.base, plan.zc, plan.block
    tiles = slice(8, 8 + plan.tiles)
    rank = pos_ref[0]
    step = pl.program_id(0)
    mask = masks(plan)

    @pl.when(step == 0)
    def _():
        e_ref[...] = jnp.zeros_like(e_ref)
        g_ref[...] = jnp.zeros_like(g_ref)
        zy_ref[...] = jnp.zeros_like(zy_ref)
        count_tables(plan, cross_ref, box_ref)
        e_ref[0, base : base + zc, tiles] = own_ref[:zc]
        for h in range(1, hops + 1):
            n = zc if h < hops else plan.rest
            first = base - (h - 1) * zc - n
            e_ref[0, first : first + n, tiles] = below[h - 1][:n]
            first = base + h * zc
            e_ref[0, first : first + n, tiles] = above[h - 1][:n]
        e_ref[0, base - 1, tiles] += own_ref[zc]
        e_ref[0, base + zc, tiles] += own_ref[zc + 1]
        for h in range(1, hops + 1):
            if h < hops:
                e_ref[0, base - h * zc - 1, tiles] += below[h - 1][zc]
                e_ref[0, base + (h + 1) * zc, tiles] += above[h - 1][zc + 1]
                e_ref[0, base - (h - 1) * zc, tiles] += below[h - 1][zc + 1]
                e_ref[0, base + h * zc - 1, tiles] += above[h - 1][zc]
            else:
                e_ref[0, base - (h - 1) * zc, tiles] += below[h - 1][plan.rest]
                e_ref[0, base + h * zc - 1, tiles] += above[h - 1][plan.rest]

        def sigmoid(logits):
            small = jnp.exp(-jnp.abs(logits))
            part = 1.0 / (1.0 + small)
            return jnp.where(logits >= 0, part, small * part)

        for n in range(plan.span):
            p_ref[n] = sigmoid(e_ref[0, base - 1 + n, tiles] + bias_ref[0])

        def fill(plane):
            out = []
            for n in range(plan.erode_block):
                at = plane + n
                inside = 1.0 - kind_of(plan, rank, at - base)[1]
                predict = sigmoid(e_ref[0, at, tiles] + bias_ref[0])
                out.append((e_ref, (0, at, tiles), jnp.exp(-temper * predict) * inside))
                out.append((g_ref, (0, at), jnp.exp(temper * predict) * inside))
            store_all(out)

        over(1, zc + 2 * HALO, plan.erode_block, fill)

    now = step % 2
    reach = 1 + ITERS - step
    count = zc + 2 * reach
    erode(plan, rank, mask, e_ref, g_ref, cross_ref, now, base, -reach, count, plan.erode_block)
    spread(plan, mask, g_ref, 1 - now, zy_ref, base, 0, zc, size)
    grown_ref[0] = g_ref[1 - now, base - 1 : base + zc + 1]

    def point(plane, opening):
        out = []
        for n in range(size):
            at = plane + n
            box = x_box(plan, mask, zy_ref, at)
            kind, outside = kind_of(plan, rank, at)
            e = e_ref[now, at + base, tiles]
            over_box, slope, scaled = thin(e, box, box_ref[kind], outside)
            if opening:
                grown, a = scaled * -LOG, slope
            else:
                s = s_ref[at]
                grown, rate = lift(scaled, s)
                a = rate * (1.0 - s) * slope
                out.append((m_ref, (0, at), 1.0 + rate * scaled * LOG))
            out.append((s_ref, at, grown))
            out.append((q_ref, (0, at), a * over_box))
            out.append((t_ref, (0, at), a * g_ref[now, at + base]))
        store_all(out)

    @pl.when(step == 0)
    def _():
        over(0, zc, size, lambda at: point(at, True))
        m_ref[...] = jnp.ones_like(m_ref)

    @pl.when(step > 0)
    def _():
        over(0, zc, size, lambda at: point(at, False))

    @pl.when(step == SECTIONS - 1)
    def _():
        def add(n, totals):
            ps, predict, target = s_ref[n], p_ref[1 + n], label_ref[n].astype(f32)
            terms = (ps * target, ps, predict * target, predict, target)
            return tuple(total + term for total, term in zip(totals, terms))

        zero = jnp.zeros((plan.tiles, LANES), f32)
        put_sums(plan, sums_ref, lax.fori_loop(0, zc, add, (zero,) * 5))


def backward_kernel(plan, *refs):
    hops = plan.back_hops
    pos_ref, sums_ref, label_ref, m_ref, q_ref, t_ref, grown_ref = refs[:7]
    mine_ref = refs[7]
    up, down = refs[8 : 8 + hops], refs[8 + hops : 8 + 2 * hops]
    w_ref, push_ref, wt_ref, zy_ref, pull_ref, cross_ref = refs[8 + 2 * hops :]
    step = pl.program_id(0)
    rank = pos_ref[0]
    zc, base = plan.zc, plan.pull_base
    tiles = slice(8, 8 + plan.tiles)
    mask = masks(plan)
    now = step % 2

    @pl.when(step == 0)
    def _():
        s1, s2 = get_sums(sums_ref, 2)
        prec = (s1 + 1.0) / (s2 + 1.0)
        push_ref[...] = jnp.zeros_like(push_ref)
        wt_ref[...] = jnp.zeros_like(wt_ref)
        zy_ref[...] = jnp.zeros_like(zy_ref)
        pull_ref[...] = jnp.zeros_like(pull_ref)
        count_tables(plan, cross_ref, None)
        w_ref[...] = label_ref[...].astype(f32) - prec[None]

    def push(at):
        out = []
        for n in range(plan.block):
            w = w_ref[at + n]
            out.append((push_ref, at + n + 2, w * q_ref[0, at + n]))
            out.append((wt_ref, at + n + base, w * t_ref[0, at + n]))
            out.append((w_ref, at + n, w * m_ref[0, at + n]))
        store_all(out)

    over(0, zc, plan.block, push)

    def widen(at):
        out = []
        values = [push_ref[at + n] for n in range(plan.span_block + 2)]
        for n in range(plan.span_block):
            part = values[n] + values[n + 1] + values[n + 2]
            out.append((zy_ref, (at + n, tiles), part + y_neighbours(mask, part)))
        store_all(out)

    over(0, plan.span, plan.span_block, widen)

    def pull(at):
        out = []
        for n in range(plan.span_block):
            box = x_box(plan, mask, zy_ref, at + n)
            inverse = cross_ref[kind_of(plan, rank, at + n - 1)[0]]
            grown = grown_ref[0, at + n]
            spot = at + n - 1 + base
            old = pull_ref[now, spot, tiles]
            out.append((pull_ref, (now, spot, tiles), old - grown * grown * box * inverse))
        store_all(out)

    over(0, plan.span, plan.span_block, pull)
    reach = 2 + step
    last = step == SECTIONS - 1

    def join(plane, ending):
        out = []
        for n in range(plan.erode_block):
            at = plane + n + base
            cur = pull_ref[now, at, tiles]

            def load(offset, at=at):
                return pull_ref[now, at, 8 + offset : 8 + offset + plan.tiles]

            total = cur + pull_ref[now, at - 1, tiles] + pull_ref[now, at + 1, tiles]
            total = total + x_neighbours(plan, mask, load, cur) + y_neighbours(mask, cur)
            total = total + wt_ref[at]
            if not ending:
                total = total * cross_ref[kind_of(plan, rank, plane + n)[0]]
            out.append((pull_ref, (1 - now, at, tiles), total))
        store_all(out)

    @pl.when(jnp.logical_not(last))
    def _():
        over(-reach, zc + 2 * reach, plan.erode_block, lambda plane: join(plane, False))

    @pl.when(last)
    def _():
        over(-reach, zc + 2 * reach, plan.erode_block, lambda plane: join(plane, True))
        mine_ref[...] = pull_ref[1 - now, base - 1 : base + zc + 1, tiles]
        for h in range(1, hops + 1):
            n = plan.back_count(h)
            first = base + h * zc - 1
            up[h - 1][...] = pull_ref[1 - now, first : first + n, tiles]
            first = base + (1 - h) * zc - n + 1
            down[h - 1][...] = pull_ref[1 - now, first : first + n, tiles]


def finish_kernel(plan, *refs):
    hops = plan.back_hops
    pos_ref, sums_ref, skel_ref, p_ref, target_ref, ts_ref, mine_ref = refs[:7]
    below, above = refs[7 : 7 + hops], refs[7 + hops : 7 + 2 * hops]
    out_ref, loss_ref, bias_ref, h_ref, grad_ref = refs[7 + 2 * hops :]
    rank = pos_ref[0]
    zc = plan.zc
    s1, s2, s5, s6, s7 = get_sums(sums_ref, 5)
    s3, s4 = get_sums(skel_ref, 2)
    prec = (s1 + 1.0) / (s2 + 1.0)
    sens = (s3 + 1.0) / (s4 + 1.0)
    both = prec + sens
    volume = s6 + s7 + 1.0
    cl_loss = 1.0 - 2.0 * prec * sens / both
    dice_loss = 1.0 - (2.0 * s5 + 1.0) / volume
    loss_ref[...] = jnp.broadcast_to(0.5 * dice_loss + 0.5 * cl_loss, (8, LANES))
    l0 = -(sens / both) * (sens / both) / (s2 + 1.0)
    l2 = -(prec / both) * (prec / both) / (s4 + 1.0)
    l4 = -1.0 / volume
    l5 = 0.5 * (2.0 * s5 + 1.0) / (volume * volume)

    h_ref[...] = mine_ref[...]
    for h in range(1, hops + 1):
        n = plan.back_count(h)
        h_ref[:n] += below[h - 1][...]
        h_ref[plan.span - n :] += above[h - 1][...]

    total = jnp.zeros((plan.tiles, LANES), f32)
    for n in range(plan.span):
        inside = 1.0 - kind_of(plan, rank, n - 1)[1]
        predict = p_ref[n]
        skel = l0 * jnp.exp(-temper * predict) * h_ref[n]
        whole = skel + l2 * ts_ref[n] + l4 * target_ref[n] + l5
        grad = whole * predict * (1.0 - predict) * inside
        grad_ref[n * plan.tiles : (n + 1) * plan.tiles] = grad
        if 1 <= n <= zc:
            total = total + grad
    bias_ref[...] = jnp.sum(total.reshape(-1, 8, LANES), axis=0)
    lane = lane_iota((1, LANES))

    def column(tile):
        return [
            grad_ref[pl.ds(plan.tiles + tile, zc, stride=plan.tiles)],
            grad_ref[tile : tile + 1],
            grad_ref[(zc + 1) * plan.tiles + tile : (zc + 1) * plan.tiles + tile + 1],
        ]

    for a in range(plan.gx):
        pieces = [column(a * plan.own + q) for q in range(plan.own)]
        zero = [jnp.zeros((zc, LANES), f32)] + [jnp.zeros((1, LANES), f32)] * 2
        after = column((a + 1) * plan.own) if a < plan.gx - 1 else zero
        before = column(a * plan.own - 1) if a > 0 else zero
        if plan.shared:
            pieces.append(
                [
                    jnp.where(lane < plan.Y, x, 0.0) + jnp.where(lane >= LANES - plan.Y, y, 0.0)
                    for x, y in zip(after, before)
                ]
            )
        else:
            pieces += [after, before]
        edges = [edge for piece in pieces for edge in piece[1:]]
        rows = plan.R16
        edges += [jnp.zeros((1, LANES), f32)] * (plan.extra16 * rows - len(edges))
        whole = [piece[0] for piece in pieces]
        if rows > zc:
            fill = jnp.zeros((rows - zc, LANES), f32)
            whole = [jnp.concatenate([piece, fill], axis=0) for piece in whole]
        whole += [
            jnp.concatenate(edges[n * rows : (n + 1) * rows], axis=0) for n in range(plan.extra16)
        ]
        for q, piece in enumerate(whole):
            piece = piece.astype(bf16)
            for b in range(plan.gy):
                out_ref[a * plan.gy + b, q] = piece


def weight_kernel(plan, pos_ref, f_ref, bias_ref, got_ref, gw_ref, g_ref, dw_ref):
    rows, inner = plan.Y, plan.ch * plan.ny
    zc, nz = plan.zc, plan.nz
    lane = lane_iota((rows, nz))
    places = {}
    for x in range(-1, plan.nx + 1):
        tile, first = plan.slot(x)
        places.setdefault(tile, {})[first] = x
    for tile in range(plan.sent):
        stack = [got_ref[p, tile].astype(f32)[:zc] for p in range(plan.members)]
        turned = jnp.concatenate(stack, axis=0).T
        ends = []
        for end, p in ((0, 0), (1, plan.members - 1)):
            n = 2 * tile + end
            row = got_ref[p, plan.sent + n // plan.R16].astype(f32)
            ends.append(row[n % plan.R16 : n % plan.R16 + 1])
        ends = jnp.concatenate(ends + [jnp.zeros((LANES - 2, LANES), f32)], axis=0).T
        for first, x in places[tile].items():
            g = turned[first : first + rows]
            end = ends[first : first + rows]
            down = jnp.where(lane == nz - 1, pltpu.roll(end, nz - 2, 1), pltpu.roll(g, nz - 1, 1))
            up = jnp.where(lane == 0, end, pltpu.roll(g, 1, 1))
            g_ref[x + 1] = jnp.concatenate([down, g, up], axis=0).astype(bf16)

    dw_ref[...] = jnp.zeros_like(dw_ref)

    def at_x(x, carry):
        block = f_ref[:, x].reshape(inner, nz)
        moved = jnp.concatenate([g_ref[x + 2], g_ref[x + 1], g_ref[x]], axis=0)
        dw_ref[...] += lax.dot_general(
            moved, block, (((1,), (1,)), ((), ())), preferred_element_type=f32
        )
        return carry

    lax.fori_loop(0, plan.nx, at_x, 0)

    tap_y = tap_condition(plan, pos_ref[1], (rows, inner), 0, 1)
    taps = []
    for t in range(27):
        i, j, k = t // 9, t // 3 % 3, t % 3
        at = (3 * i + k) * rows
        taps.append(jnp.sum(jnp.where(tap_y == j, dw_ref[at : at + rows], 0.0), axis=0, keepdims=True))
    taps += [jnp.zeros((1, inner), f32)] * 5
    total = jnp.zeros((8, LANES), f32)
    for n in range(4):
        place = (
            lax.broadcasted_iota(jnp.int32, (inner, LANES), 0) // plan.ny + 32 * n
            == lax.broadcasted_iota(jnp.int32, (inner, LANES), 1)
        ).astype(f32)
        total = total + jnp.dot(
            jnp.concatenate(taps[8 * n : 8 * n + 8], axis=0),
            place,
            precision=lax.Precision.HIGHEST,
            preferred_element_type=f32,
        )
    spot = (row_iota((8, LANES)) == 3) & (lane_iota((8, LANES)) == 96)
    total = jnp.where(spot, jnp.sum(bias_ref[...]), total)
    gw_ref[...] = jnp.broadcast_to(total[None], (plan.ranks, 8, LANES))


def feature_kernel(plan, pos_ref, wt_ref, g_ref, after_ref, gf_ref, wide_ref):
    del after_ref
    rows, inner, bands = plan.Y, plan.ch * plan.ny, 9 * plan.Y
    spread = (
        lax.broadcasted_iota(jnp.int32, (inner, plan.ch), 0) // plan.ny
        == lax.broadcasted_iota(jnp.int32, (inner, plan.ch), 1)
    ).astype(f32)
    tap_y = tap_condition(plan, pos_ref[1], (inner, bands), 1, 0)
    wide = jnp.zeros((inner, bands), f32)
    tap = lax.broadcasted_iota(jnp.int32, (27, bands), 0)
    band = lax.broadcasted_iota(jnp.int32, (27, bands), 1) // rows
    for j in range(3):
        pick = (tap == 9 * (band // 3) + 3 * j + band % 3).astype(f32)
        chosen = jnp.dot(wt_ref[...].astype(f32), pick, preferred_element_type=f32)
        full = jnp.dot(spread, chosen, preferred_element_type=f32)
        wide = jnp.where(tap_y == j, full, wide)
    wide_ref[...] = wide.astype(bf16)

    def at_x(x, carry):
        moved = jnp.concatenate([g_ref[x + 2], g_ref[x + 1], g_ref[x]], axis=0)
        out = jnp.dot(wide_ref[...], moved, preferred_element_type=f32)
        gf_ref[:, x] = out.astype(bf16).reshape(plan.ch, plan.ny, plan.nz)
        return carry

    lax.fori_loop(0, plan.nx, at_x, 0)


def final_kernel(plan, got_ref, gw_ref, gb_ref):
    total = jnp.sum(got_ref[...], axis=0)
    for n in range(4):
        count = min(8, 27 - 8 * n)
        gw_ref[8 * n : 8 * n + count] = total[:count, 32 * n : 32 * n + plan.ch]
    gb_ref[...] = total[3:4, 96:97]


VMEM = pl.BlockSpec(memory_space=pltpu.VMEM)
SMEM = pl.BlockSpec(memory_space=pltpu.SMEM)
ANY = pl.BlockSpec(memory_space=pl.ANY)
FAR = pl.BlockSpec(memory_space=pltpu.HBM)
MIB = 1024 * 1024
ALMOST_ALL = 65_680_000


def shape(dims, dtype=f32):
    return jax.ShapeDtypeStruct(dims, dtype)


def held(dims, dtype):
    if len(dims) < 2:
        return 4096
    size = jnp.dtype(dtype).itemsize
    rows = 8 * 4 // size
    total = -(-dims[-2] // rows) * rows * -(-dims[-1] // LANES) * LANES * size
    for n in dims[:-2]:
        total *= n
    return total


def limits(arrays, scratch, micros, least=0):
    total = sum(held(a.shape, a.dtype) for a in arrays)
    total += sum(held(a.shape, a.dtype) for a in scratch if len(a.shape) > 1)
    limit = max(least, min(63 * MIB, total + total // 8 + 4 * MIB))
    return dict(
        compiler_params=pltpu.CompilerParams(vmem_limit_bytes=limit),
        cost_estimate=pl.CostEstimate(
            flops=0, transcendentals=0, bytes_accessed=int(micros * 2.5e6)
        ),
    )


def per_device(mesh_shape, features, weight, bias, label):
    plan = Plan(mesh_shape, features.shape)
    members, sent, own, tiles = plan.members, plan.sent, plan.own, plan.tiles
    inner, bands = plan.ch * plan.ny, 9 * plan.Y
    place = (lax.axis_index("gz") * members + lax.axis_index(GROUP)).astype(jnp.int32)
    pos = jnp.stack([place, lax.axis_index("gy").astype(jnp.int32)])

    def call(kernel, out_shape, in_specs, operands, micros, scratch=(), least=0):
        outs = jax.tree.leaves(out_shape)
        ins = [a for spec, a in zip(in_specs, operands) if spec is VMEM]
        return pl.pallas_call(
            functools.partial(kernel, plan),
            out_shape=out_shape,
            in_specs=in_specs,
            out_specs=jax.tree.map(lambda s: VMEM, out_shape),
            scratch_shapes=list(scratch),
            **limits(ins + outs, scratch, micros, least),
        )(*operands)

    def exchange(array):
        return lax.all_to_all(array, GROUP, 0, 0, tiled=True)

    def everywhere(array):
        return lax.all_to_all(array, ALL_AXES, 0, 0, tiled=True)

    def hop(array, distance):
        def device(r):
            return (r % members) * plan.gz + r // members

        pairs = [
            (device(r), device(r + distance))
            for r in range(plan.ranks)
            if 0 <= r + distance < plan.ranks
        ]
        return lax.ppermute(array, ALL_AXES, pairs)

    label_sent = call(
        label_kernel, shape((members, own, plan.zc, LANES), bf16), [SMEM, VMEM], (pos, label), 1.5
    )
    sent_logits = call(
        conv_kernel,
        shape((members, sent + plan.extra, plan.R, LANES)),
        [SMEM, VMEM, FAR, ANY],
        (pos, weight, features, label_sent),
        7,
        [
            pltpu.VMEM((bands, inner), bf16),
            pltpu.VMEM((plan.nx + 2, 3 * plan.Y, plan.nz), f32),
            pltpu.VMEM(features.shape, bf16),
            pltpu.SemaphoreType.DMA((4,)),
        ],
        ALMOST_ALL,
    )

    def planes(array):
        return array.reshape(-1, tiles, LANES)

    def hops_of(parts, count):
        whole, head, tail = parts
        below = [hop(whole if h < count else tail, h) for h in range(1, count + 1)]
        above = [hop(whole if h < count else head, -h) for h in range(1, count + 1)]
        return below + above

    zc = plan.zc
    short = plan.label_rest * tiles
    label_parts = call(
        label_gather_kernel,
        [shape((zc * tiles, LANES), bf16)] + [shape((short, LANES), bf16)] * 2,
        [VMEM],
        (exchange(label_sent),),
        1.5,
        [pltpu.VMEM((zc * tiles, LANES), f32)],
    )
    label_parts = [planes(part) for part in label_parts]
    short = (plan.rest + 1) * tiles
    parts = call(
        gather_kernel,
        [shape(((zc + 2) * tiles, LANES))] + [shape((short, LANES))] * 2,
        [VMEM],
        (exchange(sent_logits),),
        1.5,
    )
    parts = [planes(part) for part in parts]
    around = hops_of(parts, plan.hops)
    label_around = hops_of(label_parts, plan.label_hops)

    slab = (zc, tiles, LANES)
    span = (plan.span, tiles, LANES)
    everyone = shape((plan.ranks, 8, LANES))
    table = pltpu.VMEM((3, tiles, LANES), f32)

    def section_grid(kernel, operands, streamed, outs, records, micros, scratch, backwards):
        def spec(dims):
            if backwards:
                return pl.BlockSpec((1,) + dims, lambda n: (SECTIONS - 1 - n, 0, 0, 0))
            return pl.BlockSpec((1,) + dims, lambda n: (n, 0, 0, 0))

        blocks = [shape(a.shape[1:]) for a in streamed] + [shape(r) for r in records]
        fixed = [a for a in operands if a.ndim > 1]
        return pl.pallas_call(
            functools.partial(kernel, plan),
            grid=(SECTIONS,),
            out_shape=[shape((SECTIONS,) + r) for r in records] + outs,
            in_specs=[VMEM if a.ndim > 1 else SMEM for a in operands]
            + [spec(a.shape[1:]) for a in streamed],
            out_specs=[spec(r) for r in records] + [VMEM] * len(outs),
            scratch_shapes=scratch,
            **limits(blocks * 2 + outs + fixed, scratch, micros, ALMOST_ALL),
        )(*operands, *streamed)

    m, q, t, grown, predict, sums = section_grid(
        forward_kernel,
        (pos, bias, label_parts[0], parts[0], *around),
        (),
        [shape(span), everyone],
        [slab, slab, slab, span],
        11,
        [
            pltpu.VMEM((2, plan.planes, plan.pad, LANES), f32),
            pltpu.VMEM((2, plan.planes, tiles, LANES), f32),
            pltpu.VMEM((zc, plan.pad, LANES), f32),
            pltpu.VMEM(slab, f32),
            table,
            table,
        ],
        False,
    )
    sums = everywhere(sums)
    room = plan.win + 2 + plan.erode_block
    target, ts, skel_sums = call(
        target_kernel,
        [shape(span), shape(span), everyone],
        [SMEM] + [VMEM] * (2 + 2 * plan.label_hops),
        (pos, predict, label_parts[0], *label_around),
        13,
        [
            pltpu.VMEM((plan.win, tiles, LANES), f32),
            pltpu.VMEM((2, room, plan.pad, LANES), f32),
            pltpu.VMEM((2, room, tiles, LANES), f32),
            pltpu.VMEM((plan.span, plan.pad, LANES), f32),
            table,
            table,
        ],
    )
    skel_sums = everywhere(skel_sums)
    outer = [
        shape((plan.back_count(h), tiles, LANES)) for h in range(1, plan.back_hops + 1)
    ]
    mine, *outer = section_grid(
        backward_kernel,
        (pos, sums, label_parts[0]),
        (m, q, t, grown),
        [shape(span)] + outer * 2,
        [],
        11,
        [
            pltpu.VMEM(slab, f32),
            pltpu.VMEM((zc + 4, tiles, LANES), f32),
            pltpu.VMEM((plan.pull_planes, tiles, LANES), f32),
            pltpu.VMEM((plan.span, plan.pad, LANES), f32),
            pltpu.VMEM((2, plan.pull_planes, plan.pad, LANES), f32),
            table,
        ],
        True,
    )
    beyond = []
    for sign, arrays in ((1, outer[: plan.back_hops]), (-1, outer[plan.back_hops :])):
        for h in range(1, plan.back_hops + 1):
            beyond.append(hop(arrays[h - 1], sign * h))
    grad_sent, loss, bias_part = call(
        finish_kernel,
        [
            shape((members, sent + plan.extra16, plan.R16, LANES), bf16),
            shape((8, LANES)),
            shape((8, LANES)),
        ],
        [SMEM] + [VMEM] * (6 + 2 * plan.back_hops),
        (pos, sums, skel_sums, predict, target, ts, mine, *beyond),
        2,
        [pltpu.VMEM(span, f32), pltpu.VMEM((plan.span * tiles, LANES), f32)],
    )

    moved = shape((plan.nx + 2, 3 * plan.Y, plan.nz), bf16)
    partial, g = call(
        weight_kernel,
        [shape((plan.ranks, 8, LANES)), moved],
        [SMEM, VMEM, VMEM, VMEM],
        (pos, features, bias_part, exchange(grad_sent)),
        5,
        [pltpu.VMEM((bands, inner), f32)],
    )
    grad_features = call(
        feature_kernel,
        shape(features.shape, bf16),
        [SMEM, VMEM, VMEM, ANY],
        (pos, weight.T, g, partial),
        5,
        [pltpu.VMEM((inner, bands), bf16)],
    )
    grad_weight, grad_bias = call(
        final_kernel,
        [shape((27, plan.ch)), shape((1, 1))],
        [VMEM],
        (everywhere(partial),),
        1.5,
    )
    return (loss[0, :1], grad_features, grad_weight, grad_bias.reshape(1))


def solution(mesh):
    in_specs = (P(None, "gx", "gy", "gz"), P(), P(), P("gx", "gy", "gz"))
    out_specs = (P(), P(None, "gx", "gy", "gz"), P(), P())

    def body(*args):
        return per_device(dict(mesh.shape), *args)

    return jax.shard_map(
        body, mesh=mesh, in_specs=in_specs, out_specs=out_specs, check_vma=False
    )
```

```python
import functools

import jax
import jax.numpy as jnp
from jax import lax
from jax.experimental import pallas as pl
from jax.experimental.pallas import tpu as pltpu
from jax.sharding import PartitionSpec as P

ITERS = 10
SECTIONS = ITERS + 1
LANES = 128
HALO = SECTIONS + 2
BACK = SECTIONS + 1

BLOCK = 32
SPAN_BLOCK = 40
ERODE_BLOCK = 20

temper = 20.0
sharpness = 40.0

GROUP = ("gx", "gy")
ALL_AXES = ("gx", "gy", "gz")
f32 = jnp.float32
bf16 = jnp.bfloat16


def up8(value):
    return -(-value // 8) * 8


class Plan:
    def __init__(self, mesh_shape, block):
        self.ch, self.nx, self.ny, self.nz = block
        self.gx, self.gy, self.gz = (mesh_shape[a] for a in ALL_AXES)
        self.members = self.gx * self.gy
        self.ranks = self.members * self.gz
        self.X = self.nx * self.gx
        self.Y = self.ny * self.gy
        self.Z = self.nz * self.gz
        assert LANES % self.Y == 0 and self.nz == LANES
        assert self.nz % self.members == 0
        self.zc = self.nz // self.members
        self.per = LANES // self.Y
        assert self.nx % self.per == 0
        self.tiles = self.X // self.per
        self.own = self.nx // self.per
        self.shared = self.per > 1
        self.sent = self.own + (1 if self.shared else 2)
        self.R = up8(self.zc)
        self.extra = -(-2 * self.sent // self.R)
        self.R16 = -(-self.zc // 16) * 16
        self.extra16 = -(-2 * self.sent // self.R16)
        self.pad = self.tiles + 16
        self.win = self.zc + 2 * HALO
        self.span = self.zc + 2
        self.block = self.blocks_of(self.zc, BLOCK)
        self.span_block = self.blocks_of(self.span, SPAN_BLOCK)
        self.win_block = self.blocks_of(self.win, 32)
        self.erode_block = max(1, ERODE_BLOCK * 8 // self.tiles)
        self.base = HALO + 1
        self.planes = self.zc + 2 * HALO + 2 + self.erode_block
        self.pull_base = BACK + 2
        self.pull_planes = self.zc + 2 * BACK + 4 + self.erode_block
        self.hops = -(-HALO // self.zc)
        self.rest = HALO - (self.hops - 1) * self.zc
        self.records = 3 * self.zc + self.span
        assert self.ny == 16 and self.gy > 1
        self.back_hops = -(-(BACK + 1) // self.zc)

    def back_count(self, h):
        return min(self.zc + BACK + 1 - h * self.zc, self.span)

    def blocks_of(self, count, most):
        fits = [n for n in range(1, count + 1) if count % n == 0 and n * self.tiles <= 8 * most]
        return fits[-1] if fits else 1

    def slab(self, member):
        x, y = member // self.gy, member % self.gy
        return y * self.gx + (x if y % 2 == 0 else self.gx - 1 - x)

    def member(self, slab, odd):
        slab = self.members - 1 - slab if odd else slab
        return next(p for p in range(self.members) if self.slab(p) == slab)

    def member_now(self, slab, pos_ref):
        odd = pos_ref[0] // self.members % 2 == 1
        return jnp.where(odd, self.member(slab, True), self.member(slab, False))

    def label_lane(self, member_y):
        return 0 if member_y == self.gy - 1 else (member_y + 1) * self.ny + 8

    def slot(self, x):
        if 0 <= x < self.nx:
            return x // self.per, (x % self.per) * self.Y
        if x == self.nx:
            return self.own, 0
        return self.sent - 1, LANES - self.Y


def lane_iota(shape):
    return lax.broadcasted_iota(jnp.int32, shape, len(shape) - 1)


def row_iota(shape):
    return lax.broadcasted_iota(jnp.int32, shape, len(shape) - 2)


def masks(plan):
    return lane_iota((plan.tiles, LANES))


def x_neighbours(plan, mask, load, cur):
    lower, upper = load(-1), load(1)
    if plan.Y == LANES:
        return lower + upper
    lower = pltpu.roll(jnp.where(mask >= LANES - plan.Y, lower, cur), plan.Y, 1)
    upper = pltpu.roll(jnp.where(mask < plan.Y, upper, cur), LANES - plan.Y, 1)
    return lower + upper


def y_matrix(plan, ref):
    row = row_iota((2 * LANES, LANES)) % LANES
    lane = lane_iota((2 * LANES, LANES))
    near = (row == lane - 1) | (row == lane + 1)
    ref[...] = (near & (row // plan.Y == lane // plan.Y)).astype(f32).astype(bf16)


def y_neighbours(ref, block):
    flat = block.reshape(-1, LANES)
    high = flat.astype(bf16)
    low = (flat - high.astype(f32)).astype(bf16)
    both = jnp.concatenate([high, low], axis=1)
    return jnp.dot(both, ref[...], preferred_element_type=f32).reshape(block.shape)


def count_tables(plan, cross_ref, box_ref):
    flat = row_iota((plan.tiles, LANES)) * LANES + lane_iota((plan.tiles, LANES))
    y, x = flat % plan.Y, flat // plan.Y

    def along(spot, size):
        return 3.0 - (spot == 0).astype(f32) - (spot == size - 1).astype(f32)

    cx, cy = along(x, plan.X), along(y, plan.Y)
    for kind, cz in ((1, 2.0), (2, 3.0)):
        if cross_ref is not None:
            cross_ref[kind] = 1.0 / (cx + cy + cz - 2.0)
        if box_ref is not None:
            box_ref[kind] = 1.0 / (cx * cy * cz)
    for ref in (cross_ref, box_ref):
        if ref is not None:
            ref[0] = jnp.zeros((plan.tiles, LANES), f32)


def kind_of(plan, rank, plane):
    z = rank * plan.zc + plane
    inside = (z >= 0) & (z < plan.Z)
    edge = (z == 0) | (z == plan.Z - 1)
    return jnp.where(inside, jnp.where(edge, 1, 2), 0), jnp.where(inside, 0.0, 1.0)


def store_all(pairs):
    for ref, at, value in pairs:
        ref[at] = value


def over(first, count, size, body):
    def at(n, carry):
        body(first + n * size)
        return carry

    lax.fori_loop(0, (count + size - 1) // size, at, 0)


def tap_condition(plan, member_y, shape, y_dim, in_dim):
    y = lax.broadcasted_iota(jnp.int32, shape, y_dim) % plan.Y
    own = lax.broadcasted_iota(jnp.int32, shape, in_dim) % plan.ny
    return own + member_y * plan.ny - y + 1


PARTS = 4


def stream(plan, far_ref, near_ref, sem_ref):
    width = plan.nx // PARTS
    copies = []
    for n in range(PARTS):
        span = pl.ds(n * width, width)
        copies.append(
            pltpu.make_async_copy(far_ref.at[:, span], near_ref.at[:, span], sem_ref.at[n])
        )
        copies[-1].start()
    return copies


def columns(plan, ref, first, count):
    blocks = [ref[:, x].reshape(-1, plan.nz) for x in range(first, first + count)]
    return jnp.concatenate(blocks, axis=1)


def moved_columns(ref, first, count):
    blocks = [
        jnp.concatenate([ref[x + 2], ref[x + 1], ref[x]], axis=0)
        for x in range(first, first + count)
    ]
    return jnp.concatenate(blocks, axis=1)


def conv_kernel(
    plan, pos_ref, w_ref, far_ref, label_ref, out_ref, wide_ref, acc_ref, f_ref, sem_ref
):
    width = plan.nx // PARTS
    copies = stream(plan, far_ref, f_ref, sem_ref)
    rows, inner = plan.Y, plan.ch * plan.ny
    spread = (
        lax.broadcasted_iota(jnp.int32, (plan.ch, inner), 0)
        == lax.broadcasted_iota(jnp.int32, (plan.ch, inner), 1) // plan.ny
    )
    taps = jnp.dot(
        w_ref[...], spread.astype(f32).astype(bf16), preferred_element_type=f32
    )
    tap_y = tap_condition(plan, pos_ref[1], (rows, inner), 0, 1)
    for i in range(3):
        for k in range(3):
            band = jnp.zeros((rows, inner), f32)
            for j in range(3):
                t = 9 * i + 3 * j + k
                band = jnp.where(tap_y == j, taps[t : t + 1], band)
            at = (3 * i + k) * rows
            wide_ref[at : at + rows] = band.astype(bf16)
    acc_ref[...] = jnp.zeros_like(acc_ref)

    for n in range(PARTS):
        copies[n].wait()
        first = n * width
        out = jnp.dot(
            wide_ref[...], columns(plan, f_ref, first, width), preferred_element_type=f32
        )
        for slot in range(first, first + width + 2):
            terms = [
                out[3 * i * rows : 3 * (i + 1) * rows, (x - first) * plan.nz : (x - first + 1) * plan.nz]
                for i in range(3)
                for x in (slot - 2 + i,)
                if first <= x < first + width
            ]
            acc_ref[slot] += functools.reduce(jnp.add, terms)

    out_ref[...] = jnp.zeros_like(out_ref)
    places = {}
    for x in range(-1, plan.nx + 1):
        tile, lane = plan.slot(x)
        places.setdefault(tile, {})[lane] = x
    lane = lane_iota((rows, plan.nz))
    words = [label_ref[x, 0:8] + 2 * label_ref[x, 8:16] for x in range(plan.nx)]
    first_group = jnp.where(
        pos_ref[1] == plan.gy - 1, 0, (pos_ref[1] + 1) * (plan.ny // 8) + 1
    )
    labelled = lax.broadcasted_iota(jnp.int32, (rows, plan.nz), 0) // 8 == first_group
    for tile in range(plan.sent):
        parts, spills = [], []
        for first in range(0, LANES, rows):
            x = places[tile].get(first)
            if x is None:
                parts.append(jnp.zeros((rows, plan.nz), f32))
                spills.append(jnp.zeros((rows, plan.nz), f32))
                continue
            low = acc_ref[x + 1, 0:rows]
            mid = acc_ref[x + 1, rows : 2 * rows]
            high = acc_ref[x + 1, 2 * rows : 3 * rows]
            total = mid + jnp.where(lane == 0, 0.0, pltpu.roll(low, 1, 1))
            total = total + jnp.where(lane == plan.nz - 1, 0.0, pltpu.roll(high, plan.nz - 1, 1))
            if 0 <= x < plan.nx:
                word = jnp.concatenate([words[x].astype(f32)] * (rows // 8), axis=0)
                total = total + jnp.where(labelled, word, 0.0)
            parts.append(total)
            spill = jnp.where(lane == 1, pltpu.roll(low, 2, 1), 0.0)
            spills.append(jnp.where(lane == 0, high, spill))
        turned = jnp.concatenate(parts, axis=0).T
        spill = jnp.concatenate(spills, axis=0).T
        for j in range(plan.members):
            p = plan.member_now(j, pos_ref)
            out_ref[p, tile, 0 : plan.zc] = turned[j * plan.zc : (j + 1) * plan.zc]
        for end, j in ((0, 0), (1, plan.members - 1)):
            n = 2 * tile + end
            at = plan.sent + n // plan.R
            p = plan.member_now(j, pos_ref)
            out_ref[p, at, n % plan.R : n % plan.R + 1] = spill[end : end + 1]


def gather_kernel(plan, got_ref, out_ref, label_ref, head_ref, tail_ref):
    tiles, zc, rest = plan.tiles, plan.zc, plan.rest
    lane = lane_iota((1, LANES))
    spot = lane % plan.Y

    def part(p, q):
        values = [got_ref[p, q, 0:zc]]
        for end in range(2):
            n = 2 * q + end
            at = plan.sent + n // plan.R
            values.append(got_ref[p, at, n % plan.R : n % plan.R + 1])
        return values

    for a in range(plan.gx):
        for q in range(plan.own):
            parts = []
            label = jnp.zeros((zc, LANES), f32)
            for b in range(plan.gy):
                start = b * plan.ny
                values = part(a * plan.gy + b, q)
                second = (values[0] >= 1.5).astype(f32)
                first = values[0] - 2.0 * second
                move = start - plan.label_lane(b)
                first = pltpu.roll(first, move % LANES, 1)
                second = pltpu.roll(second, (move + 8) % LANES, 1)
                label = jnp.where((spot >= start) & (spot < start + 8), first, label)
                label = jnp.where((spot >= start + 8) & (spot < start + 16), second, label)
                mine = (spot >= start - 1) & (spot <= start + plan.ny)
                parts.append([jnp.where(mine, v, 0.0) for v in values])
                if q == plan.own - 1 and a < plan.gx - 1:
                    edge = part((a + 1) * plan.gy + b, plan.sent - 1)
                    parts.append([jnp.where(lane >= LANES - plan.Y, v, 0.0) for v in edge])
                if q == 0 and a > 0:
                    edge = part((a - 1) * plan.gy + b, plan.own)
                    parts.append([jnp.where(lane < plan.Y, v, 0.0) for v in edge])
            whole, low, high = (functools.reduce(jnp.add, vs) for vs in zip(*parts))
            tile = a * plan.own + q
            label_ref[pl.ds(tile, zc, stride=tiles)] = label
            out_ref[pl.ds(tile, zc, stride=tiles)] = whole
            out_ref[zc * tiles + tile : zc * tiles + tile + 1] = low
            out_ref[(zc + 1) * tiles + tile : (zc + 1) * tiles + tile + 1] = high

    def pack(ref, at, first, count):
        half = -(-count // 2)
        for n in range(half):
            word = label_ref[(first + n) * tiles : (first + n + 1) * tiles]
            if n + half < count:
                other = first + n + half
                word = word + 2.0 * label_ref[other * tiles : (other + 1) * tiles]
            ref[(at + n) * tiles : (at + n + 1) * tiles] = word

    pack(out_ref, zc + 2, 0, zc)
    head_ref[: rest * tiles] = out_ref[: rest * tiles]
    head_ref[rest * tiles : (rest + 1) * tiles] = out_ref[zc * tiles : (zc + 1) * tiles]
    pack(head_ref, rest + 1, 0, rest)
    tail_ref[: rest * tiles] = out_ref[(zc - rest) * tiles : zc * tiles]
    tail_ref[rest * tiles : (rest + 1) * tiles] = out_ref[(zc + 1) * tiles : (zc + 2) * tiles]
    pack(tail_ref, rest + 1, zc - rest, rest)


LOG = 1.0 / sharpness


def thin(e, box, inverse, outside):
    box = box + outside
    ratio = e * box * inverse + outside
    square = ratio * ratio
    more = 1.0 + square
    joint = 1.0 / (box * more)
    slope = joint * box
    return joint * more, slope, jnp.log(square * slope)


def lift(scaled, s):
    small = jnp.exp(scaled * (s - 1.0))
    more = 1.0 + small
    return s + jnp.log(more) * LOG, small * (1.0 / more)


def erode(plan, rank, mask, y_ref, source, result, grown_ref, table_ref, base, first, count):
    tiles = slice(8, 8 + plan.tiles)

    def body(plane):
        beside = y_neighbours(y_ref, source[pl.ds(plane + base, plan.erode_block), tiles])
        for n in range(plan.erode_block):
            at = plane + n + base
            cur = source[at, tiles]

            def load(offset, at=at):
                return source[at, 8 + offset : 8 + offset + plan.tiles]

            total = cur + source[at - 1, tiles] + source[at + 1, tiles]
            total = total + x_neighbours(plan, mask, load, cur) + beside[n]
            kind, outside = kind_of(plan, rank, plane + n)
            total = total * table_ref[kind]
            result[at, tiles] = total
            grown_ref[at] = 1.0 / (total + outside) - outside

    over(first, count, plan.erode_block, body)


def spread(plan, y_ref, grown_ref, zy_ref, base, first, count, size):
    tiles = slice(8, 8 + plan.tiles)

    def body(plane):
        at = plane + base
        part = grown_ref[pl.ds(at - 1, size)] + grown_ref[pl.ds(at, size)]
        part = part + grown_ref[pl.ds(at + 1, size)]
        zy_ref[pl.ds(plane - first, size), tiles] = part + y_neighbours(y_ref, part)

    over(first, count, size, body)


def in_turn(section):
    section(0, 0, 1, True)

    def pair(n, carry):
        section(2 * n + 1, 1, 0, False)
        section(2 * n + 2, 0, 1, False)
        return carry

    lax.fori_loop(0, ITERS // 2, pair, 0)


def x_box(plan, mask, zy_ref, at):
    cur = zy_ref[at, 8 : 8 + plan.tiles]

    def load(offset):
        return zy_ref[at, 8 + offset : 8 + offset + plan.tiles]

    return cur + x_neighbours(plan, mask, load, cur)


def target_kernel(plan, *refs):
    hops = plan.hops
    pos_ref, p_ref, own_ref = refs[:3]
    below, above = refs[3 : 3 + hops], refs[3 + hops : 3 + 2 * hops]
    target_ref, ts_ref, sums_ref = refs[3 + 2 * hops : 6 + 2 * hops]
    all_ref, e0_ref, e1_ref, g_ref, zy_ref, cross_ref, box_ref, y_ref = refs[6 + 2 * hops :]
    zc, win, span = plan.zc, plan.win, plan.span
    size = plan.span_block
    base = HALO + 1
    tiles = slice(8, 8 + plan.tiles)
    rank = pos_ref[0]
    mask = masks(plan)
    count_tables(plan, cross_ref, box_ref)
    y_matrix(plan, y_ref)
    e_refs = (e0_ref, e1_ref)
    e0_ref[...] = jnp.zeros_like(e0_ref)
    e1_ref[...] = jnp.zeros_like(e1_ref)
    zy_ref[...] = jnp.zeros_like(zy_ref)
    all_ref[HALO : HALO + zc] = own_ref[...]
    for h in range(1, hops + 1):
        count = zc if h < hops else plan.rest
        at = zc + 2 if h < hops else plan.rest + 1
        half = -(-count // 2)
        for refs_of, first in ((below, HALO - (h - 1) * zc - count), (above, HALO + h * zc)):
            words = refs_of[h - 1][at : at + half]
            second = (words >= 1.5).astype(f32)
            all_ref[first : first + half] = words - 2.0 * second
            if count > half:
                all_ref[first + half : first + count] = second[: count - half]
    target_ref[...] = all_ref[HALO - 1 : HALO + zc + 1]

    def fill(plane):
        out = []
        for n in range(plan.win_block):
            at = plane + n
            inside = 1.0 - kind_of(plan, rank, at - HALO)[1]
            out.append((e0_ref, (at + 1, tiles), jnp.exp(-temper * all_ref[at]) * inside))
        store_all(out)

    over(0, win, plan.win_block, fill)

    def section(step, source, result, opening):
        e_ref = e_refs[source]
        reach = 2 + ITERS - step
        count = zc + 2 * reach
        erode(
            plan, rank, mask, y_ref, e_ref, e_refs[result], g_ref, cross_ref, base, -reach, count
        )
        spread(plan, y_ref, g_ref, zy_ref, base, -1, span, size)

        def point(plane):
            before = [None if opening else ts_ref[plane + n] for n in range(size)]
            for n in range(size):
                at = plane + n
                box = x_box(plan, mask, zy_ref, at)
                kind, outside = kind_of(plan, rank, at - 1)
                _, _, scaled = thin(e_ref[at - 1 + base, tiles], box, box_ref[kind], outside)
                ts_ref[at] = scaled * -LOG if opening else lift(scaled, before[n])[0]

        over(0, span, size, point)

    in_turn(section)

    def add(n, totals):
        ts = ts_ref[1 + n]
        return totals[0] + ts * p_ref[1 + n], totals[1] + ts

    zero = jnp.zeros((plan.tiles, LANES), f32)
    put_sums(plan, sums_ref, lax.fori_loop(0, zc, add, (zero,) * 2))


def put_sums(plan, ref, totals):
    lines = [jnp.sum(total, axis=0, keepdims=True) for total in totals]
    lines += [jnp.zeros((1, LANES), f32)] * (8 - len(lines))
    ref[...] = jnp.broadcast_to(jnp.concatenate(lines, axis=0)[None], (plan.ranks, 8, LANES))


def get_sums(ref, count):
    lines = jnp.sum(jnp.sum(ref[...], axis=0), axis=1, keepdims=True)
    return [lines[n : n + 1] for n in range(count)]


def forward_kernel(plan, *refs):
    hops = plan.hops
    pos_ref, bias_ref, label_ref, own_ref = refs[:4]
    refs = refs[4:]
    below, above = refs[:hops], refs[hops : 2 * hops]
    refs = refs[2 * hops :]
    far_ref, p_ref, sums_ref = refs[:3]
    e0_ref, e1_ref, g0_ref, g1_ref, zy_ref, s_ref, cross_ref, box_ref = refs[3:11]
    y_ref, record_ref, sem_ref = refs[11:]
    e_refs, g_refs = (e0_ref, e1_ref), (g0_ref, g1_ref)
    base, zc, size = plan.base, plan.zc, plan.block
    tiles = slice(8, 8 + plan.tiles)
    rank = pos_ref[0]
    mask = masks(plan)

    for ref in e_refs + g_refs:
        ref[...] = jnp.zeros_like(ref)
    zy_ref[...] = jnp.zeros_like(zy_ref)
    count_tables(plan, cross_ref, box_ref)
    y_matrix(plan, y_ref)
    e0_ref[base : base + zc, tiles] = own_ref[:zc]
    for h in range(1, hops + 1):
        n = zc if h < hops else plan.rest
        first = base - (h - 1) * zc - n
        e0_ref[first : first + n, tiles] = below[h - 1][:n]
        first = base + h * zc
        e0_ref[first : first + n, tiles] = above[h - 1][:n]
    e0_ref[base - 1, tiles] += own_ref[zc]
    e0_ref[base + zc, tiles] += own_ref[zc + 1]
    for h in range(1, hops + 1):
        if h < hops:
            e0_ref[base - h * zc - 1, tiles] += below[h - 1][zc]
            e0_ref[base + (h + 1) * zc, tiles] += above[h - 1][zc + 1]
            e0_ref[base - (h - 1) * zc, tiles] += below[h - 1][zc + 1]
            e0_ref[base + h * zc - 1, tiles] += above[h - 1][zc]
        else:
            e0_ref[base - (h - 1) * zc, tiles] += below[h - 1][plan.rest]
            e0_ref[base + h * zc - 1, tiles] += above[h - 1][plan.rest]

    def sigmoid(logits):
        small = jnp.exp(-jnp.abs(logits))
        part = 1.0 / (1.0 + small)
        return jnp.where(logits >= 0, part, small * part)

    for n in range(plan.span):
        p_ref[n] = sigmoid(e0_ref[base - 1 + n, tiles] + bias_ref[0])

    def fill(plane):
        out = []
        for n in range(plan.erode_block):
            at = plane + n
            inside = 1.0 - kind_of(plan, rank, at - base)[1]
            predict = sigmoid(e0_ref[at, tiles] + bias_ref[0])
            out.append((e0_ref, (at, tiles), jnp.exp(-temper * predict) * inside))
            out.append((g0_ref, at, jnp.exp(temper * predict) * inside))
        store_all(out)

    over(1, zc + 2 * HALO, plan.erode_block, fill)


    def out_copy(step):
        return pltpu.make_async_copy(record_ref.at[step], far_ref.at[step], sem_ref.at[step])

    def section(step, source, result, opening):
        e_ref, g_ref, after_ref = e_refs[source], g_refs[source], g_refs[result]
        reach = 1 + ITERS - step
        count = zc + 2 * reach
        erode(
            plan, rank, mask, y_ref, e_ref, e_refs[result], after_ref, cross_ref, base, -reach,
            count,
        )
        spread(plan, y_ref, after_ref, zy_ref, base, 0, zc, size)
        record_ref[step, 3 * zc :] = after_ref[base - 1 : base + zc + 1]

        def point(plane):
            before = [None if opening else s_ref[plane + n] for n in range(size)]
            for n in range(size):
                at = plane + n
                box = x_box(plan, mask, zy_ref, at)
                kind, outside = kind_of(plan, rank, at)
                e = e_ref[at + base, tiles]
                over_box, slope, scaled = thin(e, box, box_ref[kind], outside)
                if opening:
                    grown, a = scaled * -LOG, slope
                    record_ref[step, at] = jnp.ones_like(a)
                else:
                    s = before[n]
                    grown, rate = lift(scaled, s)
                    a = rate * (1.0 - s) * slope
                    record_ref[step, at] = 1.0 + rate * scaled * LOG
                s_ref[at] = grown
                record_ref[step, at + zc] = a * over_box
                record_ref[step, at + 2 * zc] = a * g_ref[at + base]

        over(0, zc, size, point)
        out_copy(step).start()

    in_turn(section)

    def add(n, totals):
        ps, predict, target = s_ref[n], p_ref[1 + n], label_ref[n]
        terms = (ps * target, ps, predict * target, predict, target)
        return tuple(total + term for total, term in zip(totals, terms))

    zero = jnp.zeros((plan.tiles, LANES), f32)
    put_sums(plan, sums_ref, lax.fori_loop(0, zc, add, (zero,) * 5))

    def drain(step, carry):
        out_copy(step).wait()
        return carry

    lax.fori_loop(0, SECTIONS, drain, 0)


def backward_kernel(plan, *refs):
    hops = plan.back_hops
    pos_ref, sums_ref, label_ref, far_ref, mine_ref = refs[:5]
    up, down = refs[5 : 5 + hops], refs[5 + hops : 5 + 2 * hops]
    w_ref, push_ref, wt_ref, zy_ref, pull0_ref, pull1_ref, cross_ref = refs[5 + 2 * hops : -3]
    y_ref, record_ref, sem_ref = refs[-3:]
    pull_refs = (pull0_ref, pull1_ref)
    rank = pos_ref[0]
    zc, base = plan.zc, plan.pull_base
    tiles = slice(8, 8 + plan.tiles)
    mask = masks(plan)

    def in_copy(left):
        return pltpu.make_async_copy(far_ref.at[left], record_ref.at[left], sem_ref.at[left])

    for left in reversed(range(SECTIONS)):
        in_copy(left).start()
    s1, s2 = get_sums(sums_ref, 2)
    prec = (s1 + 1.0) / (s2 + 1.0)
    push_ref[...] = jnp.zeros_like(push_ref)
    wt_ref[...] = jnp.zeros_like(wt_ref)
    zy_ref[...] = jnp.zeros_like(zy_ref)
    for ref in pull_refs:
        ref[...] = jnp.zeros_like(ref)
    count_tables(plan, cross_ref, None)
    y_matrix(plan, y_ref)
    w_ref[...] = label_ref[...] - prec[None]

    def section(step, source, result, ending):
        pull_ref, next_ref = pull_refs[source], pull_refs[result]
        left = SECTIONS - 1 - step
        in_copy(left).wait()

        def push(at):
            out = []
            for n in range(plan.block):
                w = w_ref[at + n]
                out.append((push_ref, at + n + 2, w * record_ref[left, at + n + zc]))
                out.append((wt_ref, at + n + base, w * record_ref[left, at + n + 2 * zc]))
                out.append((w_ref, at + n, w * record_ref[left, at + n]))
            store_all(out)

        over(0, zc, plan.block, push)

        def widen(at):
            size = plan.span_block
            part = push_ref[pl.ds(at, size)] + push_ref[pl.ds(at + 1, size)]
            part = part + push_ref[pl.ds(at + 2, size)]
            zy_ref[pl.ds(at, size), tiles] = part + y_neighbours(y_ref, part)

        over(0, plan.span, plan.span_block, widen)

        def pull(at):
            out = []
            for n in range(plan.span_block):
                box = x_box(plan, mask, zy_ref, at + n)
                inverse = cross_ref[kind_of(plan, rank, at + n - 1)[0]]
                grown = record_ref[left, at + n + 3 * zc]
                spot = at + n - 1 + base
                old = pull_ref[spot, tiles]
                out.append((pull_ref, (spot, tiles), old - grown * grown * box * inverse))
            store_all(out)

        over(0, plan.span, plan.span_block, pull)
        reach = 2 + step

        def join(plane):
            beside = y_neighbours(y_ref, pull_ref[pl.ds(plane + base, plan.erode_block), tiles])
            for n in range(plan.erode_block):
                at = plane + n + base
                cur = pull_ref[at, tiles]

                def load(offset, at=at):
                    return pull_ref[at, 8 + offset : 8 + offset + plan.tiles]

                total = cur + pull_ref[at - 1, tiles] + pull_ref[at + 1, tiles]
                total = total + x_neighbours(plan, mask, load, cur)
                total = total + beside[n] + wt_ref[at]
                if not ending:
                    total = total * cross_ref[kind_of(plan, rank, plane + n)[0]]
                next_ref[at, tiles] = total

        over(-reach, zc + 2 * reach, plan.erode_block, join)

    def pair(n, carry):
        section(2 * n, 0, 1, False)
        section(2 * n + 1, 1, 0, False)
        return carry

    lax.fori_loop(0, ITERS // 2, pair, 0)
    section(ITERS, 0, 1, True)
    mine_ref[...] = pull1_ref[base - 1 : base + zc + 1, tiles]
    for h in range(1, hops + 1):
        n = plan.back_count(h)
        first = base + h * zc - 1
        up[h - 1][...] = pull1_ref[first : first + n, tiles]
        first = base + (1 - h) * zc - n + 1
        down[h - 1][...] = pull1_ref[first : first + n, tiles]


def finish_kernel(plan, *refs):
    hops = plan.back_hops
    pos_ref, sums_ref, skel_ref, p_ref, target_ref, ts_ref, mine_ref = refs[:7]
    below, above = refs[7 : 7 + hops], refs[7 + hops : 7 + 2 * hops]
    out_ref, loss_ref, bias_ref, h_ref, grad_ref = refs[7 + 2 * hops :]
    rank = pos_ref[0]
    zc = plan.zc
    s1, s2, s5, s6, s7 = get_sums(sums_ref, 5)
    s3, s4 = get_sums(skel_ref, 2)
    prec = (s1 + 1.0) / (s2 + 1.0)
    sens = (s3 + 1.0) / (s4 + 1.0)
    both = prec + sens
    volume = s6 + s7 + 1.0
    cl_loss = 1.0 - 2.0 * prec * sens / both
    dice_loss = 1.0 - (2.0 * s5 + 1.0) / volume
    loss_ref[...] = jnp.broadcast_to(0.5 * dice_loss + 0.5 * cl_loss, (8, LANES))
    l0 = -(sens / both) * (sens / both) / (s2 + 1.0)
    l2 = -(prec / both) * (prec / both) / (s4 + 1.0)
    l4 = -1.0 / volume
    l5 = 0.5 * (2.0 * s5 + 1.0) / (volume * volume)

    h_ref[...] = mine_ref[...]
    for h in range(1, hops + 1):
        n = plan.back_count(h)
        h_ref[:n] += below[h - 1][...]
        h_ref[plan.span - n :] += above[h - 1][...]

    total = jnp.zeros((plan.tiles, LANES), f32)
    for n in range(plan.span):
        inside = 1.0 - kind_of(plan, rank, n - 1)[1]
        predict = p_ref[n]
        skel = l0 * jnp.exp(-temper * predict) * h_ref[n]
        whole = skel + l2 * ts_ref[n] + l4 * target_ref[n] + l5
        grad = whole * predict * (1.0 - predict) * inside
        grad_ref[n * plan.tiles : (n + 1) * plan.tiles] = grad
        if 1 <= n <= zc:
            total = total + grad
    bias_ref[...] = jnp.sum(total.reshape(-1, 8, LANES), axis=0)
    lane = lane_iota((1, LANES))

    def column(tile):
        return [
            grad_ref[pl.ds(plan.tiles + tile, zc, stride=plan.tiles)],
            grad_ref[tile : tile + 1],
            grad_ref[(zc + 1) * plan.tiles + tile : (zc + 1) * plan.tiles + tile + 1],
        ]

    for a in range(plan.gx):
        pieces = [column(a * plan.own + q) for q in range(plan.own)]
        zero = [jnp.zeros((zc, LANES), f32)] + [jnp.zeros((1, LANES), f32)] * 2
        after = column((a + 1) * plan.own) if a < plan.gx - 1 else zero
        before = column(a * plan.own - 1) if a > 0 else zero
        if plan.shared:
            pieces.append(
                [
                    jnp.where(lane < plan.Y, x, 0.0) + jnp.where(lane >= LANES - plan.Y, y, 0.0)
                    for x, y in zip(after, before)
                ]
            )
        else:
            pieces += [after, before]
        edges = [edge for piece in pieces for edge in piece[1:]]
        rows = plan.R16
        edges += [jnp.zeros((1, LANES), f32)] * (plan.extra16 * rows - len(edges))
        whole = [piece[0] for piece in pieces]
        if rows > zc:
            fill = jnp.zeros((rows - zc, LANES), f32)
            whole = [jnp.concatenate([piece, fill], axis=0) for piece in whole]
        whole += [
            jnp.concatenate(edges[n * rows : (n + 1) * rows], axis=0) for n in range(plan.extra16)
        ]
        for q, piece in enumerate(whole):
            piece = piece.astype(bf16)
            for b in range(plan.gy):
                out_ref[a * plan.gy + b, q] = piece


def weight_kernel(
    plan, pos_ref, far_ref, bias_ref, got_ref, gw_ref, g_ref, dw_ref, f_ref, sem_ref
):
    copies = stream(plan, far_ref, f_ref, sem_ref)
    rows, inner = plan.Y, plan.ch * plan.ny
    zc, nz = plan.zc, plan.nz
    lane = lane_iota((rows, nz))
    places = {}
    for x in range(-1, plan.nx + 1):
        tile, first = plan.slot(x)
        places.setdefault(tile, {})[first] = x
    for tile in range(plan.sent):
        order = [plan.member_now(j, pos_ref) for j in range(plan.members)]
        stack = [got_ref[p, tile].astype(f32)[:zc] for p in order]
        turned = jnp.concatenate(stack, axis=0).T
        ends = []
        for end, p in ((0, order[0]), (1, order[-1])):
            n = 2 * tile + end
            row = got_ref[p, plan.sent + n // plan.R16].astype(f32)
            ends.append(row[n % plan.R16 : n % plan.R16 + 1])
        ends = jnp.concatenate(ends + [jnp.zeros((LANES - 2, LANES), f32)], axis=0).T
        for first, x in places[tile].items():
            g = turned[first : first + rows]
            end = ends[first : first + rows]
            down = jnp.where(lane == nz - 1, pltpu.roll(end, nz - 2, 1), pltpu.roll(g, nz - 1, 1))
            up = jnp.where(lane == 0, end, pltpu.roll(g, 1, 1))
            g_ref[x + 1] = jnp.concatenate([down, g, up], axis=0).astype(bf16)

    dw_ref[...] = jnp.zeros_like(dw_ref)

    width = plan.nx // PARTS
    for n in range(PARTS):
        copies[n].wait()
        dw_ref[...] += lax.dot_general(
            moved_columns(g_ref, n * width, width),
            columns(plan, f_ref, n * width, width),
            (((1,), (1,)), ((), ())),
            preferred_element_type=f32,
        )

    tap_y = tap_condition(plan, pos_ref[1], (rows, inner), 0, 1)
    taps = []
    for t in range(27):
        i, j, k = t // 9, t // 3 % 3, t % 3
        at = (3 * i + k) * rows
        taps.append(jnp.sum(jnp.where(tap_y == j, dw_ref[at : at + rows], 0.0), axis=0, keepdims=True))
    taps += [jnp.zeros((1, inner), f32)] * 5
    taps = jnp.concatenate(taps, axis=0)
    high = taps.astype(bf16)
    taps = taps - high.astype(f32)
    middle = taps.astype(bf16)
    low = (taps - middle.astype(f32)).astype(bf16)
    place = (
        lax.broadcasted_iota(jnp.int32, (inner, LANES), 0) // plan.ny
        == lax.broadcasted_iota(jnp.int32, (inner, LANES), 1)
    )
    sums = jnp.dot(
        jnp.concatenate([high, middle, low], axis=0),
        place.astype(f32).astype(bf16),
        preferred_element_type=f32,
    )
    sums = sums[0:32] + sums[32:64] + sums[64:96]
    total = sums[0:8]
    for n in range(1, 4):
        total = total + pltpu.roll(sums[8 * n : 8 * n + 8], 32 * n, 1)
    spot = (row_iota((8, LANES)) == 3) & (lane_iota((8, LANES)) == 96)
    total = jnp.where(spot, jnp.sum(bias_ref[...]), total)
    gw_ref[...] = jnp.broadcast_to(total[None], (plan.ranks, 8, LANES))


def wide_kernel(plan, pos_ref, wt_ref, after_ref, wide_ref):
    del after_ref
    rows, inner, bands = plan.Y, plan.ch * plan.ny, 9 * plan.Y
    spread = (
        lax.broadcasted_iota(jnp.int32, (inner, plan.ch), 0) // plan.ny
        == lax.broadcasted_iota(jnp.int32, (inner, plan.ch), 1)
    )
    spread = spread.astype(f32).astype(bf16)
    tap_y = tap_condition(plan, pos_ref[1], (inner, bands), 1, 0)
    wide = jnp.zeros((inner, bands), f32)
    tap = lax.broadcasted_iota(jnp.int32, (27, bands), 0)
    band = lax.broadcasted_iota(jnp.int32, (27, bands), 1) // rows
    for j in range(3):
        pick = (tap == 9 * (band // 3) + 3 * j + band % 3).astype(f32).astype(bf16)
        chosen = jnp.dot(wt_ref[...], pick, preferred_element_type=f32).astype(bf16)
        full = jnp.dot(spread, chosen, preferred_element_type=f32)
        wide = jnp.where(tap_y == j, full, wide)
    wide_ref[...] = wide.astype(bf16)


def feature_kernel(plan, wide_ref, g_ref, after_ref, gf_ref):
    del after_ref
    width = plan.nx // PARTS
    for n in range(PARTS):
        out = jnp.dot(
            wide_ref[...],
            moved_columns(g_ref, n * width, width),
            preferred_element_type=f32,
        )
        for x in range(width):
            part = out[:, x * plan.nz : (x + 1) * plan.nz].astype(bf16)
            gf_ref[:, n * width + x] = part.reshape(plan.ch, plan.ny, plan.nz)


def final_kernel(plan, got_ref, gw_ref, gb_ref):
    total = jnp.sum(got_ref[...], axis=0)
    for n in range(4):
        count = min(8, 27 - 8 * n)
        gw_ref[8 * n : 8 * n + count] = total[:count, 32 * n : 32 * n + plan.ch]
    gb_ref[...] = total[3:4, 96:97]


VMEM = pl.BlockSpec(memory_space=pltpu.VMEM)
SMEM = pl.BlockSpec(memory_space=pltpu.SMEM)
ANY = pl.BlockSpec(memory_space=pl.ANY)
FAR = pl.BlockSpec(memory_space=pltpu.HBM)
MIB = 1024 * 1024


def shape(dims, dtype=f32):
    return jax.ShapeDtypeStruct(dims, dtype)


def held(dims, dtype):
    if len(dims) < 2:
        return 4096
    size = jnp.dtype(dtype).itemsize
    rows = 8 * 4 // size
    total = -(-dims[-2] // rows) * rows * -(-dims[-1] // LANES) * LANES * size
    for n in dims[:-2]:
        total *= n
    return total


def limits(arrays, scratch, micros):
    total = sum(held(a.shape, a.dtype) for a in arrays)
    total += sum(held(a.shape, a.dtype) for a in scratch if len(a.shape) > 1)
    limit = min(63 * MIB, total + total // 8 + 4 * MIB)
    return dict(
        compiler_params=pltpu.CompilerParams(vmem_limit_bytes=limit),
        cost_estimate=pl.CostEstimate(
            flops=0, transcendentals=0, bytes_accessed=int(micros * 2.5e4)
        ),
    )


def per_device(mesh_shape, features, weight, bias, label):
    plan = Plan(mesh_shape, features.shape)
    members, sent, tiles = plan.members, plan.sent, plan.tiles
    inner, bands = plan.ch * plan.ny, 9 * plan.Y
    x, y, z = (lax.axis_index(axis).astype(jnp.int32) for axis in ALL_AXES)
    mine = y * plan.gx + jnp.where(y % 2 == 0, x, plan.gx - 1 - x)
    place = z * members + jnp.where(z % 2 == 0, mine, members - 1 - mine)
    pos = jnp.stack([place, y])

    def call(
        kernel, out_shape, in_specs, operands, micros, scratch=(), out_specs=None
    ):
        outs = jax.tree.leaves(out_shape)
        ins = [a for spec, a in zip(in_specs, operands) if spec is VMEM]
        return pl.pallas_call(
            functools.partial(kernel, plan),
            out_shape=out_shape,
            in_specs=in_specs,
            out_specs=out_specs or jax.tree.map(lambda s: VMEM, out_shape),
            scratch_shapes=list(scratch),
            **limits(ins + outs, scratch, micros),
        )(*operands)

    def exchange(array):
        return lax.all_to_all(array, GROUP, 0, 0, tiled=True)

    def everywhere(array):
        return lax.all_to_all(array, ALL_AXES, 0, 0, tiled=True)

    def hop(array, distance):
        def device(r):
            z = r // members
            return plan.member(r % members, z % 2 == 1) * plan.gz + z

        pairs = [
            (device(r), device(r + distance))
            for r in range(plan.ranks)
            if 0 <= r + distance < plan.ranks
        ]
        return lax.ppermute(array, ALL_AXES, pairs)

    turned = weight.T
    features, weight, label = (
        pltpu.with_memory_space_constraint(a, pltpu.HBM) for a in (features, weight, label)
    )
    features_near = [pltpu.VMEM(features.shape, bf16), pltpu.SemaphoreType.DMA((PARTS,))]
    sent_logits = call(
        conv_kernel,
        shape((members, sent + plan.extra, plan.R, LANES)),
        [SMEM, VMEM, FAR, VMEM],
        (pos, weight, features, label),
        7,
        [
            pltpu.VMEM((bands, inner), bf16),
            pltpu.VMEM((plan.nx + 2, 3 * plan.Y, plan.nz), f32),
        ]
        + features_near,
    )

    def planes(array):
        return array.reshape(-1, tiles, LANES)

    zc, rest = plan.zc, plan.rest
    short = shape(((rest + 1 + -(-rest // 2)) * tiles, LANES))
    whole, label_own, head, tail = call(
        gather_kernel,
        [
            shape(((zc + 2 + -(-zc // 2)) * tiles, LANES)),
            shape((zc * tiles, LANES)),
            short,
            short,
        ],
        [VMEM],
        (exchange(sent_logits),),
        1.5,
    )
    whole, label_own, head, tail = (planes(part) for part in (whole, label_own, head, tail))
    around = [
        hop(whole if h < plan.hops else part, sign * h)
        for sign, part in ((1, tail), (-1, head))
        for h in range(1, plan.hops + 1)
    ]

    slab = (zc, tiles, LANES)
    span = (plan.span, tiles, LANES)
    everyone = shape((plan.ranks, 8, LANES))
    table = pltpu.VMEM((3, tiles, LANES), f32)

    records = pltpu.HBM((SECTIONS, plan.records, tiles, LANES), f32)
    y_near = pltpu.VMEM((2 * LANES, LANES), bf16)
    record_near = [
        y_near,
        pltpu.VMEM(records.shape, f32),
        pltpu.SemaphoreType.DMA((SECTIONS,)),
    ]
    record, predict, sums = call(
        forward_kernel,
        [records, shape(span), everyone],
        [SMEM, SMEM] + [VMEM] * (2 + 2 * plan.hops),
        (pos, bias, label_own, whole, *around),
        11,
        [
            pltpu.VMEM((plan.planes, plan.pad, LANES), f32),
            pltpu.VMEM((plan.planes, plan.pad, LANES), f32),
            pltpu.VMEM((plan.planes, tiles, LANES), f32),
            pltpu.VMEM((plan.planes, tiles, LANES), f32),
            pltpu.VMEM((zc, plan.pad, LANES), f32),
            pltpu.VMEM(slab, f32),
            table,
            table,
        ]
        + record_near,
        [FAR, VMEM, VMEM],
    )
    record = pltpu.with_memory_space_constraint(record, pltpu.HBM)
    sums = everywhere(sums)
    room = plan.win + 2 + plan.erode_block
    target, ts, skel_sums = call(
        target_kernel,
        [shape(span), shape(span), everyone],
        [SMEM] + [VMEM] * (2 + 2 * plan.hops),
        (pos, predict, label_own, *around),
        13,
        [
            pltpu.VMEM((plan.win, tiles, LANES), f32),
            pltpu.VMEM((room, plan.pad, LANES), f32),
            pltpu.VMEM((room, plan.pad, LANES), f32),
            pltpu.VMEM((room, tiles, LANES), f32),
            pltpu.VMEM((plan.span, plan.pad, LANES), f32),
            table,
            table,
            y_near,
        ],
    )
    skel_sums = everywhere(skel_sums)
    outer = [
        shape((plan.back_count(h), tiles, LANES)) for h in range(1, plan.back_hops + 1)
    ]
    mine, *outer = call(
        backward_kernel,
        [shape(span)] + outer * 2,
        [SMEM, VMEM, VMEM, FAR],
        (pos, sums, label_own, record),
        11,
        [
            pltpu.VMEM(slab, f32),
            pltpu.VMEM((zc + 4, tiles, LANES), f32),
            pltpu.VMEM((plan.pull_planes, tiles, LANES), f32),
            pltpu.VMEM((plan.span, plan.pad, LANES), f32),
            pltpu.VMEM((plan.pull_planes, plan.pad, LANES), f32),
            pltpu.VMEM((plan.pull_planes, plan.pad, LANES), f32),
            table,
        ]
        + record_near,
    )
    wide = call(
        wide_kernel, shape((inner, bands), bf16), [SMEM, VMEM, ANY], (pos, turned, mine), 2
    )
    beyond = []
    for sign, arrays in ((1, outer[: plan.back_hops]), (-1, outer[plan.back_hops :])):
        for h in range(1, plan.back_hops + 1):
            beyond.append(hop(arrays[h - 1], sign * h))
    grad_sent, loss, bias_part = call(
        finish_kernel,
        [
            shape((members, sent + plan.extra16, plan.R16, LANES), bf16),
            shape((8, LANES)),
            shape((8, LANES)),
        ],
        [SMEM] + [VMEM] * (6 + 2 * plan.back_hops),
        (pos, sums, skel_sums, predict, target, ts, mine, *beyond),
        2,
        [pltpu.VMEM(span, f32), pltpu.VMEM((plan.span * tiles, LANES), f32)],
    )

    moved = shape((plan.nx + 2, 3 * plan.Y, plan.nz), bf16)
    partial, g = call(
        weight_kernel,
        [shape((plan.ranks, 8, LANES)), moved],
        [SMEM, FAR, VMEM, VMEM],
        (pos, features, bias_part, exchange(grad_sent)),
        5,
        [pltpu.VMEM((bands, inner), f32)] + features_near,
    )
    grad_features = call(
        feature_kernel,
        shape(features.shape, bf16),
        [VMEM, VMEM, ANY],
        (wide, g, partial),
        5,
    )
    grad_weight, grad_bias = call(
        final_kernel,
        [shape((27, plan.ch)), shape((1, 1))],
        [VMEM],
        (everywhere(partial),),
        1.5,
    )
    return (loss[0, :1], grad_features, grad_weight, grad_bias.reshape(1))


def solution(mesh):
    in_specs = (P(None, "gx", "gy", "gz"), P(), P(), P("gx", "gy", "gz"))
    out_specs = (P(), P(None, "gx", "gy", "gz"), P(), P())

    def body(*args):
        return per_device(dict(mesh.shape), *args)

    return jax.shard_map(
        body, mesh=mesh, in_specs=in_specs, out_specs=out_specs, check_vma=False
    )
```

```python
import functools

import jax
import jax.numpy as jnp
from jax import lax
from jax.experimental import pallas as pl
from jax.experimental.pallas import tpu as pltpu
from jax.sharding import PartitionSpec as P

ITERS = 10
SECTIONS = ITERS + 1
LANES = 128
HALO = SECTIONS + 2
BACK = SECTIONS + 1

BLOCK = 32
SPAN_BLOCK = 40
ERODE_BLOCK = 20

temper = 20.0
sharpness = 40.0

GROUP = ("gx", "gy")
ALL_AXES = ("gx", "gy", "gz")
f32 = jnp.float32
bf16 = jnp.bfloat16


def up8(value):
    return -(-value // 8) * 8


class Plan:
    def __init__(self, mesh_shape, block):
        self.ch, self.nx, self.ny, self.nz = block
        self.gx, self.gy, self.gz = (mesh_shape[a] for a in ALL_AXES)
        self.members = self.gx * self.gy
        self.ranks = self.members * self.gz
        self.X = self.nx * self.gx
        self.Y = self.ny * self.gy
        self.Z = self.nz * self.gz
        assert LANES % self.Y == 0 and self.nz == LANES
        assert self.nz % self.members == 0
        self.zc = self.nz // self.members
        self.per = LANES // self.Y
        assert self.nx % self.per == 0
        self.tiles = self.X // self.per
        self.own = self.nx // self.per
        self.shared = self.per > 1
        self.sent = self.own + (1 if self.shared else 2)
        self.R = up8(self.zc)
        self.extra = -(-2 * self.sent // self.R)
        self.R16 = -(-self.zc // 16) * 16
        self.extra16 = -(-2 * self.sent // self.R16)
        self.pad = self.tiles + 16
        self.win = self.zc + 2 * HALO
        self.span = self.zc + 2
        self.block = self.blocks_of(self.zc, BLOCK)
        self.span_block = self.blocks_of(self.span, SPAN_BLOCK)
        self.win_block = self.blocks_of(self.win, 32)
        self.erode_block = max(1, ERODE_BLOCK * 8 // self.tiles)
        self.base = HALO + 1
        self.planes = self.zc + 2 * HALO + 2 + self.erode_block
        self.pull_base = BACK + 2
        self.pull_planes = self.zc + 2 * BACK + 4 + self.erode_block
        self.hops = -(-HALO // self.zc)
        self.rest = HALO - (self.hops - 1) * self.zc
        self.records = 3 * self.zc + self.span
        assert self.ny == 16 and self.gy > 1
        self.back_hops = -(-(BACK + 1) // self.zc)

    def back_count(self, h):
        return min(self.zc + BACK + 1 - h * self.zc, self.span)

    def blocks_of(self, count, most):
        fits = [n for n in range(1, count + 1) if count % n == 0 and n * self.tiles <= 8 * most]
        return fits[-1] if fits else 1

    def slab(self, member):
        x, y = member // self.gy, member % self.gy
        return y * self.gx + (x if y % 2 == 0 else self.gx - 1 - x)

    def member(self, slab, odd):
        slab = self.members - 1 - slab if odd else slab
        return next(p for p in range(self.members) if self.slab(p) == slab)

    def member_now(self, slab, pos_ref):
        odd = pos_ref[0] // self.members % 2 == 1
        return jnp.where(odd, self.member(slab, True), self.member(slab, False))

    def label_lane(self, member_y):
        return 0 if member_y == self.gy - 1 else (member_y + 1) * self.ny + 8

    def slot(self, x):
        if 0 <= x < self.nx:
            return x // self.per, (x % self.per) * self.Y
        if x == self.nx:
            return self.own, 0
        return self.sent - 1, LANES - self.Y


def lane_iota(shape):
    return lax.broadcasted_iota(jnp.int32, shape, len(shape) - 1)


def row_iota(shape):
    return lax.broadcasted_iota(jnp.int32, shape, len(shape) - 2)


def place_of(plan, x):
    return x % plan.tiles, x // plan.tiles


def in_group(plan, group):
    return lane_iota((1, LANES)) // plan.Y == group


def x_neighbours(plan, ref, at):
    return ref[at, 7 : 7 + plan.tiles] + ref[at, 9 : 9 + plan.tiles]


def wrap(plan, ref, at, value):
    tiles = plan.tiles
    ref[at, 8 : 8 + tiles] = value
    if plan.per == 1:
        return
    lane = lane_iota((8, LANES))
    lower = pltpu.roll(value[tiles - 8 :], plan.Y, 1)
    upper = pltpu.roll(value[:8], LANES - plan.Y, 1)
    ref[at, 7:8] = jnp.where(lane < plan.Y, 0.0, lower)[7:8]
    ref[at, 8 + tiles : 9 + tiles] = jnp.where(lane >= LANES - plan.Y, 0.0, upper)[0:1]


def y_matrix(plan, ref):
    row = row_iota((2 * LANES, LANES)) % LANES
    lane = lane_iota((2 * LANES, LANES))
    near = (row == lane - 1) | (row == lane + 1)
    ref[...] = (near & (row // plan.Y == lane // plan.Y)).astype(f32).astype(bf16)


def y_neighbours(ref, block):
    flat = block.reshape(-1, LANES)
    high = flat.astype(bf16)
    low = (flat - high.astype(f32)).astype(bf16)
    both = jnp.concatenate([high, low], axis=1)
    return jnp.dot(both, ref[...], preferred_element_type=f32).reshape(block.shape)


def count_tables(plan, cross_ref, box_ref):
    lane = lane_iota((plan.tiles, LANES))
    y, x = lane % plan.Y, lane // plan.Y * plan.tiles + row_iota((plan.tiles, LANES))

    def along(spot, size):
        return 3.0 - (spot == 0).astype(f32) - (spot == size - 1).astype(f32)

    cx, cy = along(x, plan.X), along(y, plan.Y)
    for kind, cz in ((1, 2.0), (2, 3.0)):
        if cross_ref is not None:
            cross_ref[kind] = 1.0 / (cx + cy + cz - 2.0)
        if box_ref is not None:
            box_ref[kind] = 1.0 / (cx * cy * cz)
    for ref in (cross_ref, box_ref):
        if ref is not None:
            ref[0] = jnp.zeros((plan.tiles, LANES), f32)


def kind_of(plan, rank, plane):
    z = rank * plan.zc + plane
    inside = (z >= 0) & (z < plan.Z)
    edge = (z == 0) | (z == plan.Z - 1)
    return jnp.where(inside, jnp.where(edge, 1, 2), 0), jnp.where(inside, 0.0, 1.0)


def store_all(pairs):
    for ref, at, value in pairs:
        ref[at] = value


def over(first, count, size, body):
    def at(n, carry):
        body(first + n * size)
        return carry

    lax.fori_loop(0, (count + size - 1) // size, at, 0)


def tap_condition(plan, member_y, shape, y_dim, in_dim):
    y = lax.broadcasted_iota(jnp.int32, shape, y_dim) % plan.Y
    own = lax.broadcasted_iota(jnp.int32, shape, in_dim) % plan.ny
    return own + member_y * plan.ny - y + 1


PARTS = 4


def stream(plan, far_ref, near_ref, sem_ref):
    width = plan.nx // PARTS
    copies = []
    for n in range(PARTS):
        span = pl.ds(n * width, width)
        copies.append(
            pltpu.make_async_copy(far_ref.at[:, span], near_ref.at[:, span], sem_ref.at[n])
        )
        copies[-1].start()
    return copies


def columns(plan, ref, first, count):
    blocks = [ref[:, x].reshape(-1, plan.nz) for x in range(first, first + count)]
    return jnp.concatenate(blocks, axis=1)


def moved_columns(ref, first, count):
    blocks = [
        jnp.concatenate([ref[x + 2], ref[x + 1], ref[x]], axis=0)
        for x in range(first, first + count)
    ]
    return jnp.concatenate(blocks, axis=1)


def conv_kernel(
    plan, pos_ref, w_ref, far_ref, label_ref, out_ref, wide_ref, acc_ref, f_ref, sem_ref
):
    width = plan.nx // PARTS
    copies = stream(plan, far_ref, f_ref, sem_ref)
    rows, inner = plan.Y, plan.ch * plan.ny
    spread = (
        lax.broadcasted_iota(jnp.int32, (plan.ch, inner), 0)
        == lax.broadcasted_iota(jnp.int32, (plan.ch, inner), 1) // plan.ny
    )
    taps = jnp.dot(
        w_ref[...], spread.astype(f32).astype(bf16), preferred_element_type=f32
    )
    tap_y = tap_condition(plan, pos_ref[1], (rows, inner), 0, 1)
    for i in range(3):
        for k in range(3):
            band = jnp.zeros((rows, inner), f32)
            for j in range(3):
                t = 9 * i + 3 * j + k
                band = jnp.where(tap_y == j, taps[t : t + 1], band)
            at = (3 * i + k) * rows
            wide_ref[at : at + rows] = band.astype(bf16)
    acc_ref[...] = jnp.zeros_like(acc_ref)

    for n in range(PARTS):
        copies[n].wait()
        first = n * width
        out = jnp.dot(
            wide_ref[...], columns(plan, f_ref, first, width), preferred_element_type=f32
        )
        for slot in range(first, first + width + 2):
            terms = [
                out[3 * i * rows : 3 * (i + 1) * rows, (x - first) * plan.nz : (x - first + 1) * plan.nz]
                for i in range(3)
                for x in (slot - 2 + i,)
                if first <= x < first + width
            ]
            acc_ref[slot] += functools.reduce(jnp.add, terms)

    out_ref[...] = jnp.zeros_like(out_ref)
    places = {}
    for x in range(-1, plan.nx + 1):
        tile, lane = plan.slot(x)
        places.setdefault(tile, {})[lane] = x
    lane = lane_iota((rows, plan.nz))
    words = [label_ref[x, 0:8] + 2 * label_ref[x, 8:16] for x in range(plan.nx)]
    first_group = jnp.where(
        pos_ref[1] == plan.gy - 1, 0, (pos_ref[1] + 1) * (plan.ny // 8) + 1
    )
    labelled = lax.broadcasted_iota(jnp.int32, (rows, plan.nz), 0) // 8 == first_group
    for tile in range(plan.sent):
        parts, spills = [], []
        for first in range(0, LANES, rows):
            x = places[tile].get(first)
            if x is None:
                parts.append(jnp.zeros((rows, plan.nz), f32))
                spills.append(jnp.zeros((rows, plan.nz), f32))
                continue
            low = acc_ref[x + 1, 0:rows]
            mid = acc_ref[x + 1, rows : 2 * rows]
            high = acc_ref[x + 1, 2 * rows : 3 * rows]
            total = mid + jnp.where(lane == 0, 0.0, pltpu.roll(low, 1, 1))
            total = total + jnp.where(lane == plan.nz - 1, 0.0, pltpu.roll(high, plan.nz - 1, 1))
            if 0 <= x < plan.nx:
                word = jnp.concatenate([words[x].astype(f32)] * (rows // 8), axis=0)
                total = total + jnp.where(labelled, word, 0.0)
            parts.append(total)
            spill = jnp.where(lane == 1, pltpu.roll(low, 2, 1), 0.0)
            spills.append(jnp.where(lane == 0, high, spill))
        turned = jnp.concatenate(parts, axis=0).T
        spill = jnp.concatenate(spills, axis=0).T
        for j in range(plan.members):
            p = plan.member_now(j, pos_ref)
            out_ref[p, tile, 0 : plan.zc] = turned[j * plan.zc : (j + 1) * plan.zc]
        for end, j in ((0, 0), (1, plan.members - 1)):
            n = 2 * tile + end
            at = plan.sent + n // plan.R
            p = plan.member_now(j, pos_ref)
            out_ref[p, at, n % plan.R : n % plan.R + 1] = spill[end : end + 1]


def gather_kernel(plan, got_ref, out_ref, label_ref, head_ref, tail_ref):
    tiles, zc, rest = plan.tiles, plan.zc, plan.rest
    lane = lane_iota((1, LANES))
    spot = lane % plan.Y

    def part(p, q):
        values = [got_ref[p, q, 0:zc]]
        for end in range(2):
            n = 2 * q + end
            at = plan.sent + n // plan.R
            values.append(got_ref[p, at, n % plan.R : n % plan.R + 1])
        return values

    parts = {t: [] for t in range(tiles)}
    labels = {t: jnp.zeros((zc, LANES), f32) for t in range(tiles)}

    def move(value, group, to):
        shift = (to - group) * plan.Y % LANES
        value = pltpu.roll(value, shift, 1) if shift else value
        return jnp.where(in_group(plan, to), value, 0.0)

    for a in range(plan.gx):
        for q in range(plan.sent):
            whole, label = [], jnp.zeros((zc, LANES), f32)
            for b in range(plan.gy):
                start = b * plan.ny
                values = part(a * plan.gy + b, q)
                mine = (spot >= start - 1) & (spot <= start + plan.ny)
                whole.append([jnp.where(mine, v, 0.0) for v in values])
                if q >= plan.own:
                    continue
                second = (values[0] >= 1.5).astype(f32)
                first = values[0] - 2.0 * second
                turn = start - plan.label_lane(b)
                first = pltpu.roll(first, turn % LANES, 1)
                second = pltpu.roll(second, (turn + 8) % LANES, 1)
                label = jnp.where((spot >= start) & (spot < start + 8), first, label)
                label = jnp.where((spot >= start + 8) & (spot < start + 16), second, label)
            whole = [functools.reduce(jnp.add, vs) for vs in zip(*whole)]
            ends = jnp.concatenate(whole[1:], axis=0)
            for n in range(plan.per):
                if q < plan.own:
                    x = plan.per * q + n
                elif plan.shared:
                    x = {0: plan.nx, plan.per - 1: -1}.get(n)
                else:
                    x = plan.nx if q == plan.own else -1
                if x is None or not 0 <= a * plan.nx + x < plan.X:
                    continue
                t, to = place_of(plan, a * plan.nx + x)
                parts[t].append((move(whole[0], n, to), move(ends, n, to)))
                if q < plan.own:
                    labels[t] = labels[t] + move(label, n, to)
    for t in range(tiles):
        whole, ends = (functools.reduce(jnp.add, vs) for vs in zip(*parts[t]))
        label_ref[pl.ds(t, zc, stride=tiles)] = labels[t]
        out_ref[pl.ds(t, zc, stride=tiles)] = whole
        out_ref[zc * tiles + t : zc * tiles + t + 1] = ends[0:1]
        out_ref[(zc + 1) * tiles + t : (zc + 1) * tiles + t + 1] = ends[1:2]

    def pack(ref, at, first, count):
        half = -(-count // 2)
        for n in range(half):
            word = label_ref[(first + n) * tiles : (first + n + 1) * tiles]
            if n + half < count:
                other = first + n + half
                word = word + 2.0 * label_ref[other * tiles : (other + 1) * tiles]
            ref[(at + n) * tiles : (at + n + 1) * tiles] = word

    pack(out_ref, zc + 2, 0, zc)
    head_ref[: rest * tiles] = out_ref[: rest * tiles]
    head_ref[rest * tiles : (rest + 1) * tiles] = out_ref[zc * tiles : (zc + 1) * tiles]
    pack(head_ref, rest + 1, 0, rest)
    tail_ref[: rest * tiles] = out_ref[(zc - rest) * tiles : zc * tiles]
    tail_ref[rest * tiles : (rest + 1) * tiles] = out_ref[(zc + 1) * tiles : (zc + 2) * tiles]
    pack(tail_ref, rest + 1, zc - rest, rest)


LOG = 1.0 / sharpness


def thin(e, box, inverse, outside):
    box = box + outside
    ratio = e * box * inverse + outside
    square = ratio * ratio
    more = 1.0 + square
    joint = 1.0 / (box * more)
    slope = joint * box
    return joint * more, slope, jnp.log(square * slope)


def lift(scaled, s):
    small = jnp.exp(scaled * (s - 1.0))
    more = 1.0 + small
    return s + jnp.log(more) * LOG, small * (1.0 / more)


def erode(plan, rank, y_ref, source, result, grown_ref, table_ref, base, first, count):
    tiles = slice(8, 8 + plan.tiles)

    def body(plane):
        beside = y_neighbours(y_ref, source[pl.ds(plane + base, plan.erode_block), tiles])
        for n in range(plan.erode_block):
            at = plane + n + base
            total = source[at, tiles] + source[at - 1, tiles] + source[at + 1, tiles]
            total = total + x_neighbours(plan, source, at) + beside[n]
            kind, outside = kind_of(plan, rank, plane + n)
            total = total * table_ref[kind]
            wrap(plan, result, at, total)
            grown_ref[at] = 1.0 / (total + outside) - outside

    over(first, count, plan.erode_block, body)


def spread(plan, y_ref, grown_ref, zy_ref, base, first, count, size):
    def body(plane):
        at = plane + base
        part = grown_ref[pl.ds(at - 1, size)] + grown_ref[pl.ds(at, size)]
        part = part + grown_ref[pl.ds(at + 1, size)]
        part = part + y_neighbours(y_ref, part)
        for n in range(size):
            wrap(plan, zy_ref, plane - first + n, part[n])

    over(first, count, size, body)


def in_turn(section):
    section(0, 0, 1, True)

    def pair(n, carry):
        section(2 * n + 1, 1, 0, False)
        section(2 * n + 2, 0, 1, False)
        return carry

    lax.fori_loop(0, ITERS // 2, pair, 0)


def x_box(plan, zy_ref, at):
    return zy_ref[at, 8 : 8 + plan.tiles] + x_neighbours(plan, zy_ref, at)


def target_kernel(plan, *refs):
    hops = plan.hops
    pos_ref, p_ref, own_ref = refs[:3]
    below, above = refs[3 : 3 + hops], refs[3 + hops : 3 + 2 * hops]
    target_ref, ts_ref, sums_ref = refs[3 + 2 * hops : 6 + 2 * hops]
    all_ref, e0_ref, e1_ref, g_ref, zy_ref, cross_ref, box_ref, y_ref = refs[6 + 2 * hops :]
    zc, win, span = plan.zc, plan.win, plan.span
    size = plan.span_block
    base = HALO + 1
    tiles = slice(8, 8 + plan.tiles)
    rank = pos_ref[0]
    count_tables(plan, cross_ref, box_ref)
    y_matrix(plan, y_ref)
    e_refs = (e0_ref, e1_ref)
    e0_ref[...] = jnp.zeros_like(e0_ref)
    e1_ref[...] = jnp.zeros_like(e1_ref)
    zy_ref[...] = jnp.zeros_like(zy_ref)
    all_ref[HALO : HALO + zc] = own_ref[...]
    for h in range(1, hops + 1):
        count = zc if h < hops else plan.rest
        at = zc + 2 if h < hops else plan.rest + 1
        half = -(-count // 2)
        for refs_of, first in ((below, HALO - (h - 1) * zc - count), (above, HALO + h * zc)):
            words = refs_of[h - 1][at : at + half]
            second = (words >= 1.5).astype(f32)
            all_ref[first : first + half] = words - 2.0 * second
            if count > half:
                all_ref[first + half : first + count] = second[: count - half]
    target_ref[...] = all_ref[HALO - 1 : HALO + zc + 1]

    def fill(plane):
        out = []
        for n in range(plan.win_block):
            at = plane + n
            inside = 1.0 - kind_of(plan, rank, at - HALO)[1]
            out.append((at + 1, jnp.exp(-temper * all_ref[at]) * inside))
        for at, value in out:
            wrap(plan, e0_ref, at, value)

    over(0, win, plan.win_block, fill)

    def section(step, source, result, opening):
        e_ref = e_refs[source]
        reach = 2 + ITERS - step
        count = zc + 2 * reach
        erode(
            plan, rank, y_ref, e_ref, e_refs[result], g_ref, cross_ref, base, -reach, count
        )
        spread(plan, y_ref, g_ref, zy_ref, base, -1, span, size)

        def point(plane):
            before = [None if opening else ts_ref[plane + n] for n in range(size)]
            for n in range(size):
                at = plane + n
                box = x_box(plan, zy_ref, at)
                kind, outside = kind_of(plan, rank, at - 1)
                _, _, scaled = thin(e_ref[at - 1 + base, tiles], box, box_ref[kind], outside)
                ts_ref[at] = scaled * -LOG if opening else lift(scaled, before[n])[0]

        over(0, span, size, point)

    in_turn(section)

    def add(n, totals):
        ts = ts_ref[1 + n]
        return totals[0] + ts * p_ref[1 + n], totals[1] + ts

    zero = jnp.zeros((plan.tiles, LANES), f32)
    put_sums(plan, sums_ref, lax.fori_loop(0, zc, add, (zero,) * 2))


def put_sums(plan, ref, totals):
    lines = [jnp.sum(total, axis=0, keepdims=True) for total in totals]
    lines += [jnp.zeros((1, LANES), f32)] * (8 - len(lines))
    ref[...] = jnp.broadcast_to(jnp.concatenate(lines, axis=0)[None], (plan.ranks, 8, LANES))


def get_sums(ref, count):
    lines = jnp.sum(jnp.sum(ref[...], axis=0), axis=1, keepdims=True)
    return [lines[n : n + 1] for n in range(count)]


def forward_kernel(plan, *refs):
    hops = plan.hops
    pos_ref, bias_ref, label_ref, own_ref = refs[:4]
    refs = refs[4:]
    below, above = refs[:hops], refs[hops : 2 * hops]
    refs = refs[2 * hops :]
    far_ref, p_ref, sums_ref = refs[:3]
    e0_ref, e1_ref, g0_ref, g1_ref, zy_ref, s_ref, cross_ref, box_ref = refs[3:11]
    y_ref, record_ref, sem_ref = refs[11:]
    e_refs, g_refs = (e0_ref, e1_ref), (g0_ref, g1_ref)
    base, zc, size = plan.base, plan.zc, plan.block
    tiles = slice(8, 8 + plan.tiles)
    rank = pos_ref[0]

    for ref in e_refs + g_refs:
        ref[...] = jnp.zeros_like(ref)
    zy_ref[...] = jnp.zeros_like(zy_ref)
    count_tables(plan, cross_ref, box_ref)
    y_matrix(plan, y_ref)
    e0_ref[base : base + zc, tiles] = own_ref[:zc]
    for h in range(1, hops + 1):
        n = zc if h < hops else plan.rest
        first = base - (h - 1) * zc - n
        e0_ref[first : first + n, tiles] = below[h - 1][:n]
        first = base + h * zc
        e0_ref[first : first + n, tiles] = above[h - 1][:n]
    e0_ref[base - 1, tiles] += own_ref[zc]
    e0_ref[base + zc, tiles] += own_ref[zc + 1]
    for h in range(1, hops + 1):
        if h < hops:
            e0_ref[base - h * zc - 1, tiles] += below[h - 1][zc]
            e0_ref[base + (h + 1) * zc, tiles] += above[h - 1][zc + 1]
            e0_ref[base - (h - 1) * zc, tiles] += below[h - 1][zc + 1]
            e0_ref[base + h * zc - 1, tiles] += above[h - 1][zc]
        else:
            e0_ref[base - (h - 1) * zc, tiles] += below[h - 1][plan.rest]
            e0_ref[base + h * zc - 1, tiles] += above[h - 1][plan.rest]

    def sigmoid(logits):
        small = jnp.exp(-jnp.abs(logits))
        part = 1.0 / (1.0 + small)
        return jnp.where(logits >= 0, part, small * part)

    for n in range(plan.span):
        p_ref[n] = sigmoid(e0_ref[base - 1 + n, tiles] + bias_ref[0])

    def fill(plane):
        out = []
        for n in range(plan.erode_block):
            at = plane + n
            inside = 1.0 - kind_of(plan, rank, at - base)[1]
            predict = sigmoid(e0_ref[at, tiles] + bias_ref[0])
            out.append((at, jnp.exp(-temper * predict) * inside))
            g0_ref[at] = jnp.exp(temper * predict) * inside
        for at, value in out:
            wrap(plan, e0_ref, at, value)

    over(1, zc + 2 * HALO, plan.erode_block, fill)


    def out_copy(step):
        return pltpu.make_async_copy(record_ref.at[step], far_ref.at[step], sem_ref.at[step])

    def section(step, source, result, opening):
        e_ref, g_ref, after_ref = e_refs[source], g_refs[source], g_refs[result]
        reach = 1 + ITERS - step
        count = zc + 2 * reach
        erode(
            plan, rank, y_ref, e_ref, e_refs[result], after_ref, cross_ref, base, -reach,
            count,
        )
        spread(plan, y_ref, after_ref, zy_ref, base, 0, zc, size)
        record_ref[step, 3 * zc :] = after_ref[base - 1 : base + zc + 1]

        def point(plane):
            before = [None if opening else s_ref[plane + n] for n in range(size)]
            for n in range(size):
                at = plane + n
                box = x_box(plan, zy_ref, at)
                kind, outside = kind_of(plan, rank, at)
                e = e_ref[at + base, tiles]
                over_box, slope, scaled = thin(e, box, box_ref[kind], outside)
                if opening:
                    grown, a = scaled * -LOG, slope
                    record_ref[step, at] = jnp.ones_like(a)
                else:
                    s = before[n]
                    grown, rate = lift(scaled, s)
                    a = rate * (1.0 - s) * slope
                    record_ref[step, at] = 1.0 + rate * scaled * LOG
                s_ref[at] = grown
                record_ref[step, at + zc] = a * over_box
                record_ref[step, at + 2 * zc] = a * g_ref[at + base]

        over(0, zc, size, point)
        out_copy(step).start()

    in_turn(section)

    def add(n, totals):
        ps, predict, target = s_ref[n], p_ref[1 + n], label_ref[n]
        terms = (ps * target, ps, predict * target, predict, target)
        return tuple(total + term for total, term in zip(totals, terms))

    zero = jnp.zeros((plan.tiles, LANES), f32)
    put_sums(plan, sums_ref, lax.fori_loop(0, zc, add, (zero,) * 5))

    def drain(step, carry):
        out_copy(step).wait()
        return carry

    lax.fori_loop(0, SECTIONS, drain, 0)


def backward_kernel(plan, *refs):
    hops = plan.back_hops
    pos_ref, sums_ref, label_ref, far_ref, mine_ref = refs[:5]
    up, down = refs[5 : 5 + hops], refs[5 + hops : 5 + 2 * hops]
    w_ref, push_ref, wt_ref, zy_ref, pull0_ref, pull1_ref, cross_ref = refs[5 + 2 * hops : -3]
    y_ref, record_ref, sem_ref = refs[-3:]
    pull_refs = (pull0_ref, pull1_ref)
    rank = pos_ref[0]
    zc, base = plan.zc, plan.pull_base
    tiles = slice(8, 8 + plan.tiles)

    def in_copy(left):
        return pltpu.make_async_copy(far_ref.at[left], record_ref.at[left], sem_ref.at[left])

    for left in reversed(range(SECTIONS)):
        in_copy(left).start()
    s1, s2 = get_sums(sums_ref, 2)
    prec = (s1 + 1.0) / (s2 + 1.0)
    push_ref[...] = jnp.zeros_like(push_ref)
    wt_ref[...] = jnp.zeros_like(wt_ref)
    zy_ref[...] = jnp.zeros_like(zy_ref)
    for ref in pull_refs:
        ref[...] = jnp.zeros_like(ref)
    count_tables(plan, cross_ref, None)
    y_matrix(plan, y_ref)
    w_ref[...] = label_ref[...] - prec[None]

    def section(step, source, result, ending):
        pull_ref, next_ref = pull_refs[source], pull_refs[result]
        left = SECTIONS - 1 - step
        in_copy(left).wait()

        def push(at):
            out = []
            for n in range(plan.block):
                w = w_ref[at + n]
                out.append((push_ref, at + n + 2, w * record_ref[left, at + n + zc]))
                out.append((wt_ref, at + n + base, w * record_ref[left, at + n + 2 * zc]))
                out.append((w_ref, at + n, w * record_ref[left, at + n]))
            store_all(out)

        over(0, zc, plan.block, push)

        def widen(at):
            size = plan.span_block
            part = push_ref[pl.ds(at, size)] + push_ref[pl.ds(at + 1, size)]
            part = part + push_ref[pl.ds(at + 2, size)]
            part = part + y_neighbours(y_ref, part)
            for n in range(size):
                wrap(plan, zy_ref, at + n, part[n])

        over(0, plan.span, plan.span_block, widen)

        def pull(at):
            out = []
            for n in range(plan.span_block):
                box = x_box(plan, zy_ref, at + n)
                inverse = cross_ref[kind_of(plan, rank, at + n - 1)[0]]
                grown = record_ref[left, at + n + 3 * zc]
                spot = at + n - 1 + base
                old = pull_ref[spot, tiles]
                out.append((spot, old - grown * grown * box * inverse))
            for spot, value in out:
                wrap(plan, pull_ref, spot, value)

        over(0, plan.span, plan.span_block, pull)
        reach = 2 + step

        def join(plane):
            beside = y_neighbours(y_ref, pull_ref[pl.ds(plane + base, plan.erode_block), tiles])
            for n in range(plan.erode_block):
                at = plane + n + base
                total = pull_ref[at, tiles] + pull_ref[at - 1, tiles] + pull_ref[at + 1, tiles]
                total = total + x_neighbours(plan, pull_ref, at) + beside[n] + wt_ref[at]
                if not ending:
                    total = total * cross_ref[kind_of(plan, rank, plane + n)[0]]
                wrap(plan, next_ref, at, total)

        over(-reach, zc + 2 * reach, plan.erode_block, join)

    def pair(n, carry):
        section(2 * n, 0, 1, False)
        section(2 * n + 1, 1, 0, False)
        return carry

    lax.fori_loop(0, ITERS // 2, pair, 0)
    section(ITERS, 0, 1, True)
    mine_ref[...] = pull1_ref[base - 1 : base + zc + 1, tiles]
    for h in range(1, hops + 1):
        n = plan.back_count(h)
        first = base + h * zc - 1
        up[h - 1][...] = pull1_ref[first : first + n, tiles]
        first = base + (1 - h) * zc - n + 1
        down[h - 1][...] = pull1_ref[first : first + n, tiles]


def finish_kernel(plan, *refs):
    hops = plan.back_hops
    pos_ref, sums_ref, skel_ref, p_ref, target_ref, ts_ref, mine_ref = refs[:7]
    below, above = refs[7 : 7 + hops], refs[7 + hops : 7 + 2 * hops]
    out_ref, loss_ref, bias_ref, h_ref, grad_ref = refs[7 + 2 * hops :]
    rank = pos_ref[0]
    zc = plan.zc
    s1, s2, s5, s6, s7 = get_sums(sums_ref, 5)
    s3, s4 = get_sums(skel_ref, 2)
    prec = (s1 + 1.0) / (s2 + 1.0)
    sens = (s3 + 1.0) / (s4 + 1.0)
    both = prec + sens
    volume = s6 + s7 + 1.0
    cl_loss = 1.0 - 2.0 * prec * sens / both
    dice_loss = 1.0 - (2.0 * s5 + 1.0) / volume
    loss_ref[...] = jnp.broadcast_to(0.5 * dice_loss + 0.5 * cl_loss, (8, LANES))
    l0 = -(sens / both) * (sens / both) / (s2 + 1.0)
    l2 = -(prec / both) * (prec / both) / (s4 + 1.0)
    l4 = -1.0 / volume
    l5 = 0.5 * (2.0 * s5 + 1.0) / (volume * volume)

    h_ref[...] = mine_ref[...]
    for h in range(1, hops + 1):
        n = plan.back_count(h)
        h_ref[:n] += below[h - 1][...]
        h_ref[plan.span - n :] += above[h - 1][...]

    total = jnp.zeros((plan.tiles, LANES), f32)
    for n in range(plan.span):
        inside = 1.0 - kind_of(plan, rank, n - 1)[1]
        predict = p_ref[n]
        skel = l0 * jnp.exp(-temper * predict) * h_ref[n]
        whole = skel + l2 * ts_ref[n] + l4 * target_ref[n] + l5
        grad = whole * predict * (1.0 - predict) * inside
        grad_ref[n * plan.tiles : (n + 1) * plan.tiles] = grad
        if 1 <= n <= zc:
            total = total + grad
    bias_ref[...] = jnp.sum(total.reshape(-1, 8, LANES), axis=0)
    lane = lane_iota((1, LANES))

    def column(tile):
        return [
            grad_ref[pl.ds(plan.tiles + tile, zc, stride=plan.tiles)],
            grad_ref[tile : tile + 1],
            grad_ref[(zc + 1) * plan.tiles + tile : (zc + 1) * plan.tiles + tile + 1],
        ]

    tile_columns = [column(t) for t in range(plan.tiles)]

    def gathered(rows_of):
        piece = None
        for n, x in enumerate(rows_of):
            if x is None or not 0 <= x < plan.X:
                continue
            t, group = place_of(plan, x)
            shift = (n - group) * plan.Y % LANES
            ends = jnp.concatenate(tile_columns[t][1:], axis=0)
            values = [tile_columns[t][0], ends]
            if shift:
                values = [pltpu.roll(v, shift, 1) for v in values]
            values = [jnp.where(in_group(plan, n), v, 0.0) for v in values]
            piece = values if piece is None else [x + y for x, y in zip(piece, values)]
        if piece is None:
            piece = [jnp.zeros((zc, LANES), f32), jnp.zeros((2, LANES), f32)]
        return [piece[0], piece[1][0:1], piece[1][1:2]]

    for a in range(plan.gx):
        first, per = a * plan.nx, plan.per
        pieces = [
            gathered([first + per * q + n for n in range(per)]) for q in range(plan.own)
        ]
        if plan.shared:
            pieces.append(gathered([first + plan.nx] + [None] * (per - 2) + [first - 1]))
        else:
            pieces += [gathered([first + plan.nx]), gathered([first - 1])]
        edges = [edge for piece in pieces for edge in piece[1:]]
        rows = plan.R16
        edges += [jnp.zeros((1, LANES), f32)] * (plan.extra16 * rows - len(edges))
        whole = [piece[0] for piece in pieces]
        if rows > zc:
            fill = jnp.zeros((rows - zc, LANES), f32)
            whole = [jnp.concatenate([piece, fill], axis=0) for piece in whole]
        whole += [
            jnp.concatenate(edges[n * rows : (n + 1) * rows], axis=0) for n in range(plan.extra16)
        ]
        for q, piece in enumerate(whole):
            piece = piece.astype(bf16)
            for b in range(plan.gy):
                out_ref[a * plan.gy + b, q] = piece


def weight_kernel(
    plan, pos_ref, far_ref, bias_ref, got_ref, gw_ref, g_ref, dw_ref, f_ref, sem_ref
):
    copies = stream(plan, far_ref, f_ref, sem_ref)
    rows, inner = plan.Y, plan.ch * plan.ny
    zc, nz = plan.zc, plan.nz
    lane = lane_iota((rows, nz))
    places = {}
    for x in range(-1, plan.nx + 1):
        tile, first = plan.slot(x)
        places.setdefault(tile, {})[first] = x
    for tile in range(plan.sent):
        order = [plan.member_now(j, pos_ref) for j in range(plan.members)]
        stack = [got_ref[p, tile].astype(f32)[:zc] for p in order]
        turned = jnp.concatenate(stack, axis=0).T
        ends = []
        for end, p in ((0, order[0]), (1, order[-1])):
            n = 2 * tile + end
            row = got_ref[p, plan.sent + n // plan.R16].astype(f32)
            ends.append(row[n % plan.R16 : n % plan.R16 + 1])
        ends = jnp.concatenate(ends + [jnp.zeros((LANES - 2, LANES), f32)], axis=0).T
        for first, x in places[tile].items():
            g = turned[first : first + rows]
            end = ends[first : first + rows]
            down = jnp.where(lane == nz - 1, pltpu.roll(end, nz - 2, 1), pltpu.roll(g, nz - 1, 1))
            up = jnp.where(lane == 0, end, pltpu.roll(g, 1, 1))
            g_ref[x + 1] = jnp.concatenate([down, g, up], axis=0).astype(bf16)

    dw_ref[...] = jnp.zeros_like(dw_ref)

    width = plan.nx // PARTS
    for n in range(PARTS):
        copies[n].wait()
        dw_ref[...] += lax.dot_general(
            moved_columns(g_ref, n * width, width),
            columns(plan, f_ref, n * width, width),
            (((1,), (1,)), ((), ())),
            preferred_element_type=f32,
        )

    tap_y = tap_condition(plan, pos_ref[1], (rows, inner), 0, 1)
    taps = []
    for t in range(27):
        i, j, k = t // 9, t // 3 % 3, t % 3
        at = (3 * i + k) * rows
        taps.append(jnp.sum(jnp.where(tap_y == j, dw_ref[at : at + rows], 0.0), axis=0, keepdims=True))
    taps += [jnp.zeros((1, inner), f32)] * 5
    taps = jnp.concatenate(taps, axis=0)
    high = taps.astype(bf16)
    taps = taps - high.astype(f32)
    middle = taps.astype(bf16)
    low = (taps - middle.astype(f32)).astype(bf16)
    place = (
        lax.broadcasted_iota(jnp.int32, (inner, LANES), 0) // plan.ny
        == lax.broadcasted_iota(jnp.int32, (inner, LANES), 1)
    )
    sums = jnp.dot(
        jnp.concatenate([high, middle, low], axis=0),
        place.astype(f32).astype(bf16),
        preferred_element_type=f32,
    )
    sums = sums[0:32] + sums[32:64] + sums[64:96]
    total = sums[0:8]
    for n in range(1, 4):
        total = total + pltpu.roll(sums[8 * n : 8 * n + 8], 32 * n, 1)
    spot = (row_iota((8, LANES)) == 3) & (lane_iota((8, LANES)) == 96)
    total = jnp.where(spot, jnp.sum(bias_ref[...]), total)
    gw_ref[...] = jnp.broadcast_to(total[None], (plan.ranks, 8, LANES))


def wide_kernel(plan, pos_ref, wt_ref, after_ref, wide_ref):
    del after_ref
    rows, inner, bands = plan.Y, plan.ch * plan.ny, 9 * plan.Y
    spread = (
        lax.broadcasted_iota(jnp.int32, (inner, plan.ch), 0) // plan.ny
        == lax.broadcasted_iota(jnp.int32, (inner, plan.ch), 1)
    )
    spread = spread.astype(f32).astype(bf16)
    tap_y = tap_condition(plan, pos_ref[1], (inner, bands), 1, 0)
    wide = jnp.zeros((inner, bands), f32)
    tap = lax.broadcasted_iota(jnp.int32, (27, bands), 0)
    band = lax.broadcasted_iota(jnp.int32, (27, bands), 1) // rows
    for j in range(3):
        pick = (tap == 9 * (band // 3) + 3 * j + band % 3).astype(f32).astype(bf16)
        chosen = jnp.dot(wt_ref[...], pick, preferred_element_type=f32).astype(bf16)
        full = jnp.dot(spread, chosen, preferred_element_type=f32)
        wide = jnp.where(tap_y == j, full, wide)
    wide_ref[...] = wide.astype(bf16)


def feature_kernel(plan, wide_ref, g_ref, after_ref, gf_ref):
    del after_ref
    width = plan.nx // PARTS
    for n in range(PARTS):
        out = jnp.dot(
            wide_ref[...],
            moved_columns(g_ref, n * width, width),
            preferred_element_type=f32,
        )
        for x in range(width):
            part = out[:, x * plan.nz : (x + 1) * plan.nz].astype(bf16)
            gf_ref[:, n * width + x] = part.reshape(plan.ch, plan.ny, plan.nz)


def final_kernel(plan, got_ref, gw_ref, gb_ref):
    total = jnp.sum(got_ref[...], axis=0)
    for n in range(4):
        count = min(8, 27 - 8 * n)
        gw_ref[8 * n : 8 * n + count] = total[:count, 32 * n : 32 * n + plan.ch]
    gb_ref[...] = total[3:4, 96:97]


VMEM = pl.BlockSpec(memory_space=pltpu.VMEM)
SMEM = pl.BlockSpec(memory_space=pltpu.SMEM)
ANY = pl.BlockSpec(memory_space=pl.ANY)
FAR = pl.BlockSpec(memory_space=pltpu.HBM)
MIB = 1024 * 1024


def shape(dims, dtype=f32):
    return jax.ShapeDtypeStruct(dims, dtype)


def held(dims, dtype):
    if len(dims) < 2:
        return 4096
    size = jnp.dtype(dtype).itemsize
    rows = 8 * 4 // size
    total = -(-dims[-2] // rows) * rows * -(-dims[-1] // LANES) * LANES * size
    for n in dims[:-2]:
        total *= n
    return total


def limits(arrays, scratch, micros):
    total = sum(held(a.shape, a.dtype) for a in arrays)
    total += sum(held(a.shape, a.dtype) for a in scratch if len(a.shape) > 1)
    limit = min(63 * MIB, total + total // 8 + 4 * MIB)
    return dict(
        compiler_params=pltpu.CompilerParams(vmem_limit_bytes=limit),
        cost_estimate=pl.CostEstimate(
            flops=0, transcendentals=0, bytes_accessed=int(micros * 2.5e4)
        ),
    )


def per_device(mesh_shape, features, weight, bias, label):
    plan = Plan(mesh_shape, features.shape)
    members, sent, tiles = plan.members, plan.sent, plan.tiles
    inner, bands = plan.ch * plan.ny, 9 * plan.Y
    x, y, z = (lax.axis_index(axis).astype(jnp.int32) for axis in ALL_AXES)
    mine = y * plan.gx + jnp.where(y % 2 == 0, x, plan.gx - 1 - x)
    place = z * members + jnp.where(z % 2 == 0, mine, members - 1 - mine)
    pos = jnp.stack([place, y])

    def call(
        kernel, out_shape, in_specs, operands, micros, scratch=(), out_specs=None
    ):
        outs = jax.tree.leaves(out_shape)
        ins = [a for spec, a in zip(in_specs, operands) if spec is VMEM]
        return pl.pallas_call(
            functools.partial(kernel, plan),
            out_shape=out_shape,
            in_specs=in_specs,
            out_specs=out_specs or jax.tree.map(lambda s: VMEM, out_shape),
            scratch_shapes=list(scratch),
            **limits(ins + outs, scratch, micros),
        )(*operands)

    def exchange(array):
        return lax.all_to_all(array, GROUP, 0, 0, tiled=True)

    def everywhere(array):
        return lax.all_to_all(array, ALL_AXES, 0, 0, tiled=True)

    def hop(array, distance):
        def device(r):
            z = r // members
            return plan.member(r % members, z % 2 == 1) * plan.gz + z

        pairs = [
            (device(r), device(r + distance))
            for r in range(plan.ranks)
            if 0 <= r + distance < plan.ranks
        ]
        return lax.ppermute(array, ALL_AXES, pairs)

    turned = weight.T
    features, weight, label = (
        pltpu.with_memory_space_constraint(a, pltpu.HBM) for a in (features, weight, label)
    )
    features_near = [pltpu.VMEM(features.shape, bf16), pltpu.SemaphoreType.DMA((PARTS,))]
    sent_logits = call(
        conv_kernel,
        shape((members, sent + plan.extra, plan.R, LANES)),
        [SMEM, VMEM, FAR, VMEM],
        (pos, weight, features, label),
        7,
        [
            pltpu.VMEM((bands, inner), bf16),
            pltpu.VMEM((plan.nx + 2, 3 * plan.Y, plan.nz), f32),
        ]
        + features_near,
    )

    def planes(array):
        return array.reshape(-1, tiles, LANES)

    zc, rest = plan.zc, plan.rest
    short = shape(((rest + 1 + -(-rest // 2)) * tiles, LANES))
    whole, label_own, head, tail = call(
        gather_kernel,
        [
            shape(((zc + 2 + -(-zc // 2)) * tiles, LANES)),
            shape((zc * tiles, LANES)),
            short,
            short,
        ],
        [VMEM],
        (exchange(sent_logits),),
        1.5,
    )
    whole, label_own, head, tail = (planes(part) for part in (whole, label_own, head, tail))
    around = [
        hop(whole if h < plan.hops else part, sign * h)
        for sign, part in ((1, tail), (-1, head))
        for h in range(1, plan.hops + 1)
    ]

    slab = (zc, tiles, LANES)
    span = (plan.span, tiles, LANES)
    everyone = shape((plan.ranks, 8, LANES))
    table = pltpu.VMEM((3, tiles, LANES), f32)

    records = pltpu.HBM((SECTIONS, plan.records, tiles, LANES), f32)
    y_near = pltpu.VMEM((2 * LANES, LANES), bf16)
    record_near = [
        y_near,
        pltpu.VMEM(records.shape, f32),
        pltpu.SemaphoreType.DMA((SECTIONS,)),
    ]
    record, predict, sums = call(
        forward_kernel,
        [records, shape(span), everyone],
        [SMEM, SMEM] + [VMEM] * (2 + 2 * plan.hops),
        (pos, bias, label_own, whole, *around),
        11,
        [
            pltpu.VMEM((plan.planes, plan.pad, LANES), f32),
            pltpu.VMEM((plan.planes, plan.pad, LANES), f32),
            pltpu.VMEM((plan.planes, tiles, LANES), f32),
            pltpu.VMEM((plan.planes, tiles, LANES), f32),
            pltpu.VMEM((zc, plan.pad, LANES), f32),
            pltpu.VMEM(slab, f32),
            table,
            table,
        ]
        + record_near,
        [FAR, VMEM, VMEM],
    )
    record = pltpu.with_memory_space_constraint(record, pltpu.HBM)
    sums = everywhere(sums)
    room = plan.win + 2 + plan.erode_block
    target, ts, skel_sums = call(
        target_kernel,
        [shape(span), shape(span), everyone],
        [SMEM] + [VMEM] * (2 + 2 * plan.hops),
        (pos, predict, label_own, *around),
        13,
        [
            pltpu.VMEM((plan.win, tiles, LANES), f32),
            pltpu.VMEM((room, plan.pad, LANES), f32),
            pltpu.VMEM((room, plan.pad, LANES), f32),
            pltpu.VMEM((room, tiles, LANES), f32),
            pltpu.VMEM((plan.span, plan.pad, LANES), f32),
            table,
            table,
            y_near,
        ],
    )
    skel_sums = everywhere(skel_sums)
    outer = [
        shape((plan.back_count(h), tiles, LANES)) for h in range(1, plan.back_hops + 1)
    ]
    mine, *outer = call(
        backward_kernel,
        [shape(span)] + outer * 2,
        [SMEM, VMEM, VMEM, FAR],
        (pos, sums, label_own, record),
        11,
        [
            pltpu.VMEM(slab, f32),
            pltpu.VMEM((zc + 4, tiles, LANES), f32),
            pltpu.VMEM((plan.pull_planes, tiles, LANES), f32),
            pltpu.VMEM((plan.span, plan.pad, LANES), f32),
            pltpu.VMEM((plan.pull_planes, plan.pad, LANES), f32),
            pltpu.VMEM((plan.pull_planes, plan.pad, LANES), f32),
            table,
        ]
        + record_near,
    )
    wide = call(
        wide_kernel, shape((inner, bands), bf16), [SMEM, VMEM, ANY], (pos, turned, mine), 2
    )
    beyond = []
    for sign, arrays in ((1, outer[: plan.back_hops]), (-1, outer[plan.back_hops :])):
        for h in range(1, plan.back_hops + 1):
            beyond.append(hop(arrays[h - 1], sign * h))
    grad_sent, loss, bias_part = call(
        finish_kernel,
        [
            shape((members, sent + plan.extra16, plan.R16, LANES), bf16),
            shape((8, LANES)),
            shape((8, LANES)),
        ],
        [SMEM] + [VMEM] * (6 + 2 * plan.back_hops),
        (pos, sums, skel_sums, predict, target, ts, mine, *beyond),
        2,
        [pltpu.VMEM(span, f32), pltpu.VMEM((plan.span * tiles, LANES), f32)],
    )

    moved = shape((plan.nx + 2, 3 * plan.Y, plan.nz), bf16)
    partial, g = call(
        weight_kernel,
        [shape((plan.ranks, 8, LANES)), moved],
        [SMEM, FAR, VMEM, VMEM],
        (pos, features, bias_part, exchange(grad_sent)),
        5,
        [pltpu.VMEM((bands, inner), f32)] + features_near,
    )
    grad_features = call(
        feature_kernel,
        shape(features.shape, bf16),
        [VMEM, VMEM, ANY],
        (wide, g, partial),
        5,
    )
    grad_weight, grad_bias = call(
        final_kernel,
        [shape((27, plan.ch)), shape((1, 1))],
        [VMEM],
        (everywhere(partial),),
        1.5,
    )
    return (loss[0, :1], grad_features, grad_weight, grad_bias.reshape(1))


def solution(mesh):
    in_specs = (P(None, "gx", "gy", "gz"), P(), P(), P("gx", "gy", "gz"))
    out_specs = (P(), P(None, "gx", "gy", "gz"), P(), P())

    def body(*args):
        return per_device(dict(mesh.shape), *args)

    return jax.shard_map(
        body, mesh=mesh, in_specs=in_specs, out_specs=out_specs, check_vma=False
    )
```

```python
import functools

import jax
import jax.numpy as jnp
from jax import lax
from jax.experimental import pallas as pl
from jax.experimental.pallas import tpu as pltpu
from jax.sharding import PartitionSpec as P

ITERS = 10
SECTIONS = ITERS + 1
LANES = 128
HALO = SECTIONS + 2
BACK = SECTIONS + 1

BLOCK = 32
SPAN_BLOCK = 40
ERODE_BLOCK = 20

temper = 20.0
sharpness = 40.0

GROUP = ("gx", "gy")
ALL_AXES = ("gx", "gy", "gz")
f32 = jnp.float32
bf16 = jnp.bfloat16


def up8(value):
    return -(-value // 8) * 8


class Plan:
    def __init__(self, mesh_shape, block):
        self.ch, self.nx, self.ny, self.nz = block
        self.gx, self.gy, self.gz = (mesh_shape[a] for a in ALL_AXES)
        self.members = self.gx * self.gy
        self.ranks = self.members * self.gz
        self.X = self.nx * self.gx
        self.Y = self.ny * self.gy
        self.Z = self.nz * self.gz
        assert LANES % self.Y == 0 and self.nz == LANES
        assert self.nz % self.members == 0
        self.zc = self.nz // self.members
        self.per = LANES // self.Y
        assert self.nx % self.per == 0
        self.tiles = self.X // self.per
        self.own = self.nx // self.per
        self.shared = self.per > 1
        self.sent = self.own + (1 if self.shared else 2)
        self.R = up8(self.zc)
        self.extra = -(-2 * self.sent // self.R)
        self.R16 = -(-self.zc // 16) * 16
        self.extra16 = -(-2 * self.sent // self.R16)
        self.pad = self.tiles + 16
        self.win = self.zc + 2 * HALO
        self.span = self.zc + 2
        self.block = self.blocks_of(self.zc, BLOCK)
        self.span_block = self.blocks_of(self.span, SPAN_BLOCK)
        self.win_block = self.blocks_of(self.win, 32)
        self.erode_block = max(1, ERODE_BLOCK * 8 // self.tiles)
        self.base = HALO + 1
        self.planes = self.zc + 2 * HALO + 2 + self.erode_block
        self.pull_base = BACK + 2
        self.pull_planes = self.zc + 2 * BACK + 4 + self.erode_block
        self.hops = -(-HALO // self.zc)
        self.rest = HALO - (self.hops - 1) * self.zc
        self.records = 3 * self.zc + self.span
        assert self.ny == 16 and self.gy > 1
        self.back_hops = -(-(BACK + 1) // self.zc)

    def back_count(self, h):
        return min(self.zc + BACK + 1 - h * self.zc, self.span)

    def blocks_of(self, count, most):
        fits = [n for n in range(1, count + 1) if count % n == 0 and n * self.tiles <= 8 * most]
        return fits[-1] if fits else 1

    def slab(self, member):
        x, y = member // self.gy, member % self.gy
        return y * self.gx + (x if y % 2 == 0 else self.gx - 1 - x)

    def member(self, slab, odd):
        slab = self.members - 1 - slab if odd else slab
        return next(p for p in range(self.members) if self.slab(p) == slab)

    def member_now(self, slab, pos_ref):
        odd = pos_ref[0] // self.members % 2 == 1
        return jnp.where(odd, self.member(slab, True), self.member(slab, False))

    def label_lane(self, member_y):
        return 0 if member_y == self.gy - 1 else (member_y + 1) * self.ny + 8

    def slot(self, x):
        if 0 <= x < self.nx:
            return x // self.per, (x % self.per) * self.Y
        if x == self.nx:
            return self.own, 0
        return self.sent - 1, LANES - self.Y


def lane_iota(shape):
    return lax.broadcasted_iota(jnp.int32, shape, len(shape) - 1)


def row_iota(shape):
    return lax.broadcasted_iota(jnp.int32, shape, len(shape) - 2)


def masks(plan):
    return lane_iota((plan.tiles, LANES))


def x_neighbours(plan, mask, load, cur):
    lower, upper = load(-1), load(1)
    if plan.Y == LANES:
        return lower + upper
    lower = pltpu.roll(jnp.where(mask >= LANES - plan.Y, lower, cur), plan.Y, 1)
    upper = pltpu.roll(jnp.where(mask < plan.Y, upper, cur), LANES - plan.Y, 1)
    return lower + upper


def y_matrix(plan, ref):
    row = row_iota((2 * LANES, LANES)) % LANES
    lane = lane_iota((2 * LANES, LANES))
    near = (row == lane - 1) | (row == lane + 1)
    ref[...] = (near & (row // plan.Y == lane // plan.Y)).astype(f32).astype(bf16)


def y_neighbours(ref, block):
    flat = block.reshape(-1, LANES)
    high = flat.astype(bf16)
    low = (flat - high.astype(f32)).astype(bf16)
    both = jnp.concatenate([high, low], axis=1)
    return jnp.dot(both, ref[...], preferred_element_type=f32).reshape(block.shape)


def count_tables(plan, cross_ref, box_ref):
    flat = row_iota((plan.tiles, LANES)) * LANES + lane_iota((plan.tiles, LANES))
    y, x = flat % plan.Y, flat // plan.Y

    def along(spot, size):
        return 3.0 - (spot == 0).astype(f32) - (spot == size - 1).astype(f32)

    cx, cy = along(x, plan.X), along(y, plan.Y)
    for kind, cz in ((1, 2.0), (2, 3.0)):
        if cross_ref is not None:
            cross_ref[kind] = 1.0 / (cx + cy + cz - 2.0)
        if box_ref is not None:
            box_ref[kind] = 1.0 / (cx * cy * cz)
    for ref in (cross_ref, box_ref):
        if ref is not None:
            ref[0] = jnp.zeros((plan.tiles, LANES), f32)


def kind_of(plan, rank, plane):
    z = rank * plan.zc + plane
    inside = (z >= 0) & (z < plan.Z)
    edge = (z == 0) | (z == plan.Z - 1)
    return jnp.where(inside, jnp.where(edge, 1, 2), 0), jnp.where(inside, 0.0, 1.0)


def store_all(pairs):
    for ref, at, value in pairs:
        ref[at] = value


def over(first, count, size, body):
    def at(n, carry):
        body(first + n * size)
        return carry

    lax.fori_loop(0, (count + size - 1) // size, at, 0)


def tap_condition(plan, member_y, shape, y_dim, in_dim):
    y = lax.broadcasted_iota(jnp.int32, shape, y_dim) % plan.Y
    own = lax.broadcasted_iota(jnp.int32, shape, in_dim) % plan.ny
    return own + member_y * plan.ny - y + 1


PARTS = 4


def stream(plan, far_ref, near_ref, sem_ref):
    width = plan.nx // PARTS
    copies = []
    for n in range(PARTS):
        span = pl.ds(n * width, width)
        copies.append(
            pltpu.make_async_copy(far_ref.at[:, span], near_ref.at[:, span], sem_ref.at[n])
        )
        copies[-1].start()
    return copies


def columns(plan, ref, first, count):
    blocks = [ref[:, x].reshape(-1, plan.nz) for x in range(first, first + count)]
    return jnp.concatenate(blocks, axis=1)


def moved_columns(ref, first, count):
    blocks = [
        jnp.concatenate([ref[x + 2], ref[x + 1], ref[x]], axis=0)
        for x in range(first, first + count)
    ]
    return jnp.concatenate(blocks, axis=1)


def conv_kernel(
    plan, pos_ref, w_ref, far_ref, label_ref, out_ref, wide_ref, acc_ref, f_ref, sem_ref
):
    width = plan.nx // PARTS
    copies = stream(plan, far_ref, f_ref, sem_ref)
    rows, inner = plan.Y, plan.ch * plan.ny
    spread = (
        lax.broadcasted_iota(jnp.int32, (plan.ch, inner), 0)
        == lax.broadcasted_iota(jnp.int32, (plan.ch, inner), 1) // plan.ny
    )
    taps = jnp.dot(
        w_ref[...], spread.astype(f32).astype(bf16), preferred_element_type=f32
    )
    tap_y = tap_condition(plan, pos_ref[1], (rows, inner), 0, 1)
    for i in range(3):
        for k in range(3):
            band = jnp.zeros((rows, inner), f32)
            for j in range(3):
                t = 9 * i + 3 * j + k
                band = jnp.where(tap_y == j, taps[t : t + 1], band)
            at = (3 * i + k) * rows
            wide_ref[at : at + rows] = band.astype(bf16)
    acc_ref[...] = jnp.zeros_like(acc_ref)

    for n in range(PARTS):
        copies[n].wait()
        first = n * width
        out = jnp.dot(
            wide_ref[...], columns(plan, f_ref, first, width), preferred_element_type=f32
        )
        for slot in range(first, first + width + 2):
            terms = [
                out[3 * i * rows : 3 * (i + 1) * rows, (x - first) * plan.nz : (x - first + 1) * plan.nz]
                for i in range(3)
                for x in (slot - 2 + i,)
                if first <= x < first + width
            ]
            acc_ref[slot] += functools.reduce(jnp.add, terms)

    out_ref[...] = jnp.zeros_like(out_ref)
    places = {}
    for x in range(-1, plan.nx + 1):
        tile, lane = plan.slot(x)
        places.setdefault(tile, {})[lane] = x
    lane = lane_iota((rows, plan.nz))
    words = [label_ref[x, 0:8] + 2 * label_ref[x, 8:16] for x in range(plan.nx)]
    first_group = jnp.where(
        pos_ref[1] == plan.gy - 1, 0, (pos_ref[1] + 1) * (plan.ny // 8) + 1
    )
    labelled = lax.broadcasted_iota(jnp.int32, (rows, plan.nz), 0) // 8 == first_group
    for tile in range(plan.sent):
        parts, spills = [], []
        for first in range(0, LANES, rows):
            x = places[tile].get(first)
            if x is None:
                parts.append(jnp.zeros((rows, plan.nz), f32))
                spills.append(jnp.zeros((rows, plan.nz), f32))
                continue
            low = acc_ref[x + 1, 0:rows]
            mid = acc_ref[x + 1, rows : 2 * rows]
            high = acc_ref[x + 1, 2 * rows : 3 * rows]
            total = mid + jnp.where(lane == 0, 0.0, pltpu.roll(low, 1, 1))
            total = total + jnp.where(lane == plan.nz - 1, 0.0, pltpu.roll(high, plan.nz - 1, 1))
            if 0 <= x < plan.nx:
                word = jnp.concatenate([words[x].astype(f32)] * (rows // 8), axis=0)
                total = total + jnp.where(labelled, word, 0.0)
            parts.append(total)
            spill = jnp.where(lane == 1, pltpu.roll(low, 2, 1), 0.0)
            spills.append(jnp.where(lane == 0, high, spill))
        turned = jnp.concatenate(parts, axis=0).T
        spill = jnp.concatenate(spills, axis=0).T
        for j in range(plan.members):
            p = plan.member_now(j, pos_ref)
            out_ref[p, tile, 0 : plan.zc] = turned[j * plan.zc : (j + 1) * plan.zc]
        for end, j in ((0, 0), (1, plan.members - 1)):
            n = 2 * tile + end
            at = plan.sent + n // plan.R
            p = plan.member_now(j, pos_ref)
            out_ref[p, at, n % plan.R : n % plan.R + 1] = spill[end : end + 1]


def gather_kernel(plan, got_ref, out_ref, label_ref, head_ref, tail_ref):
    tiles, zc, rest = plan.tiles, plan.zc, plan.rest
    lane = lane_iota((1, LANES))
    spot = lane % plan.Y

    def part(p, q):
        values = [got_ref[p, q, 0:zc]]
        for end in range(2):
            n = 2 * q + end
            at = plan.sent + n // plan.R
            values.append(got_ref[p, at, n % plan.R : n % plan.R + 1])
        return values

    for a in range(plan.gx):
        for q in range(plan.own):
            parts = []
            label = jnp.zeros((zc, LANES), f32)
            for b in range(plan.gy):
                start = b * plan.ny
                values = part(a * plan.gy + b, q)
                second = (values[0] >= 1.5).astype(f32)
                first = values[0] - 2.0 * second
                move = start - plan.label_lane(b)
                first = pltpu.roll(first, move % LANES, 1)
                second = pltpu.roll(second, (move + 8) % LANES, 1)
                label = jnp.where((spot >= start) & (spot < start + 8), first, label)
                label = jnp.where((spot >= start + 8) & (spot < start + 16), second, label)
                mine = (spot >= start - 1) & (spot <= start + plan.ny)
                parts.append([jnp.where(mine, v, 0.0) for v in values])
                if q == plan.own - 1 and a < plan.gx - 1:
                    edge = part((a + 1) * plan.gy + b, plan.sent - 1)
                    parts.append([jnp.where(lane >= LANES - plan.Y, v, 0.0) for v in edge])
                if q == 0 and a > 0:
                    edge = part((a - 1) * plan.gy + b, plan.own)
                    parts.append([jnp.where(lane < plan.Y, v, 0.0) for v in edge])
            whole, low, high = (functools.reduce(jnp.add, vs) for vs in zip(*parts))
            tile = a * plan.own + q
            label_ref[pl.ds(tile, zc, stride=tiles)] = label
            out_ref[pl.ds(tile, zc, stride=tiles)] = whole
            out_ref[zc * tiles + tile : zc * tiles + tile + 1] = low
            out_ref[(zc + 1) * tiles + tile : (zc + 1) * tiles + tile + 1] = high

    def pack(ref, at, first, count):
        half = -(-count // 2)
        for n in range(half):
            word = label_ref[(first + n) * tiles : (first + n + 1) * tiles]
            if n + half < count:
                other = first + n + half
                word = word + 2.0 * label_ref[other * tiles : (other + 1) * tiles]
            ref[(at + n) * tiles : (at + n + 1) * tiles] = word

    pack(out_ref, zc + 2, 0, zc)
    head_ref[: rest * tiles] = out_ref[: rest * tiles]
    head_ref[rest * tiles : (rest + 1) * tiles] = out_ref[zc * tiles : (zc + 1) * tiles]
    pack(head_ref, rest + 1, 0, rest)
    tail_ref[: rest * tiles] = out_ref[(zc - rest) * tiles : zc * tiles]
    tail_ref[rest * tiles : (rest + 1) * tiles] = out_ref[(zc + 1) * tiles : (zc + 2) * tiles]
    pack(tail_ref, rest + 1, zc - rest, rest)


LOG = 1.0 / sharpness


def thin(e, box, inverse, outside):
    box = box + outside
    ratio = e * box * inverse + outside
    square = ratio * ratio
    more = 1.0 + square
    joint = 1.0 / (box * more)
    slope = joint * box
    return joint * more, slope, jnp.log(square * slope)


def lift(scaled, s):
    small = jnp.exp(scaled * (s - 1.0))
    more = 1.0 + small
    return s + jnp.log(more) * LOG, small * (1.0 / more)


def erode(plan, rank, mask, y_ref, source, result, grown_ref, table_ref, base, first, count):
    tiles = slice(8, 8 + plan.tiles)

    def body(plane):
        beside = y_neighbours(y_ref, source[pl.ds(plane + base, plan.erode_block), tiles])
        for n in range(plan.erode_block):
            at = plane + n + base
            cur = source[at, tiles]

            def load(offset, at=at):
                return source[at, 8 + offset : 8 + offset + plan.tiles]

            total = cur + source[at - 1, tiles] + source[at + 1, tiles]
            total = total + x_neighbours(plan, mask, load, cur) + beside[n]
            kind, outside = kind_of(plan, rank, plane + n)
            total = total * table_ref[kind]
            result[at, tiles] = total
            grown_ref[at] = 1.0 / (total + outside) - outside

    over(first, count, plan.erode_block, body)


def spread(plan, y_ref, grown_ref, zy_ref, base, first, count, size):
    tiles = slice(8, 8 + plan.tiles)

    def body(plane):
        at = plane + base
        part = grown_ref[pl.ds(at - 1, size)] + grown_ref[pl.ds(at, size)]
        part = part + grown_ref[pl.ds(at + 1, size)]
        zy_ref[pl.ds(plane - first, size), tiles] = part + y_neighbours(y_ref, part)

    over(first, count, size, body)


def in_turn(section):
    section(0, 0, 1, True)

    def pair(n, carry):
        section(2 * n + 1, 1, 0, False)
        section(2 * n + 2, 0, 1, False)
        return carry

    lax.fori_loop(0, ITERS // 2, pair, 0)


def x_box(plan, mask, zy_ref, at):
    cur = zy_ref[at, 8 : 8 + plan.tiles]

    def load(offset):
        return zy_ref[at, 8 + offset : 8 + offset + plan.tiles]

    return cur + x_neighbours(plan, mask, load, cur)


def target_kernel(plan, *refs):
    hops = plan.hops
    pos_ref, p_ref, own_ref = refs[:3]
    below, above = refs[3 : 3 + hops], refs[3 + hops : 3 + 2 * hops]
    target_ref, ts_ref, sums_ref = refs[3 + 2 * hops : 6 + 2 * hops]
    all_ref, e0_ref, e1_ref, g_ref, zy_ref, cross_ref, box_ref, y_ref = refs[6 + 2 * hops :]
    zc, win, span = plan.zc, plan.win, plan.span
    size = plan.span_block
    base = HALO + 1
    tiles = slice(8, 8 + plan.tiles)
    rank = pos_ref[0]
    mask = masks(plan)
    count_tables(plan, cross_ref, box_ref)
    y_matrix(plan, y_ref)
    e_refs = (e0_ref, e1_ref)
    e0_ref[...] = jnp.zeros_like(e0_ref)
    e1_ref[...] = jnp.zeros_like(e1_ref)
    zy_ref[...] = jnp.zeros_like(zy_ref)
    all_ref[HALO : HALO + zc] = own_ref[...]
    for h in range(1, hops + 1):
        count = zc if h < hops else plan.rest
        at = zc + 2 if h < hops else plan.rest + 1
        half = -(-count // 2)
        for refs_of, first in ((below, HALO - (h - 1) * zc - count), (above, HALO + h * zc)):
            words = refs_of[h - 1][at : at + half]
            second = (words >= 1.5).astype(f32)
            all_ref[first : first + half] = words - 2.0 * second
            if count > half:
                all_ref[first + half : first + count] = second[: count - half]
    target_ref[...] = all_ref[HALO - 1 : HALO + zc + 1]

    def fill(plane):
        out = []
        for n in range(plan.win_block):
            at = plane + n
            inside = 1.0 - kind_of(plan, rank, at - HALO)[1]
            out.append((e0_ref, (at + 1, tiles), jnp.exp(-temper * all_ref[at]) * inside))
        store_all(out)

    over(0, win, plan.win_block, fill)

    def section(step, source, result, opening):
        e_ref = e_refs[source]
        reach = 2 + ITERS - step
        count = zc + 2 * reach
        erode(
            plan, rank, mask, y_ref, e_ref, e_refs[result], g_ref, cross_ref, base, -reach, count
        )
        spread(plan, y_ref, g_ref, zy_ref, base, -1, span, size)

        def point(plane):
            before = [None if opening else ts_ref[plane + n] for n in range(size)]
            for n in range(size):
                at = plane + n
                box = x_box(plan, mask, zy_ref, at)
                kind, outside = kind_of(plan, rank, at - 1)
                _, _, scaled = thin(e_ref[at - 1 + base, tiles], box, box_ref[kind], outside)
                ts_ref[at] = scaled * -LOG if opening else lift(scaled, before[n])[0]

        over(0, span, size, point)

    in_turn(section)

    def add(n, totals):
        ts = ts_ref[1 + n]
        return totals[0] + ts * p_ref[1 + n], totals[1] + ts

    zero = jnp.zeros((plan.tiles, LANES), f32)
    put_sums(plan, sums_ref, lax.fori_loop(0, zc, add, (zero,) * 2))


def put_sums(plan, ref, totals):
    lines = [jnp.sum(total, axis=0, keepdims=True) for total in totals]
    lines += [jnp.zeros((1, LANES), f32)] * (8 - len(lines))
    ref[...] = jnp.broadcast_to(jnp.concatenate(lines, axis=0)[None], (plan.ranks, 8, LANES))


def get_sums(ref, count):
    lines = jnp.sum(jnp.sum(ref[...], axis=0), axis=1, keepdims=True)
    return [lines[n : n + 1] for n in range(count)]


def forward_kernel(plan, *refs):
    hops = plan.hops
    pos_ref, bias_ref, label_ref, own_ref = refs[:4]
    refs = refs[4:]
    below, above = refs[:hops], refs[hops : 2 * hops]
    refs = refs[2 * hops :]
    far_ref, p_ref, sums_ref = refs[:3]
    e0_ref, e1_ref, g0_ref, g1_ref, zy_ref, s_ref, cross_ref, box_ref = refs[3:11]
    y_ref, record_ref, sem_ref = refs[11:]
    e_refs, g_refs = (e0_ref, e1_ref), (g0_ref, g1_ref)
    base, zc, size = plan.base, plan.zc, plan.block
    tiles = slice(8, 8 + plan.tiles)
    rank = pos_ref[0]
    mask = masks(plan)

    for ref in e_refs:
        ref[...] = jnp.zeros_like(ref)
    zy_ref[...] = jnp.zeros_like(zy_ref)
    count_tables(plan, cross_ref, box_ref)
    y_matrix(plan, y_ref)
    e0_ref[base : base + zc, tiles] = own_ref[:zc]
    for h in range(1, hops + 1):
        n = zc if h < hops else plan.rest
        first = base - (h - 1) * zc - n
        e0_ref[first : first + n, tiles] = below[h - 1][:n]
        first = base + h * zc
        e0_ref[first : first + n, tiles] = above[h - 1][:n]
    e0_ref[base - 1, tiles] += own_ref[zc]
    e0_ref[base + zc, tiles] += own_ref[zc + 1]
    for h in range(1, hops + 1):
        if h < hops:
            e0_ref[base - h * zc - 1, tiles] += below[h - 1][zc]
            e0_ref[base + (h + 1) * zc, tiles] += above[h - 1][zc + 1]
            e0_ref[base - (h - 1) * zc, tiles] += below[h - 1][zc + 1]
            e0_ref[base + h * zc - 1, tiles] += above[h - 1][zc]
        else:
            e0_ref[base - (h - 1) * zc, tiles] += below[h - 1][plan.rest]
            e0_ref[base + h * zc - 1, tiles] += above[h - 1][plan.rest]

    def sigmoid(logits):
        small = jnp.exp(-jnp.abs(logits))
        part = 1.0 / (1.0 + small)
        return jnp.where(logits >= 0, part, small * part)

    for n in range(plan.span):
        p_ref[n] = sigmoid(e0_ref[base - 1 + n, tiles] + bias_ref[0])

    def fill(plane):
        out = []
        for n in range(plan.erode_block):
            at = plane + n
            inside = 1.0 - kind_of(plan, rank, at - base)[1]
            predict = sigmoid(e0_ref[at, tiles] + bias_ref[0])
            out.append((e0_ref, (at, tiles), jnp.exp(-temper * predict) * inside))
            out.append((g0_ref, at, jnp.exp(temper * predict) * inside))
        store_all(out)

    over(1, zc + 2 * HALO, plan.erode_block, fill)


    def out_copy(step):
        return pltpu.make_async_copy(record_ref.at[step], far_ref.at[step], sem_ref.at[step])

    def section(step, source, result, opening):
        e_ref, g_ref, after_ref = e_refs[source], g_refs[source], g_refs[result]
        reach = 1 + ITERS - step
        count = zc + 2 * reach
        erode(
            plan, rank, mask, y_ref, e_ref, e_refs[result], after_ref, cross_ref, base, -reach,
            count,
        )
        spread(plan, y_ref, after_ref, zy_ref, base, 0, zc, size)
        record_ref[step, 3 * zc :] = after_ref[base - 1 : base + zc + 1]

        def point(plane):
            before = [None if opening else s_ref[plane + n] for n in range(size)]
            for n in range(size):
                at = plane + n
                box = x_box(plan, mask, zy_ref, at)
                kind, outside = kind_of(plan, rank, at)
                e = e_ref[at + base, tiles]
                over_box, slope, scaled = thin(e, box, box_ref[kind], outside)
                if opening:
                    grown, a = scaled * -LOG, slope
                    record_ref[step, at] = jnp.ones_like(a)
                else:
                    s = before[n]
                    grown, rate = lift(scaled, s)
                    a = rate * (1.0 - s) * slope
                    record_ref[step, at] = 1.0 + rate * scaled * LOG
                s_ref[at] = grown
                record_ref[step, at + zc] = a * over_box
                record_ref[step, at + 2 * zc] = a * g_ref[at + base]

        over(0, zc, size, point)
        out_copy(step).start()

    in_turn(section)

    def add(n, totals):
        ps, predict, target = s_ref[n], p_ref[1 + n], label_ref[n]
        terms = (ps * target, ps, predict * target, predict, target)
        return tuple(total + term for total, term in zip(totals, terms))

    zero = jnp.zeros((plan.tiles, LANES), f32)
    put_sums(plan, sums_ref, lax.fori_loop(0, zc, add, (zero,) * 5))

    def drain(step, carry):
        out_copy(step).wait()
        return carry

    lax.fori_loop(0, SECTIONS, drain, 0)


def backward_kernel(plan, *refs):
    hops = plan.back_hops
    pos_ref, sums_ref, label_ref, far_ref, mine_ref = refs[:5]
    up, down = refs[5 : 5 + hops], refs[5 + hops : 5 + 2 * hops]
    w_ref, push_ref, wt_ref, zy_ref, pull0_ref, pull1_ref, cross_ref = refs[5 + 2 * hops : -3]
    y_ref, record_ref, sem_ref = refs[-3:]
    pull_refs = (pull0_ref, pull1_ref)
    rank = pos_ref[0]
    zc, base = plan.zc, plan.pull_base
    tiles = slice(8, 8 + plan.tiles)
    mask = masks(plan)

    def in_copy(left):
        return pltpu.make_async_copy(far_ref.at[left], record_ref.at[left], sem_ref.at[left])

    for left in reversed(range(SECTIONS)):
        in_copy(left).start()
    s1, s2 = get_sums(sums_ref, 2)
    prec = (s1 + 1.0) / (s2 + 1.0)
    push_ref[...] = jnp.zeros_like(push_ref)
    wt_ref[...] = jnp.zeros_like(wt_ref)
    zy_ref[...] = jnp.zeros_like(zy_ref)
    for ref in pull_refs:
        ref[...] = jnp.zeros_like(ref)
    count_tables(plan, cross_ref, None)
    y_matrix(plan, y_ref)
    w_ref[...] = label_ref[...] - prec[None]

    def section(step, source, result, ending):
        pull_ref, next_ref = pull_refs[source], pull_refs[result]
        left = SECTIONS - 1 - step
        in_copy(left).wait()

        def push(at):
            out = []
            for n in range(plan.block):
                w = w_ref[at + n]
                out.append((push_ref, at + n + 2, w * record_ref[left, at + n + zc]))
                out.append((wt_ref, at + n + base, w * record_ref[left, at + n + 2 * zc]))
                out.append((w_ref, at + n, w * record_ref[left, at + n]))
            store_all(out)

        over(0, zc, plan.block, push)

        def widen(at):
            size = plan.span_block
            part = push_ref[pl.ds(at, size)] + push_ref[pl.ds(at + 1, size)]
            part = part + push_ref[pl.ds(at + 2, size)]
            zy_ref[pl.ds(at, size), tiles] = part + y_neighbours(y_ref, part)

        over(0, plan.span, plan.span_block, widen)

        def pull(at):
            out = []
            for n in range(plan.span_block):
                box = x_box(plan, mask, zy_ref, at + n)
                inverse = cross_ref[kind_of(plan, rank, at + n - 1)[0]]
                grown = record_ref[left, at + n + 3 * zc]
                spot = at + n - 1 + base
                old = pull_ref[spot, tiles]
                out.append((pull_ref, (spot, tiles), old - grown * grown * box * inverse))
            store_all(out)

        over(0, plan.span, plan.span_block, pull)
        reach = 2 + step

        def join(plane):
            beside = y_neighbours(y_ref, pull_ref[pl.ds(plane + base, plan.erode_block), tiles])
            for n in range(plan.erode_block):
                at = plane + n + base
                cur = pull_ref[at, tiles]

                def load(offset, at=at):
                    return pull_ref[at, 8 + offset : 8 + offset + plan.tiles]

                total = cur + pull_ref[at - 1, tiles] + pull_ref[at + 1, tiles]
                total = total + x_neighbours(plan, mask, load, cur)
                total = total + beside[n] + wt_ref[at]
                if not ending:
                    total = total * cross_ref[kind_of(plan, rank, plane + n)[0]]
                next_ref[at, tiles] = total

        over(-reach, zc + 2 * reach, plan.erode_block, join)

    def pair(n, carry):
        section(2 * n, 0, 1, False)
        section(2 * n + 1, 1, 0, False)
        return carry

    lax.fori_loop(0, ITERS // 2, pair, 0)
    section(ITERS, 0, 1, True)
    mine_ref[...] = pull1_ref[base - 1 : base + zc + 1, tiles]
    for h in range(1, hops + 1):
        n = plan.back_count(h)
        first = base + h * zc - 1
        up[h - 1][...] = pull1_ref[first : first + n, tiles]
        first = base + (1 - h) * zc - n + 1
        down[h - 1][...] = pull1_ref[first : first + n, tiles]


def finish_kernel(plan, *refs):
    hops = plan.back_hops
    pos_ref, sums_ref, skel_ref, p_ref, target_ref, ts_ref, mine_ref = refs[:7]
    below, above = refs[7 : 7 + hops], refs[7 + hops : 7 + 2 * hops]
    out_ref, loss_ref, bias_ref, h_ref, grad_ref = refs[7 + 2 * hops :]
    rank = pos_ref[0]
    zc = plan.zc
    s1, s2, s5, s6, s7 = get_sums(sums_ref, 5)
    s3, s4 = get_sums(skel_ref, 2)
    prec = (s1 + 1.0) / (s2 + 1.0)
    sens = (s3 + 1.0) / (s4 + 1.0)
    both = prec + sens
    volume = s6 + s7 + 1.0
    cl_loss = 1.0 - 2.0 * prec * sens / both
    dice_loss = 1.0 - (2.0 * s5 + 1.0) / volume
    loss_ref[...] = jnp.broadcast_to(0.5 * dice_loss + 0.5 * cl_loss, (8, LANES))
    l0 = -(sens / both) * (sens / both) / (s2 + 1.0)
    l2 = -(prec / both) * (prec / both) / (s4 + 1.0)
    l4 = -1.0 / volume
    l5 = 0.5 * (2.0 * s5 + 1.0) / (volume * volume)

    h_ref[...] = mine_ref[...]
    for h in range(1, hops + 1):
        n = plan.back_count(h)
        h_ref[:n] += below[h - 1][...]
        h_ref[plan.span - n :] += above[h - 1][...]

    total = jnp.zeros((plan.tiles, LANES), f32)
    for n in range(plan.span):
        inside = 1.0 - kind_of(plan, rank, n - 1)[1]
        predict = p_ref[n]
        skel = l0 * jnp.exp(-temper * predict) * h_ref[n]
        whole = skel + l2 * ts_ref[n] + l4 * target_ref[n] + l5
        grad = whole * predict * (1.0 - predict) * inside
        grad_ref[n * plan.tiles : (n + 1) * plan.tiles] = grad
        if 1 <= n <= zc:
            total = total + grad
    bias_ref[...] = jnp.sum(total.reshape(-1, 8, LANES), axis=0)
    lane = lane_iota((1, LANES))

    def column(tile):
        return [
            grad_ref[pl.ds(plan.tiles + tile, zc, stride=plan.tiles)],
            grad_ref[tile : tile + 1],
            grad_ref[(zc + 1) * plan.tiles + tile : (zc + 1) * plan.tiles + tile + 1],
        ]

    for a in range(plan.gx):
        pieces = [column(a * plan.own + q) for q in range(plan.own)]
        zero = [jnp.zeros((zc, LANES), f32)] + [jnp.zeros((1, LANES), f32)] * 2
        after = column((a + 1) * plan.own) if a < plan.gx - 1 else zero
        before = column(a * plan.own - 1) if a > 0 else zero
        if plan.shared:
            pieces.append(
                [
                    jnp.where(lane < plan.Y, x, 0.0) + jnp.where(lane >= LANES - plan.Y, y, 0.0)
                    for x, y in zip(after, before)
                ]
            )
        else:
            pieces += [after, before]
        edges = [edge for piece in pieces for edge in piece[1:]]
        rows = plan.R16
        edges += [jnp.zeros((1, LANES), f32)] * (plan.extra16 * rows - len(edges))
        whole = [piece[0] for piece in pieces]
        if rows > zc:
            fill = jnp.zeros((rows - zc, LANES), f32)
            whole = [jnp.concatenate([piece, fill], axis=0) for piece in whole]
        whole += [
            jnp.concatenate(edges[n * rows : (n + 1) * rows], axis=0) for n in range(plan.extra16)
        ]
        for q, piece in enumerate(whole):
            piece = piece.astype(bf16)
            for b in range(plan.gy):
                out_ref[a * plan.gy + b, q] = piece


def weight_kernel(
    plan, pos_ref, f_ref, bias_ref, got_ref, gw_ref, g_ref, dw_ref
):
    rows, inner = plan.Y, plan.ch * plan.ny
    zc, nz = plan.zc, plan.nz
    lane = lane_iota((rows, nz))
    places = {}
    for x in range(-1, plan.nx + 1):
        tile, first = plan.slot(x)
        places.setdefault(tile, {})[first] = x
    for tile in range(plan.sent):
        order = [plan.member_now(j, pos_ref) for j in range(plan.members)]
        stack = [got_ref[p, tile].astype(f32)[:zc] for p in order]
        turned = jnp.concatenate(stack, axis=0).T
        ends = []
        for end, p in ((0, order[0]), (1, order[-1])):
            n = 2 * tile + end
            row = got_ref[p, plan.sent + n // plan.R16].astype(f32)
            ends.append(row[n % plan.R16 : n % plan.R16 + 1])
        ends = jnp.concatenate(ends + [jnp.zeros((LANES - 2, LANES), f32)], axis=0).T
        for first, x in places[tile].items():
            g = turned[first : first + rows]
            end = ends[first : first + rows]
            down = jnp.where(lane == nz - 1, pltpu.roll(end, nz - 2, 1), pltpu.roll(g, nz - 1, 1))
            up = jnp.where(lane == 0, end, pltpu.roll(g, 1, 1))
            g_ref[x + 1] = jnp.concatenate([down, g, up], axis=0).astype(bf16)

    dw_ref[...] = jnp.zeros_like(dw_ref)

    width = plan.nx // PARTS
    for n in range(PARTS):
        dw_ref[...] += lax.dot_general(
            moved_columns(g_ref, n * width, width),
            columns(plan, f_ref, n * width, width),
            (((1,), (1,)), ((), ())),
            preferred_element_type=f32,
        )

    tap_y = tap_condition(plan, pos_ref[1], (rows, inner), 0, 1)
    taps = []
    for t in range(27):
        i, j, k = t // 9, t // 3 % 3, t % 3
        at = (3 * i + k) * rows
        taps.append(jnp.sum(jnp.where(tap_y == j, dw_ref[at : at + rows], 0.0), axis=0, keepdims=True))
    taps += [jnp.zeros((1, inner), f32)] * 5
    taps = jnp.concatenate(taps, axis=0)
    high = taps.astype(bf16)
    taps = taps - high.astype(f32)
    middle = taps.astype(bf16)
    low = (taps - middle.astype(f32)).astype(bf16)
    place = (
        lax.broadcasted_iota(jnp.int32, (inner, LANES), 0) // plan.ny
        == lax.broadcasted_iota(jnp.int32, (inner, LANES), 1)
    )
    sums = jnp.dot(
        jnp.concatenate([high, middle, low], axis=0),
        place.astype(f32).astype(bf16),
        preferred_element_type=f32,
    )
    sums = sums[0:32] + sums[32:64] + sums[64:96]
    total = sums[0:8]
    for n in range(1, 4):
        total = total + pltpu.roll(sums[8 * n : 8 * n + 8], 32 * n, 1)
    spot = (row_iota((8, LANES)) == 3) & (lane_iota((8, LANES)) == 96)
    total = jnp.where(spot, jnp.sum(bias_ref[...]), total)
    gw_ref[...] = jnp.broadcast_to(total[None], (plan.ranks, 8, LANES))


def wide_kernel(plan, pos_ref, wt_ref, after_ref, wide_ref):
    del after_ref
    rows, inner, bands = plan.Y, plan.ch * plan.ny, 9 * plan.Y
    spread = (
        lax.broadcasted_iota(jnp.int32, (inner, plan.ch), 0) // plan.ny
        == lax.broadcasted_iota(jnp.int32, (inner, plan.ch), 1)
    )
    spread = spread.astype(f32).astype(bf16)
    tap_y = tap_condition(plan, pos_ref[1], (inner, bands), 1, 0)
    wide = jnp.zeros((inner, bands), f32)
    tap = lax.broadcasted_iota(jnp.int32, (27, bands), 0)
    band = lax.broadcasted_iota(jnp.int32, (27, bands), 1) // rows
    for j in range(3):
        pick = (tap == 9 * (band // 3) + 3 * j + band % 3).astype(f32).astype(bf16)
        chosen = jnp.dot(wt_ref[...], pick, preferred_element_type=f32).astype(bf16)
        full = jnp.dot(spread, chosen, preferred_element_type=f32)
        wide = jnp.where(tap_y == j, full, wide)
    wide_ref[...] = wide.astype(bf16)


def feature_kernel(plan, wide_ref, g_ref, after_ref, gf_ref):
    del after_ref
    width = plan.nx // PARTS
    for n in range(PARTS):
        out = jnp.dot(
            wide_ref[...],
            moved_columns(g_ref, n * width, width),
            preferred_element_type=f32,
        )
        for x in range(width):
            part = out[:, x * plan.nz : (x + 1) * plan.nz].astype(bf16)
            gf_ref[:, n * width + x] = part.reshape(plan.ch, plan.ny, plan.nz)


def final_kernel(plan, got_ref, gw_ref, gb_ref):
    total = jnp.sum(got_ref[...], axis=0)
    for n in range(4):
        count = min(8, 27 - 8 * n)
        gw_ref[8 * n : 8 * n + count] = total[:count, 32 * n : 32 * n + plan.ch]
    gb_ref[...] = total[3:4, 96:97]


VMEM = pl.BlockSpec(memory_space=pltpu.VMEM)
SMEM = pl.BlockSpec(memory_space=pltpu.SMEM)
ANY = pl.BlockSpec(memory_space=pl.ANY)
FAR = pl.BlockSpec(memory_space=pltpu.HBM)
MIB = 1024 * 1024


def shape(dims, dtype=f32):
    return jax.ShapeDtypeStruct(dims, dtype)


def held(dims, dtype):
    if len(dims) < 2:
        return 4096
    size = jnp.dtype(dtype).itemsize
    rows = 8 * 4 // size
    total = -(-dims[-2] // rows) * rows * -(-dims[-1] // LANES) * LANES * size
    for n in dims[:-2]:
        total *= n
    return total


def limits(arrays, scratch, micros):
    total = sum(held(a.shape, a.dtype) for a in arrays)
    total += sum(held(a.shape, a.dtype) for a in scratch if len(a.shape) > 1)
    limit = min(63 * MIB, total + total // 8 + 4 * MIB)
    return dict(
        compiler_params=pltpu.CompilerParams(vmem_limit_bytes=limit),
        cost_estimate=pl.CostEstimate(
            flops=0, transcendentals=0, bytes_accessed=int(micros * 2.5e4)
        ),
    )


def per_device(mesh_shape, features, weight, bias, label):
    plan = Plan(mesh_shape, features.shape)
    members, sent, tiles = plan.members, plan.sent, plan.tiles
    inner, bands = plan.ch * plan.ny, 9 * plan.Y
    x, y, z = (lax.axis_index(axis).astype(jnp.int32) for axis in ALL_AXES)
    mine = y * plan.gx + jnp.where(y % 2 == 0, x, plan.gx - 1 - x)
    place = z * members + jnp.where(z % 2 == 0, mine, members - 1 - mine)
    pos = pltpu.with_memory_space_constraint(jnp.stack([place, y]), pltpu.HBM)

    def call(
        kernel, out_shape, in_specs, operands, micros, scratch=(), out_specs=None
    ):
        outs = jax.tree.leaves(out_shape)
        ins = [a for spec, a in zip(in_specs, operands) if spec is VMEM]
        return pl.pallas_call(
            functools.partial(kernel, plan),
            out_shape=out_shape,
            in_specs=in_specs,
            out_specs=out_specs or jax.tree.map(lambda s: VMEM, out_shape),
            scratch_shapes=list(scratch),
            **limits(ins + outs, scratch, micros),
        )(*operands)

    def exchange(array):
        return lax.all_to_all(array, GROUP, 0, 0, tiled=True)

    def everywhere(array):
        return lax.all_to_all(array, ALL_AXES, 0, 0, tiled=True)

    def hop(array, distance):
        def device(r):
            z = r // members
            return plan.member(r % members, z % 2 == 1) * plan.gz + z

        pairs = [
            (device(r), device(r + distance))
            for r in range(plan.ranks)
            if 0 <= r + distance < plan.ranks
        ]
        return lax.ppermute(array, ALL_AXES, pairs)

    turned = pltpu.with_memory_space_constraint(weight.T, pltpu.HBM)
    features_ahead = features
    features, weight, label = (
        pltpu.with_memory_space_constraint(a, pltpu.HBM) for a in (features, weight, label)
    )
    features_near = [pltpu.VMEM(features.shape, bf16), pltpu.SemaphoreType.DMA((PARTS,))]
    sent_logits = call(
        conv_kernel,
        shape((members, sent + plan.extra, plan.R, LANES)),
        [SMEM, VMEM, FAR, VMEM],
        (pos, weight, features, label),
        7,
        [
            pltpu.VMEM((bands, inner), bf16),
            pltpu.VMEM((plan.nx + 2, 3 * plan.Y, plan.nz), f32),
        ]
        + features_near,
    )

    def planes(array):
        return array.reshape(-1, tiles, LANES)

    zc, rest = plan.zc, plan.rest
    short = shape(((rest + 1 + -(-rest // 2)) * tiles, LANES))
    whole, label_own, head, tail = call(
        gather_kernel,
        [
            shape(((zc + 2 + -(-zc // 2)) * tiles, LANES)),
            shape((zc * tiles, LANES)),
            short,
            short,
        ],
        [VMEM],
        (exchange(sent_logits),),
        1.5,
    )
    whole, label_own, head, tail = (planes(part) for part in (whole, label_own, head, tail))
    around = [
        hop(whole if h < plan.hops else part, sign * h)
        for sign, part in ((1, tail), (-1, head))
        for h in range(1, plan.hops + 1)
    ]

    slab = (zc, tiles, LANES)
    span = (plan.span, tiles, LANES)
    everyone = shape((plan.ranks, 8, LANES))
    table = pltpu.VMEM((3, tiles, LANES), f32)

    records = pltpu.HBM((SECTIONS, plan.records, tiles, LANES), f32)
    y_near = pltpu.VMEM((2 * LANES, LANES), bf16)
    record_near = [
        y_near,
        pltpu.VMEM(records.shape, f32),
        pltpu.SemaphoreType.DMA((SECTIONS,)),
    ]
    record, predict, sums = call(
        forward_kernel,
        [records, shape(span), everyone],
        [SMEM, SMEM] + [VMEM] * (2 + 2 * plan.hops),
        (pos, bias, label_own, whole, *around),
        11,
        [
            pltpu.VMEM((plan.planes, plan.pad, LANES), f32),
            pltpu.VMEM((plan.planes, plan.pad, LANES), f32),
            pltpu.VMEM((plan.planes, tiles, LANES), f32),
            pltpu.VMEM((plan.planes, tiles, LANES), f32),
            pltpu.VMEM((zc, plan.pad, LANES), f32),
            pltpu.VMEM(slab, f32),
            table,
            table,
        ]
        + record_near,
        [FAR, VMEM, VMEM],
    )
    record = pltpu.with_memory_space_constraint(record, pltpu.HBM)
    sums = everywhere(sums)
    room = plan.win + 2 + plan.erode_block
    target, ts, skel_sums = call(
        target_kernel,
        [shape(span), shape(span), everyone],
        [SMEM] + [VMEM] * (2 + 2 * plan.hops),
        (pos, predict, label_own, *around),
        13,
        [
            pltpu.VMEM((plan.win, tiles, LANES), f32),
            pltpu.VMEM((room, plan.pad, LANES), f32),
            pltpu.VMEM((room, plan.pad, LANES), f32),
            pltpu.VMEM((room, tiles, LANES), f32),
            pltpu.VMEM((plan.span, plan.pad, LANES), f32),
            table,
            table,
            y_near,
        ],
    )
    skel_sums = everywhere(skel_sums)
    outer = [
        shape((plan.back_count(h), tiles, LANES)) for h in range(1, plan.back_hops + 1)
    ]
    mine, *outer = call(
        backward_kernel,
        [shape(span)] + outer * 2,
        [SMEM, VMEM, VMEM, FAR],
        (pos, sums, label_own, record),
        11,
        [
            pltpu.VMEM(slab, f32),
            pltpu.VMEM((zc + 4, tiles, LANES), f32),
            pltpu.VMEM((plan.pull_planes, tiles, LANES), f32),
            pltpu.VMEM((plan.span, plan.pad, LANES), f32),
            pltpu.VMEM((plan.pull_planes, plan.pad, LANES), f32),
            pltpu.VMEM((plan.pull_planes, plan.pad, LANES), f32),
            table,
        ]
        + record_near,
    )
    wide = call(
        wide_kernel, shape((inner, bands), bf16), [SMEM, VMEM, ANY], (pos, turned, mine), 2
    )
    beyond = []
    for sign, arrays in ((1, outer[: plan.back_hops]), (-1, outer[plan.back_hops :])):
        for h in range(1, plan.back_hops + 1):
            beyond.append(hop(arrays[h - 1], sign * h))
    grad_sent, loss, bias_part = call(
        finish_kernel,
        [
            shape((members, sent + plan.extra16, plan.R16, LANES), bf16),
            shape((8, LANES)),
            shape((8, LANES)),
        ],
        [SMEM] + [VMEM] * (6 + 2 * plan.back_hops),
        (pos, sums, skel_sums, predict, target, ts, mine, *beyond),
        2,
        [pltpu.VMEM(span, f32), pltpu.VMEM((plan.span * tiles, LANES), f32)],
    )

    moved = shape((plan.nx + 2, 3 * plan.Y, plan.nz), bf16)
    partial, g = call(
        weight_kernel,
        [shape((plan.ranks, 8, LANES)), moved],
        [SMEM, VMEM, VMEM, VMEM],
        (pos, features_ahead, bias_part, exchange(grad_sent)),
        5,
        [pltpu.VMEM((bands, inner), f32)],
    )
    grad_features = call(
        feature_kernel,
        shape(features.shape, bf16),
        [VMEM, VMEM, ANY],
        (wide, g, partial),
        5,
    )
    grad_weight, grad_bias = call(
        final_kernel,
        [shape((27, plan.ch)), shape((1, 1))],
        [VMEM],
        (everywhere(partial),),
        1.5,
    )
    return (loss[0, :1], grad_features, grad_weight, grad_bias.reshape(1))


def solution(mesh):
    in_specs = (P(None, "gx", "gy", "gz"), P(), P(), P("gx", "gy", "gz"))
    out_specs = (P(), P(None, "gx", "gy", "gz"), P(), P())

    def body(*args):
        return per_device(dict(mesh.shape), *args)

    return jax.shard_map(
        body, mesh=mesh, in_specs=in_specs, out_specs=out_specs, check_vma=False
    )
```

```python
import functools

import jax
import jax.numpy as jnp
from jax import lax
from jax.experimental import pallas as pl
from jax.experimental.pallas import tpu as pltpu
from jax.sharding import PartitionSpec as P

ITERS = 10
SECTIONS = ITERS + 1
LANES = 128
HALO = SECTIONS + 2
BACK = SECTIONS + 1

BLOCK = 32
SPAN_BLOCK = 40
ERODE_BLOCK = 20

temper = 20.0
sharpness = 40.0

GROUP = ("gx", "gy")
ALL_AXES = ("gx", "gy", "gz")
f32 = jnp.float32
bf16 = jnp.bfloat16


def up8(value):
    return -(-value // 8) * 8


class Plan:
    def __init__(self, mesh_shape, block):
        self.ch, self.nx, self.ny, self.nz = block
        self.gx, self.gy, self.gz = (mesh_shape[a] for a in ALL_AXES)
        self.members = self.gx * self.gy
        self.ranks = self.members * self.gz
        self.X = self.nx * self.gx
        self.Y = self.ny * self.gy
        self.Z = self.nz * self.gz
        assert LANES % self.Y == 0 and self.nz == LANES
        assert self.nz % self.members == 0
        self.zc = self.nz // self.members
        self.per = LANES // self.Y
        assert self.nx % self.per == 0
        self.tiles = self.X // self.per
        self.own = self.nx // self.per
        self.shared = self.per > 1
        self.sent = self.own + (1 if self.shared else 2)
        self.R = up8(self.zc)
        self.extra = -(-2 * self.sent // self.R)
        self.R16 = -(-self.zc // 16) * 16
        self.extra16 = -(-2 * self.sent // self.R16)
        self.pad = self.tiles + 16
        self.win = self.zc + 2 * HALO
        self.span = self.zc + 2
        self.block = self.blocks_of(self.zc, BLOCK)
        self.span_block = self.blocks_of(self.span, SPAN_BLOCK)
        self.win_block = self.blocks_of(self.win, 32)
        self.erode_block = max(1, ERODE_BLOCK * 8 // self.tiles)
        self.base = HALO + 1
        self.planes = self.zc + 2 * HALO + 2 + self.erode_block
        self.pull_base = BACK + 2
        self.pull_planes = self.zc + 2 * BACK + 4 + self.erode_block
        self.hops = -(-HALO // self.zc)
        self.rest = HALO - (self.hops - 1) * self.zc
        self.records = 3 * self.zc + self.span
        assert self.ny == 16 and self.gy > 1
        self.back_hops = -(-(BACK + 1) // self.zc)

    def back_count(self, h):
        return min(self.zc + BACK + 1 - h * self.zc, self.span)

    def blocks_of(self, count, most):
        fits = [n for n in range(1, count + 1) if count % n == 0 and n * self.tiles <= 8 * most]
        return fits[-1] if fits else 1

    def slab(self, member):
        x, y = member // self.gy, member % self.gy
        return y * self.gx + (x if y % 2 == 0 else self.gx - 1 - x)

    def member(self, slab, odd):
        slab = self.members - 1 - slab if odd else slab
        return next(p for p in range(self.members) if self.slab(p) == slab)

    def member_now(self, slab, pos_ref):
        odd = pos_ref[0] // self.members % 2 == 1
        return jnp.where(odd, self.member(slab, True), self.member(slab, False))

    def label_lane(self, member_y):
        return 0 if member_y == self.gy - 1 else (member_y + 1) * self.ny + 8

    def slot(self, x):
        if 0 <= x < self.nx:
            return x // self.per, (x % self.per) * self.Y
        if x == self.nx:
            return self.own, 0
        return self.sent - 1, LANES - self.Y


def lane_iota(shape):
    return lax.broadcasted_iota(jnp.int32, shape, len(shape) - 1)


def row_iota(shape):
    return lax.broadcasted_iota(jnp.int32, shape, len(shape) - 2)


def masks(plan):
    return lane_iota((plan.tiles, LANES))


def x_neighbours(plan, mask, load, cur):
    lower, upper = load(-1), load(1)
    if plan.Y == LANES:
        return lower + upper
    lower = pltpu.roll(jnp.where(mask >= LANES - plan.Y, lower, cur), plan.Y, 1)
    upper = pltpu.roll(jnp.where(mask < plan.Y, upper, cur), LANES - plan.Y, 1)
    return lower + upper


def y_matrix(plan, ref):
    row = row_iota((2 * LANES, LANES)) % LANES
    lane = lane_iota((2 * LANES, LANES))
    near = (row == lane - 1) | (row == lane + 1)
    ref[...] = (near & (row // plan.Y == lane // plan.Y)).astype(f32).astype(bf16)


def y_neighbours(ref, block):
    flat = block.reshape(-1, LANES)
    high = flat.astype(bf16)
    low = (flat - high.astype(f32)).astype(bf16)
    both = jnp.concatenate([high, low], axis=1)
    return jnp.dot(both, ref[...], preferred_element_type=f32).reshape(block.shape)


def count_tables(plan, cross_ref, box_ref):
    flat = row_iota((plan.tiles, LANES)) * LANES + lane_iota((plan.tiles, LANES))
    y, x = flat % plan.Y, flat // plan.Y

    def along(spot, size):
        return 3.0 - (spot == 0).astype(f32) - (spot == size - 1).astype(f32)

    cx, cy = along(x, plan.X), along(y, plan.Y)
    for kind, cz in ((1, 2.0), (2, 3.0)):
        if cross_ref is not None:
            cross_ref[kind] = 1.0 / (cx + cy + cz - 2.0)
        if box_ref is not None:
            box_ref[kind] = 1.0 / (cx * cy * cz)
    for ref in (cross_ref, box_ref):
        if ref is not None:
            ref[0] = jnp.zeros((plan.tiles, LANES), f32)


def kind_of(plan, rank, plane):
    z = rank * plan.zc + plane
    inside = (z >= 0) & (z < plan.Z)
    edge = (z == 0) | (z == plan.Z - 1)
    return jnp.where(inside, jnp.where(edge, 1, 2), 0), jnp.where(inside, 0.0, 1.0)


def store_all(pairs):
    for ref, at, value in pairs:
        ref[at] = value


def over(first, count, size, body):
    def at(n, carry):
        body(first + n * size)
        return carry

    lax.fori_loop(0, (count + size - 1) // size, at, 0)


def tap_condition(plan, member_y, shape, y_dim, in_dim):
    y = lax.broadcasted_iota(jnp.int32, shape, y_dim) % plan.Y
    own = lax.broadcasted_iota(jnp.int32, shape, in_dim) % plan.ny
    return own + member_y * plan.ny - y + 1


PARTS = 4


def stream(plan, far_ref, near_ref, sem_ref):
    width = plan.nx // PARTS
    copies = []
    for n in range(PARTS):
        span = pl.ds(n * width, width)
        copies.append(
            pltpu.make_async_copy(far_ref.at[:, span], near_ref.at[:, span], sem_ref.at[n])
        )
        copies[-1].start()
    return copies


def columns(plan, ref, first, count):
    blocks = [ref[:, x].reshape(-1, plan.nz) for x in range(first, first + count)]
    return jnp.concatenate(blocks, axis=1)


def moved_columns(ref, first, count):
    blocks = [
        jnp.concatenate([ref[x + 2], ref[x + 1], ref[x]], axis=0)
        for x in range(first, first + count)
    ]
    return jnp.concatenate(blocks, axis=1)


def conv_kernel(
    plan, pos_ref, w_ref, far_ref, label_ref, out_ref, wide_ref, acc_ref, f_ref, sem_ref
):
    width = plan.nx // PARTS
    copies = stream(plan, far_ref, f_ref, sem_ref)
    rows, inner = plan.Y, plan.ch * plan.ny
    spread = (
        lax.broadcasted_iota(jnp.int32, (plan.ch, inner), 0)
        == lax.broadcasted_iota(jnp.int32, (plan.ch, inner), 1) // plan.ny
    )
    taps = jnp.dot(
        w_ref[...], spread.astype(f32).astype(bf16), preferred_element_type=f32
    )
    tap_y = tap_condition(plan, pos_ref[1], (rows, inner), 0, 1)
    for i in range(3):
        for k in range(3):
            band = jnp.zeros((rows, inner), f32)
            for j in range(3):
                t = 9 * i + 3 * j + k
                band = jnp.where(tap_y == j, taps[t : t + 1], band)
            at = (3 * i + k) * rows
            wide_ref[at : at + rows] = band.astype(bf16)
    acc_ref[...] = jnp.zeros_like(acc_ref)

    for n in range(PARTS):
        copies[n].wait()
        first = n * width
        out = jnp.dot(
            wide_ref[...], columns(plan, f_ref, first, width), preferred_element_type=f32
        )
        for slot in range(first, first + width + 2):
            terms = [
                out[3 * i * rows : 3 * (i + 1) * rows, (x - first) * plan.nz : (x - first + 1) * plan.nz]
                for i in range(3)
                for x in (slot - 2 + i,)
                if first <= x < first + width
            ]
            acc_ref[slot] += functools.reduce(jnp.add, terms)

    out_ref[...] = jnp.zeros_like(out_ref)
    places = {}
    for x in range(-1, plan.nx + 1):
        tile, lane = plan.slot(x)
        places.setdefault(tile, {})[lane] = x
    lane = lane_iota((rows, plan.nz))
    words = [label_ref[x, 0:8] + 2 * label_ref[x, 8:16] for x in range(plan.nx)]
    first_group = jnp.where(
        pos_ref[1] == plan.gy - 1, 0, (pos_ref[1] + 1) * (plan.ny // 8) + 1
    )
    labelled = lax.broadcasted_iota(jnp.int32, (rows, plan.nz), 0) // 8 == first_group
    for tile in range(plan.sent):
        parts, spills = [], []
        for first in range(0, LANES, rows):
            x = places[tile].get(first)
            if x is None:
                parts.append(jnp.zeros((rows, plan.nz), f32))
                spills.append(jnp.zeros((rows, plan.nz), f32))
                continue
            low = acc_ref[x + 1, 0:rows]
            mid = acc_ref[x + 1, rows : 2 * rows]
            high = acc_ref[x + 1, 2 * rows : 3 * rows]
            total = mid + jnp.where(lane == 0, 0.0, pltpu.roll(low, 1, 1))
            total = total + jnp.where(lane == plan.nz - 1, 0.0, pltpu.roll(high, plan.nz - 1, 1))
            if 0 <= x < plan.nx:
                word = jnp.concatenate([words[x].astype(f32)] * (rows // 8), axis=0)
                total = total + jnp.where(labelled, word, 0.0)
            parts.append(total)
            spill = jnp.where(lane == 1, pltpu.roll(low, 2, 1), 0.0)
            spills.append(jnp.where(lane == 0, high, spill))
        turned = jnp.concatenate(parts, axis=0).T
        spill = jnp.concatenate(spills, axis=0).T
        for j in range(plan.members):
            p = plan.member_now(j, pos_ref)
            out_ref[p, tile, 0 : plan.zc] = turned[j * plan.zc : (j + 1) * plan.zc]
        for end, j in ((0, 0), (1, plan.members - 1)):
            n = 2 * tile + end
            at = plan.sent + n // plan.R
            p = plan.member_now(j, pos_ref)
            out_ref[p, at, n % plan.R : n % plan.R + 1] = spill[end : end + 1]


def gather_kernel(plan, got_ref, out_ref, label_ref, head_ref, tail_ref):
    tiles, zc, rest = plan.tiles, plan.zc, plan.rest
    lane = lane_iota((1, LANES))
    spot = lane % plan.Y

    def part(p, q):
        values = [got_ref[p, q, 0:zc]]
        for end in range(2):
            n = 2 * q + end
            at = plan.sent + n // plan.R
            values.append(got_ref[p, at, n % plan.R : n % plan.R + 1])
        return values

    for a in range(plan.gx):
        for q in range(plan.own):
            parts = []
            label = jnp.zeros((zc, LANES), f32)
            for b in range(plan.gy):
                start = b * plan.ny
                values = part(a * plan.gy + b, q)
                second = (values[0] >= 1.5).astype(f32)
                first = values[0] - 2.0 * second
                move = start - plan.label_lane(b)
                first = pltpu.roll(first, move % LANES, 1)
                second = pltpu.roll(second, (move + 8) % LANES, 1)
                label = jnp.where((spot >= start) & (spot < start + 8), first, label)
                label = jnp.where((spot >= start + 8) & (spot < start + 16), second, label)
                mine = (spot >= start - 1) & (spot <= start + plan.ny)
                parts.append([jnp.where(mine, v, 0.0) for v in values])
                if q == plan.own - 1 and a < plan.gx - 1:
                    edge = part((a + 1) * plan.gy + b, plan.sent - 1)
                    parts.append([jnp.where(lane >= LANES - plan.Y, v, 0.0) for v in edge])
                if q == 0 and a > 0:
                    edge = part((a - 1) * plan.gy + b, plan.own)
                    parts.append([jnp.where(lane < plan.Y, v, 0.0) for v in edge])
            whole, low, high = (functools.reduce(jnp.add, vs) for vs in zip(*parts))
            tile = a * plan.own + q
            label_ref[pl.ds(tile, zc, stride=tiles)] = label
            out_ref[pl.ds(tile, zc, stride=tiles)] = whole
            out_ref[zc * tiles + tile : zc * tiles + tile + 1] = low
            out_ref[(zc + 1) * tiles + tile : (zc + 1) * tiles + tile + 1] = high

    def pack(ref, at, first, count):
        half = -(-count // 2)
        for n in range(half):
            word = label_ref[(first + n) * tiles : (first + n + 1) * tiles]
            if n + half < count:
                other = first + n + half
                word = word + 2.0 * label_ref[other * tiles : (other + 1) * tiles]
            ref[(at + n) * tiles : (at + n + 1) * tiles] = word

    pack(out_ref, zc + 2, 0, zc)
    head_ref[: rest * tiles] = out_ref[: rest * tiles]
    head_ref[rest * tiles : (rest + 1) * tiles] = out_ref[zc * tiles : (zc + 1) * tiles]
    pack(head_ref, rest + 1, 0, rest)
    tail_ref[: rest * tiles] = out_ref[(zc - rest) * tiles : zc * tiles]
    tail_ref[rest * tiles : (rest + 1) * tiles] = out_ref[(zc + 1) * tiles : (zc + 2) * tiles]
    pack(tail_ref, rest + 1, zc - rest, rest)


LOG = 1.0 / sharpness


def thin(e, box, inverse, outside):
    box = box + outside
    ratio = e * box * inverse + outside
    square = ratio * ratio
    more = 1.0 + square
    joint = 1.0 / (box * more)
    slope = joint * box
    return joint * more, slope, jnp.log(square * slope)


def lift(scaled, s):
    small = jnp.exp(scaled * (s - 1.0))
    more = 1.0 + small
    return s + jnp.log(more) * LOG, small * (1.0 / more)


def erode(plan, rank, mask, y_ref, source, result, grown_ref, table_ref, base, first, count):
    tiles = slice(8, 8 + plan.tiles)

    def body(plane):
        beside = y_neighbours(y_ref, source[pl.ds(plane + base, plan.erode_block), tiles])
        for n in range(plan.erode_block):
            at = plane + n + base
            cur = source[at, tiles]

            def load(offset, at=at):
                return source[at, 8 + offset : 8 + offset + plan.tiles]

            total = cur + source[at - 1, tiles] + source[at + 1, tiles]
            total = total + x_neighbours(plan, mask, load, cur) + beside[n]
            kind, outside = kind_of(plan, rank, plane + n)
            total = total * table_ref[kind]
            result[at, tiles] = total
            grown_ref[at] = 1.0 / (total + outside) - outside

    over(first, count, plan.erode_block, body)


def spread(plan, y_ref, grown_ref, zy_ref, base, first, count, size):
    tiles = slice(8, 8 + plan.tiles)

    def body(plane):
        at = plane + base
        part = grown_ref[pl.ds(at - 1, size)] + grown_ref[pl.ds(at, size)]
        part = part + grown_ref[pl.ds(at + 1, size)]
        zy_ref[pl.ds(plane - first, size), tiles] = part + y_neighbours(y_ref, part)

    over(first, count, size, body)


def in_turn(section):
    section(0, 0, 1, True)

    def pair(n, carry):
        section(2 * n + 1, 1, 0, False)
        section(2 * n + 2, 0, 1, False)
        return carry

    lax.fori_loop(0, ITERS // 2, pair, 0)


def x_box(plan, mask, zy_ref, at):
    cur = zy_ref[at, 8 : 8 + plan.tiles]

    def load(offset):
        return zy_ref[at, 8 + offset : 8 + offset + plan.tiles]

    return cur + x_neighbours(plan, mask, load, cur)


def target_kernel(plan, *refs):
    hops = plan.hops
    pos_ref, p_ref, own_ref = refs[:3]
    below, above = refs[3 : 3 + hops], refs[3 + hops : 3 + 2 * hops]
    target_ref, ts_ref, sums_ref = refs[3 + 2 * hops : 6 + 2 * hops]
    all_ref, e0_ref, e1_ref, g_ref, zy_ref, cross_ref, box_ref, y_ref = refs[6 + 2 * hops :]
    zc, win, span = plan.zc, plan.win, plan.span
    size = plan.span_block
    base = HALO + 1
    tiles = slice(8, 8 + plan.tiles)
    rank = pos_ref[0]
    mask = masks(plan)
    count_tables(plan, cross_ref, box_ref)
    y_matrix(plan, y_ref)
    e_refs = (e0_ref, e1_ref)
    e0_ref[...] = jnp.zeros_like(e0_ref)
    e1_ref[...] = jnp.zeros_like(e1_ref)
    zy_ref[...] = jnp.zeros_like(zy_ref)
    all_ref[HALO : HALO + zc] = own_ref[...]
    for h in range(1, hops + 1):
        count = zc if h < hops else plan.rest
        at = zc + 2 if h < hops else plan.rest + 1
        half = -(-count // 2)
        for refs_of, first in ((below, HALO - (h - 1) * zc - count), (above, HALO + h * zc)):
            words = refs_of[h - 1][at : at + half]
            second = (words >= 1.5).astype(f32)
            all_ref[first : first + half] = words - 2.0 * second
            if count > half:
                all_ref[first + half : first + count] = second[: count - half]
    target_ref[...] = all_ref[HALO - 1 : HALO + zc + 1]

    def fill(plane):
        out = []
        for n in range(plan.win_block):
            at = plane + n
            inside = 1.0 - kind_of(plan, rank, at - HALO)[1]
            out.append((e0_ref, (at + 1, tiles), jnp.exp(-temper * all_ref[at]) * inside))
        store_all(out)

    over(0, win, plan.win_block, fill)

    def section(step, source, result, opening):
        e_ref = e_refs[source]
        reach = 2 + ITERS - step
        count = zc + 2 * reach
        erode(
            plan, rank, mask, y_ref, e_ref, e_refs[result], g_ref, cross_ref, base, -reach, count
        )
        spread(plan, y_ref, g_ref, zy_ref, base, -1, span, size)

        def point(plane):
            before = [None if opening else ts_ref[plane + n] for n in range(size)]
            for n in range(size):
                at = plane + n
                box = x_box(plan, mask, zy_ref, at)
                kind, outside = kind_of(plan, rank, at - 1)
                _, _, scaled = thin(e_ref[at - 1 + base, tiles], box, box_ref[kind], outside)
                ts_ref[at] = scaled * -LOG if opening else lift(scaled, before[n])[0]

        over(0, span, size, point)

    in_turn(section)

    def add(n, totals):
        ts = ts_ref[1 + n]
        return totals[0] + ts * p_ref[1 + n], totals[1] + ts

    zero = jnp.zeros((plan.tiles, LANES), f32)
    put_sums(plan, sums_ref, lax.fori_loop(0, zc, add, (zero,) * 2))


def put_sums(plan, ref, totals):
    lines = [jnp.sum(total, axis=0, keepdims=True) for total in totals]
    lines += [jnp.zeros((1, LANES), f32)] * (8 - len(lines))
    ref[...] = jnp.broadcast_to(jnp.concatenate(lines, axis=0)[None], (plan.ranks, 8, LANES))


def get_sums(ref, count):
    lines = jnp.sum(jnp.sum(ref[...], axis=0), axis=1, keepdims=True)
    return [lines[n : n + 1] for n in range(count)]


def forward_kernel(plan, *refs):
    hops = plan.hops
    pos_ref, bias_ref, label_ref, own_ref = refs[:4]
    refs = refs[4:]
    below, above = refs[:hops], refs[hops : 2 * hops]
    refs = refs[2 * hops :]
    far_ref, p_ref, sums_ref = refs[:3]
    e0_ref, e1_ref, g0_ref, g1_ref, zy_ref, s_ref, cross_ref, box_ref = refs[3:11]
    y_ref, record_ref, sem_ref = refs[11:]
    e_refs, g_refs = (e0_ref, e1_ref), (g0_ref, g1_ref)
    base, zc, size = plan.base, plan.zc, plan.block
    tiles = slice(8, 8 + plan.tiles)
    rank = pos_ref[0]
    mask = masks(plan)

    for ref in e_refs + g_refs:
        ref[...] = jnp.zeros_like(ref)
    zy_ref[...] = jnp.zeros_like(zy_ref)
    count_tables(plan, cross_ref, box_ref)
    y_matrix(plan, y_ref)
    e0_ref[base : base + zc, tiles] = own_ref[:zc]
    for h in range(1, hops + 1):
        n = zc if h < hops else plan.rest
        first = base - (h - 1) * zc - n
        e0_ref[first : first + n, tiles] = below[h - 1][:n]
        first = base + h * zc
        e0_ref[first : first + n, tiles] = above[h - 1][:n]
    e0_ref[base - 1, tiles] += own_ref[zc]
    e0_ref[base + zc, tiles] += own_ref[zc + 1]
    for h in range(1, hops + 1):
        if h < hops:
            e0_ref[base - h * zc - 1, tiles] += below[h - 1][zc]
            e0_ref[base + (h + 1) * zc, tiles] += above[h - 1][zc + 1]
            e0_ref[base - (h - 1) * zc, tiles] += below[h - 1][zc + 1]
            e0_ref[base + h * zc - 1, tiles] += above[h - 1][zc]
        else:
            e0_ref[base - (h - 1) * zc, tiles] += below[h - 1][plan.rest]
            e0_ref[base + h * zc - 1, tiles] += above[h - 1][plan.rest]

    def sigmoid(logits):
        small = jnp.exp(-jnp.abs(logits))
        part = 1.0 / (1.0 + small)
        return jnp.where(logits >= 0, part, small * part)

    for n in range(plan.span):
        p_ref[n] = sigmoid(e0_ref[base - 1 + n, tiles] + bias_ref[0])

    def fill(plane):
        out = []
        for n in range(plan.erode_block):
            at = plane + n
            inside = 1.0 - kind_of(plan, rank, at - base)[1]
            predict = sigmoid(e0_ref[at, tiles] + bias_ref[0])
            out.append((e0_ref, (at, tiles), jnp.exp(-temper * predict) * inside))
            out.append((g0_ref, at, jnp.exp(temper * predict) * inside))
        store_all(out)

    over(1, zc + 2 * HALO, plan.erode_block, fill)


    def out_copy(step):
        return pltpu.make_async_copy(record_ref.at[step], far_ref.at[step], sem_ref.at[step])

    def section(step, source, result, opening):
        e_ref, g_ref, after_ref = e_refs[source], g_refs[source], g_refs[result]
        reach = 1 + ITERS - step
        count = zc + 2 * reach
        erode(
            plan, rank, mask, y_ref, e_ref, e_refs[result], after_ref, cross_ref, base, -reach,
            count,
        )
        spread(plan, y_ref, after_ref, zy_ref, base, 0, zc, size)
        record_ref[step, 3 * zc :] = after_ref[base - 1 : base + zc + 1]

        def point(plane):
            before = [None if opening else s_ref[plane + n] for n in range(size)]
            for n in range(size):
                at = plane + n
                box = x_box(plan, mask, zy_ref, at)
                kind, outside = kind_of(plan, rank, at)
                e = e_ref[at + base, tiles]
                over_box, slope, scaled = thin(e, box, box_ref[kind], outside)
                if opening:
                    grown, a = scaled * -LOG, slope
                    record_ref[step, at] = jnp.ones_like(a)
                else:
                    s = before[n]
                    grown, rate = lift(scaled, s)
                    a = rate * (1.0 - s) * slope
                    record_ref[step, at] = 1.0 + rate * scaled * LOG
                s_ref[at] = grown
                record_ref[step, at + zc] = a * over_box
                record_ref[step, at + 2 * zc] = a * g_ref[at + base]

        over(0, zc, size, point)
        out_copy(step).start()

    in_turn(section)

    def add(n, totals):
        ps, predict, target = s_ref[n], p_ref[1 + n], label_ref[n]
        terms = (ps * target, ps, predict * target, predict, target)
        return tuple(total + term for total, term in zip(totals, terms))

    zero = jnp.zeros((plan.tiles, LANES), f32)
    put_sums(plan, sums_ref, lax.fori_loop(0, zc, add, (zero,) * 5))

    def drain(step, carry):
        out_copy(step).wait()
        return carry

    lax.fori_loop(0, SECTIONS, drain, 0)


def backward_kernel(plan, *refs):
    hops = plan.back_hops
    pos_ref, sums_ref, label_ref, far_ref, mine_ref = refs[:5]
    up, down = refs[5 : 5 + hops], refs[5 + hops : 5 + 2 * hops]
    w_ref, push_ref, wt_ref, zy_ref, pull0_ref, pull1_ref, cross_ref = refs[5 + 2 * hops : -3]
    y_ref, record_ref, sem_ref = refs[-3:]
    pull_refs = (pull0_ref, pull1_ref)
    rank = pos_ref[0]
    zc, base = plan.zc, plan.pull_base
    tiles = slice(8, 8 + plan.tiles)
    mask = masks(plan)

    def in_copy(left):
        return pltpu.make_async_copy(far_ref.at[left], record_ref.at[left], sem_ref.at[left])

    for left in reversed(range(SECTIONS)):
        in_copy(left).start()
    s1, s2 = get_sums(sums_ref, 2)
    prec = (s1 + 1.0) / (s2 + 1.0)
    push_ref[...] = jnp.zeros_like(push_ref)
    wt_ref[...] = jnp.zeros_like(wt_ref)
    zy_ref[...] = jnp.zeros_like(zy_ref)
    for ref in pull_refs:
        ref[...] = jnp.zeros_like(ref)
    count_tables(plan, cross_ref, None)
    y_matrix(plan, y_ref)
    w_ref[...] = label_ref[...] - prec[None]

    def section(step, source, result, ending):
        pull_ref, next_ref = pull_refs[source], pull_refs[result]
        left = SECTIONS - 1 - step
        in_copy(left).wait()

        def push(at):
            out = []
            for n in range(plan.block):
                w = w_ref[at + n]
                out.append((push_ref, at + n + 2, w * record_ref[left, at + n + zc]))
                out.append((wt_ref, at + n + base, w * record_ref[left, at + n + 2 * zc]))
                out.append((w_ref, at + n, w * record_ref[left, at + n]))
            store_all(out)

        over(0, zc, plan.block, push)

        def widen(at):
            size = plan.span_block
            part = push_ref[pl.ds(at, size)] + push_ref[pl.ds(at + 1, size)]
            part = part + push_ref[pl.ds(at + 2, size)]
            zy_ref[pl.ds(at, size), tiles] = part + y_neighbours(y_ref, part)

        over(0, plan.span, plan.span_block, widen)

        def pull(at):
            out = []
            for n in range(plan.span_block):
                box = x_box(plan, mask, zy_ref, at + n)
                inverse = cross_ref[kind_of(plan, rank, at + n - 1)[0]]
                grown = record_ref[left, at + n + 3 * zc]
                spot = at + n - 1 + base
                old = pull_ref[spot, tiles]
                out.append((pull_ref, (spot, tiles), old - grown * grown * box * inverse))
            store_all(out)

        over(0, plan.span, plan.span_block, pull)
        reach = 2 + step

        def join(plane):
            beside = y_neighbours(y_ref, pull_ref[pl.ds(plane + base, plan.erode_block), tiles])
            for n in range(plan.erode_block):
                at = plane + n + base
                cur = pull_ref[at, tiles]

                def load(offset, at=at):
                    return pull_ref[at, 8 + offset : 8 + offset + plan.tiles]

                total = cur + pull_ref[at - 1, tiles] + pull_ref[at + 1, tiles]
                total = total + x_neighbours(plan, mask, load, cur)
                total = total + beside[n] + wt_ref[at]
                if not ending:
                    total = total * cross_ref[kind_of(plan, rank, plane + n)[0]]
                next_ref[at, tiles] = total

        over(-reach, zc + 2 * reach, plan.erode_block, join)

    def pair(n, carry):
        section(2 * n, 0, 1, False)
        section(2 * n + 1, 1, 0, False)
        return carry

    lax.fori_loop(0, ITERS // 2, pair, 0)
    section(ITERS, 0, 1, True)
    mine_ref[...] = pull1_ref[base - 1 : base + zc + 1, tiles]
    for h in range(1, hops + 1):
        n = plan.back_count(h)
        first = base + h * zc - 1
        up[h - 1][...] = pull1_ref[first : first + n, tiles]
        first = base + (1 - h) * zc - n + 1
        down[h - 1][...] = pull1_ref[first : first + n, tiles]


def finish_kernel(plan, *refs):
    hops = plan.back_hops
    pos_ref, sums_ref, skel_ref, p_ref, target_ref, ts_ref, mine_ref = refs[:7]
    below, above = refs[7 : 7 + hops], refs[7 + hops : 7 + 2 * hops]
    out_ref, loss_ref, bias_ref, h_ref, grad_ref = refs[7 + 2 * hops :]
    rank = pos_ref[0]
    zc = plan.zc
    s1, s2, s5, s6, s7 = get_sums(sums_ref, 5)
    s3, s4 = get_sums(skel_ref, 2)
    prec = (s1 + 1.0) / (s2 + 1.0)
    sens = (s3 + 1.0) / (s4 + 1.0)
    both = prec + sens
    volume = s6 + s7 + 1.0
    cl_loss = 1.0 - 2.0 * prec * sens / both
    dice_loss = 1.0 - (2.0 * s5 + 1.0) / volume
    loss_ref[...] = jnp.broadcast_to(0.5 * dice_loss + 0.5 * cl_loss, (8, LANES))
    l0 = -(sens / both) * (sens / both) / (s2 + 1.0)
    l2 = -(prec / both) * (prec / both) / (s4 + 1.0)
    l4 = -1.0 / volume
    l5 = 0.5 * (2.0 * s5 + 1.0) / (volume * volume)

    h_ref[...] = mine_ref[...]
    for h in range(1, hops + 1):
        n = plan.back_count(h)
        h_ref[:n] += below[h - 1][...]
        h_ref[plan.span - n :] += above[h - 1][...]

    total = jnp.zeros((plan.tiles, LANES), f32)
    for n in range(plan.span):
        inside = 1.0 - kind_of(plan, rank, n - 1)[1]
        predict = p_ref[n]
        skel = l0 * jnp.exp(-temper * predict) * h_ref[n]
        whole = skel + l2 * ts_ref[n] + l4 * target_ref[n] + l5
        grad = whole * predict * (1.0 - predict) * inside
        grad_ref[n * plan.tiles : (n + 1) * plan.tiles] = grad
        if 1 <= n <= zc:
            total = total + grad
    bias_ref[...] = jnp.sum(total.reshape(-1, 8, LANES), axis=0)
    lane = lane_iota((1, LANES))

    def column(tile):
        return [
            grad_ref[pl.ds(plan.tiles + tile, zc, stride=plan.tiles)],
            grad_ref[tile : tile + 1],
            grad_ref[(zc + 1) * plan.tiles + tile : (zc + 1) * plan.tiles + tile + 1],
        ]

    for a in range(plan.gx):
        pieces = [column(a * plan.own + q) for q in range(plan.own)]
        zero = [jnp.zeros((zc, LANES), f32)] + [jnp.zeros((1, LANES), f32)] * 2
        after = column((a + 1) * plan.own) if a < plan.gx - 1 else zero
        before = column(a * plan.own - 1) if a > 0 else zero
        if plan.shared:
            pieces.append(
                [
                    jnp.where(lane < plan.Y, x, 0.0) + jnp.where(lane >= LANES - plan.Y, y, 0.0)
                    for x, y in zip(after, before)
                ]
            )
        else:
            pieces += [after, before]
        edges = [edge for piece in pieces for edge in piece[1:]]
        rows = plan.R16
        edges += [jnp.zeros((1, LANES), f32)] * (plan.extra16 * rows - len(edges))
        whole = [piece[0] for piece in pieces]
        if rows > zc:
            fill = jnp.zeros((rows - zc, LANES), f32)
            whole = [jnp.concatenate([piece, fill], axis=0) for piece in whole]
        whole += [
            jnp.concatenate(edges[n * rows : (n + 1) * rows], axis=0) for n in range(plan.extra16)
        ]
        for q, piece in enumerate(whole):
            piece = piece.astype(bf16)
            for b in range(plan.gy):
                out_ref[a * plan.gy + b, q] = piece


def fetch_kernel(plan, far_ref, after_ref, near_ref, sem_ref):
    del plan, after_ref
    copy = pltpu.make_async_copy(far_ref, near_ref, sem_ref.at[0])
    copy.start()
    copy.wait()


def weight_kernel(
    plan, pos_ref, f_ref, bias_ref, got_ref, gw_ref, g_ref, dw_ref
):
    rows, inner = plan.Y, plan.ch * plan.ny
    zc, nz = plan.zc, plan.nz
    lane = lane_iota((rows, nz))
    places = {}
    for x in range(-1, plan.nx + 1):
        tile, first = plan.slot(x)
        places.setdefault(tile, {})[first] = x
    for tile in range(plan.sent):
        order = [plan.member_now(j, pos_ref) for j in range(plan.members)]
        stack = [got_ref[p, tile].astype(f32)[:zc] for p in order]
        turned = jnp.concatenate(stack, axis=0).T
        ends = []
        for end, p in ((0, order[0]), (1, order[-1])):
            n = 2 * tile + end
            row = got_ref[p, plan.sent + n // plan.R16].astype(f32)
            ends.append(row[n % plan.R16 : n % plan.R16 + 1])
        ends = jnp.concatenate(ends + [jnp.zeros((LANES - 2, LANES), f32)], axis=0).T
        for first, x in places[tile].items():
            g = turned[first : first + rows]
            end = ends[first : first + rows]
            down = jnp.where(lane == nz - 1, pltpu.roll(end, nz - 2, 1), pltpu.roll(g, nz - 1, 1))
            up = jnp.where(lane == 0, end, pltpu.roll(g, 1, 1))
            g_ref[x + 1] = jnp.concatenate([down, g, up], axis=0).astype(bf16)

    dw_ref[...] = jnp.zeros_like(dw_ref)

    width = plan.nx // PARTS
    for n in range(PARTS):
        dw_ref[...] += lax.dot_general(
            moved_columns(g_ref, n * width, width),
            columns(plan, f_ref, n * width, width),
            (((1,), (1,)), ((), ())),
            preferred_element_type=f32,
        )

    tap_y = tap_condition(plan, pos_ref[1], (rows, inner), 0, 1)
    taps = []
    for t in range(27):
        i, j, k = t // 9, t // 3 % 3, t % 3
        at = (3 * i + k) * rows
        taps.append(jnp.sum(jnp.where(tap_y == j, dw_ref[at : at + rows], 0.0), axis=0, keepdims=True))
    taps += [jnp.zeros((1, inner), f32)] * 5
    taps = jnp.concatenate(taps, axis=0)
    high = taps.astype(bf16)
    taps = taps - high.astype(f32)
    middle = taps.astype(bf16)
    low = (taps - middle.astype(f32)).astype(bf16)
    place = (
        lax.broadcasted_iota(jnp.int32, (inner, LANES), 0) // plan.ny
        == lax.broadcasted_iota(jnp.int32, (inner, LANES), 1)
    )
    sums = jnp.dot(
        jnp.concatenate([high, middle, low], axis=0),
        place.astype(f32).astype(bf16),
        preferred_element_type=f32,
    )
    sums = sums[0:32] + sums[32:64] + sums[64:96]
    total = sums[0:8]
    for n in range(1, 4):
        total = total + pltpu.roll(sums[8 * n : 8 * n + 8], 32 * n, 1)
    spot = (row_iota((8, LANES)) == 3) & (lane_iota((8, LANES)) == 96)
    total = jnp.where(spot, jnp.sum(bias_ref[...]), total)
    gw_ref[...] = jnp.broadcast_to(total[None], (plan.ranks, 8, LANES))


def wide_kernel(plan, pos_ref, wt_ref, after_ref, wide_ref):
    del after_ref
    rows, inner, bands = plan.Y, plan.ch * plan.ny, 9 * plan.Y
    spread = (
        lax.broadcasted_iota(jnp.int32, (inner, plan.ch), 0) // plan.ny
        == lax.broadcasted_iota(jnp.int32, (inner, plan.ch), 1)
    )
    spread = spread.astype(f32).astype(bf16)
    tap_y = tap_condition(plan, pos_ref[1], (inner, bands), 1, 0)
    wide = jnp.zeros((inner, bands), f32)
    tap = lax.broadcasted_iota(jnp.int32, (27, bands), 0)
    band = lax.broadcasted_iota(jnp.int32, (27, bands), 1) // rows
    for j in range(3):
        pick = (tap == 9 * (band // 3) + 3 * j + band % 3).astype(f32).astype(bf16)
        chosen = jnp.dot(wt_ref[...], pick, preferred_element_type=f32).astype(bf16)
        full = jnp.dot(spread, chosen, preferred_element_type=f32)
        wide = jnp.where(tap_y == j, full, wide)
    wide_ref[...] = wide.astype(bf16)


def feature_kernel(plan, wide_ref, g_ref, after_ref, gf_ref):
    del after_ref
    width = plan.nx // PARTS
    for n in range(PARTS):
        out = jnp.dot(
            wide_ref[...],
            moved_columns(g_ref, n * width, width),
            preferred_element_type=f32,
        )
        for x in range(width):
            part = out[:, x * plan.nz : (x + 1) * plan.nz].astype(bf16)
            gf_ref[:, n * width + x] = part.reshape(plan.ch, plan.ny, plan.nz)


def final_kernel(plan, got_ref, gw_ref, gb_ref):
    total = jnp.sum(got_ref[...], axis=0)
    for n in range(4):
        count = min(8, 27 - 8 * n)
        gw_ref[8 * n : 8 * n + count] = total[:count, 32 * n : 32 * n + plan.ch]
    gb_ref[...] = total[3:4, 96:97]


VMEM = pl.BlockSpec(memory_space=pltpu.VMEM)
SMEM = pl.BlockSpec(memory_space=pltpu.SMEM)
ANY = pl.BlockSpec(memory_space=pl.ANY)
FAR = pl.BlockSpec(memory_space=pltpu.HBM)
MIB = 1024 * 1024


def shape(dims, dtype=f32):
    return jax.ShapeDtypeStruct(dims, dtype)


def held(dims, dtype):
    if len(dims) < 2:
        return 4096
    size = jnp.dtype(dtype).itemsize
    rows = 8 * 4 // size
    total = -(-dims[-2] // rows) * rows * -(-dims[-1] // LANES) * LANES * size
    for n in dims[:-2]:
        total *= n
    return total


def limits(arrays, scratch, micros):
    total = sum(held(a.shape, a.dtype) for a in arrays)
    total += sum(held(a.shape, a.dtype) for a in scratch if len(a.shape) > 1)
    limit = min(63 * MIB, total + total // 8 + 4 * MIB)
    return dict(
        compiler_params=pltpu.CompilerParams(vmem_limit_bytes=limit),
        cost_estimate=pl.CostEstimate(
            flops=0, transcendentals=0, bytes_accessed=int(micros * 2.5e4)
        ),
    )


def per_device(mesh_shape, features, weight, bias, label):
    plan = Plan(mesh_shape, features.shape)
    members, sent, tiles = plan.members, plan.sent, plan.tiles
    inner, bands = plan.ch * plan.ny, 9 * plan.Y
    x, y, z = (lax.axis_index(axis).astype(jnp.int32) for axis in ALL_AXES)
    mine = y * plan.gx + jnp.where(y % 2 == 0, x, plan.gx - 1 - x)
    place = z * members + jnp.where(z % 2 == 0, mine, members - 1 - mine)
    pos = jnp.stack([place, y])

    def call(
        kernel, out_shape, in_specs, operands, micros, scratch=(), out_specs=None
    ):
        outs = jax.tree.leaves(out_shape)
        ins = [a for spec, a in zip(in_specs, operands) if spec is VMEM]
        return pl.pallas_call(
            functools.partial(kernel, plan),
            out_shape=out_shape,
            in_specs=in_specs,
            out_specs=out_specs or jax.tree.map(lambda s: VMEM, out_shape),
            scratch_shapes=list(scratch),
            **limits(ins + outs, scratch, micros),
        )(*operands)

    def exchange(array):
        return lax.all_to_all(array, GROUP, 0, 0, tiled=True)

    def everywhere(array):
        return lax.all_to_all(array, ALL_AXES, 0, 0, tiled=True)

    def hop(array, distance):
        def device(r):
            z = r // members
            return plan.member(r % members, z % 2 == 1) * plan.gz + z

        pairs = [
            (device(r), device(r + distance))
            for r in range(plan.ranks)
            if 0 <= r + distance < plan.ranks
        ]
        return lax.ppermute(array, ALL_AXES, pairs)

    turned = weight.T
    features, weight, label = (
        pltpu.with_memory_space_constraint(a, pltpu.HBM) for a in (features, weight, label)
    )
    features_near = [pltpu.VMEM(features.shape, bf16), pltpu.SemaphoreType.DMA((PARTS,))]
    sent_logits = call(
        conv_kernel,
        shape((members, sent + plan.extra, plan.R, LANES)),
        [SMEM, VMEM, FAR, VMEM],
        (pos, weight, features, label),
        7,
        [
            pltpu.VMEM((bands, inner), bf16),
            pltpu.VMEM((plan.nx + 2, 3 * plan.Y, plan.nz), f32),
        ]
        + features_near,
    )

    def planes(array):
        return array.reshape(-1, tiles, LANES)

    zc, rest = plan.zc, plan.rest
    short = shape(((rest + 1 + -(-rest // 2)) * tiles, LANES))
    whole, label_own, head, tail = call(
        gather_kernel,
        [
            shape(((zc + 2 + -(-zc // 2)) * tiles, LANES)),
            shape((zc * tiles, LANES)),
            short,
            short,
        ],
        [VMEM],
        (exchange(sent_logits),),
        1.5,
    )
    whole, label_own, head, tail = (planes(part) for part in (whole, label_own, head, tail))
    around = [
        hop(whole if h < plan.hops else part, sign * h)
        for sign, part in ((1, tail), (-1, head))
        for h in range(1, plan.hops + 1)
    ]

    slab = (zc, tiles, LANES)
    span = (plan.span, tiles, LANES)
    everyone = shape((plan.ranks, 8, LANES))
    table = pltpu.VMEM((3, tiles, LANES), f32)

    records = pltpu.HBM((SECTIONS, plan.records, tiles, LANES), f32)
    y_near = pltpu.VMEM((2 * LANES, LANES), bf16)
    record_near = [
        y_near,
        pltpu.VMEM(records.shape, f32),
        pltpu.SemaphoreType.DMA((SECTIONS,)),
    ]
    record, predict, sums = call(
        forward_kernel,
        [records, shape(span), everyone],
        [SMEM, SMEM] + [VMEM] * (2 + 2 * plan.hops),
        (pos, bias, label_own, whole, *around),
        11,
        [
            pltpu.VMEM((plan.planes, plan.pad, LANES), f32),
            pltpu.VMEM((plan.planes, plan.pad, LANES), f32),
            pltpu.VMEM((plan.planes, tiles, LANES), f32),
            pltpu.VMEM((plan.planes, tiles, LANES), f32),
            pltpu.VMEM((zc, plan.pad, LANES), f32),
            pltpu.VMEM(slab, f32),
            table,
            table,
        ]
        + record_near,
        [FAR, VMEM, VMEM],
    )
    record = pltpu.with_memory_space_constraint(record, pltpu.HBM)
    sums = everywhere(sums)
    room = plan.win + 2 + plan.erode_block
    target, ts, skel_sums = call(
        target_kernel,
        [shape(span), shape(span), everyone],
        [SMEM] + [VMEM] * (2 + 2 * plan.hops),
        (pos, predict, label_own, *around),
        13,
        [
            pltpu.VMEM((plan.win, tiles, LANES), f32),
            pltpu.VMEM((room, plan.pad, LANES), f32),
            pltpu.VMEM((room, plan.pad, LANES), f32),
            pltpu.VMEM((room, tiles, LANES), f32),
            pltpu.VMEM((plan.span, plan.pad, LANES), f32),
            table,
            table,
            y_near,
        ],
    )
    skel_sums = everywhere(skel_sums)
    outer = [
        shape((plan.back_count(h), tiles, LANES)) for h in range(1, plan.back_hops + 1)
    ]
    mine, *outer = call(
        backward_kernel,
        [shape(span)] + outer * 2,
        [SMEM, VMEM, VMEM, FAR],
        (pos, sums, label_own, record),
        11,
        [
            pltpu.VMEM(slab, f32),
            pltpu.VMEM((zc + 4, tiles, LANES), f32),
            pltpu.VMEM((plan.pull_planes, tiles, LANES), f32),
            pltpu.VMEM((plan.span, plan.pad, LANES), f32),
            pltpu.VMEM((plan.pull_planes, plan.pad, LANES), f32),
            pltpu.VMEM((plan.pull_planes, plan.pad, LANES), f32),
            table,
        ]
        + record_near,
    )
    wide = call(
        wide_kernel, shape((inner, bands), bf16), [SMEM, VMEM, ANY], (pos, turned, mine), 2
    )
    beyond = []
    for sign, arrays in ((1, outer[: plan.back_hops]), (-1, outer[plan.back_hops :])):
        for h in range(1, plan.back_hops + 1):
            beyond.append(hop(arrays[h - 1], sign * h))
    grad_sent, loss, bias_part = call(
        finish_kernel,
        [
            shape((members, sent + plan.extra16, plan.R16, LANES), bf16),
            shape((8, LANES)),
            shape((8, LANES)),
        ],
        [SMEM] + [VMEM] * (6 + 2 * plan.back_hops),
        (pos, sums, skel_sums, predict, target, ts, mine, *beyond),
        2,
        [pltpu.VMEM(span, f32), pltpu.VMEM((plan.span * tiles, LANES), f32)],
    )

    features_ahead = call(
        fetch_kernel,
        pltpu.VMEM(features.shape, bf16),
        [FAR, ANY],
        (features, bias_part),
        1,
        [pltpu.SemaphoreType.DMA((1,))],
    )
    moved = shape((plan.nx + 2, 3 * plan.Y, plan.nz), bf16)
    partial, g = call(
        weight_kernel,
        [shape((plan.ranks, 8, LANES)), moved],
        [SMEM, VMEM, VMEM, VMEM],
        (pos, features_ahead, bias_part, exchange(grad_sent)),
        5,
        [pltpu.VMEM((bands, inner), f32)],
    )
    grad_features = call(
        feature_kernel,
        shape(features.shape, bf16),
        [VMEM, VMEM, ANY],
        (wide, g, partial),
        5,
    )
    grad_weight, grad_bias = call(
        final_kernel,
        [shape((27, plan.ch)), shape((1, 1))],
        [VMEM],
        (everywhere(partial),),
        1.5,
    )
    return (loss[0, :1], grad_features, grad_weight, grad_bias.reshape(1))


def solution(mesh):
    in_specs = (P(None, "gx", "gy", "gz"), P(), P(), P("gx", "gy", "gz"))
    out_specs = (P(), P(None, "gx", "gy", "gz"), P(), P())

    def body(*args):
        return per_device(dict(mesh.shape), *args)

    return jax.shard_map(
        body, mesh=mesh, in_specs=in_specs, out_specs=out_specs, check_vma=False
    )
```

```python
import functools

import jax
import jax.numpy as jnp
from jax import lax
from jax.experimental import pallas as pl
from jax.experimental.pallas import tpu as pltpu
from jax.sharding import PartitionSpec as P

ITERS = 10
SECTIONS = ITERS + 1
LANES = 128
HALO = SECTIONS + 2
BACK = SECTIONS + 1

BLOCK = 32
SPAN_BLOCK = 40
ERODE_BLOCK = 20

temper = 20.0
sharpness = 40.0

GROUP = ("gx", "gy")
ALL_AXES = ("gx", "gy", "gz")
f32 = jnp.float32
bf16 = jnp.bfloat16


def up8(value):
    return -(-value // 8) * 8


class Plan:
    def __init__(self, mesh_shape, block):
        self.ch, self.nx, self.ny, self.nz = block
        self.gx, self.gy, self.gz = (mesh_shape[a] for a in ALL_AXES)
        self.members = self.gx * self.gy
        self.ranks = self.members * self.gz
        self.X = self.nx * self.gx
        self.Y = self.ny * self.gy
        self.Z = self.nz * self.gz
        assert LANES % self.Y == 0 and self.nz == LANES
        assert self.nz % self.members == 0
        self.zc = self.nz // self.members
        self.per = LANES // self.Y
        assert self.nx % self.per == 0
        self.tiles = self.X // self.per
        self.own = self.nx // self.per
        self.shared = self.per > 1
        self.sent = self.own + (1 if self.shared else 2)
        self.R = up8(self.zc)
        self.extra = -(-2 * self.sent // self.R)
        self.R16 = -(-self.zc // 16) * 16
        self.extra16 = -(-2 * self.sent // self.R16)
        self.pad = self.tiles + 16
        self.win = self.zc + 2 * HALO
        self.span = self.zc + 2
        self.block = self.blocks_of(self.zc, BLOCK)
        self.span_block = self.blocks_of(self.span, SPAN_BLOCK)
        self.win_block = self.blocks_of(self.win, 32)
        self.erode_block = max(1, ERODE_BLOCK * 8 // self.tiles)
        self.base = HALO + 1
        self.planes = self.zc + 2 * HALO + 2 + self.erode_block
        self.pull_base = BACK + 2
        self.pull_planes = self.zc + 2 * BACK + 4 + self.erode_block
        self.hops = -(-HALO // self.zc)
        self.rest = HALO - (self.hops - 1) * self.zc
        self.records = 3 * self.zc + self.span
        assert self.ny == 16 and self.gy > 1
        self.back_hops = -(-(BACK + 1) // self.zc)

    def back_count(self, h):
        return min(self.zc + BACK + 1 - h * self.zc, self.span)

    def blocks_of(self, count, most):
        fits = [n for n in range(1, count + 1) if count % n == 0 and n * self.tiles <= 8 * most]
        return fits[-1] if fits else 1

    def slab(self, member):
        x, y = member // self.gy, member % self.gy
        return y * self.gx + (x if y % 2 == 0 else self.gx - 1 - x)

    def member(self, slab, odd):
        slab = self.members - 1 - slab if odd else slab
        return next(p for p in range(self.members) if self.slab(p) == slab)

    def member_now(self, slab, pos_ref):
        odd = pos_ref[0] // self.members % 2 == 1
        return jnp.where(odd, self.member(slab, True), self.member(slab, False))

    def label_lane(self, member_y):
        return 0 if member_y == self.gy - 1 else (member_y + 1) * self.ny + 8

    def slot(self, x):
        if 0 <= x < self.nx:
            return x // self.per, (x % self.per) * self.Y
        if x == self.nx:
            return self.own, 0
        return self.sent - 1, LANES - self.Y


def lane_iota(shape):
    return lax.broadcasted_iota(jnp.int32, shape, len(shape) - 1)


def row_iota(shape):
    return lax.broadcasted_iota(jnp.int32, shape, len(shape) - 2)


def masks(plan):
    return lane_iota((plan.tiles, LANES))


def x_neighbours(plan, mask, load, cur):
    lower, upper = load(-1), load(1)
    if plan.Y == LANES:
        return lower + upper
    lower = pltpu.roll(jnp.where(mask >= LANES - plan.Y, lower, cur), plan.Y, 1)
    upper = pltpu.roll(jnp.where(mask < plan.Y, upper, cur), LANES - plan.Y, 1)
    return lower + upper


def y_matrix(plan, ref):
    row = row_iota((2 * LANES, LANES)) % LANES
    lane = lane_iota((2 * LANES, LANES))
    near = (row == lane - 1) | (row == lane + 1)
    ref[...] = (near & (row // plan.Y == lane // plan.Y)).astype(f32).astype(bf16)


def y_neighbours(ref, block):
    flat = block.reshape(-1, LANES)
    high = flat.astype(bf16)
    low = (flat - high.astype(f32)).astype(bf16)
    both = jnp.concatenate([high, low], axis=1)
    return jnp.dot(both, ref[...], preferred_element_type=f32).reshape(block.shape)


def count_tables(plan, cross_ref, box_ref):
    flat = row_iota((plan.tiles, LANES)) * LANES + lane_iota((plan.tiles, LANES))
    y, x = flat % plan.Y, flat // plan.Y

    def along(spot, size):
        return 3.0 - (spot == 0).astype(f32) - (spot == size - 1).astype(f32)

    cx, cy = along(x, plan.X), along(y, plan.Y)
    for kind, cz in ((1, 2.0), (2, 3.0)):
        if cross_ref is not None:
            cross_ref[kind] = 1.0 / (cx + cy + cz - 2.0)
        if box_ref is not None:
            box_ref[kind] = 1.0 / (cx * cy * cz)
    for ref in (cross_ref, box_ref):
        if ref is not None:
            ref[0] = jnp.zeros((plan.tiles, LANES), f32)


def kind_of(plan, rank, plane):
    z = rank * plan.zc + plane
    inside = (z >= 0) & (z < plan.Z)
    edge = (z == 0) | (z == plan.Z - 1)
    return jnp.where(inside, jnp.where(edge, 1, 2), 0), jnp.where(inside, 0.0, 1.0)


def store_all(pairs):
    for ref, at, value in pairs:
        ref[at] = value


def over(first, count, size, body):
    def at(n, carry):
        body(first + n * size)
        return carry

    lax.fori_loop(0, (count + size - 1) // size, at, 0)


def tap_condition(plan, member_y, shape, y_dim, in_dim):
    y = lax.broadcasted_iota(jnp.int32, shape, y_dim) % plan.Y
    own = lax.broadcasted_iota(jnp.int32, shape, in_dim) % plan.ny
    return own + member_y * plan.ny - y + 1


PARTS = 4


def stream(plan, far_ref, near_ref, sem_ref):
    width = plan.nx // PARTS
    copies = []
    for n in range(PARTS):
        span = pl.ds(n * width, width)
        copies.append(
            pltpu.make_async_copy(far_ref.at[:, span], near_ref.at[:, span], sem_ref.at[n])
        )
        copies[-1].start()
    return copies


def columns(plan, ref, first, count):
    blocks = [ref[:, x].reshape(-1, plan.nz) for x in range(first, first + count)]
    return jnp.concatenate(blocks, axis=1)


def moved_columns(ref, first, count):
    blocks = [
        jnp.concatenate([ref[x + 2], ref[x + 1], ref[x]], axis=0)
        for x in range(first, first + count)
    ]
    return jnp.concatenate(blocks, axis=1)


def conv_kernel(
    plan, pos_ref, w_ref, far_ref, label_ref, out_ref, wide_ref, acc_ref, f_ref, sem_ref
):
    width = plan.nx // PARTS
    copies = stream(plan, far_ref, f_ref, sem_ref)
    rows, inner = plan.Y, plan.ch * plan.ny
    spread = (
        lax.broadcasted_iota(jnp.int32, (plan.ch, inner), 0)
        == lax.broadcasted_iota(jnp.int32, (plan.ch, inner), 1) // plan.ny
    )
    taps = jnp.dot(
        w_ref[...], spread.astype(f32).astype(bf16), preferred_element_type=f32
    )
    tap_y = tap_condition(plan, pos_ref[1], (rows, inner), 0, 1)
    for i in range(3):
        for k in range(3):
            band = jnp.zeros((rows, inner), f32)
            for j in range(3):
                t = 9 * i + 3 * j + k
                band = jnp.where(tap_y == j, taps[t : t + 1], band)
            at = (3 * i + k) * rows
            wide_ref[at : at + rows] = band.astype(bf16)
    acc_ref[...] = jnp.zeros_like(acc_ref)

    for n in range(PARTS):
        copies[n].wait()
        first = n * width
        out = jnp.dot(
            wide_ref[...], columns(plan, f_ref, first, width), preferred_element_type=f32
        )
        for slot in range(first, first + width + 2):
            terms = [
                out[3 * i * rows : 3 * (i + 1) * rows, (x - first) * plan.nz : (x - first + 1) * plan.nz]
                for i in range(3)
                for x in (slot - 2 + i,)
                if first <= x < first + width
            ]
            acc_ref[slot] += functools.reduce(jnp.add, terms)

    out_ref[...] = jnp.zeros_like(out_ref)
    places = {}
    for x in range(-1, plan.nx + 1):
        tile, lane = plan.slot(x)
        places.setdefault(tile, {})[lane] = x
    lane = lane_iota((rows, plan.nz))
    words = [label_ref[x, 0:8] + 2 * label_ref[x, 8:16] for x in range(plan.nx)]
    first_group = jnp.where(
        pos_ref[1] == plan.gy - 1, 0, (pos_ref[1] + 1) * (plan.ny // 8) + 1
    )
    labelled = lax.broadcasted_iota(jnp.int32, (rows, plan.nz), 0) // 8 == first_group
    for tile in range(plan.sent):
        parts, spills = [], []
        for first in range(0, LANES, rows):
            x = places[tile].get(first)
            if x is None:
                parts.append(jnp.zeros((rows, plan.nz), f32))
                spills.append(jnp.zeros((rows, plan.nz), f32))
                continue
            low = acc_ref[x + 1, 0:rows]
            mid = acc_ref[x + 1, rows : 2 * rows]
            high = acc_ref[x + 1, 2 * rows : 3 * rows]
            total = mid + jnp.where(lane == 0, 0.0, pltpu.roll(low, 1, 1))
            total = total + jnp.where(lane == plan.nz - 1, 0.0, pltpu.roll(high, plan.nz - 1, 1))
            if 0 <= x < plan.nx:
                word = jnp.concatenate([words[x].astype(f32)] * (rows // 8), axis=0)
                total = total + jnp.where(labelled, word, 0.0)
            parts.append(total)
            spill = jnp.where(lane == 1, pltpu.roll(low, 2, 1), 0.0)
            spills.append(jnp.where(lane == 0, high, spill))
        turned = jnp.concatenate(parts, axis=0).T
        spill = jnp.concatenate(spills, axis=0).T
        for j in range(plan.members):
            p = plan.member_now(j, pos_ref)
            out_ref[p, tile, 0 : plan.zc] = turned[j * plan.zc : (j + 1) * plan.zc]
        for end, j in ((0, 0), (1, plan.members - 1)):
            n = 2 * tile + end
            at = plan.sent + n // plan.R
            p = plan.member_now(j, pos_ref)
            out_ref[p, at, n % plan.R : n % plan.R + 1] = spill[end : end + 1]


def gather_kernel(plan, got_ref, out_ref, label_ref, head_ref, tail_ref):
    tiles, zc, rest = plan.tiles, plan.zc, plan.rest
    lane = lane_iota((1, LANES))
    spot = lane % plan.Y

    def part(p, q):
        values = [got_ref[p, q, 0:zc]]
        for end in range(2):
            n = 2 * q + end
            at = plan.sent + n // plan.R
            values.append(got_ref[p, at, n % plan.R : n % plan.R + 1])
        return values

    for a in range(plan.gx):
        for q in range(plan.own):
            parts = []
            label = jnp.zeros((zc, LANES), f32)
            for b in range(plan.gy):
                start = b * plan.ny
                values = part(a * plan.gy + b, q)
                second = (values[0] >= 1.5).astype(f32)
                first = values[0] - 2.0 * second
                move = start - plan.label_lane(b)
                first = pltpu.roll(first, move % LANES, 1)
                second = pltpu.roll(second, (move + 8) % LANES, 1)
                label = jnp.where((spot >= start) & (spot < start + 8), first, label)
                label = jnp.where((spot >= start + 8) & (spot < start + 16), second, label)
                mine = (spot >= start - 1) & (spot <= start + plan.ny)
                parts.append([jnp.where(mine, v, 0.0) for v in values])
                if q == plan.own - 1 and a < plan.gx - 1:
                    edge = part((a + 1) * plan.gy + b, plan.sent - 1)
                    parts.append([jnp.where(lane >= LANES - plan.Y, v, 0.0) for v in edge])
                if q == 0 and a > 0:
                    edge = part((a - 1) * plan.gy + b, plan.own)
                    parts.append([jnp.where(lane < plan.Y, v, 0.0) for v in edge])
            whole, low, high = (functools.reduce(jnp.add, vs) for vs in zip(*parts))
            tile = a * plan.own + q
            label_ref[pl.ds(tile, zc, stride=tiles)] = label
            out_ref[pl.ds(tile, zc, stride=tiles)] = whole
            out_ref[zc * tiles + tile : zc * tiles + tile + 1] = low
            out_ref[(zc + 1) * tiles + tile : (zc + 1) * tiles + tile + 1] = high

    def pack(ref, at, first, count):
        half = -(-count // 2)
        for n in range(half):
            word = label_ref[(first + n) * tiles : (first + n + 1) * tiles]
            if n + half < count:
                other = first + n + half
                word = word + 2.0 * label_ref[other * tiles : (other + 1) * tiles]
            ref[(at + n) * tiles : (at + n + 1) * tiles] = word

    pack(out_ref, zc + 2, 0, zc)
    head_ref[: rest * tiles] = out_ref[: rest * tiles]
    head_ref[rest * tiles : (rest + 1) * tiles] = out_ref[zc * tiles : (zc + 1) * tiles]
    pack(head_ref, rest + 1, 0, rest)
    tail_ref[: rest * tiles] = out_ref[(zc - rest) * tiles : zc * tiles]
    tail_ref[rest * tiles : (rest + 1) * tiles] = out_ref[(zc + 1) * tiles : (zc + 2) * tiles]
    pack(tail_ref, rest + 1, zc - rest, rest)


LOG = 1.0 / sharpness


def thin(e, box, inverse, outside):
    box = box + outside
    ratio = e * box * inverse + outside
    square = ratio * ratio
    more = 1.0 + square
    joint = 1.0 / (box * more)
    slope = joint * box
    return joint * more, slope, jnp.log(square * slope)


def lift(scaled, s):
    small = jnp.exp(scaled * (s - 1.0))
    more = 1.0 + small
    return s + jnp.log(more) * LOG, small * (1.0 / more)


def erode(plan, rank, mask, y_ref, source, result, grown_ref, table_ref, base, first, count):
    tiles = slice(8, 8 + plan.tiles)

    def body(plane):
        beside = y_neighbours(y_ref, source[pl.ds(plane + base, plan.erode_block), tiles])
        for n in range(plan.erode_block):
            at = plane + n + base
            cur = source[at, tiles]

            def load(offset, at=at):
                return source[at, 8 + offset : 8 + offset + plan.tiles]

            total = cur + source[at - 1, tiles] + source[at + 1, tiles]
            total = total + x_neighbours(plan, mask, load, cur) + beside[n]
            kind, outside = kind_of(plan, rank, plane + n)
            total = total * table_ref[kind]
            result[at, tiles] = total
            grown_ref[at] = 1.0 / (total + outside) - outside

    over(first, count, plan.erode_block, body)


def spread(plan, y_ref, grown_ref, zy_ref, base, first, count, size):
    tiles = slice(8, 8 + plan.tiles)

    def body(plane):
        at = plane + base
        part = grown_ref[pl.ds(at - 1, size)] + grown_ref[pl.ds(at, size)]
        part = part + grown_ref[pl.ds(at + 1, size)]
        zy_ref[pl.ds(plane - first, size), tiles] = part + y_neighbours(y_ref, part)

    over(first, count, size, body)


def in_turn(section):
    section(0, 0, 1, True)

    def pair(n, carry):
        section(2 * n + 1, 1, 0, False)
        section(2 * n + 2, 0, 1, False)
        return carry

    lax.fori_loop(0, ITERS // 2, pair, 0)


def x_box(plan, mask, zy_ref, at):
    cur = zy_ref[at, 8 : 8 + plan.tiles]

    def load(offset):
        return zy_ref[at, 8 + offset : 8 + offset + plan.tiles]

    return cur + x_neighbours(plan, mask, load, cur)


def target_kernel(plan, *refs):
    hops = plan.hops
    pos_ref, p_ref, own_ref = refs[:3]
    below, above = refs[3 : 3 + hops], refs[3 + hops : 3 + 2 * hops]
    target_ref, ts_ref, sums_ref = refs[3 + 2 * hops : 6 + 2 * hops]
    all_ref, e0_ref, e1_ref, g_ref, zy_ref, cross_ref, box_ref, y_ref = refs[6 + 2 * hops :]
    zc, win, span = plan.zc, plan.win, plan.span
    size = plan.span_block
    base = HALO + 1
    tiles = slice(8, 8 + plan.tiles)
    rank = pos_ref[0]
    mask = masks(plan)
    count_tables(plan, cross_ref, box_ref)
    y_matrix(plan, y_ref)
    e_refs = (e0_ref, e1_ref)
    e0_ref[...] = jnp.zeros_like(e0_ref)
    e1_ref[...] = jnp.zeros_like(e1_ref)
    zy_ref[...] = jnp.zeros_like(zy_ref)
    all_ref[HALO : HALO + zc] = own_ref[...]
    for h in range(1, hops + 1):
        count = zc if h < hops else plan.rest
        at = zc + 2 if h < hops else plan.rest + 1
        half = -(-count // 2)
        for refs_of, first in ((below, HALO - (h - 1) * zc - count), (above, HALO + h * zc)):
            words = refs_of[h - 1][at : at + half]
            second = (words >= 1.5).astype(f32)
            all_ref[first : first + half] = words - 2.0 * second
            if count > half:
                all_ref[first + half : first + count] = second[: count - half]
    target_ref[...] = all_ref[HALO - 1 : HALO + zc + 1]

    def fill(plane):
        out = []
        for n in range(plan.win_block):
            at = plane + n
            inside = 1.0 - kind_of(plan, rank, at - HALO)[1]
            out.append((e0_ref, (at + 1, tiles), jnp.exp(-temper * all_ref[at]) * inside))
        store_all(out)

    over(0, win, plan.win_block, fill)

    def section(step, source, result, opening):
        e_ref = e_refs[source]
        reach = 2 + ITERS - step
        count = zc + 2 * reach
        erode(
            plan, rank, mask, y_ref, e_ref, e_refs[result], g_ref, cross_ref, base, -reach, count
        )
        spread(plan, y_ref, g_ref, zy_ref, base, -1, span, size)

        def point(plane):
            before = [None if opening else ts_ref[plane + n] for n in range(size)]
            for n in range(size):
                at = plane + n
                box = x_box(plan, mask, zy_ref, at)
                kind, outside = kind_of(plan, rank, at - 1)
                _, _, scaled = thin(e_ref[at - 1 + base, tiles], box, box_ref[kind], outside)
                ts_ref[at] = scaled * -LOG if opening else lift(scaled, before[n])[0]

        over(0, span, size, point)

    in_turn(section)

    def add(n, totals):
        ts = ts_ref[1 + n]
        return totals[0] + ts * p_ref[1 + n], totals[1] + ts

    zero = jnp.zeros((plan.tiles, LANES), f32)
    put_sums(plan, sums_ref, lax.fori_loop(0, zc, add, (zero,) * 2))


def put_sums(plan, ref, totals):
    lane = lane_iota((1, LANES))
    line = jnp.zeros((1, LANES), f32)
    for n, total in enumerate(totals):
        whole = jnp.sum(jnp.sum(total, axis=0, keepdims=True), axis=1, keepdims=True)
        line = jnp.where(lane == n, whole, line)
    ref[...] = jnp.broadcast_to(line[None], (plan.ranks, 1, LANES))


def get_sums(ref, count):
    line = jnp.sum(ref[...], axis=0)
    lane = lane_iota((1, LANES))
    return [
        jnp.sum(jnp.where(lane == n, line, 0.0), axis=1, keepdims=True) for n in range(count)
    ]


def forward_kernel(plan, *refs):
    hops = plan.hops
    pos_ref, bias_ref, label_ref, own_ref = refs[:4]
    refs = refs[4:]
    below, above = refs[:hops], refs[hops : 2 * hops]
    refs = refs[2 * hops :]
    far_ref, p_ref, sums_ref = refs[:3]
    e0_ref, e1_ref, g0_ref, g1_ref, zy_ref, s_ref, cross_ref, box_ref = refs[3:11]
    y_ref, record_ref, sem_ref = refs[11:]
    e_refs, g_refs = (e0_ref, e1_ref), (g0_ref, g1_ref)
    base, zc, size = plan.base, plan.zc, plan.block
    tiles = slice(8, 8 + plan.tiles)
    rank = pos_ref[0]
    mask = masks(plan)

    for ref in e_refs + g_refs:
        ref[...] = jnp.zeros_like(ref)
    zy_ref[...] = jnp.zeros_like(zy_ref)
    count_tables(plan, cross_ref, box_ref)
    y_matrix(plan, y_ref)
    e0_ref[base : base + zc, tiles] = own_ref[:zc]
    for h in range(1, hops + 1):
        n = zc if h < hops else plan.rest
        first = base - (h - 1) * zc - n
        e0_ref[first : first + n, tiles] = below[h - 1][:n]
        first = base + h * zc
        e0_ref[first : first + n, tiles] = above[h - 1][:n]
    e0_ref[base - 1, tiles] += own_ref[zc]
    e0_ref[base + zc, tiles] += own_ref[zc + 1]
    for h in range(1, hops + 1):
        if h < hops:
            e0_ref[base - h * zc - 1, tiles] += below[h - 1][zc]
            e0_ref[base + (h + 1) * zc, tiles] += above[h - 1][zc + 1]
            e0_ref[base - (h - 1) * zc, tiles] += below[h - 1][zc + 1]
            e0_ref[base + h * zc - 1, tiles] += above[h - 1][zc]
        else:
            e0_ref[base - (h - 1) * zc, tiles] += below[h - 1][plan.rest]
            e0_ref[base + h * zc - 1, tiles] += above[h - 1][plan.rest]

    def sigmoid(logits):
        small = jnp.exp(-jnp.abs(logits))
        part = 1.0 / (1.0 + small)
        return jnp.where(logits >= 0, part, small * part)

    for n in range(plan.span):
        p_ref[n] = sigmoid(e0_ref[base - 1 + n, tiles] + bias_ref[0])

    def fill(plane):
        out = []
        for n in range(plan.erode_block):
            at = plane + n
            inside = 1.0 - kind_of(plan, rank, at - base)[1]
            predict = sigmoid(e0_ref[at, tiles] + bias_ref[0])
            out.append((e0_ref, (at, tiles), jnp.exp(-temper * predict) * inside))
            out.append((g0_ref, at, jnp.exp(temper * predict) * inside))
        store_all(out)

    over(1, zc + 2 * HALO, plan.erode_block, fill)


    def out_copy(step):
        return pltpu.make_async_copy(record_ref.at[step], far_ref.at[step], sem_ref.at[step])

    def section(step, source, result, opening):
        e_ref, g_ref, after_ref = e_refs[source], g_refs[source], g_refs[result]
        reach = 1 + ITERS - step
        count = zc + 2 * reach
        erode(
            plan, rank, mask, y_ref, e_ref, e_refs[result], after_ref, cross_ref, base, -reach,
            count,
        )
        spread(plan, y_ref, after_ref, zy_ref, base, 0, zc, size)
        record_ref[step, 3 * zc :] = after_ref[base - 1 : base + zc + 1]

        def point(plane):
            before = [None if opening else s_ref[plane + n] for n in range(size)]
            for n in range(size):
                at = plane + n
                box = x_box(plan, mask, zy_ref, at)
                kind, outside = kind_of(plan, rank, at)
                e = e_ref[at + base, tiles]
                over_box, slope, scaled = thin(e, box, box_ref[kind], outside)
                if opening:
                    grown, a = scaled * -LOG, slope
                    record_ref[step, at] = jnp.ones_like(a)
                else:
                    s = before[n]
                    grown, rate = lift(scaled, s)
                    a = rate * (1.0 - s) * slope
                    record_ref[step, at] = 1.0 + rate * scaled * LOG
                s_ref[at] = grown
                record_ref[step, at + zc] = a * over_box
                record_ref[step, at + 2 * zc] = a * g_ref[at + base]

        over(0, zc, size, point)
        out_copy(step).start()

    in_turn(section)

    def add(n, totals):
        ps, predict, target = s_ref[n], p_ref[1 + n], label_ref[n]
        terms = (ps * target, ps, predict * target, predict, target)
        return tuple(total + term for total, term in zip(totals, terms))

    zero = jnp.zeros((plan.tiles, LANES), f32)
    put_sums(plan, sums_ref, lax.fori_loop(0, zc, add, (zero,) * 5))

    def drain(step, carry):
        out_copy(step).wait()
        return carry

    lax.fori_loop(0, SECTIONS, drain, 0)


def backward_kernel(plan, *refs):
    hops = plan.back_hops
    pos_ref, sums_ref, label_ref, far_ref, mine_ref = refs[:5]
    up, down = refs[5 : 5 + hops], refs[5 + hops : 5 + 2 * hops]
    w_ref, push_ref, wt_ref, zy_ref, pull0_ref, pull1_ref, cross_ref = refs[5 + 2 * hops : -3]
    y_ref, record_ref, sem_ref = refs[-3:]
    pull_refs = (pull0_ref, pull1_ref)
    rank = pos_ref[0]
    zc, base = plan.zc, plan.pull_base
    tiles = slice(8, 8 + plan.tiles)
    mask = masks(plan)

    def in_copy(left):
        return pltpu.make_async_copy(far_ref.at[left], record_ref.at[left], sem_ref.at[left])

    for left in reversed(range(SECTIONS)):
        in_copy(left).start()
    s1, s2 = get_sums(sums_ref, 2)
    prec = (s1 + 1.0) / (s2 + 1.0)
    push_ref[...] = jnp.zeros_like(push_ref)
    wt_ref[...] = jnp.zeros_like(wt_ref)
    zy_ref[...] = jnp.zeros_like(zy_ref)
    for ref in pull_refs:
        ref[...] = jnp.zeros_like(ref)
    count_tables(plan, cross_ref, None)
    y_matrix(plan, y_ref)
    w_ref[...] = label_ref[...] - prec[None]

    def section(step, source, result, ending):
        pull_ref, next_ref = pull_refs[source], pull_refs[result]
        left = SECTIONS - 1 - step
        in_copy(left).wait()

        def push(at):
            out = []
            for n in range(plan.block):
                w = w_ref[at + n]
                out.append((push_ref, at + n + 2, w * record_ref[left, at + n + zc]))
                out.append((wt_ref, at + n + base, w * record_ref[left, at + n + 2 * zc]))
                out.append((w_ref, at + n, w * record_ref[left, at + n]))
            store_all(out)

        over(0, zc, plan.block, push)

        def widen(at):
            size = plan.span_block
            part = push_ref[pl.ds(at, size)] + push_ref[pl.ds(at + 1, size)]
            part = part + push_ref[pl.ds(at + 2, size)]
            zy_ref[pl.ds(at, size), tiles] = part + y_neighbours(y_ref, part)

        over(0, plan.span, plan.span_block, widen)

        def pull(at):
            out = []
            for n in range(plan.span_block):
                box = x_box(plan, mask, zy_ref, at + n)
                inverse = cross_ref[kind_of(plan, rank, at + n - 1)[0]]
                grown = record_ref[left, at + n + 3 * zc]
                spot = at + n - 1 + base
                old = pull_ref[spot, tiles]
                out.append((pull_ref, (spot, tiles), old - grown * grown * box * inverse))
            store_all(out)

        over(0, plan.span, plan.span_block, pull)
        reach = 2 + step

        def join(plane):
            beside = y_neighbours(y_ref, pull_ref[pl.ds(plane + base, plan.erode_block), tiles])
            for n in range(plan.erode_block):
                at = plane + n + base
                cur = pull_ref[at, tiles]

                def load(offset, at=at):
                    return pull_ref[at, 8 + offset : 8 + offset + plan.tiles]

                total = cur + pull_ref[at - 1, tiles] + pull_ref[at + 1, tiles]
                total = total + x_neighbours(plan, mask, load, cur)
                total = total + beside[n] + wt_ref[at]
                if not ending:
                    total = total * cross_ref[kind_of(plan, rank, plane + n)[0]]
                next_ref[at, tiles] = total

        over(-reach, zc + 2 * reach, plan.erode_block, join)

    def pair(n, carry):
        section(2 * n, 0, 1, False)
        section(2 * n + 1, 1, 0, False)
        return carry

    lax.fori_loop(0, ITERS // 2, pair, 0)
    section(ITERS, 0, 1, True)
    mine_ref[...] = pull1_ref[base - 1 : base + zc + 1, tiles]
    for h in range(1, hops + 1):
        n = plan.back_count(h)
        first = base + h * zc - 1
        up[h - 1][...] = pull1_ref[first : first + n, tiles]
        first = base + (1 - h) * zc - n + 1
        down[h - 1][...] = pull1_ref[first : first + n, tiles]


def finish_kernel(plan, *refs):
    hops = plan.back_hops
    pos_ref, sums_ref, skel_ref, p_ref, target_ref, ts_ref, mine_ref = refs[:7]
    below, above = refs[7 : 7 + hops], refs[7 + hops : 7 + 2 * hops]
    out_ref, loss_ref, bias_ref, h_ref, grad_ref = refs[7 + 2 * hops :]
    rank = pos_ref[0]
    zc = plan.zc
    s1, s2, s5, s6, s7 = get_sums(sums_ref, 5)
    s3, s4 = get_sums(skel_ref, 2)
    prec = (s1 + 1.0) / (s2 + 1.0)
    sens = (s3 + 1.0) / (s4 + 1.0)
    both = prec + sens
    volume = s6 + s7 + 1.0
    cl_loss = 1.0 - 2.0 * prec * sens / both
    dice_loss = 1.0 - (2.0 * s5 + 1.0) / volume
    loss_ref[...] = jnp.broadcast_to(0.5 * dice_loss + 0.5 * cl_loss, (8, LANES))
    l0 = -(sens / both) * (sens / both) / (s2 + 1.0)
    l2 = -(prec / both) * (prec / both) / (s4 + 1.0)
    l4 = -1.0 / volume
    l5 = 0.5 * (2.0 * s5 + 1.0) / (volume * volume)

    h_ref[...] = mine_ref[...]
    for h in range(1, hops + 1):
        n = plan.back_count(h)
        h_ref[:n] += below[h - 1][...]
        h_ref[plan.span - n :] += above[h - 1][...]

    total = jnp.zeros((plan.tiles, LANES), f32)
    for n in range(plan.span):
        inside = 1.0 - kind_of(plan, rank, n - 1)[1]
        predict = p_ref[n]
        skel = l0 * jnp.exp(-temper * predict) * h_ref[n]
        whole = skel + l2 * ts_ref[n] + l4 * target_ref[n] + l5
        grad = whole * predict * (1.0 - predict) * inside
        grad_ref[n * plan.tiles : (n + 1) * plan.tiles] = grad
        if 1 <= n <= zc:
            total = total + grad
    bias_ref[...] = jnp.sum(total.reshape(-1, 8, LANES), axis=0)
    lane = lane_iota((1, LANES))

    def column(tile):
        return [
            grad_ref[pl.ds(plan.tiles + tile, zc, stride=plan.tiles)],
            grad_ref[tile : tile + 1],
            grad_ref[(zc + 1) * plan.tiles + tile : (zc + 1) * plan.tiles + tile + 1],
        ]

    for a in range(plan.gx):
        pieces = [column(a * plan.own + q) for q in range(plan.own)]
        zero = [jnp.zeros((zc, LANES), f32)] + [jnp.zeros((1, LANES), f32)] * 2
        after = column((a + 1) * plan.own) if a < plan.gx - 1 else zero
        before = column(a * plan.own - 1) if a > 0 else zero
        if plan.shared:
            pieces.append(
                [
                    jnp.where(lane < plan.Y, x, 0.0) + jnp.where(lane >= LANES - plan.Y, y, 0.0)
                    for x, y in zip(after, before)
                ]
            )
        else:
            pieces += [after, before]
        edges = [edge for piece in pieces for edge in piece[1:]]
        rows = plan.R16
        edges += [jnp.zeros((1, LANES), f32)] * (plan.extra16 * rows - len(edges))
        whole = [piece[0] for piece in pieces]
        if rows > zc:
            fill = jnp.zeros((rows - zc, LANES), f32)
            whole = [jnp.concatenate([piece, fill], axis=0) for piece in whole]
        whole += [
            jnp.concatenate(edges[n * rows : (n + 1) * rows], axis=0) for n in range(plan.extra16)
        ]
        for q, piece in enumerate(whole):
            piece = piece.astype(bf16)
            for b in range(plan.gy):
                out_ref[a * plan.gy + b, q] = piece


def fetch_kernel(plan, far_ref, after_ref, near_ref, sem_ref):
    del plan, after_ref
    copy = pltpu.make_async_copy(far_ref, near_ref, sem_ref.at[0])
    copy.start()
    copy.wait()


def weight_kernel(
    plan, pos_ref, f_ref, bias_ref, got_ref, gw_ref, g_ref, dw_ref
):
    rows, inner = plan.Y, plan.ch * plan.ny
    zc, nz = plan.zc, plan.nz
    lane = lane_iota((rows, nz))
    places = {}
    for x in range(-1, plan.nx + 1):
        tile, first = plan.slot(x)
        places.setdefault(tile, {})[first] = x
    for tile in range(plan.sent):
        order = [plan.member_now(j, pos_ref) for j in range(plan.members)]
        stack = [got_ref[p, tile].astype(f32)[:zc] for p in order]
        turned = jnp.concatenate(stack, axis=0).T
        ends = []
        for end, p in ((0, order[0]), (1, order[-1])):
            n = 2 * tile + end
            row = got_ref[p, plan.sent + n // plan.R16].astype(f32)
            ends.append(row[n % plan.R16 : n % plan.R16 + 1])
        ends = jnp.concatenate(ends + [jnp.zeros((LANES - 2, LANES), f32)], axis=0).T
        for first, x in places[tile].items():
            g = turned[first : first + rows]
            end = ends[first : first + rows]
            down = jnp.where(lane == nz - 1, pltpu.roll(end, nz - 2, 1), pltpu.roll(g, nz - 1, 1))
            up = jnp.where(lane == 0, end, pltpu.roll(g, 1, 1))
            g_ref[x + 1] = jnp.concatenate([down, g, up], axis=0).astype(bf16)

    dw_ref[...] = jnp.zeros_like(dw_ref)

    width = plan.nx // PARTS
    for n in range(PARTS):
        dw_ref[...] += lax.dot_general(
            moved_columns(g_ref, n * width, width),
            columns(plan, f_ref, n * width, width),
            (((1,), (1,)), ((), ())),
            preferred_element_type=f32,
        )

    tap_y = tap_condition(plan, pos_ref[1], (rows, inner), 0, 1)
    taps = []
    for t in range(27):
        i, j, k = t // 9, t // 3 % 3, t % 3
        at = (3 * i + k) * rows
        taps.append(jnp.sum(jnp.where(tap_y == j, dw_ref[at : at + rows], 0.0), axis=0, keepdims=True))
    taps += [jnp.zeros((1, inner), f32)] * 5
    taps = jnp.concatenate(taps, axis=0)
    high = taps.astype(bf16)
    taps = taps - high.astype(f32)
    middle = taps.astype(bf16)
    low = (taps - middle.astype(f32)).astype(bf16)
    place = (
        lax.broadcasted_iota(jnp.int32, (inner, LANES), 0) // plan.ny
        == lax.broadcasted_iota(jnp.int32, (inner, LANES), 1)
    )
    sums = jnp.dot(
        jnp.concatenate([high, middle, low], axis=0),
        place.astype(f32).astype(bf16),
        preferred_element_type=f32,
    )
    sums = sums[0:32] + sums[32:64] + sums[64:96]
    total = sums[0:8]
    for n in range(1, 4):
        total = total + pltpu.roll(sums[8 * n : 8 * n + 8], 32 * n, 1)
    spot = (row_iota((8, LANES)) == 3) & (lane_iota((8, LANES)) == 96)
    total = jnp.where(spot, jnp.sum(bias_ref[...]), total)
    gw_ref[...] = jnp.broadcast_to(total[None], (plan.ranks, 8, LANES))


def wide_kernel(plan, pos_ref, wt_ref, after_ref, wide_ref):
    del after_ref
    rows, inner, bands = plan.Y, plan.ch * plan.ny, 9 * plan.Y
    spread = (
        lax.broadcasted_iota(jnp.int32, (inner, plan.ch), 0) // plan.ny
        == lax.broadcasted_iota(jnp.int32, (inner, plan.ch), 1)
    )
    spread = spread.astype(f32).astype(bf16)
    tap_y = tap_condition(plan, pos_ref[1], (inner, bands), 1, 0)
    wide = jnp.zeros((inner, bands), f32)
    tap = lax.broadcasted_iota(jnp.int32, (27, bands), 0)
    band = lax.broadcasted_iota(jnp.int32, (27, bands), 1) // rows
    for j in range(3):
        pick = (tap == 9 * (band // 3) + 3 * j + band % 3).astype(f32).astype(bf16)
        chosen = jnp.dot(wt_ref[...], pick, preferred_element_type=f32).astype(bf16)
        full = jnp.dot(spread, chosen, preferred_element_type=f32)
        wide = jnp.where(tap_y == j, full, wide)
    wide_ref[...] = wide.astype(bf16)


def feature_kernel(plan, wide_ref, g_ref, after_ref, gf_ref):
    del after_ref
    width = plan.nx // PARTS
    for n in range(PARTS):
        out = jnp.dot(
            wide_ref[...],
            moved_columns(g_ref, n * width, width),
            preferred_element_type=f32,
        )
        for x in range(width):
            part = out[:, x * plan.nz : (x + 1) * plan.nz].astype(bf16)
            gf_ref[:, n * width + x] = part.reshape(plan.ch, plan.ny, plan.nz)


def final_kernel(plan, got_ref, gw_ref, gb_ref):
    total = jnp.sum(got_ref[...], axis=0)
    for n in range(4):
        count = min(8, 27 - 8 * n)
        gw_ref[8 * n : 8 * n + count] = total[:count, 32 * n : 32 * n + plan.ch]
    gb_ref[...] = total[3:4, 96:97]


VMEM = pl.BlockSpec(memory_space=pltpu.VMEM)
SMEM = pl.BlockSpec(memory_space=pltpu.SMEM)
ANY = pl.BlockSpec(memory_space=pl.ANY)
FAR = pl.BlockSpec(memory_space=pltpu.HBM)
MIB = 1024 * 1024


def shape(dims, dtype=f32):
    return jax.ShapeDtypeStruct(dims, dtype)


def held(dims, dtype):
    if len(dims) < 2:
        return 4096
    size = jnp.dtype(dtype).itemsize
    rows = 8 * 4 // size
    total = -(-dims[-2] // rows) * rows * -(-dims[-1] // LANES) * LANES * size
    for n in dims[:-2]:
        total *= n
    return total


def limits(arrays, scratch, micros):
    total = sum(held(a.shape, a.dtype) for a in arrays)
    total += sum(held(a.shape, a.dtype) for a in scratch if len(a.shape) > 1)
    limit = min(63 * MIB, total + total // 8 + 4 * MIB)
    return dict(
        compiler_params=pltpu.CompilerParams(vmem_limit_bytes=limit),
        cost_estimate=pl.CostEstimate(
            flops=0, transcendentals=0, bytes_accessed=int(micros * 2.5e4)
        ),
    )


def per_device(mesh_shape, features, weight, bias, label):
    plan = Plan(mesh_shape, features.shape)
    members, sent, tiles = plan.members, plan.sent, plan.tiles
    inner, bands = plan.ch * plan.ny, 9 * plan.Y
    x, y, z = (lax.axis_index(axis).astype(jnp.int32) for axis in ALL_AXES)
    mine = y * plan.gx + jnp.where(y % 2 == 0, x, plan.gx - 1 - x)
    place = z * members + jnp.where(z % 2 == 0, mine, members - 1 - mine)
    pos = jnp.stack([place, y])

    def call(
        kernel, out_shape, in_specs, operands, micros, scratch=(), out_specs=None
    ):
        outs = jax.tree.leaves(out_shape)
        ins = [a for spec, a in zip(in_specs, operands) if spec is VMEM]
        return pl.pallas_call(
            functools.partial(kernel, plan),
            out_shape=out_shape,
            in_specs=in_specs,
            out_specs=out_specs or jax.tree.map(lambda s: VMEM, out_shape),
            scratch_shapes=list(scratch),
            **limits(ins + outs, scratch, micros),
        )(*operands)

    def exchange(array):
        return lax.all_to_all(array, GROUP, 0, 0, tiled=True)

    def everywhere(array):
        return lax.all_to_all(array, ALL_AXES, 0, 0, tiled=True)

    def hop(array, distance):
        def device(r):
            z = r // members
            return plan.member(r % members, z % 2 == 1) * plan.gz + z

        pairs = [
            (device(r), device(r + distance))
            for r in range(plan.ranks)
            if 0 <= r + distance < plan.ranks
        ]
        return lax.ppermute(array, ALL_AXES, pairs)

    turned = weight.T
    features, weight, label = (
        pltpu.with_memory_space_constraint(a, pltpu.HBM) for a in (features, weight, label)
    )
    features_near = [pltpu.VMEM(features.shape, bf16), pltpu.SemaphoreType.DMA((PARTS,))]
    sent_logits = call(
        conv_kernel,
        shape((members, sent + plan.extra, plan.R, LANES)),
        [SMEM, VMEM, FAR, VMEM],
        (pos, weight, features, label),
        7,
        [
            pltpu.VMEM((bands, inner), bf16),
            pltpu.VMEM((plan.nx + 2, 3 * plan.Y, plan.nz), f32),
        ]
        + features_near,
    )

    def planes(array):
        return array.reshape(-1, tiles, LANES)

    zc, rest = plan.zc, plan.rest
    short = shape(((rest + 1 + -(-rest // 2)) * tiles, LANES))
    whole, label_own, head, tail = call(
        gather_kernel,
        [
            shape(((zc + 2 + -(-zc // 2)) * tiles, LANES)),
            shape((zc * tiles, LANES)),
            short,
            short,
        ],
        [VMEM],
        (exchange(sent_logits),),
        1.5,
    )
    whole, label_own, head, tail = (planes(part) for part in (whole, label_own, head, tail))
    around = [
        hop(whole if h < plan.hops else part, sign * h)
        for sign, part in ((1, tail), (-1, head))
        for h in range(1, plan.hops + 1)
    ]

    slab = (zc, tiles, LANES)
    span = (plan.span, tiles, LANES)
    everyone = shape((plan.ranks, 1, LANES))
    table = pltpu.VMEM((3, tiles, LANES), f32)

    records = pltpu.HBM((SECTIONS, plan.records, tiles, LANES), f32)
    y_near = pltpu.VMEM((2 * LANES, LANES), bf16)
    record_near = [
        y_near,
        pltpu.VMEM(records.shape, f32),
        pltpu.SemaphoreType.DMA((SECTIONS,)),
    ]
    record, predict, sums = call(
        forward_kernel,
        [records, shape(span), everyone],
        [SMEM, SMEM] + [VMEM] * (2 + 2 * plan.hops),
        (pos, bias, label_own, whole, *around),
        11,
        [
            pltpu.VMEM((plan.planes, plan.pad, LANES), f32),
            pltpu.VMEM((plan.planes, plan.pad, LANES), f32),
            pltpu.VMEM((plan.planes, tiles, LANES), f32),
            pltpu.VMEM((plan.planes, tiles, LANES), f32),
            pltpu.VMEM((zc, plan.pad, LANES), f32),
            pltpu.VMEM(slab, f32),
            table,
            table,
        ]
        + record_near,
        [FAR, VMEM, VMEM],
    )
    record = pltpu.with_memory_space_constraint(record, pltpu.HBM)
    sums = everywhere(sums)
    room = plan.win + 2 + plan.erode_block
    target, ts, skel_sums = call(
        target_kernel,
        [shape(span), shape(span), everyone],
        [SMEM] + [VMEM] * (2 + 2 * plan.hops),
        (pos, predict, label_own, *around),
        13,
        [
            pltpu.VMEM((plan.win, tiles, LANES), f32),
            pltpu.VMEM((room, plan.pad, LANES), f32),
            pltpu.VMEM((room, plan.pad, LANES), f32),
            pltpu.VMEM((room, tiles, LANES), f32),
            pltpu.VMEM((plan.span, plan.pad, LANES), f32),
            table,
            table,
            y_near,
        ],
    )
    skel_sums = everywhere(skel_sums)
    outer = [
        shape((plan.back_count(h), tiles, LANES)) for h in range(1, plan.back_hops + 1)
    ]
    mine, *outer = call(
        backward_kernel,
        [shape(span)] + outer * 2,
        [SMEM, VMEM, VMEM, FAR],
        (pos, sums, label_own, record),
        11,
        [
            pltpu.VMEM(slab, f32),
            pltpu.VMEM((zc + 4, tiles, LANES), f32),
            pltpu.VMEM((plan.pull_planes, tiles, LANES), f32),
            pltpu.VMEM((plan.span, plan.pad, LANES), f32),
            pltpu.VMEM((plan.pull_planes, plan.pad, LANES), f32),
            pltpu.VMEM((plan.pull_planes, plan.pad, LANES), f32),
            table,
        ]
        + record_near,
    )
    wide = call(
        wide_kernel, shape((inner, bands), bf16), [SMEM, VMEM, ANY], (pos, turned, mine), 2
    )
    beyond = []
    for sign, arrays in ((1, outer[: plan.back_hops]), (-1, outer[plan.back_hops :])):
        for h in range(1, plan.back_hops + 1):
            beyond.append(hop(arrays[h - 1], sign * h))
    grad_sent, loss, bias_part = call(
        finish_kernel,
        [
            shape((members, sent + plan.extra16, plan.R16, LANES), bf16),
            shape((8, LANES)),
            shape((8, LANES)),
        ],
        [SMEM] + [VMEM] * (6 + 2 * plan.back_hops),
        (pos, sums, skel_sums, predict, target, ts, mine, *beyond),
        2,
        [pltpu.VMEM(span, f32), pltpu.VMEM((plan.span * tiles, LANES), f32)],
    )

    features_ahead = call(
        fetch_kernel,
        pltpu.VMEM(features.shape, bf16),
        [FAR, ANY],
        (features, bias_part),
        1,
        [pltpu.SemaphoreType.DMA((1,))],
    )
    moved = shape((plan.nx + 2, 3 * plan.Y, plan.nz), bf16)
    partial, g = call(
        weight_kernel,
        [shape((plan.ranks, 8, LANES)), moved],
        [SMEM, VMEM, VMEM, VMEM],
        (pos, features_ahead, bias_part, exchange(grad_sent)),
        5,
        [pltpu.VMEM((bands, inner), f32)],
    )
    grad_features = call(
        feature_kernel,
        shape(features.shape, bf16),
        [VMEM, VMEM, ANY],
        (wide, g, partial),
        5,
    )
    grad_weight, grad_bias = call(
        final_kernel,
        [shape((27, plan.ch)), shape((1, 1))],
        [VMEM],
        (everywhere(partial),),
        1.5,
    )
    return (loss[0, :1], grad_features, grad_weight, grad_bias.reshape(1))


def solution(mesh):
    in_specs = (P(None, "gx", "gy", "gz"), P(), P(), P("gx", "gy", "gz"))
    out_specs = (P(), P(None, "gx", "gy", "gz"), P(), P())

    def body(*args):
        return per_device(dict(mesh.shape), *args)

    return jax.shard_map(
        body, mesh=mesh, in_specs=in_specs, out_specs=out_specs, check_vma=False
    )
```
